32 devices in a mesh: dp: 4 (over y, x), seq: 8 (over z, core).
Axes of the slice: x: 2, y: 2, z: 4, core: 2. Of those that a mesh axis runs over, the one named last changes fastest.
Arguments:
- tokens: bfloat16 [4, 1024, 2048], P('dp', 'seq'), may hold values from -6 to 6
- qkv_weight: bfloat16 [2048, 3072], P(('dp', 'seq')), may hold values from -0.125 to 0.125
- out_weight: bfloat16 [2048, 2048], P(('dp', 'seq')), may hold values from -1 to 1
- gate_weight: bfloat16 [8192, 2048], P(('dp', 'seq')), may hold values from -0.125 to 0.125
- up_weight: bfloat16 [8192, 2048], P(('dp', 'seq')), may hold values from -0.125 to 0.125
- down_weight: bfloat16 [8192, 2048], P(('dp', 'seq')), may hold values from -0.0625 to 0.0625
- attn_gain: bfloat16 [2048], P(('dp', 'seq')), may hold values from 0.5 to 1.5
- mlp_gain: bfloat16 [2048], P(('dp', 'seq')), may hold values from 0.5 to 1.5
- cotangent: bfloat16 [4, 1024, 2048], P('dp', 'seq'), may hold values from -6 to 6
Outputs:
- block_out: bfloat16 [4, 1024, 2048], P('dp', 'seq')
- grad_tokens: float32 [4, 1024, 2048], P('dp', 'seq')
- grad_qkv: float32 [2048, 3072], P(('dp', 'seq'))
- grad_out: float32 [2048, 2048], P(('dp', 'seq'))
- grad_gate: float32 [8192, 2048], P(('dp', 'seq'))
- grad_up: float32 [8192, 2048], P(('dp', 'seq'))
- grad_down: float32 [8192, 2048], P(('dp', 'seq'))
- grad_attn_gain: float32 [2048], P(('dp', 'seq'))
- grad_mlp_gain: float32 [2048], P(('dp', 'seq'))
The draws below stay inside these ranges and needn't reach their ends.
All inputs are finite; a program needn't handle non-finite values.
Results may differ from the reference program's by a relative error of at most 0.017.
Values may be sent and summed in bfloat16 or wider, within the bound.
A program may use at most 192 MiB of HBM per device.

```python
import jax
import jax.numpy as jnp
from jax import lax

D = 2048
HEADS = 32
KV_HEADS = 8
HEAD_DIM = 64
FF = 8192
LEN = 1024
SEQS = 4
QKV_W = 3072


def steps_of(own_key, shape, shards, low, largest):
    def one(axis_at, parts):
        heights = jax.random.uniform(jax.random.fold_in(jax.random.fold_in(own_key, 6), axis_at), (parts,), jnp.float32, low / len(shards), largest / len(shards))
        return jnp.repeat(jnp.exp(heights), shape[axis_at] // parts).reshape((-1,) + (1,) * (len(shape) - axis_at - 1))

    factor_of = one(*shards[0])
    for cut in shards[1:]:
        factor_of = factor_of * one(*cut)
    return factor_of


def bell_draw(stream_key, dims, scale, most, cuts=(), kind=jnp.bfloat16):
    entries = jax.random.normal(stream_key, dims, jnp.float32) * scale
    if len(cuts) > 0:
        entries = steps_of(stream_key, dims, cuts, -0.22, 0.18) * entries
    return jnp.clip(entries, min=-most, max=most).astype(kind)


def setup_inputs(seed: int = 0) -> dict:
    splits = jax.random.split(jax.random.key(seed), 10)
    return {
        "tokens": bell_draw(splits[0], (SEQS, LEN, D), 1.0, 6.0, ((0, 4), (1, 8))),
        "qkv_weight": bell_draw(splits[1], (D, QKV_W), D ** -0.5, 0.125, ((0, 32),)),
        "out_weight": bell_draw(splits[2], (D, D), (max(1, D * 16 // LEN)) ** -0.5, 1.0, ((0, 32),)),
        "gate_weight": bell_draw(splits[3], (FF, D), D ** -0.5, 0.125, ((0, 32),)),
        "up_weight": bell_draw(splits[4], (FF, D), D ** -0.5, 0.125, ((0, 32),)),
        "down_weight": bell_draw(splits[5], (FF, D), FF ** -0.5, 0.0625, ((0, 32),)),
        "attn_gain": jnp.clip(1.0 + 0.1 * jax.random.normal(splits[6], (D,), jnp.float32), 0.5, 1.5).astype(jnp.bfloat16),
        "mlp_gain": jnp.clip(1.0 + 0.1 * jax.random.normal(splits[7], (D,), jnp.float32), 0.5, 1.5).astype(jnp.bfloat16),
        "cotangent": bell_draw(splits[8], (SEQS, LEN, D), 1.0, 6.0, ((0, 4), (1, 8))),
    }


@jax.custom_vjp
def low(v):
    return lax.optimization_barrier(v.astype(jnp.bfloat16)).astype(jnp.float32)

@jax.custom_vjp
def low_back(v):
    return v

def low_keep(v):
    return (low(v), None)

def low_pass(kept, grad):
    return (grad,)

def back_keep(v):
    return (v, None)

def back_low(kept, grad):
    return (low(grad),)
low.defvjp(low_keep, low_pass)
low_back.defvjp(back_keep, back_low)
epsilon = 1e-05
rope_base = 500000.0
masked_value = -1e+30
contract_cols = (((1,), (1,)), ((), ()))

def matmul(left, right):
    return jnp.dot(left, right, precision=lax.Precision.HIGHEST, preferred_element_type=jnp.float32)

def matmul_cols(left, right):
    return lax.dot_general(left, right, contract_cols, precision=lax.Precision.HIGHEST, preferred_element_type=jnp.float32)

def rms_scale(values, gain):
    return values * lax.rsqrt(lax.optimization_barrier(jnp.mean(values * values, axis=-1, keepdims=True)) + epsilon) * gain

def rope_tables(positions, head_width):
    half_width = head_width // 2
    frequency = rope_base ** (-2.0 * jnp.arange(half_width, dtype=jnp.float32) / head_width)
    angles = positions.astype(jnp.float32)[:, None] * frequency[None, :]
    return (jnp.cos(angles)[:, None, :], jnp.sin(angles)[:, None, :])

def rotate(values, cosine_table, sine_table):
    half_width = values.shape[-1] // 2
    first_half = values[..., :half_width]
    second_half = values[..., half_width:]
    return jnp.concatenate([first_half * cosine_table - second_half * sine_table, second_half * cosine_table + first_half * sine_table], axis=-1)

def layer(sequence, qkv_weight, out_weight, gate_weight, up_weight, down_weight, attn_gain, mlp_gain):
    seq_len = sequence.shape[0]
    kv_width = KV_HEADS * HEAD_DIM
    score_scale = HEAD_DIM ** (-0.5)
    normed = low(rms_scale(sequence, attn_gain))
    mixed = low_back(matmul(normed, qkv_weight))
    cosine_table, sine_table = rope_tables(jnp.arange(seq_len, dtype=jnp.int32), HEAD_DIM)
    queries = low(rotate(mixed[:, :D].reshape(seq_len, HEADS, HEAD_DIM), cosine_table, sine_table))
    keys = low(rotate(mixed[:, D:D + kv_width].reshape(seq_len, KV_HEADS, HEAD_DIM), cosine_table, sine_table))
    values = low(mixed[:, D + kv_width:].reshape(seq_len, KV_HEADS, HEAD_DIM))
    keys = jnp.repeat(keys, HEADS // KV_HEADS, axis=1)
    values = jnp.repeat(values, HEADS // KV_HEADS, axis=1)
    block_rows = min(256, seq_len)
    block_count = seq_len // block_rows
    query_blocks = queries.reshape(block_count, block_rows, HEADS, HEAD_DIM)
    block_starts = jnp.arange(block_count, dtype=jnp.int32) * block_rows

    def attend(inputs_pair):
        query_block, block_start = inputs_pair
        scores = jnp.einsum('qhd,khd->hqk', query_block, keys, precision=lax.Precision.HIGHEST) * score_scale
        scores = low_back(scores)
        rows_at = block_start + jnp.arange(block_rows, dtype=jnp.int32)
        cols_at = jnp.arange(seq_len, dtype=jnp.int32)
        allowed = (cols_at[None, :] <= rows_at[:, None])[None]
        scores = jnp.where(allowed, scores, masked_value)
        probs = low(jax.nn.softmax(scores, axis=-1))
        return jnp.einsum('hqk,khd->qhd', probs, values, precision=lax.Precision.HIGHEST)
    attended = lax.map(jax.checkpoint(attend), (query_blocks, block_starts)).reshape(seq_len, D)
    attended = low_back(low(attended))
    hidden = sequence + low_back(matmul(attended, out_weight))
    normed_two = low(rms_scale(hidden, mlp_gain))
    gate = low_back(matmul_cols(normed_two, gate_weight))
    upward = low_back(matmul_cols(normed_two, up_weight))
    inner = low(jax.nn.silu(gate) * upward)
    return hidden + low_back(matmul(inner, down_weight))

def reference(tokens, qkv_weight, out_weight, gate_weight, up_weight, down_weight, attn_gain, mlp_gain, cotangent):
    params = (qkv_weight.astype(jnp.float32), out_weight.astype(jnp.float32), gate_weight.astype(jnp.float32), up_weight.astype(jnp.float32), down_weight.astype(jnp.float32), attn_gain.astype(jnp.float32), mlp_gain.astype(jnp.float32))

    def one_sequence(totals, inputs_pair):
        sequence, gradient = inputs_pair
        result, pullback = jax.vjp(layer, sequence.astype(jnp.float32), *params)
        gradients = pullback(gradient.astype(jnp.float32))
        new_totals = tuple((running + extra for running, extra in zip(totals, gradients[1:])))
        return (new_totals, (result.astype(jnp.bfloat16), gradients[0]))
    zeros = tuple((jnp.zeros_like(param) for param in params))
    totals, outputs = lax.scan(one_sequence, zeros, (tokens, cotangent))
    return (outputs[0], outputs[1], totals[0], totals[1], totals[2], totals[3], totals[4], totals[5], totals[6])
```

```python
import functools

import jax
import jax.numpy as jnp
from jax import lax
from jax.experimental import pallas as pl
from jax.experimental.pallas import tpu as pltpu
from jax.sharding import PartitionSpec as P

HEADS = 32
KV_HEADS = 8
HEAD_DIM = 64

MESH = pl.DeviceIdType.MESH
ANY = pl.BlockSpec(memory_space=pl.ANY)
VM = pl.BlockSpec(memory_space=pltpu.VMEM)
SUB = 2

epsilon = 1e-05
rope_base = 500000.0
masked_value = -1e30
contract_rows = (((0,), (0,)), ((), ()))
contract_cols = (((1,), (1,)), ((), ()))


class Place:
    def __init__(self, dps, groups):
        self.dps, self.groups, self.chips, self.hops = dps, groups, groups // 2, dps // 2
        self.d, self.s = lax.axis_index("dp"), lax.axis_index("seq")
        self.chip, self.core = self.s // 2, self.s % 2
        self.partner = 2 * self.chip + 1 - self.core
        row, side = self.d // 2, self.d % 2
        self.turn = side * (dps - 1 - row) + (1 - side) * row

    def ring(self, distance):
        at = (self.turn + distance + self.dps) % self.dps
        side = at // self.hops
        return (1 - side) * 2 * at + side * (2 * (self.dps - 1 - at) + 1)


def remote(src, dst, send, recv, **target):
    return pltpu.make_async_remote_copy(
        src_ref=src, dst_ref=dst, send_sem=send, recv_sem=recv, device_id=target, device_id_type=MESH
    )


def greet_near(place):
    barrier = pltpu.get_barrier_semaphore()

    def signal(**target):
        pl.semaphore_signal(barrier, inc=1, device_id=target, device_id_type=MESH)

    signal(seq=place.partner)
    signal(dp=place.ring(1))
    signal(dp=place.ring(-1))

    @pl.when(place.chip > 0)
    def _():
        signal(seq=place.s - 2)

    @pl.when(place.chip < place.chips - 1)
    def _():
        signal(seq=place.s + 2)

    ends = (place.chips - place.chip) // place.chips + (place.chip + 1) // place.chips
    pl.semaphore_wait(barrier, 5 - ends)


def greet_all(place):
    barrier = pltpu.get_barrier_semaphore()
    count = place.dps * place.groups
    me = place.d * place.groups + place.s

    def signal(i, _):
        other = (me + i) % count
        pl.semaphore_signal(
            barrier,
            inc=1,
            device_id={"dp": other // place.groups, "seq": other % place.groups},
            device_id_type=MESH,
        )
        return 0

    lax.fori_loop(1, count, signal, 0)
    pl.semaphore_wait(barrier, count - 1)


DMA = pltpu.SemaphoreType.DMA


class LineGather:
    def __init__(self, x, dps, groups):
        rows, width = x.shape
        shape = (SUB, rows // SUB, width)
        self.inputs, self.in_specs = [x.reshape(shape)], [VM]
        self.outs, self.out_specs = [jax.ShapeDtypeStruct((groups,) + shape, x.dtype)], [ANY]
        self.scratch = [DMA] + [DMA((groups // 2, SUB))] * 6
        self.result = lambda out: out.reshape(groups * rows, width)

    def bind(self, place, x_ref, out_ref, own_sem, us, ur, ds, dr, ps, pr):
        s, chip, chips = place.s, place.chip, place.chips

        def copy(src, group, half, sends, recvs, at, target):
            return remote(
                src, out_ref.at[group, half], sends.at[at, half], recvs.at[at, half], seq=target
            )

        def up(src, group, hop, half):
            return copy(src, group, half, us, ur, hop, s + 2)

        def down(src, group, hop, half):
            return copy(src, group, half, ds, dr, hop, s - 2)

        def pair(src, group, half):
            return copy(src, group, half, ps, pr, group // 2, place.partner)

        own = pltpu.make_async_copy(x_ref, out_ref.at[s], own_sem)

        def start():
            own.start()
            for half in range(SUB):

                @pl.when(chip < chips - 1)
                def _():
                    up(x_ref.at[half], s, 0, half).start()

                @pl.when(chip > 0)
                def _():
                    down(x_ref.at[half], s, 0, half).start()

            for half in range(SUB):
                pair(x_ref.at[half], s, half).start()

        def step(hop, half):
            below, above = s - 2 * hop, s + 2 * hop

            @pl.when(chip - hop >= 0)
            def _():
                block = out_ref.at[below, half]
                up(block, below, hop - 1, half).wait_recv()

                @pl.when(chip < chips - 1)
                def _():
                    up(block, below, hop, half).start()

                pair(block, below, half).start()

            @pl.when(chip + hop < chips)
            def _():
                block = out_ref.at[above, half]
                down(block, above, hop - 1, half).wait_recv()

                @pl.when(chip > 0)
                def _():
                    down(block, above, hop, half).start()

                pair(block, above, half).start()

        def finish():
            own.wait()

            def each(i, _):
                k, half = i // SUB, i % SUB
                mine, other = 2 * k + place.core, 2 * k + 1 - place.core
                block = out_ref.at[mine, half]
                pair(block, other, half).wait_recv()
                pair(block, mine, half).wait_send()

                @pl.when(jnp.logical_and(chip - k >= 0, chip < chips - 1))
                def _():
                    up(block, mine, k, half).wait_send()

                @pl.when(jnp.logical_and(chip + k < chips, chip > 0))
                def _():
                    down(block, mine, k, half).wait_send()

                return 0

            lax.fori_loop(0, chips * SUB, each, 0)

        ticks = {
            (hop - 1) * SUB + half: functools.partial(step, hop, half)
            for hop in range(1, chips)
            for half in range(SUB)
        }
        return start, ticks, finish


class LineScatter:
    def __init__(self, partial, dps, groups):
        total, width = partial.shape
        rows, chips = total // groups, groups // 2
        shape = (SUB, rows // SUB, width)
        self.inputs, self.in_specs = [partial.reshape((groups,) + shape)], [VM]
        self.outs, self.out_specs = [jax.ShapeDtypeStruct(shape, jnp.float32)], [VM]
        self.scratch = [pltpu.VMEM((chips,) + shape, jnp.bfloat16)] * 5 + [DMA((chips, SUB))] * 6
        self.result = lambda out: out.reshape(rows, width)

    def bind(
        self, place, p_ref, out_ref, pairbuf, upbuf, downbuf, usend, dsend, us, ur, ds, dr, ps, pr
    ):
        s, chip, chips, core = place.s, place.chip, place.chips, place.core

        def copy(src, buffer, at, half, sends, recvs, target):
            return remote(
                src, buffer.at[at, half], sends.at[at, half], recvs.at[at, half], seq=target
            )

        def pair(at, half):
            src = p_ref.at[2 * at + 1 - core, half]
            return copy(src, pairbuf, at, half, ps, pr, place.partner)

        def up(at, half):
            return copy(usend.at[at, half], upbuf, at, half, us, ur, s + 2)

        def down(at, half):
            return copy(dsend.at[at, half], downbuf, at, half, ds, dr, s - 2)

        def wide(ref, *at):
            return ref[at].astype(jnp.float32)

        def local(at, half):
            return wide(p_ref, 2 * at + core, half) + wide(pairbuf, at, half)

        def start():
            def issue(i, _):
                low, half = i // SUB, i % SUB
                high = chips - 1 - low

                @pl.when(high > chip)
                def _():
                    pair(high, half).start()

                @pl.when(low < chip)
                def _():
                    pair(low, half).start()

                return 0

            lax.fori_loop(0, (chips - 1) * SUB, issue, 0)
            for half in range(SUB):
                pair(chip, half).start()

        def step(i):
            low, half = i // SUB, i % SUB
            high = chips - 1 - low

            @pl.when(high > chip)
            def _():
                pair(high, half).wait_recv()

                @pl.when(chip > 0)
                def _():
                    up(high, half).wait_recv()
                    total = local(high, half) + wide(upbuf, high, half)
                    usend[high, half] = total.astype(jnp.bfloat16)

                @pl.when(chip == 0)
                def _():
                    usend[high, half] = local(high, half).astype(jnp.bfloat16)

                up(high, half).start()

            @pl.when(low < chip)
            def _():
                pair(low, half).wait_recv()

                @pl.when(chip < chips - 1)
                def _():
                    down(low, half).wait_recv()
                    total = local(low, half) + wide(downbuf, low, half)
                    dsend[low, half] = total.astype(jnp.bfloat16)

                @pl.when(chip == chips - 1)
                def _():
                    dsend[low, half] = local(low, half).astype(jnp.bfloat16)

                down(low, half).start()

        def finish():
            for half in range(SUB):
                pair(chip, half).wait_recv()
                out_ref[half] = local(chip, half)

                @pl.when(chip > 0)
                def _():
                    up(chip, half).wait_recv()
                    out_ref[half] += wide(upbuf, chip, half)

                @pl.when(chip < chips - 1)
                def _():
                    down(chip, half).wait_recv()
                    out_ref[half] += wide(downbuf, chip, half)

            def each(i, _):
                at, half = i // SUB, i % SUB
                pair(at, half).wait_send()

                @pl.when(at > chip)
                def _():
                    up(at, half).wait_send()

                @pl.when(at < chip)
                def _():
                    down(at, half).wait_send()

                return 0

            lax.fori_loop(0, chips * SUB, each, 0)

        return start, {i: functools.partial(step, i) for i in range((chips - 1) * SUB)}, finish


def ring_sems(hops):
    return [DMA((hops, 2))] * 4


def ring_gather(place, own, out, rs, rr, ls, lr):
    hops = place.hops

    def right(src, chunk, hop, half):
        return remote(
            src, out(chunk, half), rs.at[hop - 1, half], rr.at[hop - 1, half], dp=place.ring(1)
        )

    def left(src, chunk, hop, half):
        return remote(
            src, out(chunk, half), ls.at[hop - 1, half], lr.at[hop - 1, half], dp=place.ring(-1)
        )

    def start():
        for half in range(2):
            right(own(half), place.d, 1, half).start()
            left(own(1 - half), place.d, 1, 1 - half).start()

    def forward(hop):
        before, after = place.ring(-hop), place.ring(hop)
        full = hop < hops - 1
        right(out(before, 0), before, hop, 0).wait_recv()
        right(out(before, 0), before, hop + 1, 0).start()
        left(out(after, 1), after, hop, 1).wait_recv()
        left(out(after, 1), after, hop + 1, 1).start()
        right(out(before, 1), before, hop, 1).wait_recv()
        left(out(after, 0), after, hop, 0).wait_recv()
        if full:
            right(out(before, 1), before, hop + 1, 1).start()
            left(out(after, 0), after, hop + 1, 0).start()

    def finish():
        right(out(place.d, 0), place.ring(-hops), hops, 0).wait_recv()
        left(out(place.d, 1), place.ring(hops), hops, 1).wait_recv()
        for hop in range(1, hops + 1):
            for half in range(2):
                if hop < hops or half == 0:
                    right(out(place.d, half), place.d, hop, half).wait_send()
                if hop < hops or half == 1:
                    left(out(place.d, half), place.d, hop, half).wait_send()

    return start, forward, finish


def ring_scatter(place, part, put, rbuf, lbuf, rout, lout, rs, rr, ls, lr):
    hops = place.hops

    def wide(ref):
        return ref[...].astype(jnp.float32)

    def right(src, hop, half):
        return remote(
            src,
            rbuf.at[hop - 1, half],
            rs.at[hop - 1, half],
            rr.at[hop - 1, half],
            dp=place.ring(1),
        )

    def left(src, hop, half):
        return remote(
            src,
            lbuf.at[hop - 1, half],
            ls.at[hop - 1, half],
            lr.at[hop - 1, half],
            dp=place.ring(-1),
        )

    def start():
        right(part(place.ring(hops), 0), hops, 0).start()
        left(part(place.ring(-hops), 1), hops, 1).start()
        right(part(place.ring(hops - 1), 1), hops - 1, 1).start()
        left(part(place.ring(1 - hops), 0), hops - 1, 0).start()

    def forward(hop):
        for first in range(2 if hop < hops - 1 else 1):
            half = first
            right(rbuf.at[hop, half], hop + 1, half).wait_recv()
            total = wide(part(place.ring(hop), half)) + wide(rbuf.at[hop, half])
            rout[hop - 1, half] = total.astype(jnp.bfloat16)
            right(rout.at[hop - 1, half], hop, half).start()
            half = 1 - first
            left(lbuf.at[hop, half], hop + 1, half).wait_recv()
            total = wide(part(place.ring(-hop), half)) + wide(lbuf.at[hop, half])
            lout[hop - 1, half] = total.astype(jnp.bfloat16)
            left(lout.at[hop - 1, half], hop, half).start()

    def finish():
        for half in range(2):
            right(rbuf.at[0, half], 1, half).wait_recv()
            left(lbuf.at[0, half], 1, half).wait_recv()
            put(
                half,
                wide(part(place.d, half)) + wide(rbuf.at[0, half]) + wide(lbuf.at[0, half]),
            )
        for hop in range(1, hops + 1):
            for half in range(2):
                if hop < hops or half == 0:
                    right(rbuf.at[0, half], hop, half).wait_send()
                if hop < hops or half == 1:
                    left(lbuf.at[0, half], hop, half).wait_send()

    return start, forward, finish


class RingGather:
    def __init__(self, x, dps, groups):
        rows, width = x.shape
        shape = (2, rows // 2, width)
        self.inputs, self.in_specs = [x.reshape(shape)], [VM]
        self.outs, self.out_specs = [jax.ShapeDtypeStruct((dps,) + shape, x.dtype)], [ANY]
        self.scratch = [DMA] + ring_sems(dps // 2)
        self.result = lambda out: out.reshape(dps * rows, width)

    def bind(self, place, x_ref, out_ref, own_sem, *sems):
        own = pltpu.make_async_copy(x_ref, out_ref.at[place.d], own_sem)
        ring = ring_gather(
            place, lambda half: x_ref.at[half], lambda chunk, half: out_ref.at[chunk, half], *sems
        )

        def start():
            ring[0]()
            own.start()

        def finish():
            own.wait()
            ring[2]()

        ticks = {2 * hop - 1: functools.partial(ring[1], hop) for hop in range(1, place.hops)}
        return start, ticks, finish


class RingScatter:
    def __init__(self, partial, dps, groups):
        total, width = partial.shape
        rows, hops = total // dps, dps // 2
        shape = (2, rows // 2, width)
        self.inputs, self.in_specs = [partial.reshape((dps,) + shape)], [VM]
        self.outs, self.out_specs = [jax.ShapeDtypeStruct(shape, jnp.float32)], [VM]
        self.scratch = (
            [pltpu.VMEM((hops,) + shape, jnp.bfloat16)] * 2
            + [pltpu.VMEM((hops - 1,) + shape, jnp.bfloat16)] * 2
            + ring_sems(hops)
        )
        self.result = lambda out: out.reshape(rows, width)

    def bind(self, place, p_ref, out_ref, *scratch):
        def put(half, value):
            out_ref[half] = value

        ring = ring_scatter(place, lambda chunk, half: p_ref.at[chunk, half], put, *scratch)
        ticks = {
            2 * (place.hops - hop) - 1: functools.partial(ring[1], hop)
            for hop in range(1, place.hops)
        }
        return ring[0], ticks, ring[2]


class Columns:
    def __init__(self, blocks, dps, groups):
        _, rows, width = blocks.shape
        self.inputs, self.in_specs = [blocks], [VM]
        self.outs = [jax.ShapeDtypeStruct((dps, groups, rows, width), blocks.dtype)]
        self.out_specs = [ANY]
        self.scratch = [
            pltpu.VMEM((groups, rows, width), blocks.dtype),
            DMA((2,)),
            DMA((groups,)),
            DMA((groups,)),
        ] + ring_sems(dps // 2)
        self.result = lambda out: out.reshape(dps * groups * rows, width)

    def bind(self, place, x_ref, out_ref, landing, own_sem, sends, recvs, *sems):
        s, groups = place.s, place.groups
        half_of = groups // 2
        here = pltpu.make_async_copy(x_ref.at[s], landing.at[s], own_sem.at[0])
        own = pltpu.make_async_copy(landing, out_ref.at[place.d], own_sem.at[1])

        def swap(i):
            to = (s + i) % groups
            return remote(x_ref.at[to], landing.at[s], sends.at[i], recvs.at[i], seq=to)

        ring = ring_gather(
            place,
            lambda half: landing.at[pl.ds(half * half_of, half_of)],
            lambda chunk, half: out_ref.at[chunk, pl.ds(half * half_of, half_of)],
            *sems,
        )

        def start():
            here.start()
            for i in range(1, groups):
                swap(i).start()

        def middle():
            here.wait()
            for i in range(1, groups):
                swap(i).wait_recv()
            ring[0]()
            own.start()

        def finish():
            for i in range(1, groups):
                swap(i).wait_send()
            own.wait()
            ring[2]()

        ticks = {1 + 2 * hop: functools.partial(ring[1], hop) for hop in range(1, place.hops)}
        ticks[1] = middle
        return start, ticks, finish


class ColumnsBack:
    def __init__(self, partial, rows, dps, groups):
        width, hops = partial.shape[1], dps // 2
        shape = (groups, rows, width)
        halves = (2, groups // 2, rows, width)
        self.inputs, self.in_specs = [partial.reshape((dps,) + halves)], [VM]
        self.outs, self.out_specs = [jax.ShapeDtypeStruct(shape, jnp.bfloat16)], [ANY]
        self.scratch = (
            [pltpu.VMEM(halves, jnp.bfloat16), DMA, DMA((groups,)), DMA((groups,))]
            + [pltpu.VMEM((hops,) + halves, jnp.bfloat16)] * 2
            + [pltpu.VMEM((hops - 1,) + halves, jnp.bfloat16)] * 2
            + ring_sems(hops)
        )
        self.result = lambda out: out

    def bind(self, place, p_ref, out_ref, total, own_sem, sends, recvs, *scratch):
        s, groups = place.s, place.groups
        half_of = groups // 2

        def put(half, value):
            total[half] = value.astype(jnp.bfloat16)

        ring = ring_scatter(place, lambda chunk, half: p_ref.at[chunk, half], put, *scratch)
        here = pltpu.make_async_copy(
            total.at[s // half_of, s % half_of], out_ref.at[s], own_sem
        )

        def swap(i):
            to = (s + i) % groups
            src = total.at[to // half_of, to % half_of]
            return remote(src, out_ref.at[s], sends.at[i], recvs.at[i], seq=to)

        def last():
            ring[2]()
            here.start()
            for i in range(1, groups):
                swap(i).start()

        def finish():
            here.wait()
            for i in range(1, groups):
                swap(i).wait_recv()
                swap(i).wait_send()

        ticks = {
            2 * (place.hops - hop) - 1: functools.partial(ring[1], hop)
            for hop in range(1, place.hops)
        }
        ticks[2 * place.hops - 1] = last
        return ring[0], ticks, finish


class Rows:
    def __init__(self, x, dps, groups):
        rows, width = x.shape
        shape = (2, rows // 2, width)
        self.inputs, self.in_specs = [x.reshape(shape)], [VM]
        self.outs, self.out_specs = [jax.ShapeDtypeStruct((dps,) + shape, x.dtype)], [ANY]
        self.scratch = [
            pltpu.VMEM((dps,) + shape, x.dtype),
            DMA((2,)),
            DMA((dps,)),
            DMA((dps,)),
        ] + ring_sems(dps // 2)
        self.result = lambda out: out.reshape(dps * rows, width)

    def bind(self, place, x_ref, out_ref, landing, own_sem, sends, recvs, *sems):
        s, dps = place.s, place.dps
        slot, base = s % dps, s // dps * dps
        first = pltpu.make_async_copy(x_ref, landing.at[place.d], own_sem.at[0])
        here = pltpu.make_async_copy(landing.at[slot], out_ref.at[slot], own_sem.at[1])
        ring = ring_gather(
            place, lambda half: x_ref.at[half], lambda chunk, half: landing.at[chunk, half], *sems
        )

        def swap(i):
            to = (slot + i) % dps
            return remote(landing.at[to], out_ref.at[slot], sends.at[i], recvs.at[i], seq=base + to)

        def start():
            ring[0]()
            first.start()

        def last():
            first.wait()
            ring[2]()
            here.start()
            for i in range(1, dps):
                swap(i).start()

        def finish():
            here.wait()
            for i in range(1, dps):
                swap(i).wait_recv()
                swap(i).wait_send()

        ticks = {2 * hop - 1: functools.partial(ring[1], hop) for hop in range(1, place.hops)}
        ticks[2 * place.hops] = last
        return start, ticks, finish


class RowsBack:
    def __init__(self, partial, rows, dps, groups):
        width, hops = partial.shape[1], dps // 2
        shape = (2, rows // 2, width)
        self.inputs, self.in_specs = [partial.reshape((dps,) + shape)], [VM]
        self.outs, self.out_specs = [jax.ShapeDtypeStruct(shape, jnp.float32)], [VM]
        self.scratch = (
            [pltpu.VMEM((dps,) + shape, jnp.bfloat16), DMA, DMA((dps,)), DMA((dps,))]
            + [pltpu.VMEM((hops,) + shape, jnp.bfloat16)] * 2
            + [pltpu.VMEM((hops - 1,) + shape, jnp.bfloat16)] * 2
            + ring_sems(hops)
        )
        self.result = lambda out: out.reshape(rows, width)

    def bind(self, place, p_ref, out_ref, landing, own_sem, sends, recvs, *scratch):
        s, dps = place.s, place.dps
        slot, base = s % dps, s // dps * dps
        here = pltpu.make_async_copy(p_ref.at[slot], landing.at[slot], own_sem)

        def swap(i):
            to = (slot + i) % dps
            return remote(p_ref.at[to], landing.at[slot], sends.at[i], recvs.at[i], seq=base + to)

        def put(half, value):
            out_ref[half] = value

        ring = ring_scatter(place, lambda chunk, half: landing.at[chunk, half], put, *scratch)

        def start():
            here.start()
            for i in range(1, dps):
                swap(i).start()

        def middle():
            here.wait()
            for i in range(1, dps):
                swap(i).wait_recv()
            ring[0]()

        def finish():
            for i in range(1, dps):
                swap(i).wait_send()
            ring[2]()

        ticks = {
            2 * (place.hops - hop) + 2: functools.partial(ring[1], hop)
            for hop in range(1, place.hops)
        }
        ticks[2] = middle
        return start, ticks, finish


class Spread:
    def __init__(self, tiles, total, dps, groups):
        count, shape = dps * groups, tiles.shape[-2:]
        self.total = total
        self.inputs, self.in_specs = [tiles], [VM]
        out = shape if total else (count,) + shape
        self.outs, self.out_specs = [jax.ShapeDtypeStruct(out, jnp.float32)], [VM]
        self.scratch = [pltpu.VMEM((count,) + shape, jnp.float32), DMA((count,)), DMA((count,))]
        self.result = lambda out: out

    def bind(self, place, x_ref, out_ref, landing, sends, recvs):
        count = place.dps * place.groups
        me = place.d * place.groups + place.s

        def copy(i):
            other = (me + i) % count
            return remote(
                x_ref.at[other] if self.total else x_ref,
                landing.at[me],
                sends.at[i],
                recvs.at[i],
                dp=other // place.groups,
                seq=other % place.groups,
            )

        def start():
            def each(i, _):
                copy(i).start()
                return 0

            lax.fori_loop(1, count, each, 0)

        def finish():
            def each(i, _):
                copy(i).wait_recv()
                copy(i).wait_send()
                return 0

            lax.fori_loop(1, count, each, 0)
            landing[me] = x_ref[me] if self.total else x_ref[...]
            out_ref[...] = jnp.sum(landing[...], axis=0) if self.total else landing[...]

        return start, {}, finish


def move(parts, dps, groups, number, greet=greet_near):
    def kernel(*refs):
        place = Place(dps, groups)
        at = [
            0,
            sum(len(part.inputs) for part in parts),
            sum(len(part.inputs) + len(part.outs) for part in parts),
        ]
        bound = []
        for part in parts:
            mine = []
            for kind, length in enumerate((len(part.inputs), len(part.outs), len(part.scratch))):
                mine += refs[at[kind] : at[kind] + length]
                at[kind] += length
            bound.append(part.bind(place, *mine))
        greet(place)
        for start, _, _ in bound:
            start()
        for tick in range(1 + max([0] + [max(list(ticks) + [0]) for _, ticks, _ in bound])):
            for _, ticks, _ in bound:
                if tick in ticks:
                    ticks[tick]()
        for _, _, finish in bound:
            finish()

    outs = pl.pallas_call(
        kernel,
        out_shape=[out for part in parts for out in part.outs],
        in_specs=[spec for part in parts for spec in part.in_specs],
        out_specs=[spec for part in parts for spec in part.out_specs],
        scratch_shapes=[one for part in parts for one in part.scratch],
        compiler_params=pltpu.CompilerParams(
            collective_id=number, has_side_effects=True, vmem_limit_bytes=56 << 20
        ),
        cost_estimate=pl.CostEstimate(flops=0, bytes_accessed=120_000_000, transcendentals=0),
        name=f"move_{number}",
    )(*[x for part in parts for x in part.inputs])
    results = []
    for part in parts:
        results.append(part.result(outs[len(results)]))
    return results


def norm_factor(values):
    return lax.rsqrt(jnp.mean(values * values, axis=-1, keepdims=True) + epsilon)


def norm_grad(values, factor, gain, gradient):
    weighted = gradient * gain
    inner_mean = jnp.mean(weighted * values, axis=-1, keepdims=True)
    return factor * weighted - values * (factor * factor * factor) * inner_mean


def rope_tables(positions, head_width):
    half_width = head_width // 2
    frequency = rope_base ** (-2.0 * jnp.arange(half_width, dtype=jnp.float32) / head_width)
    angles = positions.astype(jnp.float32)[:, None] * frequency[None, :]
    return (jnp.cos(angles)[:, None, :], jnp.sin(angles)[:, None, :])


def rotate(values, cosine_table, sine_table):
    half_width = values.shape[-1] // 2
    first_half = values[..., :half_width]
    second_half = values[..., half_width:]
    return jnp.concatenate(
        [
            first_half * cosine_table - second_half * sine_table,
            second_half * cosine_table + first_half * sine_table,
        ],
        axis=-1,
    )


def gated_grad(gate, upward, grad_inner):
    sigmoid_gate = jax.nn.sigmoid(gate)
    grad_gate = grad_inner * upward * sigmoid_gate * (1.0 + gate * (1.0 - sigmoid_gate))
    grad_upward = grad_inner * (gate * sigmoid_gate)
    return (grad_gate.astype(jnp.bfloat16), grad_upward.astype(jnp.bfloat16))


def block_scores(query_block, key_heads, lower, upper, score_scale):
    scores = (
        jnp.einsum(
            "qhd,kd->hqk", query_block, key_heads[:upper], preferred_element_type=jnp.float32
        )
        * score_scale
    )
    rows_at = lower + jnp.arange(query_block.shape[0], dtype=jnp.int32)
    cols_at = jnp.arange(upper, dtype=jnp.int32)
    allowed = (cols_at[None, :] <= rows_at[:, None])[None]
    return jnp.where(allowed, scores, masked_value)


def per_device(
    tokens,
    qkv_weight,
    out_weight,
    gate_weight,
    up_weight,
    down_weight,
    attn_gain,
    mlp_gain,
    cotangent,
):
    groups = lax.axis_size("seq")
    dps = lax.axis_size("dp")
    tok_rows = tokens.shape[1]
    model_width = tokens.shape[2]
    weight_rows = qkv_weight.shape[0]
    seq_len = tok_rows * groups
    local_heads = HEADS // groups
    local_width = local_heads * HEAD_DIM
    kv_copies = groups // KV_HEADS
    score_scale = HEAD_DIM ** (-0.5)
    block_rows = min(512, seq_len)
    block_count = seq_len // block_rows
    fold = groups // dps
    order = [(at % dps) * fold + at // dps for at in range(groups)]

    q_part = qkv_weight[:, :model_width].reshape(weight_rows, groups, local_width)
    k_part = qkv_weight[:, model_width : model_width + KV_HEADS * HEAD_DIM]
    v_part = qkv_weight[:, model_width + KV_HEADS * HEAD_DIM :]
    k_part = k_part.reshape(weight_rows, KV_HEADS, HEAD_DIM)
    v_part = v_part.reshape(weight_rows, KV_HEADS, HEAD_DIM)
    columns = jnp.stack(
        [
            jnp.concatenate(
                [q_part[:, g], k_part[:, g // kv_copies], v_part[:, g // kv_copies]], axis=1
            )
            for g in order
        ]
    )
    gain_width = attn_gain.shape[0]
    tile = jnp.zeros((8, 128), jnp.float32)
    tile = tile.at[0, :gain_width].set(attn_gain.astype(jnp.float32))
    tile = tile.at[1, :gain_width].set(mlp_gain.astype(jnp.float32))
    qkv_local, tokens_all, out_rows, gate_part, gains = move(
        [
            Columns(columns, dps, groups),
            LineGather(tokens[0], dps, groups),
            Rows(out_weight, dps, groups),
            RingGather(gate_weight, dps, groups),
            Spread(tile, False, dps, groups),
        ],
        dps,
        groups,
        1,
        greet_all,
    )
    gain_one = gains[:, 0, :gain_width].reshape(model_width)
    gain_two = gains[:, 1, :gain_width].reshape(model_width)

    x_rows = tokens[0].astype(jnp.float32)
    factor_one = norm_factor(x_rows)
    all_rows = tokens_all.astype(jnp.float32)
    normed_all = (all_rows * norm_factor(all_rows) * gain_one).astype(jnp.bfloat16)
    grad_low = cotangent[0]
    grad_low, _ = lax.optimization_barrier((grad_low, gains))
    grad_all = lax.all_gather(grad_low, "seq", axis=0, tiled=True)

    mixed = jnp.dot(normed_all, qkv_local, preferred_element_type=jnp.float32)
    cosine_table, sine_table = rope_tables(jnp.arange(seq_len, dtype=jnp.int32), HEAD_DIM)
    query_heads = rotate(
        mixed[:, :local_width].reshape(seq_len, local_heads, HEAD_DIM), cosine_table, sine_table
    ).astype(jnp.bfloat16)
    key_heads = rotate(
        mixed[:, None, local_width : local_width + HEAD_DIM], cosine_table, sine_table
    ).astype(jnp.bfloat16)[:, 0]
    value_heads = mixed[:, local_width + HEAD_DIM :].astype(jnp.bfloat16)
    outputs = []
    log_sums = []
    for block in range(block_count):
        lower = block * block_rows
        upper = lower + block_rows
        scores = block_scores(query_heads[lower:upper], key_heads, lower, upper, score_scale)
        highest = jnp.max(scores, axis=-1, keepdims=True)
        log_sum = highest + jnp.log(jnp.sum(jnp.exp(scores - highest), axis=-1, keepdims=True))
        probs = jnp.exp(scores - log_sum).astype(jnp.bfloat16)
        attended = jnp.einsum(
            "hqk,kd->qhd", probs, value_heads[:upper], preferred_element_type=jnp.float32
        )
        outputs.append(attended.astype(jnp.bfloat16))
        log_sums.append(log_sum)
    attended = jnp.concatenate(outputs, axis=0).reshape(seq_len, local_width)
    partial = jnp.dot(attended, out_rows, preferred_element_type=jnp.float32)
    summed, up_part = move(
        [
            LineScatter(partial.astype(jnp.bfloat16), dps, groups),
            RingGather(up_weight, dps, groups),
        ],
        dps,
        groups,
        2,
    )
    hidden = x_rows + summed
    factor_two = norm_factor(hidden)
    normed_two = (hidden * factor_two * gain_two).astype(jnp.bfloat16)
    hn_all, down_part = move(
        [LineGather(normed_two, dps, groups), RingGather(down_weight, dps, groups)],
        dps,
        groups,
        3,
    )

    gate = lax.dot_general(hn_all, gate_part, contract_cols, preferred_element_type=jnp.float32)
    upward = lax.dot_general(hn_all, up_part, contract_cols, preferred_element_type=jnp.float32)
    grad_inner = lax.dot_general(
        grad_all, down_part, contract_cols, preferred_element_type=jnp.float32
    )
    inner = (jax.nn.silu(gate) * upward).astype(jnp.bfloat16)
    grad_gate, grad_upward = gated_grad(gate, upward, grad_inner)
    mlp_result = lax.psum_scatter(
        jnp.dot(inner, down_part, preferred_element_type=jnp.float32).astype(jnp.bfloat16),
        "seq",
        scatter_dimension=0,
        tiled=True,
    ).astype(jnp.float32)
    down_term, gate_term, up_term = [
        lax.dot_general(left, right, contract_rows, preferred_element_type=jnp.float32).astype(
            jnp.bfloat16
        )
        for left, right in ((inner, grad_all), (grad_gate, hn_all), (grad_upward, hn_all))
    ]
    partial = jnp.dot(grad_gate, gate_part, preferred_element_type=jnp.float32) + jnp.dot(
        grad_upward, up_part, preferred_element_type=jnp.float32
    )
    grad_normed, down_owned = move(
        [
            LineScatter(partial.astype(jnp.bfloat16), dps, groups),
            RingScatter(down_term, dps, groups),
        ],
        dps,
        groups,
        4,
    )

    block_out = (hidden + mlp_result).astype(jnp.bfloat16)[None]
    gain_two_term = jnp.sum(grad_normed * hidden * factor_two, axis=0)
    grad_hidden = grad_low.astype(jnp.float32) + norm_grad(
        hidden, factor_two, gain_two, grad_normed
    )
    grad_branch, gate_owned = move(
        [
            LineGather(grad_hidden.astype(jnp.bfloat16), dps, groups),
            RingScatter(gate_term, dps, groups),
        ],
        dps,
        groups,
        5,
    )
    out_term = lax.dot_general(
        attended, grad_branch, contract_rows, preferred_element_type=jnp.float32
    ).astype(jnp.bfloat16)
    grad_heads = (
        lax.dot_general(grad_branch, out_rows, contract_cols, preferred_element_type=jnp.float32)
        .astype(jnp.bfloat16)
        .reshape(seq_len, local_heads, HEAD_DIM)
    )
    grad_keys = jnp.zeros((seq_len, HEAD_DIM), jnp.float32)
    grad_values = jnp.zeros((seq_len, HEAD_DIM), jnp.float32)
    grad_queries = []
    for block in range(block_count):
        lower = block * block_rows
        upper = lower + block_rows
        query_block = query_heads[lower:upper]
        grad_block = grad_heads[lower:upper]
        scores = block_scores(query_block, key_heads, lower, upper, score_scale)
        probs = jnp.exp(scores - log_sums[block])
        probs_low = probs.astype(jnp.bfloat16)
        grad_probs = jnp.einsum(
            "qhd,kd->hqk", grad_block, value_heads[:upper], preferred_element_type=jnp.float32
        )
        row_delta = jnp.sum(probs * grad_probs, axis=-1, keepdims=True)
        grad_scores = (probs * (grad_probs - row_delta)).astype(jnp.bfloat16)
        grad_queries.append(
            jnp.einsum(
                "hqk,kd->qhd", grad_scores, key_heads[:upper], preferred_element_type=jnp.float32
            )
            * score_scale
        )
        grad_keys = grad_keys.at[:upper].add(
            jnp.einsum("hqk,qhd->kd", grad_scores, query_block, preferred_element_type=jnp.float32)
            * score_scale
        )
        grad_values = grad_values.at[:upper].add(
            jnp.einsum("hqk,qhd->kd", probs_low, grad_block, preferred_element_type=jnp.float32)
        )
    grad_q = rotate(jnp.concatenate(grad_queries, axis=0), cosine_table, -sine_table)
    grad_k = rotate(grad_keys[:, None], cosine_table, -sine_table)[:, 0]
    grad_mixed = jnp.concatenate(
        [grad_q.reshape(seq_len, local_width), grad_k, grad_values], axis=1
    ).astype(jnp.bfloat16)
    qkv_term = lax.dot_general(
        normed_all, grad_mixed, contract_rows, preferred_element_type=jnp.float32
    )
    partial = lax.dot_general(
        grad_mixed, qkv_local, contract_cols, preferred_element_type=jnp.float32
    )
    qkv_owned, grad_normed_one, out_owned, up_owned = move(
        [
            ColumnsBack(qkv_term.astype(jnp.bfloat16), weight_rows, dps, groups),
            LineScatter(partial.astype(jnp.bfloat16), dps, groups),
            RowsBack(out_term, weight_rows, dps, groups),
            RingScatter(up_term, dps, groups),
        ],
        dps,
        groups,
        6,
        greet_all,
    )
    qkv_owned = qkv_owned.astype(jnp.float32)
    place = [order.index(g) for g in range(groups)]
    qkv_owned = jnp.concatenate(
        [qkv_owned[place[g], :, :local_width] for g in range(groups)]
        + [
            sum(
                qkv_owned[place[head * kv_copies + i], :, at : at + HEAD_DIM]
                for i in range(kv_copies)
            )
            for at in (local_width, local_width + HEAD_DIM)
            for head in range(KV_HEADS)
        ],
        axis=1,
    )
    gain_one_term = jnp.sum(grad_normed_one * x_rows * factor_one, axis=0)
    grad_input = grad_hidden + norm_grad(x_rows, factor_one, gain_one, grad_normed_one)
    terms = jnp.stack([gain_one_term, gain_two_term]).reshape(2, dps * groups, gain_width)
    terms = jnp.pad(terms.transpose(1, 0, 2), ((0, 0), (0, 6), (0, 128 - gain_width)))
    (gain_grads,) = move([Spread(terms, True, dps, groups)], dps, groups, 7, greet_all)
    return (
        block_out,
        grad_input[None],
        qkv_owned,
        out_owned,
        gate_owned,
        up_owned,
        down_owned,
        gain_grads[0, :gain_width],
        gain_grads[1, :gain_width],
    )


def solution(mesh):
    rows = P(("dp", "seq"), None)
    tokens = P("dp", "seq", None)
    gains = P(("dp", "seq"))
    return jax.shard_map(
        per_device,
        mesh=mesh,
        in_specs=(tokens, rows, rows, rows, rows, rows, gains, gains, tokens),
        out_specs=(tokens, tokens, rows, rows, rows, rows, rows, gains, gains),
        check_vma=False,
    )
```

```python
import functools

import jax
import jax.numpy as jnp
from jax import lax
from jax.experimental import pallas as pl
from jax.experimental.pallas import tpu as pltpu
from jax.sharding import PartitionSpec as P

HEADS = 32
KV_HEADS = 8
HEAD_DIM = 64

MESH = pl.DeviceIdType.MESH
ANY = pl.BlockSpec(memory_space=pl.ANY)
VM = pl.BlockSpec(memory_space=pltpu.VMEM)
SUB = 2

epsilon = 1e-05
rope_base = 500000.0
masked_value = -1e30
contract_rows = (((0,), (0,)), ((), ()))
contract_cols = (((1,), (1,)), ((), ()))


class Place:
    def __init__(self, dps, groups):
        self.dps, self.groups, self.chips, self.hops = dps, groups, groups // 2, dps // 2
        self.d, self.s = lax.axis_index("dp"), lax.axis_index("seq")
        self.chip, self.core = self.s // 2, self.s % 2
        self.partner = 2 * self.chip + 1 - self.core
        row, side = self.d // 2, self.d % 2
        self.turn = side * (dps - 1 - row) + (1 - side) * row

    def ring(self, distance):
        at = (self.turn + distance + self.dps) % self.dps
        side = at // self.hops
        return (1 - side) * 2 * at + side * (2 * (self.dps - 1 - at) + 1)


def remote(src, dst, send, recv, **target):
    return pltpu.make_async_remote_copy(
        src_ref=src, dst_ref=dst, send_sem=send, recv_sem=recv, device_id=target, device_id_type=MESH
    )


def greet_near(place):
    barrier = pltpu.get_barrier_semaphore()

    def signal(**target):
        pl.semaphore_signal(barrier, inc=1, device_id=target, device_id_type=MESH)

    signal(seq=place.partner)
    signal(dp=place.ring(1))
    signal(dp=place.ring(-1))

    @pl.when(place.chip > 0)
    def _():
        signal(seq=place.s - 2)

    @pl.when(place.chip < place.chips - 1)
    def _():
        signal(seq=place.s + 2)

    ends = (place.chips - place.chip) // place.chips + (place.chip + 1) // place.chips
    pl.semaphore_wait(barrier, 5 - ends)


def greet_all(place):
    barrier = pltpu.get_barrier_semaphore()
    count = place.dps * place.groups
    me = place.d * place.groups + place.s

    def signal(i, _):
        other = (me + i) % count
        pl.semaphore_signal(
            barrier,
            inc=1,
            device_id={"dp": other // place.groups, "seq": other % place.groups},
            device_id_type=MESH,
        )
        return 0

    lax.fori_loop(1, count, signal, 0)
    pl.semaphore_wait(barrier, count - 1)


DMA = pltpu.SemaphoreType.DMA


def line_gather(place, x_ref, out_ref, own_sem, us, ur, ds, dr, ps, pr):
    s, chip, chips = place.s, place.chip, place.chips

    def copy(src, group, half, sends, recvs, at, target):
        return remote(
            src, out_ref.at[group, half], sends.at[at, half], recvs.at[at, half], seq=target
        )

    def up(src, group, hop, half):
        return copy(src, group, half, us, ur, hop, s + 2)

    def down(src, group, hop, half):
        return copy(src, group, half, ds, dr, hop, s - 2)

    def pair(src, group, half):
        return copy(src, group, half, ps, pr, group // 2, place.partner)

    own = pltpu.make_async_copy(x_ref, out_ref.at[s], own_sem)

    def start():
        own.start()
        for half in range(SUB):

            @pl.when(chip < chips - 1)
            def _():
                up(x_ref.at[half], s, 0, half).start()

            @pl.when(chip > 0)
            def _():
                down(x_ref.at[half], s, 0, half).start()

        for half in range(SUB):
            pair(x_ref.at[half], s, half).start()

    def step(hop, half):
        below, above = s - 2 * hop, s + 2 * hop

        @pl.when(chip - hop >= 0)
        def _():
            block = out_ref.at[below, half]
            up(block, below, hop - 1, half).wait_recv()

            @pl.when(chip < chips - 1)
            def _():
                up(block, below, hop, half).start()

            pair(block, below, half).start()

        @pl.when(chip + hop < chips)
        def _():
            block = out_ref.at[above, half]
            down(block, above, hop - 1, half).wait_recv()

            @pl.when(chip > 0)
            def _():
                down(block, above, hop, half).start()

            pair(block, above, half).start()

    def arrived(at):
        for half in range(SUB):
            group = 2 * at + 1 - place.core
            pair(out_ref.at[group, half], group, half).wait_recv()

    def sent():
        def each(i, _):
            k, half = i // SUB, i % SUB
            mine = 2 * k + place.core
            block = out_ref.at[mine, half]
            pair(block, mine, half).wait_send()

            @pl.when(jnp.logical_and(chip - k >= 0, chip < chips - 1))
            def _():
                up(block, mine, k, half).wait_send()

            @pl.when(jnp.logical_and(chip + k < chips, chip > 0))
            def _():
                down(block, mine, k, half).wait_send()

            return 0

        lax.fori_loop(0, chips * SUB, each, 0)

    return own, start, step, arrived, sent


class LineGather:
    def __init__(self, x, dps, groups):
        rows, width = x.shape
        shape = (SUB, rows // SUB, width)
        self.inputs, self.in_specs = [x.reshape(shape)], [VM]
        self.outs, self.out_specs = [jax.ShapeDtypeStruct((groups,) + shape, x.dtype)], [ANY]
        self.scratch = [DMA] + [DMA((groups // 2, SUB))] * 6
        self.result = lambda out: out.reshape(groups * rows, width)

    def bind(self, place, *refs):
        own, start, step, arrived, sent = line_gather(place, *refs)

        def finish():
            own.wait()

            def each(at, _):
                arrived(at)
                return 0

            lax.fori_loop(0, place.chips, each, 0)
            sent()

        ticks = {
            (hop - 1) * SUB + half: functools.partial(step, hop, half)
            for hop in range(1, place.chips)
            for half in range(SUB)
        }
        return start, ticks, finish


def line_scatter(place, p_ref, out_ref, pairbuf, upbuf, downbuf, us, ur, ds, dr, ps, pr):
    s, chip, chips, core = place.s, place.chip, place.chips, place.core

    def copy(src, buffer, at, half, sends, recvs, target):
        return remote(src, buffer.at[at, half], sends.at[at, half], recvs.at[at, half], seq=target)

    def pair(at, half):
        src = p_ref.at[2 * at + 1 - core, half]
        return copy(src, pairbuf, at, half, ps, pr, place.partner)

    def up(at, half):
        return copy(upbuf.at[at, half], upbuf, at, half, us, ur, s + 2)

    def down(at, half):
        return copy(downbuf.at[at, half], downbuf, at, half, ds, dr, s - 2)

    def wide(ref, *at):
        return ref[at].astype(jnp.float32)

    def local(at, half):
        return wide(p_ref, 2 * at + core, half) + wide(pairbuf, at, half)

    def send(at):
        for half in range(SUB):
            pair(at, half).start()

    def step(low, half):
        high = chips - 1 - low

        @pl.when(high > chip)
        def _():
            pair(high, half).wait_recv()

            @pl.when(chip > 0)
            def _():
                up(high, half).wait_recv()
                total = local(high, half) + wide(upbuf, high, half)
                upbuf[high, half] = total.astype(jnp.bfloat16)

            @pl.when(chip == 0)
            def _():
                upbuf[high, half] = local(high, half).astype(jnp.bfloat16)

            up(high, half).start()

        @pl.when(low < chip)
        def _():
            pair(low, half).wait_recv()

            @pl.when(chip < chips - 1)
            def _():
                down(low, half).wait_recv()
                total = local(low, half) + wide(downbuf, low, half)
                downbuf[low, half] = total.astype(jnp.bfloat16)

            @pl.when(chip == chips - 1)
            def _():
                downbuf[low, half] = local(low, half).astype(jnp.bfloat16)

            down(low, half).start()

    def finish():
        for half in range(SUB):
            pair(chip, half).wait_recv()
            out_ref[half] = local(chip, half)

            @pl.when(chip > 0)
            def _():
                up(chip, half).wait_recv()
                out_ref[half] += wide(upbuf, chip, half)

            @pl.when(chip < chips - 1)
            def _():
                down(chip, half).wait_recv()
                out_ref[half] += wide(downbuf, chip, half)

        def each(i, _):
            at, half = i // SUB, i % SUB
            pair(at, half).wait_send()

            @pl.when(at > chip)
            def _():
                up(at, half).wait_send()

            @pl.when(at < chip)
            def _():
                down(at, half).wait_send()

            return 0

        lax.fori_loop(0, chips * SUB, each, 0)

    return send, step, finish


def line_scatter_scratch(chips, shape):
    return [pltpu.VMEM((chips,) + shape, jnp.bfloat16)] * 3 + [DMA((chips, SUB))] * 6


class LineScatter:
    def __init__(self, partial, dps, groups):
        total, width = partial.shape
        rows = total // groups
        shape = (SUB, rows // SUB, width)
        self.inputs, self.in_specs = [partial.reshape((groups,) + shape)], [VM]
        self.outs, self.out_specs = [jax.ShapeDtypeStruct(shape, jnp.float32)], [VM]
        self.scratch = line_scatter_scratch(groups // 2, shape)
        self.result = lambda out: out.reshape(rows, width)

    def bind(self, place, *refs):
        send, step, finish = line_scatter(place, *refs)
        chip, chips = place.chip, place.chips

        def start():
            def issue(low, _):
                high = chips - 1 - low

                @pl.when(high > chip)
                def _():
                    send(high)

                @pl.when(low < chip)
                def _():
                    send(low)

                return 0

            lax.fori_loop(0, chips - 1, issue, 0)
            send(chip)

        ticks = {
            i: functools.partial(step, i // SUB, i % SUB) for i in range((chips - 1) * SUB)
        }
        return start, ticks, finish


def ring_sems(hops):
    return [DMA((hops, 2))] * 4


def ring_gather(place, own, out, rs, rr, ls, lr):
    hops = place.hops

    def right(src, chunk, hop, half):
        return remote(
            src, out(chunk, half), rs.at[hop - 1, half], rr.at[hop - 1, half], dp=place.ring(1)
        )

    def left(src, chunk, hop, half):
        return remote(
            src, out(chunk, half), ls.at[hop - 1, half], lr.at[hop - 1, half], dp=place.ring(-1)
        )

    def start():
        for half in range(2):
            right(own(half), place.d, 1, half).start()
            left(own(1 - half), place.d, 1, 1 - half).start()

    def forward(hop):
        before, after = place.ring(-hop), place.ring(hop)
        full = hop < hops - 1
        right(out(before, 0), before, hop, 0).wait_recv()
        right(out(before, 0), before, hop + 1, 0).start()
        left(out(after, 1), after, hop, 1).wait_recv()
        left(out(after, 1), after, hop + 1, 1).start()
        right(out(before, 1), before, hop, 1).wait_recv()
        left(out(after, 0), after, hop, 0).wait_recv()
        if full:
            right(out(before, 1), before, hop + 1, 1).start()
            left(out(after, 0), after, hop + 1, 0).start()

    def finish():
        right(out(place.d, 0), place.ring(-hops), hops, 0).wait_recv()
        left(out(place.d, 1), place.ring(hops), hops, 1).wait_recv()
        for hop in range(1, hops + 1):
            for half in range(2):
                if hop < hops or half == 0:
                    right(out(place.d, half), place.d, hop, half).wait_send()
                if hop < hops or half == 1:
                    left(out(place.d, half), place.d, hop, half).wait_send()

    return start, forward, finish


def ring_scatter(place, part, put, rbuf, lbuf, rout, lout, rs, rr, ls, lr):
    hops = place.hops

    def wide(ref):
        return ref[...].astype(jnp.float32)

    def right(src, hop, half):
        return remote(
            src,
            rbuf.at[hop - 1, half],
            rs.at[hop - 1, half],
            rr.at[hop - 1, half],
            dp=place.ring(1),
        )

    def left(src, hop, half):
        return remote(
            src,
            lbuf.at[hop - 1, half],
            ls.at[hop - 1, half],
            lr.at[hop - 1, half],
            dp=place.ring(-1),
        )

    def start_far():
        right(part(place.ring(hops), 0), hops, 0).start()
        left(part(place.ring(-hops), 1), hops, 1).start()

    def start_next():
        right(part(place.ring(hops - 1), 1), hops - 1, 1).start()
        left(part(place.ring(1 - hops), 0), hops - 1, 0).start()

    def start():
        start_far()
        start_next()

    def forward(hop):
        for first in range(2 if hop < hops - 1 else 1):
            half = first
            right(rbuf.at[hop, half], hop + 1, half).wait_recv()
            total = wide(part(place.ring(hop), half)) + wide(rbuf.at[hop, half])
            rout[hop - 1, half] = total.astype(jnp.bfloat16)
            right(rout.at[hop - 1, half], hop, half).start()
            half = 1 - first
            left(lbuf.at[hop, half], hop + 1, half).wait_recv()
            total = wide(part(place.ring(-hop), half)) + wide(lbuf.at[hop, half])
            lout[hop - 1, half] = total.astype(jnp.bfloat16)
            left(lout.at[hop - 1, half], hop, half).start()

    def finish():
        for half in range(2):
            right(rbuf.at[0, half], 1, half).wait_recv()
            left(lbuf.at[0, half], 1, half).wait_recv()
            put(
                half,
                wide(part(place.d, half)) + wide(rbuf.at[0, half]) + wide(lbuf.at[0, half]),
            )
        for hop in range(1, hops + 1):
            for half in range(2):
                if hop < hops or half == 0:
                    right(rbuf.at[0, half], hop, half).wait_send()
                if hop < hops or half == 1:
                    left(lbuf.at[0, half], hop, half).wait_send()

    return start, forward, finish, start_far, start_next


class RingGather:
    def __init__(self, x, dps, groups):
        rows, width = x.shape
        shape = (2, rows // 2, width)
        self.inputs, self.in_specs = [x.reshape(shape)], [VM]
        self.outs, self.out_specs = [jax.ShapeDtypeStruct((dps,) + shape, x.dtype)], [ANY]
        self.scratch = [DMA] + ring_sems(dps // 2)
        self.result = lambda out: out.reshape(dps * rows, width)

    def bind(self, place, x_ref, out_ref, own_sem, *sems):
        own = pltpu.make_async_copy(x_ref, out_ref.at[place.d], own_sem)
        ring = ring_gather(
            place, lambda half: x_ref.at[half], lambda chunk, half: out_ref.at[chunk, half], *sems
        )

        def start():
            ring[0]()
            own.start()

        def finish():
            own.wait()
            ring[2]()

        ticks = {2 * hop - 1: functools.partial(ring[1], hop) for hop in range(1, place.hops)}
        return start, ticks, finish


class RingScatter:
    def __init__(self, partial, dps, groups):
        total, width = partial.shape
        rows, hops = total // dps, dps // 2
        shape = (2, rows // 2, width)
        self.inputs, self.in_specs = [partial.reshape((dps,) + shape)], [VM]
        self.outs, self.out_specs = [jax.ShapeDtypeStruct(shape, jnp.float32)], [VM]
        self.scratch = (
            [pltpu.VMEM((hops,) + shape, jnp.bfloat16)] * 2
            + [pltpu.VMEM((hops - 1,) + shape, jnp.bfloat16)] * 2
            + ring_sems(hops)
        )
        self.result = lambda out: out.reshape(rows, width)

    def bind(self, place, p_ref, out_ref, *scratch):
        def put(half, value):
            out_ref[half] = value

        ring = ring_scatter(place, lambda chunk, half: p_ref.at[chunk, half], put, *scratch)
        ticks = {
            2 * (place.hops - hop) - 1: functools.partial(ring[1], hop)
            for hop in range(1, place.hops)
        }
        return ring[0], ticks, ring[2]


class Columns:
    def __init__(self, blocks, dps, groups):
        _, rows, width = blocks.shape
        self.inputs, self.in_specs = [blocks], [VM]
        self.outs = [jax.ShapeDtypeStruct((dps, groups, rows, width), blocks.dtype)]
        self.out_specs = [ANY]
        self.scratch = [
            pltpu.VMEM((groups, rows, width), blocks.dtype),
            DMA((2,)),
            DMA((groups,)),
            DMA((groups,)),
        ] + ring_sems(dps // 2)
        self.result = lambda out: out.reshape(dps * groups * rows, width)

    def bind(self, place, x_ref, out_ref, landing, own_sem, sends, recvs, *sems):
        s, groups = place.s, place.groups
        half_of = groups // 2
        here = pltpu.make_async_copy(x_ref.at[s], landing.at[s], own_sem.at[0])
        own = pltpu.make_async_copy(landing, out_ref.at[place.d], own_sem.at[1])

        def swap(i):
            to = (s + i) % groups
            return remote(x_ref.at[to], landing.at[s], sends.at[i], recvs.at[i], seq=to)

        ring = ring_gather(
            place,
            lambda half: landing.at[pl.ds(half * half_of, half_of)],
            lambda chunk, half: out_ref.at[chunk, pl.ds(half * half_of, half_of)],
            *sems,
        )

        def start():
            here.start()
            for i in range(1, groups):
                swap(i).start()

        def middle():
            here.wait()
            for i in range(1, groups):
                swap(i).wait_recv()
            ring[0]()
            own.start()

        def finish():
            for i in range(1, groups):
                swap(i).wait_send()
            own.wait()
            ring[2]()

        ticks = {1 + 2 * hop: functools.partial(ring[1], hop) for hop in range(1, place.hops)}
        ticks[1] = middle
        return start, ticks, finish


class ColumnsBack:
    def __init__(self, partial, rows, dps, groups):
        width, hops = partial.shape[1], dps // 2
        shape = (groups, rows, width)
        halves = (2, groups // 2, rows, width)
        self.inputs, self.in_specs = [partial.reshape((dps,) + halves)], [VM]
        self.outs, self.out_specs = [jax.ShapeDtypeStruct(shape, jnp.bfloat16)], [ANY]
        self.scratch = (
            [pltpu.VMEM(halves, jnp.bfloat16), DMA, DMA((groups,)), DMA((groups,))]
            + [pltpu.VMEM((hops,) + halves, jnp.bfloat16)] * 2
            + [pltpu.VMEM((hops - 1,) + halves, jnp.bfloat16)] * 2
            + ring_sems(hops)
        )
        self.result = lambda out: out

    def bind(self, place, p_ref, out_ref, total, own_sem, sends, recvs, *scratch):
        s, groups = place.s, place.groups
        half_of = groups // 2

        def put(half, value):
            total[half] = value.astype(jnp.bfloat16)

        ring = ring_scatter(place, lambda chunk, half: p_ref.at[chunk, half], put, *scratch)
        here = pltpu.make_async_copy(
            total.at[s // half_of, s % half_of], out_ref.at[s], own_sem
        )

        def swap(i):
            to = (s + i) % groups
            src = total.at[to // half_of, to % half_of]
            return remote(src, out_ref.at[s], sends.at[i], recvs.at[i], seq=to)

        def last():
            ring[2]()
            here.start()
            for i in range(1, groups):
                swap(i).start()

        def finish():
            here.wait()
            for i in range(1, groups):
                swap(i).wait_recv()
                swap(i).wait_send()

        ticks = {
            2 * (place.hops - hop) - 1: functools.partial(ring[1], hop)
            for hop in range(1, place.hops)
        }
        ticks[2 * place.hops - 1] = last
        return ring[0], ticks, finish


class Rows:
    def __init__(self, x, dps, groups):
        rows, width = x.shape
        shape = (2, rows // 2, width)
        self.inputs, self.in_specs = [x.reshape(shape)], [VM]
        self.outs, self.out_specs = [jax.ShapeDtypeStruct((dps,) + shape, x.dtype)], [ANY]
        self.scratch = [
            pltpu.VMEM((dps,) + shape, x.dtype),
            DMA((2,)),
            DMA((dps,)),
            DMA((dps,)),
        ] + ring_sems(dps // 2)
        self.result = lambda out: out.reshape(dps * rows, width)

    def bind(self, place, x_ref, out_ref, landing, own_sem, sends, recvs, *sems):
        s, dps = place.s, place.dps
        slot, base = s % dps, s // dps * dps
        first = pltpu.make_async_copy(x_ref, landing.at[place.d], own_sem.at[0])
        here = pltpu.make_async_copy(landing.at[slot], out_ref.at[slot], own_sem.at[1])
        ring = ring_gather(
            place, lambda half: x_ref.at[half], lambda chunk, half: landing.at[chunk, half], *sems
        )

        def swap(i):
            to = (slot + i) % dps
            return remote(landing.at[to], out_ref.at[slot], sends.at[i], recvs.at[i], seq=base + to)

        def start():
            ring[0]()
            first.start()

        def last():
            first.wait()
            ring[2]()
            here.start()
            for i in range(1, dps):
                swap(i).start()

        def finish():
            here.wait()
            for i in range(1, dps):
                swap(i).wait_recv()
                swap(i).wait_send()

        ticks = {2 * hop - 1: functools.partial(ring[1], hop) for hop in range(1, place.hops)}
        ticks[2 * place.hops] = last
        return start, ticks, finish


class RowsBack:
    def __init__(self, partial, rows, dps, groups):
        width, hops = partial.shape[1], dps // 2
        shape = (2, rows // 2, width)
        self.inputs, self.in_specs = [partial.reshape((dps,) + shape)], [VM]
        self.outs, self.out_specs = [jax.ShapeDtypeStruct(shape, jnp.float32)], [VM]
        self.scratch = (
            [pltpu.VMEM((dps,) + shape, jnp.bfloat16), DMA, DMA((dps,)), DMA((dps,))]
            + [pltpu.VMEM((hops,) + shape, jnp.bfloat16)] * 2
            + [pltpu.VMEM((hops - 1,) + shape, jnp.bfloat16)] * 2
            + ring_sems(hops)
        )
        self.result = lambda out: out.reshape(rows, width)

    def bind(self, place, p_ref, out_ref, landing, own_sem, sends, recvs, *scratch):
        s, dps = place.s, place.dps
        slot, base = s % dps, s // dps * dps
        here = pltpu.make_async_copy(p_ref.at[slot], landing.at[slot], own_sem)

        def swap(i):
            to = (slot + i) % dps
            return remote(p_ref.at[to], landing.at[slot], sends.at[i], recvs.at[i], seq=base + to)

        def put(half, value):
            out_ref[half] = value

        ring = ring_scatter(place, lambda chunk, half: landing.at[chunk, half], put, *scratch)

        def start():
            here.start()
            for i in range(1, dps):
                swap(i).start()

        def middle():
            here.wait()
            for i in range(1, dps):
                swap(i).wait_recv()
            ring[0]()

        def finish():
            for i in range(1, dps):
                swap(i).wait_send()
            ring[2]()

        ticks = {
            2 * (place.hops - hop) + 2: functools.partial(ring[1], hop)
            for hop in range(1, place.hops)
        }
        ticks[2] = middle
        return start, ticks, finish


class Spread:
    def __init__(self, tiles, total, dps, groups):
        count, shape = dps * groups, tiles.shape[-2:]
        self.total = total
        self.inputs, self.in_specs = [tiles], [VM]
        out = shape if total else (count,) + shape
        self.outs, self.out_specs = [jax.ShapeDtypeStruct(out, jnp.float32)], [VM]
        self.scratch = [pltpu.VMEM((count,) + shape, jnp.float32), DMA((count,)), DMA((count,))]
        self.result = lambda out: out

    def bind(self, place, x_ref, out_ref, landing, sends, recvs):
        count = place.dps * place.groups
        me = place.d * place.groups + place.s

        def copy(i):
            other = (me + i) % count
            return remote(
                x_ref.at[other] if self.total else x_ref,
                landing.at[me],
                sends.at[i],
                recvs.at[i],
                dp=other // place.groups,
                seq=other % place.groups,
            )

        def start():
            def each(i, _):
                copy(i).start()
                return 0

            lax.fori_loop(1, count, each, 0)

        def finish():
            def each(i, _):
                copy(i).wait_recv()
                copy(i).wait_send()
                return 0

            lax.fori_loop(1, count, each, 0)
            landing[me] = x_ref[me] if self.total else x_ref[...]
            out_ref[...] = jnp.sum(landing[...], axis=0) if self.total else landing[...]

        return start, {}, finish


TILE = 256


class FeedForward:
    def __init__(self, normed, down, gate, up, grad_all, dps, groups):
        rows, width = normed.shape
        shape, chips = (SUB, rows // SUB, width), groups // 2
        held = gate.shape[0]
        ring = (2, down.shape[0] // 2, width)
        pair = 2 * rows
        self.inputs = [
            normed.reshape(shape),
            down.reshape(ring),
            gate,
            up,
            grad_all.reshape(chips, pair, width),
        ]
        self.in_specs = [VM, VM, ANY, ANY, ANY]
        act = jax.ShapeDtypeStruct((chips, pair, held), jnp.bfloat16)
        self.outs = [
            jax.ShapeDtypeStruct((groups,) + shape, jnp.bfloat16),
            jax.ShapeDtypeStruct((dps,) + ring, jnp.bfloat16),
            act,
            act,
            act,
        ]
        self.out_specs = [VM] * 5
        self.scratch = [
            pltpu.VMEM((held, width), jnp.bfloat16),
            pltpu.VMEM((held, width), jnp.bfloat16),
            pltpu.VMEM((chips, pair, width), jnp.bfloat16),
            pltpu.VMEM((chips, pair, held), jnp.float32),
            pltpu.VMEM((chips, pair, held), jnp.float32),
            DMA((4,)),
            DMA,
        ]
        self.scratch += [DMA((chips, SUB))] * 6 + ring_sems(dps // 2)
        self.result = lambda hn, full, *acts: (
            hn.reshape(groups * rows, width),
            full.reshape(held, width),
            *[one.reshape(groups * rows, held) for one in acts],
        )

    def bind(self, place, x_ref, shard, gate_at, up_at, grad_at, *refs):
        hn, full, inner, dgate, dup, gate_w, up_w, grads, slope, silu = refs[:10]
        loads, own_line = refs[10:12]
        line_sems, ring_refs = refs[12:18], refs[18:]
        chip, chips = place.chip, place.chips
        pair, held = inner.shape[1:]
        width = gate_w.shape[1]
        own, start_line, step, arrived, sent = line_gather(place, x_ref, hn, own_line, *line_sems)
        ring = ring_gather(
            place,
            lambda half: shard.at[half],
            lambda chunk, half: full.at[chunk, half],
            *ring_refs,
        )
        copies = [
            pltpu.make_async_copy(gate_at, gate_w, loads.at[0]),
            pltpu.make_async_copy(up_at, up_w, loads.at[1]),
            pltpu.make_async_copy(grad_at, grads, loads.at[2]),
            pltpu.make_async_copy(shard, full.at[place.d], loads.at[3]),
        ]
        wide = 512 if held % 512 == 0 else held

        def start():
            start_line()
            ring[0]()
            for one in copies:
                one.start()

        def forward(at):
            rows = hn[pl.ds(2 * at, 2)].reshape(pair, width)
            for first in range(0, held, wide):
                span = slice(first, first + wide)
                gate = lax.dot_general(
                    rows, gate_w[span, :], contract_cols, preferred_element_type=jnp.float32
                )
                upward = lax.dot_general(
                    rows, up_w[span, :], contract_cols, preferred_element_type=jnp.float32
                )
                sigmoid = jax.nn.sigmoid(gate)
                passed = gate * sigmoid
                inner[at, :, span] = (passed * upward).astype(jnp.bfloat16)
                silu[at, :, span] = passed
                slope[at, :, span] = upward * sigmoid * (1.0 + gate * (1.0 - sigmoid))

        def when_there(at, there):
            @pl.when(there)
            def _():
                arrived(at)
                forward(at)

        def tick(hop, half):
            step(hop, half)
            if hop == 1 and half == 0:
                own.wait()
                copies[0].wait()
                copies[1].wait()
                arrived(chip)
                forward(chip)
            if hop > 1 and half == 0:
                when_there(chip - hop + 1, chip - hop + 1 >= 0)
            if hop > 1 and half == SUB - 1:
                when_there(chip + hop - 1, chip + hop - 1 < chips)

        def finish():
            last = chips - 1
            when_there(chip - last, chip - last >= 0)
            when_there(chip + last, chip + last < chips)
            copies[2].wait()
            copies[3].wait()
            ring[2]()

            def back(at, _):
                rows = grads[at]
                for first in range(0, held, wide):
                    span = slice(first, first + wide)
                    chunk = full.shape[1] * full.shape[2]
                    part = full[first // chunk : (first + wide) // chunk].reshape(wide, width)
                    grad = lax.dot_general(
                        rows, part, contract_cols, preferred_element_type=jnp.float32
                    )
                    dgate[at, :, span] = (grad * slope[at, :, span]).astype(jnp.bfloat16)
                    dup[at, :, span] = (grad * silu[at, :, span]).astype(jnp.bfloat16)
                return 0

            lax.fori_loop(0, chips, back, 0)
            sent()

        ticks = {
            (hop - 1) * SUB + half: functools.partial(tick, hop, half)
            for hop in range(1, chips)
            for half in range(SUB)
        }

        def with_ring(tick, hop):
            ticks[tick]()
            ring[1](hop)

        merged = dict(ticks)
        for hop in range(1, place.hops):
            merged[2 * hop - 1] = functools.partial(with_ring, 2 * hop - 1, hop)
        return start, merged, finish


class FeedBack:
    def __init__(self, inner, dgate, dup, gate, up, down, normed, grads, dps, groups):
        length, held = inner.shape
        width, chips = normed.shape[1], groups // 2
        rows = length // groups
        shape = (SUB, rows // SUB, width)
        owned = (2, held // dps // 2, width)
        hops = dps // 2
        tile = (2, SUB, rows // SUB, width)
        self.inputs = [inner, dgate, dup, gate, up, down, normed, grads]
        self.in_specs = [ANY] * 8
        self.outs = [
            jax.ShapeDtypeStruct(shape, jnp.float32),
            jax.ShapeDtypeStruct(owned, jnp.float32),
            jax.ShapeDtypeStruct((held // TILE,) + tile, jnp.bfloat16),
            jax.ShapeDtypeStruct((held // TILE,) + tile, jnp.bfloat16),
            jax.ShapeDtypeStruct((chips,) + tile, jnp.bfloat16),
        ]
        self.out_specs = [VM, VM, ANY, ANY, ANY]
        act = pltpu.VMEM((length, held), jnp.bfloat16)
        weight = pltpu.VMEM((held, width), jnp.bfloat16)
        tokens = pltpu.VMEM((length, width), jnp.bfloat16)
        self.scratch = [act] * 3 + [weight] * 2 + [tokens] * 2
        self.scratch += [
            pltpu.VMEM((groups,) + shape, jnp.bfloat16),
            pltpu.VMEM((dps,) + owned, jnp.bfloat16),
            pltpu.VMEM((2,) + tile, jnp.bfloat16),
            DMA((8,)),
            DMA((2,)),
        ]
        self.scratch += line_scatter_scratch(chips, shape)
        self.scratch += (
            [pltpu.VMEM((hops,) + owned, jnp.bfloat16)] * 2
            + [pltpu.VMEM((hops - 1,) + owned, jnp.bfloat16)] * 2
            + ring_sems(hops)
        )
        self.result = lambda total, mine, gate_term, up_term, out: (
            total.reshape(rows, width),
            mine.reshape(held // dps, width),
            gate_term.reshape(held, width),
            up_term.reshape(held, width),
            out.reshape(length, width),
        )

    def bind(self, place, *refs):
        sources, refs = refs[:8], refs[8:]
        total_ref, own_ref, gate_out, up_out, result_out = refs[:5]
        inner, dgate, dup, gate, up, normed, grads = refs[5:12]
        p_ref, term, stage, loads, stage_sem = refs[12:17]
        line_refs, ring_refs = refs[17:26], refs[26:]
        chip, chips, hops = place.chip, place.chips, place.hops
        held, width = gate.shape
        pair = inner.shape[0] // chips
        chunk = held // place.dps
        wide = 1024 if width % 1024 == 0 else width
        send, step, finish_line = line_scatter(place, p_ref, total_ref, *line_refs)

        def put(half, value):
            own_ref[half] = value

        ring = ring_scatter(place, lambda at, half: term.at[at, half], put, *ring_refs)
        targets = [inner, dgate, dup, gate, up, gate, normed, grads]
        copies = [
            pltpu.make_async_copy(source, target, loads.at[i])
            for i, (source, target) in enumerate(zip(sources, targets))
        ]

        def start():
            for i in (0, 7, 1, 3, 2, 4, 6):
                copies[i].start()

        def rows_of(ref, at):
            return ref[pl.ds(pl.multiple_of(at * pair, pair), pair), :]

        def partial(at):
            left, right = rows_of(dgate, at), rows_of(dup, at)
            for first in range(0, width, wide):
                span = slice(first, first + wide)
                value = jnp.dot(left, gate[:, span], preferred_element_type=jnp.float32)
                value += jnp.dot(right, up[:, span], preferred_element_type=jnp.float32)
                p_ref[pl.ds(2 * at, 2), :, :, span] = value.astype(jnp.bfloat16).reshape(
                    p_ref[pl.ds(2 * at, 2), :, :, span].shape
                )
            send(at)

        def term_rows(ref, other, start, count, span):
            return lax.dot_general(
                ref[:, pl.ds(start, count)],
                other[:, span],
                contract_rows,
                preferred_element_type=jnp.float32,
            ).astype(jnp.bfloat16)

        def down_tile(at):
            if chunk % 128 == 0:
                for first in range(0, width, wide):
                    span = slice(first, first + wide)
                    value = term_rows(inner, grads, pl.multiple_of(at * chunk, chunk), chunk, span)
                    term[at, :, :, span] = value.reshape(2, chunk // 2, wide)

        def down_all():
            if chunk % 128 != 0:
                for row in range(0, held, TILE):
                    for first in range(0, width, wide):
                        span = slice(first, first + wide)
                        value = term_rows(inner, grads, row, TILE, span)
                        term[row // chunk : (row + TILE) // chunk, :, :, span] = value.reshape(
                            TILE // chunk, 2, chunk // 2, wide
                        )

        jobs = []

        def first_job():
            copies[0].wait()
            copies[7].wait()
            down_all()
            down_tile(place.ring(hops))
            ring[3]()

        def next_job(hop):
            down_tile(place.ring(hop))
            down_tile(place.ring(-hop))
            if hop == hops - 1:
                ring[4]()

        first_job_at = first_job
        for hop in range(hops - 1, 0, -1):
            jobs.append(functools.partial(next_job, hop))
            jobs.append(functools.partial(ring[1], hop))
        jobs.append(lambda: down_tile(place.d))

        count = [0]
        waits = []

        def staged(value_of, target):
            slot = count[0] % 2
            if count[0] >= 2:
                waits[count[0] - 2].wait()
            value_of(stage.at[slot])
            copy = pltpu.make_async_copy(stage.at[slot], target, stage_sem.at[slot])
            copy.start()
            waits.append(copy)
            count[0] += 1

        def weight_tile(ref, row, out):
            def fill(slot):
                for first in range(0, width, wide):
                    span = slice(first, first + wide)
                    value = term_rows(ref, normed, row, TILE, span)
                    slot[:, :, :, span] = value.reshape(slot.shape[:3] + (wide,))

            staged(fill, out.at[row // TILE])

        def result_tile(at):
            def fill(slot):
                left = rows_of(inner, at)
                for first in range(0, width, wide):
                    span = slice(first, first + wide)
                    value = jnp.dot(left, gate[:, span], preferred_element_type=jnp.float32)
                    slot[:, :, :, span] = value.astype(jnp.bfloat16).reshape(
                        slot.shape[:3] + (wide,)
                    )

            staged(fill, result_out.at[at])

        def sequence():
            first_job_at()
            for i in (1, 3, 2, 4):
                copies[i].wait()
            for low in range(chips - 1):
                high = chips - 1 - low

                @pl.when(high > chip)
                def _():
                    partial(high)

                @pl.when(low < chip)
                def _():
                    partial(low)

                if jobs:
                    jobs.pop(0)()
                for half in range(SUB):
                    step(low, half)
            partial(chip)
            for job in jobs:
                job()
            copies[5].start()
            copies[6].wait()
            for row in range(0, held, TILE):
                weight_tile(dgate, row, gate_out)
            for row in range(0, held, TILE):
                weight_tile(dup, row, up_out)
            copies[5].wait()
            for at in range(chips):
                result_tile(at)

        def finish():
            ring[2]()
            finish_line()
            for copy in waits[-2:]:
                copy.wait()

        return start, {0: sequence}, finish


def move(parts, dps, groups, number, greet=greet_near):
    def kernel(*refs):
        place = Place(dps, groups)
        at = [
            0,
            sum(len(part.inputs) for part in parts),
            sum(len(part.inputs) + len(part.outs) for part in parts),
        ]
        bound = []
        for part in parts:
            mine = []
            for kind, length in enumerate((len(part.inputs), len(part.outs), len(part.scratch))):
                mine += refs[at[kind] : at[kind] + length]
                at[kind] += length
            bound.append(part.bind(place, *mine))
        greet(place)
        for start, _, _ in bound:
            start()
        for tick in range(1 + max([0] + [max(list(ticks) + [0]) for _, ticks, _ in bound])):
            for _, ticks, _ in bound:
                if tick in ticks:
                    ticks[tick]()
        for _, _, finish in bound:
            finish()

    outs = pl.pallas_call(
        kernel,
        out_shape=[out for part in parts for out in part.outs],
        in_specs=[spec for part in parts for spec in part.in_specs],
        out_specs=[spec for part in parts for spec in part.out_specs],
        scratch_shapes=[one for part in parts for one in part.scratch],
        compiler_params=pltpu.CompilerParams(
            collective_id=number, has_side_effects=True, vmem_limit_bytes=63 << 20
        ),
        cost_estimate=pl.CostEstimate(flops=0, bytes_accessed=120_000_000, transcendentals=0),
        name=f"move_{number}",
    )(*[x for part in parts for x in part.inputs])
    results, at = [], 0
    for part in parts:
        results.append(part.result(*outs[at : at + len(part.outs)]))
        at += len(part.outs)
    return results


def norm_factor(values):
    return lax.rsqrt(jnp.mean(values * values, axis=-1, keepdims=True) + epsilon)


def norm_grad(values, factor, gain, gradient):
    weighted = gradient * gain
    inner_mean = jnp.mean(weighted * values, axis=-1, keepdims=True)
    return factor * weighted - values * (factor * factor * factor) * inner_mean


def rope_tables(positions, head_width):
    half_width = head_width // 2
    frequency = rope_base ** (-2.0 * jnp.arange(half_width, dtype=jnp.float32) / head_width)
    angles = positions.astype(jnp.float32)[:, None] * frequency[None, :]
    return (jnp.cos(angles)[:, None, :], jnp.sin(angles)[:, None, :])


def rotate(values, cosine_table, sine_table):
    half_width = values.shape[-1] // 2
    first_half = values[..., :half_width]
    second_half = values[..., half_width:]
    return jnp.concatenate(
        [
            first_half * cosine_table - second_half * sine_table,
            second_half * cosine_table + first_half * sine_table,
        ],
        axis=-1,
    )


def block_scores(query_block, key_heads, lower, upper, score_scale):
    scores = (
        jnp.einsum(
            "qhd,kd->hqk", query_block, key_heads[:upper], preferred_element_type=jnp.float32
        )
        * score_scale
    )
    rows_at = lower + jnp.arange(query_block.shape[0], dtype=jnp.int32)
    cols_at = jnp.arange(upper, dtype=jnp.int32)
    allowed = (cols_at[None, :] <= rows_at[:, None])[None]
    return jnp.where(allowed, scores, masked_value)


def per_device(
    tokens,
    qkv_weight,
    out_weight,
    gate_weight,
    up_weight,
    down_weight,
    attn_gain,
    mlp_gain,
    cotangent,
):
    groups = lax.axis_size("seq")
    dps = lax.axis_size("dp")
    tok_rows = tokens.shape[1]
    model_width = tokens.shape[2]
    weight_rows = qkv_weight.shape[0]
    seq_len = tok_rows * groups
    local_heads = HEADS // groups
    local_width = local_heads * HEAD_DIM
    kv_copies = groups // KV_HEADS
    score_scale = HEAD_DIM ** (-0.5)
    block_rows = min(512, seq_len)
    block_count = seq_len // block_rows
    fold = groups // dps
    order = [(at % dps) * fold + at // dps for at in range(groups)]

    q_part = qkv_weight[:, :model_width].reshape(weight_rows, groups, local_width)
    k_part = qkv_weight[:, model_width : model_width + KV_HEADS * HEAD_DIM]
    v_part = qkv_weight[:, model_width + KV_HEADS * HEAD_DIM :]
    k_part = k_part.reshape(weight_rows, KV_HEADS, HEAD_DIM)
    v_part = v_part.reshape(weight_rows, KV_HEADS, HEAD_DIM)
    columns = jnp.stack(
        [
            jnp.concatenate(
                [q_part[:, g], k_part[:, g // kv_copies], v_part[:, g // kv_copies]], axis=1
            )
            for g in order
        ]
    )
    gain_width = attn_gain.shape[0]
    tile = jnp.zeros((8, 128), jnp.float32)
    tile = tile.at[0, :gain_width].set(attn_gain.astype(jnp.float32))
    tile = tile.at[1, :gain_width].set(mlp_gain.astype(jnp.float32))
    qkv_local, tokens_all, out_rows, gate_part, gains = move(
        [
            Columns(columns, dps, groups),
            LineGather(tokens[0], dps, groups),
            Rows(out_weight, dps, groups),
            RingGather(gate_weight, dps, groups),
            Spread(tile, False, dps, groups),
        ],
        dps,
        groups,
        1,
        greet_all,
    )
    gain_one = gains[:, 0, :gain_width].reshape(model_width)
    gain_two = gains[:, 1, :gain_width].reshape(model_width)

    x_rows = tokens[0].astype(jnp.float32)
    factor_one = norm_factor(x_rows)
    all_rows = tokens_all.astype(jnp.float32)
    normed_all = (all_rows * norm_factor(all_rows) * gain_one).astype(jnp.bfloat16)
    grad_low = cotangent[0]
    grad_low, _ = lax.optimization_barrier((grad_low, gains))
    grad_all = lax.all_gather(grad_low, "seq", axis=0, tiled=True)

    mixed = jnp.dot(normed_all, qkv_local, preferred_element_type=jnp.float32)
    cosine_table, sine_table = rope_tables(jnp.arange(seq_len, dtype=jnp.int32), HEAD_DIM)
    query_heads = rotate(
        mixed[:, :local_width].reshape(seq_len, local_heads, HEAD_DIM), cosine_table, sine_table
    ).astype(jnp.bfloat16)
    key_heads = rotate(
        mixed[:, None, local_width : local_width + HEAD_DIM], cosine_table, sine_table
    ).astype(jnp.bfloat16)[:, 0]
    value_heads = mixed[:, local_width + HEAD_DIM :].astype(jnp.bfloat16)
    outputs = []
    log_sums = []
    for block in range(block_count):
        lower = block * block_rows
        upper = lower + block_rows
        scores = block_scores(query_heads[lower:upper], key_heads, lower, upper, score_scale)
        highest = jnp.max(scores, axis=-1, keepdims=True)
        log_sum = highest + jnp.log(jnp.sum(jnp.exp(scores - highest), axis=-1, keepdims=True))
        probs = jnp.exp(scores - log_sum).astype(jnp.bfloat16)
        attended = jnp.einsum(
            "hqk,kd->qhd", probs, value_heads[:upper], preferred_element_type=jnp.float32
        )
        outputs.append(attended.astype(jnp.bfloat16))
        log_sums.append(log_sum)
    attended = jnp.concatenate(outputs, axis=0).reshape(seq_len, local_width)
    partial = jnp.dot(attended, out_rows, preferred_element_type=jnp.float32)
    summed, up_part = move(
        [
            LineScatter(partial.astype(jnp.bfloat16), dps, groups),
            RingGather(up_weight, dps, groups),
        ],
        dps,
        groups,
        2,
    )
    hidden = x_rows + summed
    factor_two = norm_factor(hidden)
    normed_two = (hidden * factor_two * gain_two).astype(jnp.bfloat16)
    ((hn_all, down_part, inner, grad_gate, grad_upward),) = move(
        [FeedForward(normed_two, down_weight, gate_part, up_part, grad_all, dps, groups)],
        dps,
        groups,
        3,
    )
    ((grad_normed, down_owned, gate_term, up_term, result),) = move(
        [
            FeedBack(
                inner,
                grad_gate,
                grad_upward,
                gate_part,
                up_part,
                down_part,
                hn_all,
                grad_all,
                dps,
                groups,
            )
        ],
        dps,
        groups,
        4,
    )
    gain_two_term = jnp.sum(grad_normed * hidden * factor_two, axis=0)
    grad_hidden = grad_low.astype(jnp.float32) + norm_grad(
        hidden, factor_two, gain_two, grad_normed
    )
    grad_branch, gate_owned = move(
        [
            LineGather(grad_hidden.astype(jnp.bfloat16), dps, groups),
            RingScatter(gate_term, dps, groups),
        ],
        dps,
        groups,
        5,
    )
    result, grad_branch = lax.optimization_barrier((result, grad_branch))
    mlp_result = lax.psum_scatter(result, "seq", scatter_dimension=0, tiled=True)
    block_out = (hidden + mlp_result.astype(jnp.float32)).astype(jnp.bfloat16)[None]
    out_term = lax.dot_general(
        attended, grad_branch, contract_rows, preferred_element_type=jnp.float32
    ).astype(jnp.bfloat16)
    grad_heads = (
        lax.dot_general(grad_branch, out_rows, contract_cols, preferred_element_type=jnp.float32)
        .astype(jnp.bfloat16)
        .reshape(seq_len, local_heads, HEAD_DIM)
    )
    grad_keys = jnp.zeros((seq_len, HEAD_DIM), jnp.float32)
    grad_values = jnp.zeros((seq_len, HEAD_DIM), jnp.float32)
    grad_queries = []
    for block in range(block_count):
        lower = block * block_rows
        upper = lower + block_rows
        query_block = query_heads[lower:upper]
        grad_block = grad_heads[lower:upper]
        scores = block_scores(query_block, key_heads, lower, upper, score_scale)
        probs = jnp.exp(scores - log_sums[block])
        probs_low = probs.astype(jnp.bfloat16)
        grad_probs = jnp.einsum(
            "qhd,kd->hqk", grad_block, value_heads[:upper], preferred_element_type=jnp.float32
        )
        row_delta = jnp.sum(probs * grad_probs, axis=-1, keepdims=True)
        grad_scores = (probs * (grad_probs - row_delta)).astype(jnp.bfloat16)
        grad_queries.append(
            jnp.einsum(
                "hqk,kd->qhd", grad_scores, key_heads[:upper], preferred_element_type=jnp.float32
            )
            * score_scale
        )
        grad_keys = grad_keys.at[:upper].add(
            jnp.einsum("hqk,qhd->kd", grad_scores, query_block, preferred_element_type=jnp.float32)
            * score_scale
        )
        grad_values = grad_values.at[:upper].add(
            jnp.einsum("hqk,qhd->kd", probs_low, grad_block, preferred_element_type=jnp.float32)
        )
    grad_q = rotate(jnp.concatenate(grad_queries, axis=0), cosine_table, -sine_table)
    grad_k = rotate(grad_keys[:, None], cosine_table, -sine_table)[:, 0]
    grad_mixed = jnp.concatenate(
        [grad_q.reshape(seq_len, local_width), grad_k, grad_values], axis=1
    ).astype(jnp.bfloat16)
    qkv_term = lax.dot_general(
        normed_all, grad_mixed, contract_rows, preferred_element_type=jnp.float32
    )
    partial = lax.dot_general(
        grad_mixed, qkv_local, contract_cols, preferred_element_type=jnp.float32
    )
    qkv_owned, grad_normed_one, out_owned, up_owned = move(
        [
            ColumnsBack(qkv_term.astype(jnp.bfloat16), weight_rows, dps, groups),
            LineScatter(partial.astype(jnp.bfloat16), dps, groups),
            RowsBack(out_term, weight_rows, dps, groups),
            RingScatter(up_term, dps, groups),
        ],
        dps,
        groups,
        6,
        greet_all,
    )
    qkv_owned = qkv_owned.astype(jnp.float32)
    place = [order.index(g) for g in range(groups)]
    qkv_owned = jnp.concatenate(
        [qkv_owned[place[g], :, :local_width] for g in range(groups)]
        + [
            sum(
                qkv_owned[place[head * kv_copies + i], :, at : at + HEAD_DIM]
                for i in range(kv_copies)
            )
            for at in (local_width, local_width + HEAD_DIM)
            for head in range(KV_HEADS)
        ],
        axis=1,
    )
    gain_one_term = jnp.sum(grad_normed_one * x_rows * factor_one, axis=0)
    grad_input = grad_hidden + norm_grad(x_rows, factor_one, gain_one, grad_normed_one)
    terms = jnp.stack([gain_one_term, gain_two_term]).reshape(2, dps * groups, gain_width)
    terms = jnp.pad(terms.transpose(1, 0, 2), ((0, 0), (0, 6), (0, 128 - gain_width)))
    (gain_grads,) = move([Spread(terms, True, dps, groups)], dps, groups, 7, greet_all)
    return (
        block_out,
        grad_input[None],
        qkv_owned,
        out_owned,
        gate_owned,
        up_owned,
        down_owned,
        gain_grads[0, :gain_width],
        gain_grads[1, :gain_width],
    )


def solution(mesh):
    rows = P(("dp", "seq"), None)
    tokens = P("dp", "seq", None)
    gains = P(("dp", "seq"))
    return jax.shard_map(
        per_device,
        mesh=mesh,
        in_specs=(tokens, rows, rows, rows, rows, rows, gains, gains, tokens),
        out_specs=(tokens, tokens, rows, rows, rows, rows, rows, gains, gains),
        check_vma=False,
    )
```

```python
import functools

import jax
import jax.numpy as jnp
from jax import lax
from jax.experimental import pallas as pl
from jax.experimental.pallas import tpu as pltpu
from jax.sharding import PartitionSpec as P

HEADS = 32
KV_HEADS = 8
HEAD_DIM = 64

MESH = pl.DeviceIdType.MESH
ANY = pl.BlockSpec(memory_space=pl.ANY)
VM = pl.BlockSpec(memory_space=pltpu.VMEM)
SUB = 2

epsilon = 1e-05
rope_base = 500000.0
masked_value = -1e30
contract_rows = (((0,), (0,)), ((), ()))
contract_cols = (((1,), (1,)), ((), ()))


class Place:
    def __init__(self, dps, groups):
        self.dps, self.groups, self.chips, self.hops = dps, groups, groups // 2, dps // 2
        self.d, self.s = lax.axis_index("dp"), lax.axis_index("seq")
        self.chip, self.core = self.s // 2, self.s % 2
        self.partner = 2 * self.chip + 1 - self.core
        row, side = self.d // 2, self.d % 2
        self.turn = side * (dps - 1 - row) + (1 - side) * row

    def ring(self, distance):
        at = (self.turn + distance + self.dps) % self.dps
        side = at // self.hops
        return (1 - side) * 2 * at + side * (2 * (self.dps - 1 - at) + 1)


def remote(src, dst, send, recv, **target):
    return pltpu.make_async_remote_copy(
        src_ref=src, dst_ref=dst, send_sem=send, recv_sem=recv, device_id=target, device_id_type=MESH
    )


def greet_near(place):
    barrier = pltpu.get_barrier_semaphore()

    def signal(**target):
        pl.semaphore_signal(barrier, inc=1, device_id=target, device_id_type=MESH)

    signal(seq=place.partner)
    signal(dp=place.ring(1))
    signal(dp=place.ring(-1))

    @pl.when(place.chip > 0)
    def _():
        signal(seq=place.s - 2)

    @pl.when(place.chip < place.chips - 1)
    def _():
        signal(seq=place.s + 2)

    ends = (place.chips - place.chip) // place.chips + (place.chip + 1) // place.chips
    pl.semaphore_wait(barrier, 5 - ends)


def greet_all(place):
    barrier = pltpu.get_barrier_semaphore()
    count = place.dps * place.groups
    me = place.d * place.groups + place.s

    def signal(i, _):
        other = (me + i) % count
        pl.semaphore_signal(
            barrier,
            inc=1,
            device_id={"dp": other // place.groups, "seq": other % place.groups},
            device_id_type=MESH,
        )
        return 0

    lax.fori_loop(1, count, signal, 0)
    pl.semaphore_wait(barrier, count - 1)


DMA = pltpu.SemaphoreType.DMA


def line_gather(place, x_ref, out_ref, own_sem, us, ur, ds, dr, ps, pr):
    s, chip, chips = place.s, place.chip, place.chips

    def copy(src, group, half, sends, recvs, at, target):
        return remote(
            src, out_ref.at[group, half], sends.at[at, half], recvs.at[at, half], seq=target
        )

    def up(src, group, hop, half):
        return copy(src, group, half, us, ur, hop, s + 2)

    def down(src, group, hop, half):
        return copy(src, group, half, ds, dr, hop, s - 2)

    def pair(src, group, half):
        return copy(src, group, half, ps, pr, group // 2, place.partner)

    own = pltpu.make_async_copy(x_ref, out_ref.at[s], own_sem)

    def start():
        own.start()
        for half in range(SUB):

            @pl.when(chip < chips - 1)
            def _():
                up(x_ref.at[half], s, 0, half).start()

            @pl.when(chip > 0)
            def _():
                down(x_ref.at[half], s, 0, half).start()

        for half in range(SUB):
            pair(x_ref.at[half], s, half).start()

    def step(hop, half):
        below, above = s - 2 * hop, s + 2 * hop

        @pl.when(chip - hop >= 0)
        def _():
            block = out_ref.at[below, half]
            up(block, below, hop - 1, half).wait_recv()

            @pl.when(chip < chips - 1)
            def _():
                up(block, below, hop, half).start()

            pair(block, below, half).start()

        @pl.when(chip + hop < chips)
        def _():
            block = out_ref.at[above, half]
            down(block, above, hop - 1, half).wait_recv()

            @pl.when(chip > 0)
            def _():
                down(block, above, hop, half).start()

            pair(block, above, half).start()

    def arrived(at):
        for half in range(SUB):
            group = 2 * at + 1 - place.core
            pair(out_ref.at[group, half], group, half).wait_recv()

    def sent():
        def each(i, _):
            k, half = i // SUB, i % SUB
            mine = 2 * k + place.core
            block = out_ref.at[mine, half]
            pair(block, mine, half).wait_send()

            @pl.when(jnp.logical_and(chip - k >= 0, chip < chips - 1))
            def _():
                up(block, mine, k, half).wait_send()

            @pl.when(jnp.logical_and(chip + k < chips, chip > 0))
            def _():
                down(block, mine, k, half).wait_send()

            return 0

        lax.fori_loop(0, chips * SUB, each, 0)

    return own, start, step, arrived, sent


class LineGather:
    def __init__(self, x, dps, groups):
        rows, width = x.shape
        shape = (SUB, rows // SUB, width)
        self.inputs, self.in_specs = [x.reshape(shape)], [VM]
        self.outs, self.out_specs = [jax.ShapeDtypeStruct((groups,) + shape, x.dtype)], [ANY]
        self.scratch = [DMA] + [DMA((groups // 2, SUB))] * 6
        self.result = lambda out: out.reshape(groups * rows, width)

    def bind(self, place, *refs):
        own, start, step, arrived, sent = line_gather(place, *refs)

        def finish():
            own.wait()

            def each(at, _):
                arrived(at)
                return 0

            lax.fori_loop(0, place.chips, each, 0)
            sent()

        ticks = {
            (hop - 1) * SUB + half: functools.partial(step, hop, half)
            for hop in range(1, place.chips)
            for half in range(SUB)
        }
        return start, ticks, finish


def line_scatter(place, p_ref, out_ref, pairbuf, upbuf, downbuf, us, ur, ds, dr, ps, pr):
    s, chip, chips, core = place.s, place.chip, place.chips, place.core

    def copy(src, buffer, at, half, sends, recvs, target):
        return remote(src, buffer.at[at, half], sends.at[at, half], recvs.at[at, half], seq=target)

    def pair(at, half):
        src = p_ref.at[2 * at + 1 - core, half]
        return copy(src, pairbuf, at, half, ps, pr, place.partner)

    def up(at, half):
        return copy(upbuf.at[at, half], upbuf, at, half, us, ur, s + 2)

    def down(at, half):
        return copy(downbuf.at[at, half], downbuf, at, half, ds, dr, s - 2)

    def wide(ref, *at):
        return ref[at].astype(jnp.float32)

    def local(at, half):
        return wide(p_ref, 2 * at + core, half) + wide(pairbuf, at, half)

    def send(at):
        for half in range(SUB):
            pair(at, half).start()

    def step(wave, half):
        high, low = chips - 1 - wave + chip, wave - (chips - 1 - chip)

        @pl.when(chip <= wave)
        def _():
            pair(high, half).wait_recv()

            @pl.when(chip > 0)
            def _():
                up(high, half).wait_recv()
                total = local(high, half) + wide(upbuf, high, half)
                upbuf[high, half] = total.astype(jnp.bfloat16)

            @pl.when(chip == 0)
            def _():
                upbuf[high, half] = local(high, half).astype(jnp.bfloat16)

            up(high, half).start()

        @pl.when(low >= 0)
        def _():
            pair(low, half).wait_recv()

            @pl.when(chip < chips - 1)
            def _():
                down(low, half).wait_recv()
                total = local(low, half) + wide(downbuf, low, half)
                downbuf[low, half] = total.astype(jnp.bfloat16)

            @pl.when(chip == chips - 1)
            def _():
                downbuf[low, half] = local(low, half).astype(jnp.bfloat16)

            down(low, half).start()

    def finish():
        for half in range(SUB):
            pair(chip, half).wait_recv()
            out_ref[half] = local(chip, half)

            @pl.when(chip > 0)
            def _():
                up(chip, half).wait_recv()
                out_ref[half] += wide(upbuf, chip, half)

            @pl.when(chip < chips - 1)
            def _():
                down(chip, half).wait_recv()
                out_ref[half] += wide(downbuf, chip, half)

        def each(i, _):
            at, half = i // SUB, i % SUB
            pair(at, half).wait_send()

            @pl.when(at > chip)
            def _():
                up(at, half).wait_send()

            @pl.when(at < chip)
            def _():
                down(at, half).wait_send()

            return 0

        lax.fori_loop(0, chips * SUB, each, 0)

    return send, step, finish


def line_scatter_scratch(chips, shape):
    return [pltpu.VMEM((chips,) + shape, jnp.bfloat16)] * 3 + [DMA((chips, SUB))] * 6


class LineScatter:
    def __init__(self, partial, dps, groups):
        total, width = partial.shape
        rows = total // groups
        shape = (SUB, rows // SUB, width)
        self.inputs, self.in_specs = [partial.reshape((groups,) + shape)], [VM]
        self.outs, self.out_specs = [jax.ShapeDtypeStruct(shape, jnp.float32)], [VM]
        self.scratch = line_scatter_scratch(groups // 2, shape)
        self.result = lambda out: out.reshape(rows, width)

    def bind(self, place, *refs):
        send, step, finish = line_scatter(place, *refs)
        chip, chips = place.chip, place.chips

        def start():
            def issue(low, _):
                high = chips - 1 - low

                @pl.when(high > chip)
                def _():
                    send(high)

                @pl.when(low < chip)
                def _():
                    send(low)

                return 0

            lax.fori_loop(0, chips - 1, issue, 0)
            send(chip)

        ticks = {
            i: functools.partial(step, i // SUB, i % SUB) for i in range((chips - 1) * SUB)
        }
        return start, ticks, finish


def ring_sems(hops):
    return [DMA((hops, 2))] * 4


def ring_gather(place, own, out, rs, rr, ls, lr):
    hops = place.hops

    def right(src, chunk, hop, half):
        return remote(
            src, out(chunk, half), rs.at[hop - 1, half], rr.at[hop - 1, half], dp=place.ring(1)
        )

    def left(src, chunk, hop, half):
        return remote(
            src, out(chunk, half), ls.at[hop - 1, half], lr.at[hop - 1, half], dp=place.ring(-1)
        )

    def start():
        for half in range(2):
            right(own(half), place.d, 1, half).start()
            left(own(1 - half), place.d, 1, 1 - half).start()

    def forward(hop):
        before, after = place.ring(-hop), place.ring(hop)
        full = hop < hops - 1
        right(out(before, 0), before, hop, 0).wait_recv()
        right(out(before, 0), before, hop + 1, 0).start()
        left(out(after, 1), after, hop, 1).wait_recv()
        left(out(after, 1), after, hop + 1, 1).start()
        right(out(before, 1), before, hop, 1).wait_recv()
        left(out(after, 0), after, hop, 0).wait_recv()
        if full:
            right(out(before, 1), before, hop + 1, 1).start()
            left(out(after, 0), after, hop + 1, 0).start()

    def finish():
        right(out(place.d, 0), place.ring(-hops), hops, 0).wait_recv()
        left(out(place.d, 1), place.ring(hops), hops, 1).wait_recv()
        for hop in range(1, hops + 1):
            for half in range(2):
                if hop < hops or half == 0:
                    right(out(place.d, half), place.d, hop, half).wait_send()
                if hop < hops or half == 1:
                    left(out(place.d, half), place.d, hop, half).wait_send()

    return start, forward, finish


def ring_scatter(place, part, put, rbuf, lbuf, rout, lout, rs, rr, ls, lr):
    hops = place.hops

    def wide(ref):
        return ref[...].astype(jnp.float32)

    def right(src, hop, half):
        return remote(
            src,
            rbuf.at[hop - 1, half],
            rs.at[hop - 1, half],
            rr.at[hop - 1, half],
            dp=place.ring(1),
        )

    def left(src, hop, half):
        return remote(
            src,
            lbuf.at[hop - 1, half],
            ls.at[hop - 1, half],
            lr.at[hop - 1, half],
            dp=place.ring(-1),
        )

    def start_far():
        right(part(place.ring(hops), 0), hops, 0).start()
        left(part(place.ring(-hops), 1), hops, 1).start()

    def start_next():
        right(part(place.ring(hops - 1), 1), hops - 1, 1).start()
        left(part(place.ring(1 - hops), 0), hops - 1, 0).start()

    def start():
        start_far()
        start_next()

    def forward(hop):
        for first in range(2 if hop < hops - 1 else 1):
            half = first
            right(rbuf.at[hop, half], hop + 1, half).wait_recv()
            total = wide(part(place.ring(hop), half)) + wide(rbuf.at[hop, half])
            rout[hop - 1, half] = total.astype(jnp.bfloat16)
            right(rout.at[hop - 1, half], hop, half).start()
            half = 1 - first
            left(lbuf.at[hop, half], hop + 1, half).wait_recv()
            total = wide(part(place.ring(-hop), half)) + wide(lbuf.at[hop, half])
            lout[hop - 1, half] = total.astype(jnp.bfloat16)
            left(lout.at[hop - 1, half], hop, half).start()

    def finish():
        for half in range(2):
            right(rbuf.at[0, half], 1, half).wait_recv()
            left(lbuf.at[0, half], 1, half).wait_recv()
            put(
                half,
                wide(part(place.d, half)) + wide(rbuf.at[0, half]) + wide(lbuf.at[0, half]),
            )
        for hop in range(1, hops + 1):
            for half in range(2):
                if hop < hops or half == 0:
                    right(rbuf.at[0, half], hop, half).wait_send()
                if hop < hops or half == 1:
                    left(lbuf.at[0, half], hop, half).wait_send()

    return start, forward, finish, start_far, start_next


class RingGather:
    def __init__(self, x, dps, groups):
        rows, width = x.shape
        shape = (2, rows // 2, width)
        self.inputs, self.in_specs = [x.reshape(shape)], [VM]
        self.outs, self.out_specs = [jax.ShapeDtypeStruct((dps,) + shape, x.dtype)], [ANY]
        self.scratch = [DMA] + ring_sems(dps // 2)
        self.result = lambda out: out.reshape(dps * rows, width)

    def bind(self, place, x_ref, out_ref, own_sem, *sems):
        own = pltpu.make_async_copy(x_ref, out_ref.at[place.d], own_sem)
        ring = ring_gather(
            place, lambda half: x_ref.at[half], lambda chunk, half: out_ref.at[chunk, half], *sems
        )

        def start():
            ring[0]()
            own.start()

        def finish():
            own.wait()
            ring[2]()

        ticks = {2 * hop - 1: functools.partial(ring[1], hop) for hop in range(1, place.hops)}
        return start, ticks, finish


class RingScatter:
    def __init__(self, partial, dps, groups):
        total, width = partial.shape
        rows, hops = total // dps, dps // 2
        shape = (2, rows // 2, width)
        self.inputs, self.in_specs = [partial.reshape((dps,) + shape)], [VM]
        self.outs, self.out_specs = [jax.ShapeDtypeStruct(shape, jnp.float32)], [VM]
        self.scratch = (
            [pltpu.VMEM((hops,) + shape, jnp.bfloat16)] * 2
            + [pltpu.VMEM((hops - 1,) + shape, jnp.bfloat16)] * 2
            + ring_sems(hops)
        )
        self.result = lambda out: out.reshape(rows, width)

    def bind(self, place, p_ref, out_ref, *scratch):
        def put(half, value):
            out_ref[half] = value

        ring = ring_scatter(place, lambda chunk, half: p_ref.at[chunk, half], put, *scratch)
        ticks = {
            2 * (place.hops - hop) - 1: functools.partial(ring[1], hop)
            for hop in range(1, place.hops)
        }
        return ring[0], ticks, ring[2]


class Columns:
    def __init__(self, blocks, dps, groups):
        _, rows, width = blocks.shape
        self.inputs, self.in_specs = [blocks], [VM]
        self.outs = [jax.ShapeDtypeStruct((dps, groups, rows, width), blocks.dtype)]
        self.out_specs = [ANY]
        self.scratch = [
            pltpu.VMEM((groups, rows, width), blocks.dtype),
            DMA((2,)),
            DMA((groups,)),
            DMA((groups,)),
        ] + ring_sems(dps // 2)
        self.result = lambda out: out.reshape(dps * groups * rows, width)

    def bind(self, place, x_ref, out_ref, landing, own_sem, sends, recvs, *sems):
        s, groups = place.s, place.groups
        half_of = groups // 2
        here = pltpu.make_async_copy(x_ref.at[s], landing.at[s], own_sem.at[0])
        own = pltpu.make_async_copy(landing, out_ref.at[place.d], own_sem.at[1])

        def swap(i):
            to = (s + i) % groups
            return remote(x_ref.at[to], landing.at[s], sends.at[i], recvs.at[i], seq=to)

        ring = ring_gather(
            place,
            lambda half: landing.at[pl.ds(half * half_of, half_of)],
            lambda chunk, half: out_ref.at[chunk, pl.ds(half * half_of, half_of)],
            *sems,
        )

        def start():
            here.start()
            for i in range(1, groups):
                swap(i).start()

        def middle():
            here.wait()
            for i in range(1, groups):
                swap(i).wait_recv()
            ring[0]()
            own.start()

        def finish():
            for i in range(1, groups):
                swap(i).wait_send()
            own.wait()
            ring[2]()

        ticks = {1 + 2 * hop: functools.partial(ring[1], hop) for hop in range(1, place.hops)}
        ticks[1] = middle
        return start, ticks, finish


class ColumnsBack:
    def __init__(self, partial, order, heads_width, copies, rows, dps, groups):
        width, hops = partial.shape[1], dps // 2
        shape = (groups, rows, width)
        halves = (2, groups // 2, rows, width)
        self.where = [order.index(g) for g in range(groups)]
        self.heads_width, self.copies = heads_width, copies
        joint = groups * heads_width + 2 * KV_HEADS * HEAD_DIM
        self.inputs, self.in_specs = [partial.reshape((dps,) + halves)], [VM]
        self.outs, self.out_specs = [jax.ShapeDtypeStruct((rows, joint), jnp.float32)], [VM]
        self.scratch = (
            [pltpu.VMEM(shape, jnp.bfloat16), pltpu.VMEM(halves, jnp.bfloat16)]
            + [DMA, DMA((groups,)), DMA((groups,))]
            + [pltpu.VMEM((hops,) + halves, jnp.bfloat16)] * 2
            + [pltpu.VMEM((hops - 1,) + halves, jnp.bfloat16)] * 2
            + ring_sems(hops)
        )
        self.result = lambda out: out

    def bind(self, place, p_ref, joint_ref, out_ref, total, own_sem, sends, recvs, *scratch):
        s, groups = place.s, place.groups
        half_of = groups // 2

        def put(half, value):
            total[half] = value.astype(jnp.bfloat16)

        ring = ring_scatter(place, lambda chunk, half: p_ref.at[chunk, half], put, *scratch)
        here = pltpu.make_async_copy(
            total.at[s // half_of, s % half_of], out_ref.at[s], own_sem
        )

        def swap(i):
            to = (s + i) % groups
            src = total.at[to // half_of, to % half_of]
            return remote(src, out_ref.at[s], sends.at[i], recvs.at[i], seq=to)

        def last():
            ring[2]()
            here.start()
            for i in range(1, groups):
                swap(i).start()

        def keys_values(head):
            first = self.where[head * self.copies]
            span = slice(self.heads_width, self.heads_width + 2 * HEAD_DIM)
            value = out_ref[first, :, span].astype(jnp.float32)
            for i in range(1, self.copies):
                value += out_ref[self.where[head * self.copies + i], :, span].astype(jnp.float32)
            return value

        def finish():
            here.wait()
            for i in range(1, groups):
                swap(i).wait_recv()
                swap(i).wait_send()
            heads = self.heads_width
            for g in range(groups):
                value = out_ref[self.where[g], :, :heads]
                joint_ref[:, g * heads : (g + 1) * heads] = value.astype(jnp.float32)
            for head in range(0, KV_HEADS, 2):
                even, odd = keys_values(head), keys_values(head + 1)
                lanes = lax.broadcasted_iota(jnp.int32, even.shape, 1)
                at = groups * heads + head * HEAD_DIM
                joint_ref[:, at : at + 2 * HEAD_DIM] = jnp.where(
                    lanes < HEAD_DIM, even, pltpu.roll(odd, HEAD_DIM, 1)
                )
                at += KV_HEADS * HEAD_DIM
                joint_ref[:, at : at + 2 * HEAD_DIM] = jnp.where(
                    lanes < HEAD_DIM, pltpu.roll(even, HEAD_DIM, 1), odd
                )

        ticks = {
            2 * (place.hops - hop) - 1: functools.partial(ring[1], hop)
            for hop in range(1, place.hops)
        }
        ticks[2 * place.hops - 1] = last
        return ring[0], ticks, finish


class Rows:
    def __init__(self, x, dps, groups):
        rows, width = x.shape
        shape = (2, rows // 2, width)
        self.inputs, self.in_specs = [x.reshape(shape)], [VM]
        self.outs, self.out_specs = [jax.ShapeDtypeStruct((dps,) + shape, x.dtype)], [ANY]
        self.scratch = [
            pltpu.VMEM((dps,) + shape, x.dtype),
            DMA((2,)),
            DMA((dps,)),
            DMA((dps,)),
        ] + ring_sems(dps // 2)
        self.result = lambda out: out.reshape(dps * rows, width)

    def bind(self, place, x_ref, out_ref, landing, own_sem, sends, recvs, *sems):
        s, dps = place.s, place.dps
        slot, base = s % dps, s // dps * dps
        first = pltpu.make_async_copy(x_ref, landing.at[place.d], own_sem.at[0])
        here = pltpu.make_async_copy(landing.at[slot], out_ref.at[slot], own_sem.at[1])
        ring = ring_gather(
            place, lambda half: x_ref.at[half], lambda chunk, half: landing.at[chunk, half], *sems
        )

        def swap(i):
            to = (slot + i) % dps
            return remote(landing.at[to], out_ref.at[slot], sends.at[i], recvs.at[i], seq=base + to)

        def start():
            ring[0]()
            first.start()

        def last():
            first.wait()
            ring[2]()
            here.start()
            for i in range(1, dps):
                swap(i).start()

        def finish():
            here.wait()
            for i in range(1, dps):
                swap(i).wait_recv()
                swap(i).wait_send()

        ticks = {2 * hop - 1: functools.partial(ring[1], hop) for hop in range(1, place.hops)}
        ticks[2 * place.hops] = last
        return start, ticks, finish


class RowsBack:
    def __init__(self, partial, rows, dps, groups):
        width, hops = partial.shape[1], dps // 2
        shape = (2, rows // 2, width)
        self.inputs, self.in_specs = [partial.reshape((dps,) + shape)], [VM]
        self.outs, self.out_specs = [jax.ShapeDtypeStruct(shape, jnp.float32)], [VM]
        self.scratch = (
            [pltpu.VMEM((dps,) + shape, jnp.bfloat16), DMA, DMA((dps,)), DMA((dps,))]
            + [pltpu.VMEM((hops,) + shape, jnp.bfloat16)] * 2
            + [pltpu.VMEM((hops - 1,) + shape, jnp.bfloat16)] * 2
            + ring_sems(hops)
        )
        self.result = lambda out: out.reshape(rows, width)

    def bind(self, place, p_ref, out_ref, landing, own_sem, sends, recvs, *scratch):
        s, dps = place.s, place.dps
        slot, base = s % dps, s // dps * dps
        here = pltpu.make_async_copy(p_ref.at[slot], landing.at[slot], own_sem)

        def swap(i):
            to = (slot + i) % dps
            return remote(p_ref.at[to], landing.at[slot], sends.at[i], recvs.at[i], seq=base + to)

        def put(half, value):
            out_ref[half] = value

        ring = ring_scatter(place, lambda chunk, half: landing.at[chunk, half], put, *scratch)

        def start():
            here.start()
            for i in range(1, dps):
                swap(i).start()

        def middle():
            here.wait()
            for i in range(1, dps):
                swap(i).wait_recv()
            ring[0]()

        def finish():
            for i in range(1, dps):
                swap(i).wait_send()
            ring[2]()

        ticks = {
            2 * (place.hops - hop) + 2: functools.partial(ring[1], hop)
            for hop in range(1, place.hops)
        }
        ticks[2] = middle
        return start, ticks, finish


class Spread:
    def __init__(self, tiles, total, dps, groups):
        count, shape = dps * groups, tiles.shape[-2:]
        self.total = total
        self.inputs, self.in_specs = [tiles], [VM]
        out = shape if total else (count,) + shape
        self.outs, self.out_specs = [jax.ShapeDtypeStruct(out, jnp.float32)], [VM]
        self.scratch = [pltpu.VMEM((count,) + shape, jnp.float32), DMA((count,)), DMA((count,))]
        self.result = lambda out: out

    def bind(self, place, x_ref, out_ref, landing, sends, recvs):
        count = place.dps * place.groups
        me = place.d * place.groups + place.s

        def copy(i):
            other = (me + i) % count
            return remote(
                x_ref.at[other] if self.total else x_ref,
                landing.at[me],
                sends.at[i],
                recvs.at[i],
                dp=other // place.groups,
                seq=other % place.groups,
            )

        def start():
            def each(i, _):
                copy(i).start()
                return 0

            lax.fori_loop(1, count, each, 0)

        def finish():
            def each(i, _):
                copy(i).wait_recv()
                copy(i).wait_send()
                return 0

            lax.fori_loop(1, count, each, 0)
            landing[me] = x_ref[me] if self.total else x_ref[...]
            out_ref[...] = jnp.sum(landing[...], axis=0) if self.total else landing[...]

        return start, {}, finish


TILE = 256


class FeedForward:
    def __init__(self, normed, down, gate, up, grad_all, dps, groups):
        rows, width = normed.shape
        shape, chips = (SUB, rows // SUB, width), groups // 2
        held = gate.shape[0]
        ring = (2, down.shape[0] // 2, width)
        pair = 2 * rows
        self.inputs = [
            normed.reshape(shape),
            down.reshape(ring),
            gate,
            up,
            grad_all.reshape(chips, pair, width),
        ]
        self.in_specs = [VM, VM, ANY, ANY, ANY]
        act = jax.ShapeDtypeStruct((chips, pair, held), jnp.bfloat16)
        self.outs = [
            jax.ShapeDtypeStruct((groups,) + shape, jnp.bfloat16),
            jax.ShapeDtypeStruct((dps,) + ring, jnp.bfloat16),
            act,
            act,
            act,
        ]
        self.out_specs = [VM] * 5
        self.scratch = [
            pltpu.VMEM((held, width), jnp.bfloat16),
            pltpu.VMEM((held, width), jnp.bfloat16),
            pltpu.VMEM((chips, pair, width), jnp.bfloat16),
            pltpu.VMEM((chips, pair, held), jnp.float32),
            pltpu.VMEM((chips, pair, held), jnp.float32),
            DMA((4,)),
            DMA,
        ]
        self.scratch += [DMA((chips, SUB))] * 6 + ring_sems(dps // 2)
        self.result = lambda hn, full, *acts: (
            hn.reshape(groups * rows, width),
            full.reshape(held, width),
            *[one.reshape(groups * rows, held) for one in acts],
        )

    def bind(self, place, x_ref, shard, gate_at, up_at, grad_at, *refs):
        hn, full, inner, dgate, dup, gate_w, up_w, grads, slope, silu = refs[:10]
        loads, own_line = refs[10:12]
        line_sems, ring_refs = refs[12:18], refs[18:]
        chip, chips = place.chip, place.chips
        pair, held = inner.shape[1:]
        width = gate_w.shape[1]
        own, start_line, step, arrived, sent = line_gather(place, x_ref, hn, own_line, *line_sems)
        ring = ring_gather(
            place,
            lambda half: shard.at[half],
            lambda chunk, half: full.at[chunk, half],
            *ring_refs,
        )
        copies = [
            pltpu.make_async_copy(gate_at, gate_w, loads.at[0]),
            pltpu.make_async_copy(up_at, up_w, loads.at[1]),
            pltpu.make_async_copy(grad_at, grads, loads.at[2]),
            pltpu.make_async_copy(shard, full.at[place.d], loads.at[3]),
        ]
        wide = 512 if held % 512 == 0 else held

        def start():
            start_line()
            ring[0]()
            for one in copies:
                one.start()

        def forward(at):
            rows = hn[pl.ds(2 * at, 2)].reshape(pair, width)
            for first in range(0, held, wide):
                span = slice(first, first + wide)
                gate = lax.dot_general(
                    rows, gate_w[span, :], contract_cols, preferred_element_type=jnp.float32
                )
                upward = lax.dot_general(
                    rows, up_w[span, :], contract_cols, preferred_element_type=jnp.float32
                )
                sigmoid = jax.nn.sigmoid(gate)
                passed = gate * sigmoid
                inner[at, :, span] = (passed * upward).astype(jnp.bfloat16)
                silu[at, :, span] = passed
                slope[at, :, span] = upward * sigmoid * (1.0 + gate * (1.0 - sigmoid))

        def when_there(at, there):
            @pl.when(there)
            def _():
                arrived(at)
                forward(at)

        def tick(hop, half):
            step(hop, half)
            if hop == 1 and half == 0:
                own.wait()
                copies[0].wait()
                copies[1].wait()
                arrived(chip)
                forward(chip)
            if hop > 1 and half == 0:
                when_there(chip - hop + 1, chip - hop + 1 >= 0)
            if hop > 1 and half == SUB - 1:
                when_there(chip + hop - 1, chip + hop - 1 < chips)

        def finish():
            last = chips - 1
            when_there(chip - last, chip - last >= 0)
            when_there(chip + last, chip + last < chips)
            copies[2].wait()
            copies[3].wait()
            ring[2]()

            def back(at, _):
                rows = grads[at]
                for first in range(0, held, wide):
                    span = slice(first, first + wide)
                    chunk = full.shape[1] * full.shape[2]
                    part = full[first // chunk : (first + wide) // chunk].reshape(wide, width)
                    grad = lax.dot_general(
                        rows, part, contract_cols, preferred_element_type=jnp.float32
                    )
                    dgate[at, :, span] = (grad * slope[at, :, span]).astype(jnp.bfloat16)
                    dup[at, :, span] = (grad * silu[at, :, span]).astype(jnp.bfloat16)
                return 0

            lax.fori_loop(0, chips, back, 0)
            sent()

        ticks = {
            (hop - 1) * SUB + half: functools.partial(tick, hop, half)
            for hop in range(1, chips)
            for half in range(SUB)
        }

        def with_ring(tick, hop):
            ticks[tick]()
            ring[1](hop)

        merged = dict(ticks)
        for hop in range(1, place.hops):
            merged[2 * hop - 1] = functools.partial(with_ring, 2 * hop - 1, hop)
        return start, merged, finish


class FeedBack:
    def __init__(self, inner, dgate, dup, gate, up, down, normed, grads, dps, groups):
        length, held = inner.shape
        width, chips = normed.shape[1], groups // 2
        rows = length // groups
        shape = (SUB, rows // SUB, width)
        owned = (2, held // dps // 2, width)
        hops = dps // 2
        tile = (2, SUB, rows // SUB, width)
        self.inputs = [inner, dgate, dup, gate, up, down, normed, grads]
        self.in_specs = [ANY] * 8
        self.outs = [
            jax.ShapeDtypeStruct(shape, jnp.float32),
            jax.ShapeDtypeStruct(owned, jnp.float32),
            jax.ShapeDtypeStruct((held // TILE,) + tile, jnp.bfloat16),
            jax.ShapeDtypeStruct((held // TILE,) + tile, jnp.bfloat16),
            jax.ShapeDtypeStruct((chips,) + tile, jnp.bfloat16),
        ]
        self.out_specs = [VM, VM, ANY, ANY, ANY]
        act = pltpu.VMEM((length, held), jnp.bfloat16)
        weight = pltpu.VMEM((held, width), jnp.bfloat16)
        tokens = pltpu.VMEM((length, width), jnp.bfloat16)
        self.scratch = [act] * 3 + [weight] * 3 + [tokens] * 2
        self.scratch += [
            pltpu.VMEM((groups,) + shape, jnp.bfloat16),
            pltpu.VMEM((dps,) + owned, jnp.bfloat16),
            pltpu.VMEM((2,) + tile, jnp.bfloat16),
            DMA((8,)),
            DMA((2,)),
        ]
        self.scratch += line_scatter_scratch(chips, shape)
        self.scratch += (
            [pltpu.VMEM((hops,) + owned, jnp.bfloat16)] * 2
            + [pltpu.VMEM((hops - 1,) + owned, jnp.bfloat16)] * 2
            + ring_sems(hops)
        )
        self.result = lambda total, mine, gate_term, up_term, out: (
            total.reshape(rows, width),
            mine.reshape(held // dps, width),
            gate_term.reshape(held, width),
            up_term.reshape(held, width),
            out.reshape(length, width),
        )

    def bind(self, place, *refs):
        sources, refs = refs[:8], refs[8:]
        total_ref, own_ref, gate_out, up_out, result_out = refs[:5]
        inner, dgate, dup, gate, up, down, normed, grads = refs[5:13]
        p_ref, term, stage, loads, stage_sem = refs[13:18]
        line_refs, ring_refs = refs[18:27], refs[27:]
        chip, chips, hops = place.chip, place.chips, place.hops
        held, width = gate.shape
        pair = inner.shape[0] // chips
        chunk = held // place.dps
        wide = 1024 if width % 1024 == 0 else width
        send, step, finish_line = line_scatter(place, p_ref, total_ref, *line_refs)

        def put(half, value):
            own_ref[half] = value

        ring = ring_scatter(place, lambda at, half: term.at[at, half], put, *ring_refs)
        targets = [inner, dgate, dup, gate, up, down, normed, grads]
        copies = [
            pltpu.make_async_copy(source, target, loads.at[i])
            for i, (source, target) in enumerate(zip(sources, targets))
        ]

        def start():
            for i in (0, 7, 1, 3, 2, 4, 6, 5):
                copies[i].start()

        def rows_of(ref, at):
            return ref[pl.ds(pl.multiple_of(at * pair, pair), pair), :]

        def partial(at):
            left, right = rows_of(dgate, at), rows_of(dup, at)
            for first in range(0, width, wide):
                span = slice(first, first + wide)
                value = jnp.dot(left, gate[:, span], preferred_element_type=jnp.float32)
                value += jnp.dot(right, up[:, span], preferred_element_type=jnp.float32)
                p_ref[pl.ds(2 * at, 2), :, :, span] = value.astype(jnp.bfloat16).reshape(
                    p_ref[pl.ds(2 * at, 2), :, :, span].shape
                )
            send(at)

        def term_rows(ref, other, start, count, span):
            return lax.dot_general(
                ref[:, pl.ds(start, count)],
                other[:, span],
                contract_rows,
                preferred_element_type=jnp.float32,
            ).astype(jnp.bfloat16)

        def down_tile(at):
            if chunk % 128 == 0:
                for first in range(0, width, wide):
                    span = slice(first, first + wide)
                    value = term_rows(inner, grads, pl.multiple_of(at * chunk, chunk), chunk, span)
                    term[at, :, :, span] = value.reshape(2, chunk // 2, wide)

        def down_all():
            if chunk % 128 != 0:
                for row in range(0, held, TILE):
                    for first in range(0, width, wide):
                        span = slice(first, first + wide)
                        value = term_rows(inner, grads, row, TILE, span)
                        term[row // chunk : (row + TILE) // chunk, :, :, span] = value.reshape(
                            TILE // chunk, 2, chunk // 2, wide
                        )

        jobs = []

        def first_job():
            copies[0].wait()
            copies[7].wait()
            down_all()
            down_tile(place.ring(hops))
            ring[3]()

        def next_job(hop):
            down_tile(place.ring(hop))
            down_tile(place.ring(-hop))
            if hop == hops - 1:
                ring[4]()

        for hop in range(hops - 1, 0, -1):
            jobs.append(functools.partial(next_job, hop))
            jobs.append(functools.partial(ring[1], hop))
        jobs.append(lambda: down_tile(place.d))

        count = [0]
        waits = []

        def staged(value_of, target):
            slot = count[0] % 2
            if count[0] >= 2:
                waits[count[0] - 2].wait()
            value_of(stage.at[slot])
            copy = pltpu.make_async_copy(stage.at[slot], target, stage_sem.at[slot])
            copy.start()
            waits.append(copy)
            count[0] += 1

        def weight_tile(ref, row, out):
            def fill(slot):
                for first in range(0, width, wide):
                    span = slice(first, first + wide)
                    value = term_rows(ref, normed, row, TILE, span)
                    slot[:, :, :, span] = value.reshape(slot.shape[:3] + (wide,))

            staged(fill, out.at[row // TILE])

        def result_tile(at):
            def fill(slot):
                left = rows_of(inner, at)
                for first in range(0, width, wide):
                    span = slice(first, first + wide)
                    value = jnp.dot(left, down[:, span], preferred_element_type=jnp.float32)
                    slot[:, :, :, span] = value.astype(jnp.bfloat16).reshape(
                        slot.shape[:3] + (wide,)
                    )

            staged(fill, result_out.at[at])

        def sequence():
            first_job()
            for i in (1, 3, 2, 4):
                copies[i].wait()
            tiles = [
                functools.partial(weight_tile, ref, row, out)
                for ref, out in ((dgate, gate_out), (dup, up_out))
                for row in range(0, held, TILE)
            ]
            tiles += [functools.partial(result_tile, at) for at in range(chips)]
            done = [0]

            def fill(most):
                for _ in range(most):
                    if tiles:
                        if done[0] == 0:
                            copies[6].wait()
                        if done[0] == 2 * (held // TILE):
                            copies[5].wait()
                        done[0] += 1
                        tiles.pop(0)()

            for wave in range(chips - 1):
                high = chips - 1 - wave
                ups = (high > chip).astype(jnp.int32)
                downs = (wave < chip).astype(jnp.int32)

                def each(i, _, high=high, wave=wave, ups=ups):
                    partial(jnp.where(i < ups, high, wave))
                    return 0

                lax.fori_loop(0, ups + downs, each, 0)
                fill(1)
                step(wave, 0)
                if wave == 0:
                    step(wave, 1)
                    jobs.pop(0)()
                else:
                    fill(1)
                    step(wave, 1)
                    if jobs:
                        jobs.pop(0)()
            partial(chip)
            for job in jobs:
                job()
            fill(len(tiles))

        def finish():
            ring[2]()
            finish_line()
            for copy in waits[-2:]:
                copy.wait()

        return start, {0: sequence}, finish


def move(parts, dps, groups, number, greet=greet_near):
    def kernel(*refs):
        place = Place(dps, groups)
        at = [
            0,
            sum(len(part.inputs) for part in parts),
            sum(len(part.inputs) + len(part.outs) for part in parts),
        ]
        bound = []
        for part in parts:
            mine = []
            for kind, length in enumerate((len(part.inputs), len(part.outs), len(part.scratch))):
                mine += refs[at[kind] : at[kind] + length]
                at[kind] += length
            bound.append(part.bind(place, *mine))
        greet(place)
        for start, _, _ in bound:
            start()
        for tick in range(1 + max([0] + [max(list(ticks) + [0]) for _, ticks, _ in bound])):
            for _, ticks, _ in bound:
                if tick in ticks:
                    ticks[tick]()
        for _, _, finish in bound:
            finish()

    outs = pl.pallas_call(
        kernel,
        out_shape=[out for part in parts for out in part.outs],
        in_specs=[spec for part in parts for spec in part.in_specs],
        out_specs=[spec for part in parts for spec in part.out_specs],
        scratch_shapes=[one for part in parts for one in part.scratch],
        compiler_params=pltpu.CompilerParams(
            collective_id=number, has_side_effects=True, vmem_limit_bytes=63 << 20
        ),
        cost_estimate=pl.CostEstimate(flops=0, bytes_accessed=120_000_000, transcendentals=0),
        name=f"move_{number}",
    )(*[x for part in parts for x in part.inputs])
    results, at = [], 0
    for part in parts:
        results.append(part.result(*outs[at : at + len(part.outs)]))
        at += len(part.outs)
    return results


def norm_factor(values):
    return lax.rsqrt(jnp.mean(values * values, axis=-1, keepdims=True) + epsilon)


def norm_grad(values, factor, gain, gradient):
    weighted = gradient * gain
    inner_mean = jnp.mean(weighted * values, axis=-1, keepdims=True)
    return factor * weighted - values * (factor * factor * factor) * inner_mean


def rope_tables(positions, head_width):
    half_width = head_width // 2
    frequency = rope_base ** (-2.0 * jnp.arange(half_width, dtype=jnp.float32) / head_width)
    angles = positions.astype(jnp.float32)[:, None] * frequency[None, :]
    return (jnp.cos(angles)[:, None, :], jnp.sin(angles)[:, None, :])


def rotate(values, cosine_table, sine_table):
    half_width = values.shape[-1] // 2
    first_half = values[..., :half_width]
    second_half = values[..., half_width:]
    return jnp.concatenate(
        [
            first_half * cosine_table - second_half * sine_table,
            second_half * cosine_table + first_half * sine_table,
        ],
        axis=-1,
    )


def block_scores(query_block, key_heads, lower, upper, score_scale):
    scores = (
        jnp.einsum(
            "qhd,kd->hqk", query_block, key_heads[:upper], preferred_element_type=jnp.float32
        )
        * score_scale
    )
    rows_at = lower + jnp.arange(query_block.shape[0], dtype=jnp.int32)
    cols_at = jnp.arange(upper, dtype=jnp.int32)
    allowed = (cols_at[None, :] <= rows_at[:, None])[None]
    return jnp.where(allowed, scores, masked_value)


def per_device(
    tokens,
    qkv_weight,
    out_weight,
    gate_weight,
    up_weight,
    down_weight,
    attn_gain,
    mlp_gain,
    cotangent,
):
    groups = lax.axis_size("seq")
    dps = lax.axis_size("dp")
    tok_rows = tokens.shape[1]
    model_width = tokens.shape[2]
    weight_rows = qkv_weight.shape[0]
    seq_len = tok_rows * groups
    local_heads = HEADS // groups
    local_width = local_heads * HEAD_DIM
    kv_copies = groups // KV_HEADS
    score_scale = HEAD_DIM ** (-0.5)
    block_rows = min(512, seq_len)
    block_count = seq_len // block_rows
    fold = groups // dps
    order = [(at % dps) * fold + at // dps for at in range(groups)]

    q_part = qkv_weight[:, :model_width].reshape(weight_rows, groups, local_width)
    k_part = qkv_weight[:, model_width : model_width + KV_HEADS * HEAD_DIM]
    v_part = qkv_weight[:, model_width + KV_HEADS * HEAD_DIM :]
    k_part = k_part.reshape(weight_rows, KV_HEADS, HEAD_DIM)
    v_part = v_part.reshape(weight_rows, KV_HEADS, HEAD_DIM)
    columns = jnp.stack(
        [
            jnp.concatenate(
                [q_part[:, g], k_part[:, g // kv_copies], v_part[:, g // kv_copies]], axis=1
            )
            for g in order
        ]
    )
    gain_width = attn_gain.shape[0]
    tile = jnp.zeros((8, 128), jnp.float32)
    tile = tile.at[0, :gain_width].set(attn_gain.astype(jnp.float32))
    tile = tile.at[1, :gain_width].set(mlp_gain.astype(jnp.float32))
    qkv_local, tokens_all, out_rows, gate_part, gains = move(
        [
            Columns(columns, dps, groups),
            LineGather(tokens[0], dps, groups),
            Rows(out_weight, dps, groups),
            RingGather(gate_weight, dps, groups),
            Spread(tile, False, dps, groups),
        ],
        dps,
        groups,
        1,
        greet_all,
    )
    gain_one = gains[:, 0, :gain_width].reshape(model_width)
    gain_two = gains[:, 1, :gain_width].reshape(model_width)

    x_rows = tokens[0].astype(jnp.float32)
    factor_one = norm_factor(x_rows)
    all_rows = tokens_all.astype(jnp.float32)
    normed_all = (all_rows * norm_factor(all_rows) * gain_one).astype(jnp.bfloat16)
    grad_low = cotangent[0]
    grad_low, _ = lax.optimization_barrier((grad_low, gains))
    grad_all = lax.all_gather(grad_low, "seq", axis=0, tiled=True)

    mixed = jnp.dot(normed_all, qkv_local, preferred_element_type=jnp.float32)
    cosine_table, sine_table = rope_tables(jnp.arange(seq_len, dtype=jnp.int32), HEAD_DIM)
    query_heads = rotate(
        mixed[:, :local_width].reshape(seq_len, local_heads, HEAD_DIM), cosine_table, sine_table
    ).astype(jnp.bfloat16)
    key_heads = rotate(
        mixed[:, None, local_width : local_width + HEAD_DIM], cosine_table, sine_table
    ).astype(jnp.bfloat16)[:, 0]
    value_heads = mixed[:, local_width + HEAD_DIM :].astype(jnp.bfloat16)
    outputs = []
    log_sums = []
    for block in range(block_count):
        lower = block * block_rows
        upper = lower + block_rows
        scores = block_scores(query_heads[lower:upper], key_heads, lower, upper, score_scale)
        highest = jnp.max(scores, axis=-1, keepdims=True)
        log_sum = highest + jnp.log(jnp.sum(jnp.exp(scores - highest), axis=-1, keepdims=True))
        probs = jnp.exp(scores - log_sum).astype(jnp.bfloat16)
        attended = jnp.einsum(
            "hqk,kd->qhd", probs, value_heads[:upper], preferred_element_type=jnp.float32
        )
        outputs.append(attended.astype(jnp.bfloat16))
        log_sums.append(log_sum)
    attended = jnp.concatenate(outputs, axis=0).reshape(seq_len, local_width)
    partial = jnp.dot(attended, out_rows, preferred_element_type=jnp.float32)
    summed, up_part = move(
        [
            LineScatter(partial.astype(jnp.bfloat16), dps, groups),
            RingGather(up_weight, dps, groups),
        ],
        dps,
        groups,
        2,
    )
    hidden = x_rows + summed
    factor_two = norm_factor(hidden)
    normed_two = (hidden * factor_two * gain_two).astype(jnp.bfloat16)
    ((hn_all, down_part, inner, grad_gate, grad_upward),) = move(
        [FeedForward(normed_two, down_weight, gate_part, up_part, grad_all, dps, groups)],
        dps,
        groups,
        3,
    )
    ((grad_normed, down_owned, gate_term, up_term, result),) = move(
        [
            FeedBack(
                inner,
                grad_gate,
                grad_upward,
                gate_part,
                up_part,
                down_part,
                hn_all,
                grad_all,
                dps,
                groups,
            )
        ],
        dps,
        groups,
        4,
    )
    gain_two_term = jnp.sum(grad_normed * hidden * factor_two, axis=0)
    grad_hidden = grad_low.astype(jnp.float32) + norm_grad(
        hidden, factor_two, gain_two, grad_normed
    )
    grad_branch, gate_owned = move(
        [
            LineGather(grad_hidden.astype(jnp.bfloat16), dps, groups),
            RingScatter(gate_term, dps, groups),
        ],
        dps,
        groups,
        5,
    )
    result, grad_branch = lax.optimization_barrier((result, grad_branch))
    mlp_result = lax.psum_scatter(result, "seq", scatter_dimension=0, tiled=True)
    block_out = (hidden + mlp_result.astype(jnp.float32)).astype(jnp.bfloat16)[None]
    out_term = lax.dot_general(
        attended, grad_branch, contract_rows, preferred_element_type=jnp.float32
    ).astype(jnp.bfloat16)
    grad_heads = (
        lax.dot_general(grad_branch, out_rows, contract_cols, preferred_element_type=jnp.float32)
        .astype(jnp.bfloat16)
        .reshape(seq_len, local_heads, HEAD_DIM)
    )
    grad_keys = jnp.zeros((seq_len, HEAD_DIM), jnp.float32)
    grad_values = jnp.zeros((seq_len, HEAD_DIM), jnp.float32)
    grad_queries = []
    for block in range(block_count):
        lower = block * block_rows
        upper = lower + block_rows
        query_block = query_heads[lower:upper]
        grad_block = grad_heads[lower:upper]
        scores = block_scores(query_block, key_heads, lower, upper, score_scale)
        probs = jnp.exp(scores - log_sums[block])
        probs_low = probs.astype(jnp.bfloat16)
        grad_probs = jnp.einsum(
            "qhd,kd->hqk", grad_block, value_heads[:upper], preferred_element_type=jnp.float32
        )
        row_delta = jnp.sum(probs * grad_probs, axis=-1, keepdims=True)
        grad_scores = (probs * (grad_probs - row_delta)).astype(jnp.bfloat16)
        grad_queries.append(
            jnp.einsum(
                "hqk,kd->qhd", grad_scores, key_heads[:upper], preferred_element_type=jnp.float32
            )
            * score_scale
        )
        grad_keys = grad_keys.at[:upper].add(
            jnp.einsum("hqk,qhd->kd", grad_scores, query_block, preferred_element_type=jnp.float32)
            * score_scale
        )
        grad_values = grad_values.at[:upper].add(
            jnp.einsum("hqk,qhd->kd", probs_low, grad_block, preferred_element_type=jnp.float32)
        )
    grad_q = rotate(jnp.concatenate(grad_queries, axis=0), cosine_table, -sine_table)
    grad_k = rotate(grad_keys[:, None], cosine_table, -sine_table)[:, 0]
    grad_mixed = jnp.concatenate(
        [grad_q.reshape(seq_len, local_width), grad_k, grad_values], axis=1
    ).astype(jnp.bfloat16)
    qkv_term = lax.dot_general(
        normed_all, grad_mixed, contract_rows, preferred_element_type=jnp.float32
    )
    partial = lax.dot_general(
        grad_mixed, qkv_local, contract_cols, preferred_element_type=jnp.float32
    )
    qkv_term = qkv_term.astype(jnp.bfloat16)
    gain_one_term = (
        jnp.sum(qkv_term.astype(jnp.float32) * qkv_local.astype(jnp.float32), axis=1) / gain_one
    )
    terms = jnp.stack([gain_one_term, gain_two_term]).reshape(2, dps * groups, gain_width)
    terms = jnp.pad(terms.transpose(1, 0, 2), ((0, 0), (0, 6), (0, 128 - gain_width)))
    qkv_owned, grad_normed_one, out_owned, up_owned, gain_grads = move(
        [
            ColumnsBack(qkv_term, order, local_width, kv_copies, weight_rows, dps, groups),
            LineScatter(partial.astype(jnp.bfloat16), dps, groups),
            RowsBack(out_term, weight_rows, dps, groups),
            RingScatter(up_term, dps, groups),
            Spread(terms, True, dps, groups),
        ],
        dps,
        groups,
        6,
        greet_all,
    )
    grad_input = grad_hidden + norm_grad(x_rows, factor_one, gain_one, grad_normed_one)
    return (
        block_out,
        grad_input[None],
        qkv_owned,
        out_owned,
        gate_owned,
        up_owned,
        down_owned,
        gain_grads[0, :gain_width],
        gain_grads[1, :gain_width],
    )


def solution(mesh):
    rows = P(("dp", "seq"), None)
    tokens = P("dp", "seq", None)
    gains = P(("dp", "seq"))
    return jax.shard_map(
        per_device,
        mesh=mesh,
        in_specs=(tokens, rows, rows, rows, rows, rows, gains, gains, tokens),
        out_specs=(tokens, tokens, rows, rows, rows, rows, rows, gains, gains),
        check_vma=False,
    )
```

```python
import functools

import jax
import jax.numpy as jnp
from jax import lax
from jax.experimental import pallas as pl
from jax.experimental.pallas import tpu as pltpu
from jax.sharding import PartitionSpec as P

HEADS = 32
KV_HEADS = 8
HEAD_DIM = 64

MESH = pl.DeviceIdType.MESH
ANY = pl.BlockSpec(memory_space=pl.ANY)
VM = pl.BlockSpec(memory_space=pltpu.VMEM)
SUB = 2

epsilon = 1e-05
rope_base = 500000.0
masked_value = -1e30
contract_rows = (((0,), (0,)), ((), ()))
contract_cols = (((1,), (1,)), ((), ()))


class Place:
    def __init__(self, dps, groups):
        self.dps, self.groups, self.chips, self.hops = dps, groups, groups // 2, dps // 2
        self.d, self.s = lax.axis_index("dp"), lax.axis_index("seq")
        self.chip, self.core = self.s // 2, self.s % 2
        self.partner = 2 * self.chip + 1 - self.core
        row, side = self.d // 2, self.d % 2
        self.turn = side * (dps - 1 - row) + (1 - side) * row

    def ring(self, distance):
        at = (self.turn + distance + self.dps) % self.dps
        side = at // self.hops
        return (1 - side) * 2 * at + side * (2 * (self.dps - 1 - at) + 1)


def remote(src, dst, send, recv, **target):
    return pltpu.make_async_remote_copy(
        src_ref=src, dst_ref=dst, send_sem=send, recv_sem=recv, device_id=target, device_id_type=MESH
    )


def greet_near(place):
    barrier = pltpu.get_barrier_semaphore()

    def signal(**target):
        pl.semaphore_signal(barrier, inc=1, device_id=target, device_id_type=MESH)

    signal(seq=place.partner)
    signal(dp=place.ring(1))
    signal(dp=place.ring(-1))

    @pl.when(place.chip > 0)
    def _():
        signal(seq=place.s - 2)

    @pl.when(place.chip < place.chips - 1)
    def _():
        signal(seq=place.s + 2)

    ends = (place.chips - place.chip) // place.chips + (place.chip + 1) // place.chips
    pl.semaphore_wait(barrier, 5 - ends)


def greet_all(place):
    barrier = pltpu.get_barrier_semaphore()
    count = place.dps * place.groups
    me = place.d * place.groups + place.s

    def signal(i, _):
        other = (me + i) % count
        pl.semaphore_signal(
            barrier,
            inc=1,
            device_id={"dp": other // place.groups, "seq": other % place.groups},
            device_id_type=MESH,
        )
        return 0

    lax.fori_loop(1, count, signal, 0)
    pl.semaphore_wait(barrier, count - 1)


DMA = pltpu.SemaphoreType.DMA


def line_gather(place, x_ref, out_ref, own_sem, us, ur, ds, dr, ps, pr):
    s, chip, chips = place.s, place.chip, place.chips

    def copy(src, group, half, sends, recvs, at, target):
        return remote(
            src, out_ref.at[group, half], sends.at[at, half], recvs.at[at, half], seq=target
        )

    def up(src, group, hop, half):
        return copy(src, group, half, us, ur, hop, s + 2)

    def down(src, group, hop, half):
        return copy(src, group, half, ds, dr, hop, s - 2)

    def pair(src, group, half):
        return copy(src, group, half, ps, pr, group // 2, place.partner)

    own = pltpu.make_async_copy(x_ref, out_ref.at[s], own_sem)

    def start():
        own.start()
        for half in range(SUB):

            @pl.when(chip < chips - 1)
            def _():
                up(x_ref.at[half], s, 0, half).start()

            @pl.when(chip > 0)
            def _():
                down(x_ref.at[half], s, 0, half).start()

        for half in range(SUB):
            pair(x_ref.at[half], s, half).start()

    def step(hop, half):
        below, above = s - 2 * hop, s + 2 * hop

        @pl.when(chip - hop >= 0)
        def _():
            block = out_ref.at[below, half]
            up(block, below, hop - 1, half).wait_recv()

            @pl.when(chip < chips - 1)
            def _():
                up(block, below, hop, half).start()

            pair(block, below, half).start()

        @pl.when(chip + hop < chips)
        def _():
            block = out_ref.at[above, half]
            down(block, above, hop - 1, half).wait_recv()

            @pl.when(chip > 0)
            def _():
                down(block, above, hop, half).start()

            pair(block, above, half).start()

    def arrived(at):
        for half in range(SUB):
            group = 2 * at + 1 - place.core
            pair(out_ref.at[group, half], group, half).wait_recv()

    def sent():
        def each(i, _):
            k, half = i // SUB, i % SUB
            mine = 2 * k + place.core
            block = out_ref.at[mine, half]
            pair(block, mine, half).wait_send()

            @pl.when(jnp.logical_and(chip - k >= 0, chip < chips - 1))
            def _():
                up(block, mine, k, half).wait_send()

            @pl.when(jnp.logical_and(chip + k < chips, chip > 0))
            def _():
                down(block, mine, k, half).wait_send()

            return 0

        lax.fori_loop(0, chips * SUB, each, 0)

    return own, start, step, arrived, sent


class LineGather:
    def __init__(self, x, dps, groups):
        rows, width = x.shape
        shape = (SUB, rows // SUB, width)
        self.inputs, self.in_specs = [x.reshape(shape)], [VM]
        self.outs, self.out_specs = [jax.ShapeDtypeStruct((groups,) + shape, x.dtype)], [ANY]
        self.scratch = [DMA] + [DMA((groups // 2, SUB))] * 6
        self.result = lambda out: out.reshape(groups * rows, width)

    def bind(self, place, *refs):
        own, start, step, arrived, sent = line_gather(place, *refs)

        def finish():
            own.wait()

            def each(at, _):
                arrived(at)
                return 0

            lax.fori_loop(0, place.chips, each, 0)
            sent()

        ticks = {
            (hop - 1) * SUB + half: functools.partial(step, hop, half)
            for hop in range(1, place.chips)
            for half in range(SUB)
        }
        return start, ticks, finish


def line_scatter(place, p_ref, out_ref, pairbuf, upbuf, downbuf, us, ur, ds, dr, ps, pr):
    s, chip, chips, core = place.s, place.chip, place.chips, place.core

    def copy(src, buffer, at, half, sends, recvs, target):
        return remote(src, buffer.at[at, half], sends.at[at, half], recvs.at[at, half], seq=target)

    def pair(at, half):
        src = p_ref.at[2 * at + 1 - core, half]
        return copy(src, pairbuf, at, half, ps, pr, place.partner)

    def up(at, half):
        return copy(upbuf.at[at, half], upbuf, at, half, us, ur, s + 2)

    def down(at, half):
        return copy(downbuf.at[at, half], downbuf, at, half, ds, dr, s - 2)

    def wide(ref, *at):
        return ref[at].astype(jnp.float32)

    def local(at, half):
        return wide(p_ref, 2 * at + core, half) + wide(pairbuf, at, half)

    def send(at):
        for half in range(SUB):
            pair(at, half).start()

    def step(wave, half):
        high, low = chips - 1 - wave + chip, wave - (chips - 1 - chip)

        @pl.when(chip <= wave)
        def _():
            pair(high, half).wait_recv()

            @pl.when(chip > 0)
            def _():
                up(high, half).wait_recv()
                total = local(high, half) + wide(upbuf, high, half)
                upbuf[high, half] = total.astype(jnp.bfloat16)

            @pl.when(chip == 0)
            def _():
                upbuf[high, half] = local(high, half).astype(jnp.bfloat16)

            up(high, half).start()

        @pl.when(low >= 0)
        def _():
            pair(low, half).wait_recv()

            @pl.when(chip < chips - 1)
            def _():
                down(low, half).wait_recv()
                total = local(low, half) + wide(downbuf, low, half)
                downbuf[low, half] = total.astype(jnp.bfloat16)

            @pl.when(chip == chips - 1)
            def _():
                downbuf[low, half] = local(low, half).astype(jnp.bfloat16)

            down(low, half).start()

    def finish():
        for half in range(SUB):
            pair(chip, half).wait_recv()
            out_ref[half] = local(chip, half)

            @pl.when(chip > 0)
            def _():
                up(chip, half).wait_recv()
                out_ref[half] += wide(upbuf, chip, half)

            @pl.when(chip < chips - 1)
            def _():
                down(chip, half).wait_recv()
                out_ref[half] += wide(downbuf, chip, half)

        def each(i, _):
            at, half = i // SUB, i % SUB
            pair(at, half).wait_send()

            @pl.when(at > chip)
            def _():
                up(at, half).wait_send()

            @pl.when(at < chip)
            def _():
                down(at, half).wait_send()

            return 0

        lax.fori_loop(0, chips * SUB, each, 0)

    return send, step, finish


def line_scatter_scratch(chips, shape):
    return [pltpu.VMEM((chips,) + shape, jnp.bfloat16)] * 3 + [DMA((chips, SUB))] * 6


class LineScatter:
    def __init__(self, partial, dps, groups):
        total, width = partial.shape
        rows = total // groups
        shape = (SUB, rows // SUB, width)
        self.inputs, self.in_specs = [partial.reshape((groups,) + shape)], [VM]
        self.outs, self.out_specs = [jax.ShapeDtypeStruct(shape, jnp.float32)], [VM]
        self.scratch = line_scatter_scratch(groups // 2, shape)
        self.result = lambda out: out.reshape(rows, width)

    def bind(self, place, *refs):
        send, step, finish = line_scatter(place, *refs)
        chip, chips = place.chip, place.chips

        def start():
            def issue(low, _):
                high = chips - 1 - low

                @pl.when(high > chip)
                def _():
                    send(high)

                @pl.when(low < chip)
                def _():
                    send(low)

                return 0

            lax.fori_loop(0, chips - 1, issue, 0)
            send(chip)

        ticks = {
            i: functools.partial(step, i // SUB, i % SUB) for i in range((chips - 1) * SUB)
        }
        return start, ticks, finish


def ring_sems(hops):
    return [DMA((hops, 2))] * 4


def ring_gather(place, own, out, rs, rr, ls, lr):
    hops = place.hops

    def right(src, chunk, hop, half):
        return remote(
            src, out(chunk, half), rs.at[hop - 1, half], rr.at[hop - 1, half], dp=place.ring(1)
        )

    def left(src, chunk, hop, half):
        return remote(
            src, out(chunk, half), ls.at[hop - 1, half], lr.at[hop - 1, half], dp=place.ring(-1)
        )

    def start():
        for half in range(2):
            right(own(half), place.d, 1, half).start()
            left(own(1 - half), place.d, 1, 1 - half).start()

    def forward(hop):
        before, after = place.ring(-hop), place.ring(hop)
        full = hop < hops - 1
        right(out(before, 0), before, hop, 0).wait_recv()
        right(out(before, 0), before, hop + 1, 0).start()
        left(out(after, 1), after, hop, 1).wait_recv()
        left(out(after, 1), after, hop + 1, 1).start()
        if full:
            right(out(before, 1), before, hop, 1).wait_recv()
            left(out(after, 0), after, hop, 0).wait_recv()
            right(out(before, 1), before, hop + 1, 1).start()
            left(out(after, 0), after, hop + 1, 0).start()

    def near():
        before, after = place.ring(1 - hops), place.ring(hops - 1)
        right(out(before, 1), before, hops - 1, 1).wait_recv()
        left(out(after, 0), after, hops - 1, 0).wait_recv()

    def finish(waited=False):
        if not waited:
            near()
        right(out(place.d, 0), place.ring(-hops), hops, 0).wait_recv()
        left(out(place.d, 1), place.ring(hops), hops, 1).wait_recv()
        for hop in range(1, hops + 1):
            for half in range(2):
                if hop < hops or half == 0:
                    right(out(place.d, half), place.d, hop, half).wait_send()
                if hop < hops or half == 1:
                    left(out(place.d, half), place.d, hop, half).wait_send()

    return start, forward, finish, near


def ring_scatter(place, part, put, rbuf, lbuf, rout, lout, rs, rr, ls, lr):
    hops = place.hops

    def wide(ref):
        return ref[...].astype(jnp.float32)

    def right(src, hop, half):
        return remote(
            src,
            rbuf.at[hop - 1, half],
            rs.at[hop - 1, half],
            rr.at[hop - 1, half],
            dp=place.ring(1),
        )

    def left(src, hop, half):
        return remote(
            src,
            lbuf.at[hop - 1, half],
            ls.at[hop - 1, half],
            lr.at[hop - 1, half],
            dp=place.ring(-1),
        )

    def start_far():
        right(part(place.ring(hops), 0), hops, 0).start()
        left(part(place.ring(-hops), 1), hops, 1).start()

    def start_next():
        right(part(place.ring(hops - 1), 1), hops - 1, 1).start()
        left(part(place.ring(1 - hops), 0), hops - 1, 0).start()

    def start():
        start_far()
        start_next()

    def forward(hop):
        for first in range(2 if hop < hops - 1 else 1):
            half = first
            right(rbuf.at[hop, half], hop + 1, half).wait_recv()
            total = wide(part(place.ring(hop), half)) + wide(rbuf.at[hop, half])
            rout[hop - 1, half] = total.astype(jnp.bfloat16)
            right(rout.at[hop - 1, half], hop, half).start()
            half = 1 - first
            left(lbuf.at[hop, half], hop + 1, half).wait_recv()
            total = wide(part(place.ring(-hop), half)) + wide(lbuf.at[hop, half])
            lout[hop - 1, half] = total.astype(jnp.bfloat16)
            left(lout.at[hop - 1, half], hop, half).start()

    def finish():
        for half in range(2):
            right(rbuf.at[0, half], 1, half).wait_recv()
            left(lbuf.at[0, half], 1, half).wait_recv()
            put(
                half,
                wide(part(place.d, half)) + wide(rbuf.at[0, half]) + wide(lbuf.at[0, half]),
            )
        for hop in range(1, hops + 1):
            for half in range(2):
                if hop < hops or half == 0:
                    right(rbuf.at[0, half], hop, half).wait_send()
                if hop < hops or half == 1:
                    left(lbuf.at[0, half], hop, half).wait_send()

    return start, forward, finish, start_far, start_next


class RingGather:
    def __init__(self, x, dps, groups):
        rows, width = x.shape
        shape = (2, rows // 2, width)
        self.inputs, self.in_specs = [x.reshape(shape)], [VM]
        self.outs, self.out_specs = [jax.ShapeDtypeStruct((dps,) + shape, x.dtype)], [ANY]
        self.scratch = [DMA] + ring_sems(dps // 2)
        self.result = lambda out: out.reshape(dps * rows, width)

    def bind(self, place, x_ref, out_ref, own_sem, *sems):
        own = pltpu.make_async_copy(x_ref, out_ref.at[place.d], own_sem)
        ring = ring_gather(
            place, lambda half: x_ref.at[half], lambda chunk, half: out_ref.at[chunk, half], *sems
        )

        def start():
            ring[0]()
            own.start()

        def finish():
            own.wait()
            ring[2]()

        ticks = {2 * hop - 1: functools.partial(ring[1], hop) for hop in range(1, place.hops)}
        return start, ticks, finish


class RingScatter:
    def __init__(self, partial, dps, groups, late=False):
        self.late = late
        total, width = partial.shape
        rows, hops = total // dps, dps // 2
        shape = (2, rows // 2, width)
        self.inputs, self.in_specs = [partial.reshape((dps,) + shape)], [VM]
        self.outs, self.out_specs = [jax.ShapeDtypeStruct(shape, jnp.float32)], [VM]
        self.scratch = (
            [pltpu.VMEM((hops,) + shape, jnp.bfloat16)] * 2
            + [pltpu.VMEM((hops - 1,) + shape, jnp.bfloat16)] * 2
            + ring_sems(hops)
        )
        self.result = lambda out: out.reshape(rows, width)

    def bind(self, place, p_ref, out_ref, *scratch):
        def put(half, value):
            out_ref[half] = value

        ring = ring_scatter(place, lambda chunk, half: p_ref.at[chunk, half], put, *scratch)
        first = 1 if self.late else -1
        ticks = {
            2 * (place.hops - hop) + first: functools.partial(ring[1], hop)
            for hop in range(1, place.hops)
        }
        if self.late:
            ticks[1] = ring[0]
            return lambda: None, ticks, ring[2]
        return ring[0], ticks, ring[2]


class Columns:
    def __init__(self, blocks, dps, groups):
        _, rows, width = blocks.shape
        self.inputs, self.in_specs = [blocks], [VM]
        self.outs = [jax.ShapeDtypeStruct((dps, groups, rows, width), blocks.dtype)]
        self.out_specs = [ANY]
        self.scratch = [
            pltpu.VMEM((groups, rows, width), blocks.dtype),
            DMA((2,)),
            DMA((groups,)),
            DMA((groups,)),
        ] + ring_sems(dps // 2)
        self.result = lambda out: out.reshape(dps * groups * rows, width)

    def bind(self, place, x_ref, out_ref, landing, own_sem, sends, recvs, *sems):
        s, groups = place.s, place.groups
        half_of = groups // 2
        here = pltpu.make_async_copy(x_ref.at[s], landing.at[s], own_sem.at[0])
        own = pltpu.make_async_copy(landing, out_ref.at[place.d], own_sem.at[1])

        def swap(i):
            to = (s + i) % groups
            return remote(x_ref.at[to], landing.at[s], sends.at[i], recvs.at[i], seq=to)

        ring = ring_gather(
            place,
            lambda half: landing.at[pl.ds(half * half_of, half_of)],
            lambda chunk, half: out_ref.at[chunk, pl.ds(half * half_of, half_of)],
            *sems,
        )

        def start():
            here.start()
            for i in range(1, groups):
                swap(i).start()

        def middle():
            here.wait()
            for i in range(1, groups):
                swap(i).wait_recv()
            ring[0]()
            own.start()

        def finish():
            for i in range(1, groups):
                swap(i).wait_send()
            own.wait()
            ring[2]()

        ticks = {1 + 2 * hop: functools.partial(ring[1], hop) for hop in range(1, place.hops)}
        ticks[1] = middle
        return start, ticks, finish


class ColumnsBack:
    def __init__(self, partial, order, heads_width, copies, rows, dps, groups):
        width, hops = partial.shape[1], dps // 2
        shape = (groups, rows, width)
        halves = (2, groups // 2, rows, width)
        self.where = [order.index(g) for g in range(groups)]
        self.heads_width, self.copies = heads_width, copies
        joint = groups * heads_width + 2 * KV_HEADS * HEAD_DIM
        self.inputs, self.in_specs = [partial.reshape((dps,) + halves)], [VM]
        self.outs, self.out_specs = [jax.ShapeDtypeStruct((rows, joint), jnp.float32)], [VM]
        self.scratch = (
            [pltpu.VMEM(shape, jnp.bfloat16), pltpu.VMEM(halves, jnp.bfloat16)]
            + [DMA, DMA((groups,)), DMA((groups,))]
            + [pltpu.VMEM((hops,) + halves, jnp.bfloat16)] * 2
            + [pltpu.VMEM((hops - 1,) + halves, jnp.bfloat16)] * 2
            + ring_sems(hops)
        )
        self.result = lambda out: out

    def bind(self, place, p_ref, joint_ref, out_ref, total, own_sem, sends, recvs, *scratch):
        s, groups = place.s, place.groups
        half_of = groups // 2

        def put(half, value):
            total[half] = value.astype(jnp.bfloat16)

        ring = ring_scatter(place, lambda chunk, half: p_ref.at[chunk, half], put, *scratch)
        here = pltpu.make_async_copy(
            total.at[s // half_of, s % half_of], out_ref.at[s], own_sem
        )

        def swap(i):
            to = (s + i) % groups
            src = total.at[to // half_of, to % half_of]
            return remote(src, out_ref.at[s], sends.at[i], recvs.at[i], seq=to)

        def last():
            ring[2]()
            here.start()
            for i in range(1, groups):
                swap(i).start()

        def keys_values(head):
            first = self.where[head * self.copies]
            span = slice(self.heads_width, self.heads_width + 2 * HEAD_DIM)
            value = out_ref[first, :, span].astype(jnp.float32)
            for i in range(1, self.copies):
                value += out_ref[self.where[head * self.copies + i], :, span].astype(jnp.float32)
            return value

        def finish():
            here.wait()
            for i in range(1, groups):
                swap(i).wait_recv()
                swap(i).wait_send()
            heads = self.heads_width
            for g in range(groups):
                value = out_ref[self.where[g], :, :heads]
                joint_ref[:, g * heads : (g + 1) * heads] = value.astype(jnp.float32)
            for head in range(0, KV_HEADS, 2):
                even, odd = keys_values(head), keys_values(head + 1)
                lanes = lax.broadcasted_iota(jnp.int32, even.shape, 1)
                at = groups * heads + head * HEAD_DIM
                joint_ref[:, at : at + 2 * HEAD_DIM] = jnp.where(
                    lanes < HEAD_DIM, even, pltpu.roll(odd, HEAD_DIM, 1)
                )
                at += KV_HEADS * HEAD_DIM
                joint_ref[:, at : at + 2 * HEAD_DIM] = jnp.where(
                    lanes < HEAD_DIM, pltpu.roll(even, HEAD_DIM, 1), odd
                )

        ticks = {
            2 * (place.hops - hop) - 1: functools.partial(ring[1], hop)
            for hop in range(1, place.hops)
        }
        ticks[2 * place.hops - 1] = last
        return ring[0], ticks, finish


class Rows:
    def __init__(self, x, dps, groups):
        rows, width = x.shape
        shape = (2, rows // 2, width)
        self.inputs, self.in_specs = [x.reshape(shape)], [VM]
        self.outs, self.out_specs = [jax.ShapeDtypeStruct((dps,) + shape, x.dtype)], [ANY]
        self.scratch = [
            pltpu.VMEM((dps,) + shape, x.dtype),
            DMA((2,)),
            DMA((dps,)),
            DMA((dps,)),
        ] + ring_sems(dps // 2)
        self.result = lambda out: out.reshape(dps * rows, width)

    def bind(self, place, x_ref, out_ref, landing, own_sem, sends, recvs, *sems):
        s, dps = place.s, place.dps
        slot, base = s % dps, s // dps * dps
        first = pltpu.make_async_copy(x_ref, landing.at[place.d], own_sem.at[0])
        here = pltpu.make_async_copy(landing.at[slot], out_ref.at[slot], own_sem.at[1])
        ring = ring_gather(
            place, lambda half: x_ref.at[half], lambda chunk, half: landing.at[chunk, half], *sems
        )

        def swap(i):
            to = (slot + i) % dps
            return remote(landing.at[to], out_ref.at[slot], sends.at[i], recvs.at[i], seq=base + to)

        def start():
            ring[0]()
            first.start()

        def last():
            first.wait()
            ring[2]()
            here.start()
            for i in range(1, dps):
                swap(i).start()

        def finish():
            here.wait()
            for i in range(1, dps):
                swap(i).wait_recv()
                swap(i).wait_send()

        ticks = {2 * hop - 1: functools.partial(ring[1], hop) for hop in range(1, place.hops)}
        ticks[2 * place.hops] = last
        return start, ticks, finish


class RowsBack:
    def __init__(self, partial, rows, dps, groups):
        width, hops = partial.shape[1], dps // 2
        shape = (2, rows // 2, width)
        self.inputs, self.in_specs = [partial.reshape((dps,) + shape)], [VM]
        self.outs, self.out_specs = [jax.ShapeDtypeStruct(shape, jnp.float32)], [VM]
        self.scratch = (
            [pltpu.VMEM((dps,) + shape, jnp.bfloat16), DMA, DMA((dps,)), DMA((dps,))]
            + [pltpu.VMEM((hops,) + shape, jnp.bfloat16)] * 2
            + [pltpu.VMEM((hops - 1,) + shape, jnp.bfloat16)] * 2
            + ring_sems(hops)
        )
        self.result = lambda out: out.reshape(rows, width)

    def bind(self, place, p_ref, out_ref, landing, own_sem, sends, recvs, *scratch):
        s, dps = place.s, place.dps
        slot, base = s % dps, s // dps * dps
        here = pltpu.make_async_copy(p_ref.at[slot], landing.at[slot], own_sem)

        def swap(i):
            to = (slot + i) % dps
            return remote(p_ref.at[to], landing.at[slot], sends.at[i], recvs.at[i], seq=base + to)

        def put(half, value):
            out_ref[half] = value

        ring = ring_scatter(place, lambda chunk, half: landing.at[chunk, half], put, *scratch)

        def start():
            here.start()
            for i in range(1, dps):
                swap(i).start()

        def middle():
            here.wait()
            for i in range(1, dps):
                swap(i).wait_recv()
            ring[0]()

        def finish():
            for i in range(1, dps):
                swap(i).wait_send()
            ring[2]()

        ticks = {
            2 * (place.hops - hop) + 2: functools.partial(ring[1], hop)
            for hop in range(1, place.hops)
        }
        ticks[2] = middle
        return start, ticks, finish


class Spread:
    def __init__(self, tiles, total, dps, groups):
        count, shape = dps * groups, tiles.shape[-2:]
        self.total = total
        self.inputs, self.in_specs = [tiles], [VM]
        out = shape if total else (count,) + shape
        self.outs, self.out_specs = [jax.ShapeDtypeStruct(out, jnp.float32)], [VM]
        self.scratch = [pltpu.VMEM((count,) + shape, jnp.float32), DMA((count,)), DMA((count,))]
        self.result = lambda out: out

    def bind(self, place, x_ref, out_ref, landing, sends, recvs):
        count = place.dps * place.groups
        me = place.d * place.groups + place.s

        def copy(i):
            other = (me + i) % count
            return remote(
                x_ref.at[other] if self.total else x_ref,
                landing.at[me],
                sends.at[i],
                recvs.at[i],
                dp=other // place.groups,
                seq=other % place.groups,
            )

        def start():
            def each(i, _):
                copy(i).start()
                return 0

            lax.fori_loop(1, count, each, 0)

        def finish():
            def each(i, _):
                copy(i).wait_recv()
                copy(i).wait_send()
                return 0

            lax.fori_loop(1, count, each, 0)
            landing[me] = x_ref[me] if self.total else x_ref[...]
            out_ref[...] = jnp.sum(landing[...], axis=0) if self.total else landing[...]

        return start, {}, finish


TILE = 256


class FeedForward:
    def __init__(self, normed, down, gate, up, grad_all, dps, groups):
        rows, width = normed.shape
        shape, chips = (SUB, rows // SUB, width), groups // 2
        held = gate.shape[0]
        ring = (2, down.shape[0] // 2, width)
        pair = 2 * rows
        self.inputs = [
            normed.reshape(shape),
            down.reshape(ring),
            gate,
            up,
            grad_all.reshape(chips, pair, width),
        ]
        self.in_specs = [VM, VM, ANY, ANY, ANY]
        act = jax.ShapeDtypeStruct((chips, pair, held), jnp.bfloat16)
        self.outs = [
            jax.ShapeDtypeStruct((groups,) + shape, jnp.bfloat16),
            jax.ShapeDtypeStruct((dps,) + ring, jnp.bfloat16),
            act,
            act,
            act,
        ]
        self.out_specs = [VM] * 5
        self.scratch = [
            pltpu.VMEM((held, width), jnp.bfloat16),
            pltpu.VMEM((held, width), jnp.bfloat16),
            pltpu.VMEM((chips, pair, width), jnp.bfloat16),
            pltpu.VMEM((chips, pair, held), jnp.float32),
            pltpu.VMEM((chips, pair, held), jnp.float32),
            pltpu.VMEM((dps, chips, pair, held // dps), jnp.float32),
            DMA((4,)),
            DMA,
        ]
        self.scratch += [DMA((chips, SUB))] * 6 + ring_sems(dps // 2)
        self.result = lambda hn, full, *acts: (
            hn.reshape(groups * rows, width),
            full.reshape(held, width),
            *[one.reshape(groups * rows, held) for one in acts],
        )

    def bind(self, place, x_ref, shard, gate_at, up_at, grad_at, *refs):
        hn, full, inner, dgate, dup, gate_w, up_w, grads, slope, silu, dinner = refs[:11]
        loads, own_line = refs[11:13]
        line_sems, ring_refs = refs[13:19], refs[19:]
        chip, chips = place.chip, place.chips
        pair, held = inner.shape[1:]
        width = gate_w.shape[1]
        own, start_line, step, arrived, sent = line_gather(place, x_ref, hn, own_line, *line_sems)
        ring = ring_gather(
            place,
            lambda half: shard.at[half],
            lambda chunk, half: full.at[chunk, half],
            *ring_refs,
        )
        copies = [
            pltpu.make_async_copy(gate_at, gate_w, loads.at[0]),
            pltpu.make_async_copy(up_at, up_w, loads.at[1]),
            pltpu.make_async_copy(grad_at, grads, loads.at[2]),
            pltpu.make_async_copy(shard, full.at[place.d], loads.at[3]),
        ]
        wide = 512 if held % 512 == 0 else held

        def start():
            start_line()
            ring[0]()
            for one in copies:
                one.start()

        def forward(at):
            rows = hn[pl.ds(2 * at, 2)].reshape(pair, width)
            for first in range(0, held, wide):
                span = slice(first, first + wide)
                gate = lax.dot_general(
                    rows, gate_w[span, :], contract_cols, preferred_element_type=jnp.float32
                )
                upward = lax.dot_general(
                    rows, up_w[span, :], contract_cols, preferred_element_type=jnp.float32
                )
                sigmoid = jax.nn.sigmoid(gate)
                passed = gate * sigmoid
                inner[at, :, span] = (passed * upward).astype(jnp.bfloat16)
                silu[at, :, span] = passed
                slope[at, :, span] = upward * sigmoid * (1.0 + gate * (1.0 - sigmoid))

        def when_there(at, there):
            @pl.when(there)
            def _():
                arrived(at)
                forward(at)

        chunk = held // place.dps
        early = chunk % 128 == 0

        def back(owner, part):
            def each(at, _):
                dinner[owner, at] = lax.dot_general(
                    grads[at], part, contract_cols, preferred_element_type=jnp.float32
                )
                return 0

            lax.fori_loop(0, chips, each, 0)

        def back_from(owner):
            back(owner, full[owner].reshape(chunk, width))

        def tick(hop, half):
            step(hop, half)
            if early and hop == 1 and half == 1:
                copies[2].wait()
                back(place.d, shard[...].reshape(chunk, width))
            if hop == 1 and half == 0:
                own.wait()
                copies[0].wait()
                copies[1].wait()
                arrived(chip)
                forward(chip)
            if hop > 1 and half == 0:
                when_there(chip - hop + 1, chip - hop + 1 >= 0)
            if hop > 1 and half == SUB - 1:
                when_there(chip + hop - 1, chip + hop - 1 < chips)

        def finish():
            last = chips - 1
            when_there(chip - last, chip - last >= 0)
            when_there(chip + last, chip + last < chips)
            copies[3].wait()
            if not early:
                copies[2].wait()
                ring[2]()
                last_all()
            else:
                ring[2](True)
                if place.hops > 2:
                    back_between()
                back_from(place.ring(place.hops))

                def each(at, _):
                    for q in range(place.dps):
                        span = slice(q * chunk, (q + 1) * chunk)
                        grad = dinner[q, at]
                        dgate[at, :, span] = (grad * slope[at, :, span]).astype(jnp.bfloat16)
                        dup[at, :, span] = (grad * silu[at, :, span]).astype(jnp.bfloat16)
                    return 0

                lax.fori_loop(0, chips, each, 0)
            sent()

        def back_between():
            for hop in range(1, place.hops):
                back_from(place.ring(hop))
                back_from(place.ring(-hop))

        def last_all():
            def each(at, _):
                rows = grads[at]
                for first in range(0, held, wide):
                    span = slice(first, first + wide)
                    part = full[first // chunk : (first + wide) // chunk].reshape(wide, width)
                    grad = lax.dot_general(
                        rows, part, contract_cols, preferred_element_type=jnp.float32
                    )
                    dgate[at, :, span] = (grad * slope[at, :, span]).astype(jnp.bfloat16)
                    dup[at, :, span] = (grad * silu[at, :, span]).astype(jnp.bfloat16)
                return 0

            lax.fori_loop(0, chips, each, 0)

        ticks = {
            (hop - 1) * SUB + half: functools.partial(tick, hop, half)
            for hop in range(1, chips)
            for half in range(SUB)
        }

        def with_ring(tick, hop):
            ticks[tick]()
            ring[1](hop)

        def with_near(tick):
            ticks[tick]()
            ring[3]()
            if place.hops == 2:
                back_between()

        merged = dict(ticks)
        for hop in range(1, place.hops):
            merged[2 * hop - 1] = functools.partial(with_ring, 2 * hop - 1, hop)
        if early:
            merged[2 * place.hops - 1] = functools.partial(with_near, 2 * place.hops - 1)
        return start, merged, finish


class FeedBack:
    def __init__(self, inner, dgate, dup, gate, up, down, normed, grads, dps, groups):
        length, held = inner.shape
        width, chips = normed.shape[1], groups // 2
        rows = length // groups
        shape = (SUB, rows // SUB, width)
        owned = (2, held // dps // 2, width)
        hops = dps // 2
        tile = (2, SUB, rows // SUB, width)
        self.inputs = [inner, dgate, dup, gate, up, down, normed, grads]
        self.in_specs = [ANY] * 8
        self.outs = [
            jax.ShapeDtypeStruct(shape, jnp.float32),
            jax.ShapeDtypeStruct(owned, jnp.float32),
            jax.ShapeDtypeStruct((held // TILE,) + tile, jnp.bfloat16),
            jax.ShapeDtypeStruct((held // TILE,) + tile, jnp.bfloat16),
            jax.ShapeDtypeStruct((chips,) + tile, jnp.bfloat16),
        ]
        self.out_specs = [VM, VM, ANY, ANY, ANY]
        act = pltpu.VMEM((length, held), jnp.bfloat16)
        weight = pltpu.VMEM((held, width), jnp.bfloat16)
        tokens = pltpu.VMEM((length, width), jnp.bfloat16)
        self.scratch = [act] * 3 + [weight] * 3 + [tokens] * 2
        self.scratch += [
            pltpu.VMEM((groups,) + shape, jnp.bfloat16),
            pltpu.VMEM((dps,) + owned, jnp.bfloat16),
            pltpu.VMEM((2,) + tile, jnp.bfloat16),
            DMA((8,)),
            DMA((2,)),
        ]
        self.scratch += line_scatter_scratch(chips, shape)
        self.scratch += (
            [pltpu.VMEM((hops,) + owned, jnp.bfloat16)] * 2
            + [pltpu.VMEM((hops - 1,) + owned, jnp.bfloat16)] * 2
            + ring_sems(hops)
        )
        self.result = lambda total, mine, gate_term, up_term, out: (
            total.reshape(rows, width),
            mine.reshape(held // dps, width),
            gate_term.reshape(held, width),
            up_term.reshape(held, width),
            out.reshape(length, width),
        )

    def bind(self, place, *refs):
        sources, refs = refs[:8], refs[8:]
        total_ref, own_ref, gate_out, up_out, result_out = refs[:5]
        inner, dgate, dup, gate, up, down, normed, grads = refs[5:13]
        p_ref, term, stage, loads, stage_sem = refs[13:18]
        line_refs, ring_refs = refs[18:27], refs[27:]
        chip, chips, hops = place.chip, place.chips, place.hops
        held, width = gate.shape
        pair = inner.shape[0] // chips
        chunk = held // place.dps
        wide = 1024 if width % 1024 == 0 else width
        send, step, finish_line = line_scatter(place, p_ref, total_ref, *line_refs)

        def put(half, value):
            own_ref[half] = value

        ring = ring_scatter(place, lambda at, half: term.at[at, half], put, *ring_refs)
        targets = [inner, dgate, dup, gate, up, down, normed, grads]
        copies = [
            pltpu.make_async_copy(source, target, loads.at[i])
            for i, (source, target) in enumerate(zip(sources, targets))
        ]

        def start():
            for i in (0, 7, 1, 3, 2, 4, 6, 5):
                copies[i].start()

        def rows_of(ref, at):
            return ref[pl.ds(pl.multiple_of(at * pair, pair), pair), :]

        def partial(at):
            left, right = rows_of(dgate, at), rows_of(dup, at)
            for first in range(0, width, wide):
                span = slice(first, first + wide)
                value = jnp.dot(left, gate[:, span], preferred_element_type=jnp.float32)
                value += jnp.dot(right, up[:, span], preferred_element_type=jnp.float32)
                p_ref[pl.ds(2 * at, 2), :, :, span] = value.astype(jnp.bfloat16).reshape(
                    p_ref[pl.ds(2 * at, 2), :, :, span].shape
                )
            send(at)

        def term_rows(ref, other, start, count, span):
            return lax.dot_general(
                ref[:, pl.ds(start, count)],
                other[:, span],
                contract_rows,
                preferred_element_type=jnp.float32,
            ).astype(jnp.bfloat16)

        def down_tile(at):
            if chunk % 128 == 0:
                for first in range(0, width, wide):
                    span = slice(first, first + wide)
                    value = term_rows(inner, grads, pl.multiple_of(at * chunk, chunk), chunk, span)
                    term[at, :, :, span] = value.reshape(2, chunk // 2, wide)

        def down_all():
            if chunk % 128 != 0:
                for row in range(0, held, TILE):
                    for first in range(0, width, wide):
                        span = slice(first, first + wide)
                        value = term_rows(inner, grads, row, TILE, span)
                        term[row // chunk : (row + TILE) // chunk, :, :, span] = value.reshape(
                            TILE // chunk, 2, chunk // 2, wide
                        )

        jobs = []

        def first_job():
            copies[0].wait()
            copies[7].wait()
            down_all()
            down_tile(place.ring(hops))
            ring[3]()

        def next_job(hop):
            down_tile(place.ring(hop))
            down_tile(place.ring(-hop))
            if hop == hops - 1:
                ring[4]()

        for hop in range(hops - 1, 0, -1):
            jobs.append(functools.partial(next_job, hop))
            jobs.append(functools.partial(ring[1], hop))
        jobs.append(lambda: down_tile(place.d))

        count = [0]
        waits = []

        def staged(value_of, target):
            slot = count[0] % 2
            if count[0] >= 2:
                waits[count[0] - 2].wait()
            value_of(stage.at[slot])
            copy = pltpu.make_async_copy(stage.at[slot], target, stage_sem.at[slot])
            copy.start()
            waits.append(copy)
            count[0] += 1

        def weight_tile(ref, row, out):
            def fill(slot):
                for first in range(0, width, wide):
                    span = slice(first, first + wide)
                    value = term_rows(ref, normed, row, TILE, span)
                    slot[:, :, :, span] = value.reshape(slot.shape[:3] + (wide,))

            staged(fill, out.at[row // TILE])

        def result_tile(at):
            def fill(slot):
                left = rows_of(inner, at)
                for first in range(0, width, wide):
                    span = slice(first, first + wide)
                    value = jnp.dot(left, down[:, span], preferred_element_type=jnp.float32)
                    slot[:, :, :, span] = value.astype(jnp.bfloat16).reshape(
                        slot.shape[:3] + (wide,)
                    )

            staged(fill, result_out.at[at])

        def sequence():
            first_job()
            for i in (1, 3, 2, 4):
                copies[i].wait()
            tiles = [
                functools.partial(weight_tile, ref, row, out)
                for ref, out in ((dgate, gate_out), (dup, up_out))
                for row in range(0, held, TILE)
            ]
            tiles += [functools.partial(result_tile, at) for at in range(chips)]
            done = [0]

            def fill(most):
                for _ in range(most):
                    if tiles:
                        if done[0] == 0:
                            copies[6].wait()
                        if done[0] == 2 * (held // TILE):
                            copies[5].wait()
                        done[0] += 1
                        tiles.pop(0)()

            for wave in range(chips - 1):
                high = chips - 1 - wave
                ups = (high > chip).astype(jnp.int32)
                downs = (wave < chip).astype(jnp.int32)

                def each(i, _, high=high, wave=wave, ups=ups):
                    partial(jnp.where(i < ups, high, wave))
                    return 0

                lax.fori_loop(0, ups + downs, each, 0)
                fill(1)
                step(wave, 0)
                if wave == 0:
                    step(wave, 1)
                    jobs.pop(0)()
                else:
                    fill(1)
                    step(wave, 1)
                    if jobs:
                        jobs.pop(0)()
            partial(chip)
            for job in jobs:
                job()
            fill(len(tiles))

        def finish():
            ring[2]()
            finish_line()
            for copy in waits[-2:]:
                copy.wait()

        return start, {0: sequence}, finish


def move(parts, dps, groups, number, greet=greet_near):
    def kernel(*refs):
        place = Place(dps, groups)
        at = [
            0,
            sum(len(part.inputs) for part in parts),
            sum(len(part.inputs) + len(part.outs) for part in parts),
        ]
        bound = []
        for part in parts:
            mine = []
            for kind, length in enumerate((len(part.inputs), len(part.outs), len(part.scratch))):
                mine += refs[at[kind] : at[kind] + length]
                at[kind] += length
            bound.append(part.bind(place, *mine))
        greet(place)
        for start, _, _ in bound:
            start()
        for tick in range(1 + max([0] + [max(list(ticks) + [0]) for _, ticks, _ in bound])):
            for _, ticks, _ in bound:
                if tick in ticks:
                    ticks[tick]()
        for _, _, finish in bound:
            finish()

    outs = pl.pallas_call(
        kernel,
        out_shape=[out for part in parts for out in part.outs],
        in_specs=[spec for part in parts for spec in part.in_specs],
        out_specs=[spec for part in parts for spec in part.out_specs],
        scratch_shapes=[one for part in parts for one in part.scratch],
        compiler_params=pltpu.CompilerParams(
            collective_id=number, has_side_effects=True, vmem_limit_bytes=63 << 20
        ),
        cost_estimate=pl.CostEstimate(flops=0, bytes_accessed=120_000_000, transcendentals=0),
        name=f"move_{number}",
    )(*[x for part in parts for x in part.inputs])
    results, at = [], 0
    for part in parts:
        results.append(part.result(*outs[at : at + len(part.outs)]))
        at += len(part.outs)
    return results


def norm_factor(values):
    return lax.rsqrt(jnp.mean(values * values, axis=-1, keepdims=True) + epsilon)


def norm_grad(values, factor, gain, gradient):
    weighted = gradient * gain
    inner_mean = jnp.mean(weighted * values, axis=-1, keepdims=True)
    return factor * weighted - values * (factor * factor * factor) * inner_mean


def rope_tables(positions, head_width):
    half_width = head_width // 2
    frequency = rope_base ** (-2.0 * jnp.arange(half_width, dtype=jnp.float32) / head_width)
    angles = positions.astype(jnp.float32)[:, None] * frequency[None, :]
    return (jnp.cos(angles)[:, None, :], jnp.sin(angles)[:, None, :])


def rotate(values, cosine_table, sine_table):
    half_width = values.shape[-1] // 2
    first_half = values[..., :half_width]
    second_half = values[..., half_width:]
    return jnp.concatenate(
        [
            first_half * cosine_table - second_half * sine_table,
            second_half * cosine_table + first_half * sine_table,
        ],
        axis=-1,
    )


def block_scores(query_block, key_heads, lower, upper, score_scale):
    scores = (
        jnp.einsum(
            "qhd,kd->hqk", query_block, key_heads[:upper], preferred_element_type=jnp.float32
        )
        * score_scale
    )
    rows_at = lower + jnp.arange(query_block.shape[0], dtype=jnp.int32)
    cols_at = jnp.arange(upper, dtype=jnp.int32)
    allowed = (cols_at[None, :] <= rows_at[:, None])[None]
    return jnp.where(allowed, scores, masked_value)


def per_device(
    tokens,
    qkv_weight,
    out_weight,
    gate_weight,
    up_weight,
    down_weight,
    attn_gain,
    mlp_gain,
    cotangent,
):
    groups = lax.axis_size("seq")
    dps = lax.axis_size("dp")
    tok_rows = tokens.shape[1]
    model_width = tokens.shape[2]
    weight_rows = qkv_weight.shape[0]
    seq_len = tok_rows * groups
    local_heads = HEADS // groups
    local_width = local_heads * HEAD_DIM
    kv_copies = groups // KV_HEADS
    score_scale = HEAD_DIM ** (-0.5)
    block_rows = min(512, seq_len)
    block_count = seq_len // block_rows
    fold = groups // dps
    order = [(at % dps) * fold + at // dps for at in range(groups)]

    q_part = qkv_weight[:, :model_width].reshape(weight_rows, groups, local_width)
    k_part = qkv_weight[:, model_width : model_width + KV_HEADS * HEAD_DIM]
    v_part = qkv_weight[:, model_width + KV_HEADS * HEAD_DIM :]
    k_part = k_part.reshape(weight_rows, KV_HEADS, HEAD_DIM)
    v_part = v_part.reshape(weight_rows, KV_HEADS, HEAD_DIM)
    columns = jnp.stack(
        [
            jnp.concatenate(
                [q_part[:, g], k_part[:, g // kv_copies], v_part[:, g // kv_copies]], axis=1
            )
            for g in order
        ]
    )
    gain_width = attn_gain.shape[0]
    tile = jnp.zeros((8, 128), jnp.float32)
    tile = tile.at[0, :gain_width].set(attn_gain.astype(jnp.float32))
    tile = tile.at[1, :gain_width].set(mlp_gain.astype(jnp.float32))
    qkv_local, tokens_all, out_rows, gate_part, gains = move(
        [
            Columns(columns, dps, groups),
            LineGather(tokens[0], dps, groups),
            Rows(out_weight, dps, groups),
            RingGather(gate_weight, dps, groups),
            Spread(tile, False, dps, groups),
        ],
        dps,
        groups,
        1,
        greet_all,
    )
    gain_one = gains[:, 0, :gain_width].reshape(model_width)
    gain_two = gains[:, 1, :gain_width].reshape(model_width)

    x_rows = tokens[0].astype(jnp.float32)
    factor_one = norm_factor(x_rows)
    all_rows = tokens_all.astype(jnp.float32)
    normed_all = (all_rows * norm_factor(all_rows) * gain_one).astype(jnp.bfloat16)
    grad_low = cotangent[0]
    grad_low, _ = lax.optimization_barrier((grad_low, gains))
    grad_all = lax.all_gather(grad_low, "seq", axis=0, tiled=True)

    mixed = jnp.dot(normed_all, qkv_local, preferred_element_type=jnp.float32)
    cosine_table, sine_table = rope_tables(jnp.arange(seq_len, dtype=jnp.int32), HEAD_DIM)
    query_heads = rotate(
        mixed[:, :local_width].reshape(seq_len, local_heads, HEAD_DIM), cosine_table, sine_table
    ).astype(jnp.bfloat16)
    key_heads = rotate(
        mixed[:, None, local_width : local_width + HEAD_DIM], cosine_table, sine_table
    ).astype(jnp.bfloat16)[:, 0]
    value_heads = mixed[:, local_width + HEAD_DIM :].astype(jnp.bfloat16)
    outputs = []
    log_sums = []
    for block in range(block_count):
        lower = block * block_rows
        upper = lower + block_rows
        scores = block_scores(query_heads[lower:upper], key_heads, lower, upper, score_scale)
        highest = jnp.max(scores, axis=-1, keepdims=True)
        log_sum = highest + jnp.log(jnp.sum(jnp.exp(scores - highest), axis=-1, keepdims=True))
        probs = jnp.exp(scores - log_sum).astype(jnp.bfloat16)
        attended = jnp.einsum(
            "hqk,kd->qhd", probs, value_heads[:upper], preferred_element_type=jnp.float32
        )
        outputs.append(attended.astype(jnp.bfloat16))
        log_sums.append(log_sum)
    attended = jnp.concatenate(outputs, axis=0).reshape(seq_len, local_width)
    partial = jnp.dot(attended, out_rows, preferred_element_type=jnp.float32)
    summed, up_part = move(
        [
            LineScatter(partial.astype(jnp.bfloat16), dps, groups),
            RingGather(up_weight, dps, groups),
        ],
        dps,
        groups,
        2,
    )
    hidden = x_rows + summed
    factor_two = norm_factor(hidden)
    normed_two = (hidden * factor_two * gain_two).astype(jnp.bfloat16)
    ((hn_all, down_part, inner, grad_gate, grad_upward),) = move(
        [FeedForward(normed_two, down_weight, gate_part, up_part, grad_all, dps, groups)],
        dps,
        groups,
        3,
    )
    ((grad_normed, down_owned, gate_term, up_term, result),) = move(
        [
            FeedBack(
                inner,
                grad_gate,
                grad_upward,
                gate_part,
                up_part,
                down_part,
                hn_all,
                grad_all,
                dps,
                groups,
            )
        ],
        dps,
        groups,
        4,
    )
    gain_two_term = jnp.sum(grad_normed * hidden * factor_two, axis=0)
    grad_hidden = grad_low.astype(jnp.float32) + norm_grad(
        hidden, factor_two, gain_two, grad_normed
    )
    grad_branch, gate_owned = move(
        [
            LineGather(grad_hidden.astype(jnp.bfloat16), dps, groups),
            RingScatter(gate_term, dps, groups),
        ],
        dps,
        groups,
        5,
    )
    result, grad_branch = lax.optimization_barrier((result, grad_branch))
    mlp_result = lax.psum_scatter(result, "seq", scatter_dimension=0, tiled=True)
    block_out = (hidden + mlp_result.astype(jnp.float32)).astype(jnp.bfloat16)[None]
    out_term = lax.dot_general(
        attended, grad_branch, contract_rows, preferred_element_type=jnp.float32
    ).astype(jnp.bfloat16)
    grad_heads = (
        lax.dot_general(grad_branch, out_rows, contract_cols, preferred_element_type=jnp.float32)
        .astype(jnp.bfloat16)
        .reshape(seq_len, local_heads, HEAD_DIM)
    )
    grad_keys = jnp.zeros((seq_len, HEAD_DIM), jnp.float32)
    grad_values = jnp.zeros((seq_len, HEAD_DIM), jnp.float32)
    grad_queries = []
    for block in range(block_count):
        lower = block * block_rows
        upper = lower + block_rows
        query_block = query_heads[lower:upper]
        grad_block = grad_heads[lower:upper]
        scores = block_scores(query_block, key_heads, lower, upper, score_scale)
        probs = jnp.exp(scores - log_sums[block])
        probs_low = probs.astype(jnp.bfloat16)
        grad_probs = jnp.einsum(
            "qhd,kd->hqk", grad_block, value_heads[:upper], preferred_element_type=jnp.float32
        )
        row_delta = jnp.sum(probs * grad_probs, axis=-1, keepdims=True)
        grad_scores = (probs * (grad_probs - row_delta)).astype(jnp.bfloat16)
        grad_queries.append(
            jnp.einsum(
                "hqk,kd->qhd", grad_scores, key_heads[:upper], preferred_element_type=jnp.float32
            )
            * score_scale
        )
        grad_keys = grad_keys.at[:upper].add(
            jnp.einsum("hqk,qhd->kd", grad_scores, query_block, preferred_element_type=jnp.float32)
            * score_scale
        )
        grad_values = grad_values.at[:upper].add(
            jnp.einsum("hqk,qhd->kd", probs_low, grad_block, preferred_element_type=jnp.float32)
        )
    grad_q = rotate(jnp.concatenate(grad_queries, axis=0), cosine_table, -sine_table)
    grad_k = rotate(grad_keys[:, None], cosine_table, -sine_table)[:, 0]
    grad_mixed = jnp.concatenate(
        [grad_q.reshape(seq_len, local_width), grad_k, grad_values], axis=1
    ).astype(jnp.bfloat16)
    qkv_term = lax.dot_general(
        normed_all, grad_mixed, contract_rows, preferred_element_type=jnp.float32
    )
    partial = lax.dot_general(
        grad_mixed, qkv_local, contract_cols, preferred_element_type=jnp.float32
    )
    qkv_term = qkv_term.astype(jnp.bfloat16)
    gain_one_term = (
        jnp.sum(qkv_term.astype(jnp.float32) * qkv_local.astype(jnp.float32), axis=1) / gain_one
    )
    terms = jnp.stack([gain_one_term, gain_two_term]).reshape(2, dps * groups, gain_width)
    terms = jnp.pad(terms.transpose(1, 0, 2), ((0, 0), (0, 6), (0, 128 - gain_width)))
    qkv_owned, grad_normed_one, out_owned, up_owned, gain_grads = move(
        [
            ColumnsBack(qkv_term, order, local_width, kv_copies, weight_rows, dps, groups),
            LineScatter(partial.astype(jnp.bfloat16), dps, groups),
            RowsBack(out_term, weight_rows, dps, groups),
            RingScatter(up_term, dps, groups, late=True),
            Spread(terms, True, dps, groups),
        ],
        dps,
        groups,
        6,
        greet_all,
    )
    grad_input = grad_hidden + norm_grad(x_rows, factor_one, gain_one, grad_normed_one)
    return (
        block_out,
        grad_input[None],
        qkv_owned,
        out_owned,
        gate_owned,
        up_owned,
        down_owned,
        gain_grads[0, :gain_width],
        gain_grads[1, :gain_width],
    )


def solution(mesh):
    rows = P(("dp", "seq"), None)
    tokens = P("dp", "seq", None)
    gains = P(("dp", "seq"))
    return jax.shard_map(
        per_device,
        mesh=mesh,
        in_specs=(tokens, rows, rows, rows, rows, rows, gains, gains, tokens),
        out_specs=(tokens, tokens, rows, rows, rows, rows, rows, gains, gains),
        check_vma=False,
    )
```

```python
import functools

import jax
import jax.numpy as jnp
from jax import lax
from jax.experimental import pallas as pl
from jax.experimental.pallas import tpu as pltpu
from jax.sharding import PartitionSpec as P

HEADS = 32
KV_HEADS = 8
HEAD_DIM = 64

MESH = pl.DeviceIdType.MESH
ANY = pl.BlockSpec(memory_space=pl.ANY)
VM = pl.BlockSpec(memory_space=pltpu.VMEM)
SUB = 2

epsilon = 1e-05
rope_base = 500000.0
masked_value = -1e30
contract_rows = (((0,), (0,)), ((), ()))
contract_cols = (((1,), (1,)), ((), ()))


class Place:
    def __init__(self, dps, groups):
        self.dps, self.groups, self.chips, self.hops = dps, groups, groups // 2, dps // 2
        self.d, self.s = lax.axis_index("dp"), lax.axis_index("seq")
        self.chip, self.core = self.s // 2, self.s % 2
        self.partner = 2 * self.chip + 1 - self.core
        row, side = self.d // 2, self.d % 2
        self.turn = side * (dps - 1 - row) + (1 - side) * row

    def ring(self, distance):
        at = (self.turn + distance + self.dps) % self.dps
        side = at // self.hops
        return (1 - side) * 2 * at + side * (2 * (self.dps - 1 - at) + 1)


def remote(src, dst, send, recv, **target):
    return pltpu.make_async_remote_copy(
        src_ref=src, dst_ref=dst, send_sem=send, recv_sem=recv, device_id=target, device_id_type=MESH
    )


def greet_near(place):
    barrier = pltpu.get_barrier_semaphore()

    def signal(**target):
        pl.semaphore_signal(barrier, inc=1, device_id=target, device_id_type=MESH)

    signal(seq=place.partner)
    signal(dp=place.ring(1))
    signal(dp=place.ring(-1))

    @pl.when(place.chip > 0)
    def _():
        signal(seq=place.s - 2)

    @pl.when(place.chip < place.chips - 1)
    def _():
        signal(seq=place.s + 2)

    ends = (place.chips - place.chip) // place.chips + (place.chip + 1) // place.chips
    pl.semaphore_wait(barrier, 5 - ends)


def greet_all(place):
    barrier = pltpu.get_barrier_semaphore()
    count = place.dps * place.groups
    me = place.d * place.groups + place.s

    def signal(i, _):
        other = (me + i) % count
        pl.semaphore_signal(
            barrier,
            inc=1,
            device_id={"dp": other // place.groups, "seq": other % place.groups},
            device_id_type=MESH,
        )
        return 0

    lax.fori_loop(1, count, signal, 0)
    pl.semaphore_wait(barrier, count - 1)


DMA = pltpu.SemaphoreType.DMA


def line_gather(place, x_ref, out_ref, own_sem, us, ur, ds, dr, ps, pr):
    s, chip, chips = place.s, place.chip, place.chips

    def copy(src, group, half, sends, recvs, at, target):
        return remote(
            src, out_ref.at[group, half], sends.at[at, half], recvs.at[at, half], seq=target
        )

    def up(src, group, hop, half):
        return copy(src, group, half, us, ur, hop, s + 2)

    def down(src, group, hop, half):
        return copy(src, group, half, ds, dr, hop, s - 2)

    def pair(src, group, half):
        return copy(src, group, half, ps, pr, group // 2, place.partner)

    own = pltpu.make_async_copy(x_ref, out_ref.at[s], own_sem)

    def start():
        own.start()
        for half in range(SUB):

            @pl.when(chip < chips - 1)
            def _():
                up(x_ref.at[half], s, 0, half).start()

            @pl.when(chip > 0)
            def _():
                down(x_ref.at[half], s, 0, half).start()

        for half in range(SUB):
            pair(x_ref.at[half], s, half).start()

    def step(hop, half):
        below, above = s - 2 * hop, s + 2 * hop

        @pl.when(chip - hop >= 0)
        def _():
            block = out_ref.at[below, half]
            up(block, below, hop - 1, half).wait_recv()

            @pl.when(chip < chips - 1)
            def _():
                up(block, below, hop, half).start()

            pair(block, below, half).start()

        @pl.when(chip + hop < chips)
        def _():
            block = out_ref.at[above, half]
            down(block, above, hop - 1, half).wait_recv()

            @pl.when(chip > 0)
            def _():
                down(block, above, hop, half).start()

            pair(block, above, half).start()

    def arrived(at):
        for half in range(SUB):
            group = 2 * at + 1 - place.core
            pair(out_ref.at[group, half], group, half).wait_recv()

    def sent():
        def each(i, _):
            k, half = i // SUB, i % SUB
            mine = 2 * k + place.core
            block = out_ref.at[mine, half]
            pair(block, mine, half).wait_send()

            @pl.when(jnp.logical_and(chip - k >= 0, chip < chips - 1))
            def _():
                up(block, mine, k, half).wait_send()

            @pl.when(jnp.logical_and(chip + k < chips, chip > 0))
            def _():
                down(block, mine, k, half).wait_send()

            return 0

        lax.fori_loop(0, chips * SUB, each, 0)

    return own, start, step, arrived, sent


class LineGather:
    def __init__(self, x, dps, groups, normed=False):
        rows, width = x.shape
        shape = (SUB, rows // SUB, width)
        self.normed = normed
        self.inputs, self.in_specs = [x.reshape(shape)], [VM]
        self.outs, self.out_specs = [jax.ShapeDtypeStruct((groups,) + shape, x.dtype)], [ANY]
        self.scratch = [DMA] + [DMA((groups // 2, SUB))] * 6
        if normed:
            self.scratch = [pltpu.VMEM(shape, x.dtype)] + self.scratch
        self.result = lambda out: out.reshape(groups * rows, width)

    def bind(self, place, x_ref, out_ref, *refs):
        if self.normed:
            source, x_ref, refs = x_ref, refs[0], refs[1:]
            many = 16 if x_ref.shape[1] % 16 == 0 else x_ref.shape[1]

            def norm(i, _):
                span = pl.ds(pl.multiple_of(i * many, many), many)
                for half in range(SUB):
                    values = source[half, span, :].astype(jnp.float32)
                    x_ref[half, span, :] = (values * norm_factor(values)).astype(x_ref.dtype)
                return 0

            lax.fori_loop(0, x_ref.shape[1] // many, norm, 0)
        own, start, step, arrived, sent = line_gather(place, x_ref, out_ref, *refs)

        def finish():
            own.wait()

            def each(at, _):
                arrived(at)
                return 0

            lax.fori_loop(0, place.chips, each, 0)
            sent()

        ticks = {
            (hop - 1) * SUB + half: functools.partial(step, hop, half)
            for hop in range(1, place.chips)
            for half in range(SUB)
        }
        return start, ticks, finish


def line_scatter(place, p_ref, out_ref, pairbuf, upbuf, downbuf, us, ur, ds, dr, ps, pr):
    s, chip, chips, core = place.s, place.chip, place.chips, place.core

    def copy(src, buffer, at, half, sends, recvs, target):
        return remote(src, buffer.at[at, half], sends.at[at, half], recvs.at[at, half], seq=target)

    def pair(at, half):
        src = p_ref.at[2 * at + 1 - core, half]
        return copy(src, pairbuf, at, half, ps, pr, place.partner)

    def up(at, half):
        return copy(upbuf.at[at, half], upbuf, at, half, us, ur, s + 2)

    def down(at, half):
        return copy(downbuf.at[at, half], downbuf, at, half, ds, dr, s - 2)

    def wide(ref, *at):
        return ref[at].astype(jnp.float32)

    def local(at, half):
        return wide(p_ref, 2 * at + core, half) + wide(pairbuf, at, half)

    def send(at):
        for half in range(SUB):
            pair(at, half).start()

    def step(wave, half):
        high, low = chips - 1 - wave + chip, wave - (chips - 1 - chip)

        @pl.when(chip <= wave)
        def _():
            pair(high, half).wait_recv()

            @pl.when(chip > 0)
            def _():
                up(high, half).wait_recv()
                total = local(high, half) + wide(upbuf, high, half)
                upbuf[high, half] = total.astype(jnp.bfloat16)

            @pl.when(chip == 0)
            def _():
                upbuf[high, half] = local(high, half).astype(jnp.bfloat16)

            up(high, half).start()

        @pl.when(low >= 0)
        def _():
            pair(low, half).wait_recv()

            @pl.when(chip < chips - 1)
            def _():
                down(low, half).wait_recv()
                total = local(low, half) + wide(downbuf, low, half)
                downbuf[low, half] = total.astype(jnp.bfloat16)

            @pl.when(chip == chips - 1)
            def _():
                downbuf[low, half] = local(low, half).astype(jnp.bfloat16)

            down(low, half).start()

    def finish():
        for half in range(SUB):
            pair(chip, half).wait_recv()
            out_ref[half] = local(chip, half)

            @pl.when(chip > 0)
            def _():
                up(chip, half).wait_recv()
                out_ref[half] += wide(upbuf, chip, half)

            @pl.when(chip < chips - 1)
            def _():
                down(chip, half).wait_recv()
                out_ref[half] += wide(downbuf, chip, half)

        def each(i, _):
            at, half = i // SUB, i % SUB
            pair(at, half).wait_send()

            @pl.when(at > chip)
            def _():
                up(at, half).wait_send()

            @pl.when(at < chip)
            def _():
                down(at, half).wait_send()

            return 0

        lax.fori_loop(0, chips * SUB, each, 0)

    return send, step, finish


def line_scatter_scratch(chips, shape):
    return [pltpu.VMEM((chips,) + shape, jnp.bfloat16)] * 3 + [DMA((chips, SUB))] * 6


class LineScatter:
    def __init__(self, partial, dps, groups):
        total, width = partial.shape
        rows = total // groups
        shape = (SUB, rows // SUB, width)
        self.inputs, self.in_specs = [partial.reshape((groups,) + shape)], [VM]
        self.outs, self.out_specs = [jax.ShapeDtypeStruct(shape, jnp.float32)], [VM]
        self.scratch = line_scatter_scratch(groups // 2, shape)
        self.result = lambda out: out.reshape(rows, width)

    def bind(self, place, *refs):
        send, step, finish = line_scatter(place, *refs)
        chip, chips = place.chip, place.chips

        def start():
            def issue(low, _):
                high = chips - 1 - low

                @pl.when(high > chip)
                def _():
                    send(high)

                @pl.when(low < chip)
                def _():
                    send(low)

                return 0

            lax.fori_loop(0, chips - 1, issue, 0)
            send(chip)

        ticks = {
            i: functools.partial(step, i // SUB, i % SUB) for i in range((chips - 1) * SUB)
        }
        return start, ticks, finish


def ring_sems(hops):
    return [DMA((hops, 2))] * 4


def ring_gather(place, own, out, rs, rr, ls, lr):
    hops = place.hops

    def right(src, chunk, hop, half):
        return remote(
            src, out(chunk, half), rs.at[hop - 1, half], rr.at[hop - 1, half], dp=place.ring(1)
        )

    def left(src, chunk, hop, half):
        return remote(
            src, out(chunk, half), ls.at[hop - 1, half], lr.at[hop - 1, half], dp=place.ring(-1)
        )

    def begin(half):
        right(own(half), place.d, 1, half).start()
        left(own(1 - half), place.d, 1, 1 - half).start()

    def start():
        begin(0)
        begin(1)

    def forward(hop):
        before, after = place.ring(-hop), place.ring(hop)
        full = hop < hops - 1
        right(out(before, 0), before, hop, 0).wait_recv()
        right(out(before, 0), before, hop + 1, 0).start()
        left(out(after, 1), after, hop, 1).wait_recv()
        left(out(after, 1), after, hop + 1, 1).start()
        if full:
            right(out(before, 1), before, hop, 1).wait_recv()
            left(out(after, 0), after, hop, 0).wait_recv()
            right(out(before, 1), before, hop + 1, 1).start()
            left(out(after, 0), after, hop + 1, 0).start()

    def near():
        before, after = place.ring(1 - hops), place.ring(hops - 1)
        right(out(before, 1), before, hops - 1, 1).wait_recv()
        left(out(after, 0), after, hops - 1, 0).wait_recv()

    def finish(waited=False):
        if not waited:
            near()
        right(out(place.d, 0), place.ring(-hops), hops, 0).wait_recv()
        left(out(place.d, 1), place.ring(hops), hops, 1).wait_recv()
        for hop in range(1, hops + 1):
            for half in range(2):
                if hop < hops or half == 0:
                    right(out(place.d, half), place.d, hop, half).wait_send()
                if hop < hops or half == 1:
                    left(out(place.d, half), place.d, hop, half).wait_send()

    return start, forward, finish, near, begin


def ring_scatter(place, part, put, rbuf, lbuf, rout, lout, rs, rr, ls, lr):
    hops = place.hops

    def wide(ref):
        return ref[...].astype(jnp.float32)

    def right(src, hop, half):
        return remote(
            src,
            rbuf.at[hop - 1, half],
            rs.at[hop - 1, half],
            rr.at[hop - 1, half],
            dp=place.ring(1),
        )

    def left(src, hop, half):
        return remote(
            src,
            lbuf.at[hop - 1, half],
            ls.at[hop - 1, half],
            lr.at[hop - 1, half],
            dp=place.ring(-1),
        )

    def start_far():
        right(part(place.ring(hops), 0), hops, 0).start()
        left(part(place.ring(-hops), 1), hops, 1).start()

    def start_next():
        right(part(place.ring(hops - 1), 1), hops - 1, 1).start()
        left(part(place.ring(1 - hops), 0), hops - 1, 0).start()

    def start():
        start_far()
        start_next()

    def forward(hop):
        for first in range(2 if hop < hops - 1 else 1):
            half = first
            right(rbuf.at[hop, half], hop + 1, half).wait_recv()
            total = wide(part(place.ring(hop), half)) + wide(rbuf.at[hop, half])
            rout[hop - 1, half] = total.astype(jnp.bfloat16)
            right(rout.at[hop - 1, half], hop, half).start()
            half = 1 - first
            left(lbuf.at[hop, half], hop + 1, half).wait_recv()
            total = wide(part(place.ring(-hop), half)) + wide(lbuf.at[hop, half])
            lout[hop - 1, half] = total.astype(jnp.bfloat16)
            left(lout.at[hop - 1, half], hop, half).start()

    def finish():
        for half in range(2):
            right(rbuf.at[0, half], 1, half).wait_recv()
            left(lbuf.at[0, half], 1, half).wait_recv()
            put(
                half,
                wide(part(place.d, half)) + wide(rbuf.at[0, half]) + wide(lbuf.at[0, half]),
            )
        for hop in range(1, hops + 1):
            for half in range(2):
                if hop < hops or half == 0:
                    right(rbuf.at[0, half], hop, half).wait_send()
                if hop < hops or half == 1:
                    left(lbuf.at[0, half], hop, half).wait_send()

    return start, forward, finish, start_far, start_next


class RingGather:
    def __init__(self, x, dps, groups, late=False):
        self.late = late
        rows, width = x.shape
        shape = (2, rows // 2, width)
        self.inputs, self.in_specs = [x.reshape(shape)], [VM]
        self.outs, self.out_specs = [jax.ShapeDtypeStruct((dps,) + shape, x.dtype)], [ANY]
        self.scratch = [DMA] + ring_sems(dps // 2)
        self.result = lambda out: out.reshape(dps * rows, width)

    def bind(self, place, x_ref, out_ref, own_sem, *sems):
        own = pltpu.make_async_copy(x_ref, out_ref.at[place.d], own_sem)
        ring = ring_gather(
            place, lambda half: x_ref.at[half], lambda chunk, half: out_ref.at[chunk, half], *sems
        )

        def start():
            if not self.late:
                ring[0]()
            own.start()

        def finish():
            own.wait()
            ring[2]()

        first = 3 if self.late else -1
        ticks = {
            2 * hop + first: functools.partial(ring[1], hop) for hop in range(1, place.hops)
        }
        if self.late:
            ticks[1] = functools.partial(ring[4], 0)
            ticks[3] = functools.partial(ring[4], 1)
        return start, ticks, finish


class RingScatter:
    def __init__(self, partial, dps, groups, late=False):
        self.late = late
        total, width = partial.shape
        rows, hops = total // dps, dps // 2
        shape = (2, rows // 2, width)
        self.inputs, self.in_specs = [partial.reshape((dps,) + shape)], [VM]
        self.outs, self.out_specs = [jax.ShapeDtypeStruct(shape, jnp.float32)], [VM]
        self.scratch = (
            [pltpu.VMEM((hops,) + shape, jnp.bfloat16)] * 2
            + [pltpu.VMEM((hops - 1,) + shape, jnp.bfloat16)] * 2
            + ring_sems(hops)
        )
        self.result = lambda out: out.reshape(rows, width)

    def bind(self, place, p_ref, out_ref, *scratch):
        def put(half, value):
            out_ref[half] = value

        ring = ring_scatter(place, lambda chunk, half: p_ref.at[chunk, half], put, *scratch)
        first = 1 if self.late else -1
        ticks = {
            2 * (place.hops - hop) + first: functools.partial(ring[1], hop)
            for hop in range(1, place.hops)
        }
        if self.late:
            ticks[1] = ring[0]
            return lambda: None, ticks, ring[2]
        return ring[0], ticks, ring[2]


class Columns:
    def __init__(self, blocks, dps, groups):
        _, rows, width = blocks.shape
        self.inputs, self.in_specs = [blocks], [VM]
        self.outs = [jax.ShapeDtypeStruct((dps, groups, rows, width), blocks.dtype)]
        self.out_specs = [ANY]
        self.scratch = [
            pltpu.VMEM((groups, rows, width), blocks.dtype),
            DMA((2,)),
            DMA((groups,)),
            DMA((groups,)),
        ] + ring_sems(dps // 2)
        self.result = lambda out: out.reshape(dps * groups * rows, width)

    def bind(self, place, x_ref, out_ref, landing, own_sem, sends, recvs, *sems):
        s, groups = place.s, place.groups
        half_of = groups // 2
        here = pltpu.make_async_copy(x_ref.at[s], landing.at[s], own_sem.at[0])
        own = pltpu.make_async_copy(landing, out_ref.at[place.d], own_sem.at[1])

        def swap(i):
            to = (s + i) % groups
            return remote(x_ref.at[to], landing.at[s], sends.at[i], recvs.at[i], seq=to)

        ring = ring_gather(
            place,
            lambda half: landing.at[pl.ds(half * half_of, half_of)],
            lambda chunk, half: out_ref.at[chunk, pl.ds(half * half_of, half_of)],
            *sems,
        )

        def start():
            here.start()
            for i in range(1, groups):
                swap(i).start()

        def middle():
            here.wait()
            for i in range(1, groups):
                swap(i).wait_recv()
            ring[0]()
            own.start()

        def finish():
            for i in range(1, groups):
                swap(i).wait_send()
            own.wait()
            ring[2]()

        ticks = {1 + 2 * hop: functools.partial(ring[1], hop) for hop in range(1, place.hops)}
        ticks[1] = middle
        return start, ticks, finish


class ColumnsBack:
    def __init__(self, partial, order, heads_width, copies, rows, dps, groups):
        width, hops = partial.shape[1], dps // 2
        shape = (groups, rows, width)
        halves = (2, groups // 2, rows, width)
        self.where = [order.index(g) for g in range(groups)]
        self.heads_width, self.copies = heads_width, copies
        joint = groups * heads_width + 2 * KV_HEADS * HEAD_DIM
        self.inputs, self.in_specs = [partial.reshape((dps,) + halves)], [VM]
        self.outs, self.out_specs = [jax.ShapeDtypeStruct((rows, joint), jnp.float32)], [VM]
        self.scratch = (
            [pltpu.VMEM(shape, jnp.bfloat16), pltpu.VMEM(halves, jnp.bfloat16)]
            + [DMA, DMA((groups,)), DMA((groups,))]
            + [pltpu.VMEM((hops,) + halves, jnp.bfloat16)] * 2
            + [pltpu.VMEM((hops - 1,) + halves, jnp.bfloat16)] * 2
            + ring_sems(hops)
        )
        self.result = lambda out: out

    def bind(self, place, p_ref, joint_ref, out_ref, total, own_sem, sends, recvs, *scratch):
        s, groups = place.s, place.groups
        half_of = groups // 2

        def put(half, value):
            total[half] = value.astype(jnp.bfloat16)

        ring = ring_scatter(place, lambda chunk, half: p_ref.at[chunk, half], put, *scratch)
        here = pltpu.make_async_copy(
            total.at[s // half_of, s % half_of], out_ref.at[s], own_sem
        )

        def swap(i):
            to = (s + i) % groups
            src = total.at[to // half_of, to % half_of]
            return remote(src, out_ref.at[s], sends.at[i], recvs.at[i], seq=to)

        def last():
            ring[2]()
            here.start()
            for i in range(1, groups):
                swap(i).start()

        def keys_values(head):
            first = self.where[head * self.copies]
            span = slice(self.heads_width, self.heads_width + 2 * HEAD_DIM)
            value = out_ref[first, :, span].astype(jnp.float32)
            for i in range(1, self.copies):
                value += out_ref[self.where[head * self.copies + i], :, span].astype(jnp.float32)
            return value

        def finish():
            here.wait()
            for i in range(1, groups):
                swap(i).wait_recv()
                swap(i).wait_send()
            heads = self.heads_width
            for g in range(groups):
                value = out_ref[self.where[g], :, :heads]
                joint_ref[:, g * heads : (g + 1) * heads] = value.astype(jnp.float32)
            for head in range(0, KV_HEADS, 2):
                even, odd = keys_values(head), keys_values(head + 1)
                lanes = lax.broadcasted_iota(jnp.int32, even.shape, 1)
                at = groups * heads + head * HEAD_DIM
                joint_ref[:, at : at + 2 * HEAD_DIM] = jnp.where(
                    lanes < HEAD_DIM, even, pltpu.roll(odd, HEAD_DIM, 1)
                )
                at += KV_HEADS * HEAD_DIM
                joint_ref[:, at : at + 2 * HEAD_DIM] = jnp.where(
                    lanes < HEAD_DIM, pltpu.roll(even, HEAD_DIM, 1), odd
                )

        ticks = {
            2 * (place.hops - hop) - 1: functools.partial(ring[1], hop)
            for hop in range(1, place.hops)
        }
        ticks[2 * place.hops - 1] = last
        return ring[0], ticks, finish


class Rows:
    def __init__(self, x, dps, groups):
        rows, width = x.shape
        shape = (2, rows // 2, width)
        self.inputs, self.in_specs = [x.reshape(shape)], [VM]
        self.outs, self.out_specs = [jax.ShapeDtypeStruct((dps,) + shape, x.dtype)], [ANY]
        self.scratch = [
            pltpu.VMEM((dps,) + shape, x.dtype),
            DMA((2,)),
            DMA((dps,)),
            DMA((dps,)),
        ] + ring_sems(dps // 2)
        self.result = lambda out: out.reshape(dps * rows, width)

    def bind(self, place, x_ref, out_ref, landing, own_sem, sends, recvs, *sems):
        s, dps = place.s, place.dps
        slot, base = s % dps, s // dps * dps
        first = pltpu.make_async_copy(x_ref, landing.at[place.d], own_sem.at[0])
        here = pltpu.make_async_copy(landing.at[slot], out_ref.at[slot], own_sem.at[1])
        ring = ring_gather(
            place, lambda half: x_ref.at[half], lambda chunk, half: landing.at[chunk, half], *sems
        )

        def swap(i):
            to = (slot + i) % dps
            return remote(landing.at[to], out_ref.at[slot], sends.at[i], recvs.at[i], seq=base + to)

        def start():
            ring[0]()
            first.start()

        def last():
            first.wait()
            ring[2]()
            here.start()
            for i in range(1, dps):
                swap(i).start()

        def finish():
            here.wait()
            for i in range(1, dps):
                swap(i).wait_recv()
                swap(i).wait_send()

        ticks = {2 * hop - 1: functools.partial(ring[1], hop) for hop in range(1, place.hops)}
        ticks[2 * place.hops - 1] = last
        return start, ticks, finish


class RowsBack:
    def __init__(self, partial, rows, dps, groups):
        width, hops = partial.shape[1], dps // 2
        shape = (2, rows // 2, width)
        self.inputs, self.in_specs = [partial.reshape((dps,) + shape)], [VM]
        self.outs, self.out_specs = [jax.ShapeDtypeStruct(shape, jnp.float32)], [VM]
        self.scratch = (
            [pltpu.VMEM((dps,) + shape, jnp.bfloat16), DMA, DMA((dps,)), DMA((dps,))]
            + [pltpu.VMEM((hops,) + shape, jnp.bfloat16)] * 2
            + [pltpu.VMEM((hops - 1,) + shape, jnp.bfloat16)] * 2
            + ring_sems(hops)
        )
        self.result = lambda out: out.reshape(rows, width)

    def bind(self, place, p_ref, out_ref, landing, own_sem, sends, recvs, *scratch):
        s, dps = place.s, place.dps
        slot, base = s % dps, s // dps * dps
        here = pltpu.make_async_copy(p_ref.at[slot], landing.at[slot], own_sem)

        def swap(i):
            to = (slot + i) % dps
            return remote(p_ref.at[to], landing.at[slot], sends.at[i], recvs.at[i], seq=base + to)

        def put(half, value):
            out_ref[half] = value

        ring = ring_scatter(place, lambda chunk, half: landing.at[chunk, half], put, *scratch)

        def start():
            here.start()
            for i in range(1, dps):
                swap(i).start()

        def middle():
            here.wait()
            for i in range(1, dps):
                swap(i).wait_recv()
            ring[0]()

        def finish():
            for i in range(1, dps):
                swap(i).wait_send()
            ring[2]()

        ticks = {
            2 * (place.hops - hop) + 2: functools.partial(ring[1], hop)
            for hop in range(1, place.hops)
        }
        ticks[2] = middle
        return start, ticks, finish


class Spread:
    def __init__(self, tiles, total, dps, groups):
        count, shape = dps * groups, tiles.shape[-2:]
        self.total = total
        self.inputs, self.in_specs = [tiles], [VM]
        out = shape if total else (count,) + shape
        self.outs, self.out_specs = [jax.ShapeDtypeStruct(out, jnp.float32)], [VM]
        self.scratch = [pltpu.VMEM((count,) + shape, jnp.float32), DMA((count,)), DMA((count,))]
        self.result = lambda out: out

    def bind(self, place, x_ref, out_ref, landing, sends, recvs):
        count = place.dps * place.groups
        me = place.d * place.groups + place.s

        def copy(i):
            other = (me + i) % count
            return remote(
                x_ref.at[other] if self.total else x_ref,
                landing.at[me],
                sends.at[i],
                recvs.at[i],
                dp=other // place.groups,
                seq=other % place.groups,
            )

        def start():
            def each(i, _):
                copy(i).start()
                return 0

            lax.fori_loop(1, count, each, 0)

        def finish():
            def each(i, _):
                copy(i).wait_recv()
                copy(i).wait_send()
                return 0

            lax.fori_loop(1, count, each, 0)
            landing[me] = x_ref[me] if self.total else x_ref[...]
            out_ref[...] = jnp.sum(landing[...], axis=0) if self.total else landing[...]

        return start, {}, finish


TILE = 256


class FeedForward:
    def __init__(self, normed, down, gate, up, grad_all, dps, groups):
        rows, width = normed.shape
        shape, chips = (SUB, rows // SUB, width), groups // 2
        held = gate.shape[0]
        ring = (2, down.shape[0] // 2, width)
        pair = 2 * rows
        self.inputs = [
            normed.reshape(shape),
            down.reshape(ring),
            gate,
            up,
            grad_all.reshape(chips, pair, width),
        ]
        self.in_specs = [VM, VM, ANY, ANY, ANY]
        act = jax.ShapeDtypeStruct((chips, pair, held), jnp.bfloat16)
        self.outs = [
            jax.ShapeDtypeStruct((groups,) + shape, jnp.bfloat16),
            jax.ShapeDtypeStruct((dps,) + ring, jnp.bfloat16),
            act,
            act,
            act,
        ]
        self.out_specs = [VM] * 5
        self.scratch = [
            pltpu.VMEM((held, width), jnp.bfloat16),
            pltpu.VMEM((held, width), jnp.bfloat16),
            pltpu.VMEM((chips, pair, width), jnp.bfloat16),
            pltpu.VMEM((chips, pair, held), jnp.float32),
            pltpu.VMEM((chips, pair, held), jnp.float32),
            pltpu.VMEM((dps, chips, pair, held // dps), jnp.float32),
            DMA((4,)),
            DMA,
        ]
        self.scratch += [DMA((chips, SUB))] * 6 + ring_sems(dps // 2)
        self.result = lambda hn, full, *acts: (
            hn.reshape(groups * rows, width),
            full.reshape(held, width),
            *[one.reshape(groups * rows, held) for one in acts],
        )

    def bind(self, place, x_ref, shard, gate_at, up_at, grad_at, *refs):
        hn, full, inner, dgate, dup, gate_w, up_w, grads, slope, silu, dinner = refs[:11]
        loads, own_line = refs[11:13]
        line_sems, ring_refs = refs[13:19], refs[19:]
        chip, chips = place.chip, place.chips
        pair, held = inner.shape[1:]
        width = gate_w.shape[1]
        own, start_line, step, arrived, sent = line_gather(place, x_ref, hn, own_line, *line_sems)
        ring = ring_gather(
            place,
            lambda half: shard.at[half],
            lambda chunk, half: full.at[chunk, half],
            *ring_refs,
        )
        copies = [
            pltpu.make_async_copy(gate_at, gate_w, loads.at[0]),
            pltpu.make_async_copy(up_at, up_w, loads.at[1]),
            pltpu.make_async_copy(grad_at, grads, loads.at[2]),
            pltpu.make_async_copy(shard, full.at[place.d], loads.at[3]),
        ]
        wide = 512 if held % 512 == 0 else held

        def start():
            start_line()
            ring[0]()
            for one in copies:
                one.start()

        def forward(at):
            rows = hn[pl.ds(2 * at, 2)].reshape(pair, width)
            for first in range(0, held, wide):
                span = slice(first, first + wide)
                gate = lax.dot_general(
                    rows, gate_w[span, :], contract_cols, preferred_element_type=jnp.float32
                )
                upward = lax.dot_general(
                    rows, up_w[span, :], contract_cols, preferred_element_type=jnp.float32
                )
                sigmoid = jax.nn.sigmoid(gate)
                passed = gate * sigmoid
                inner[at, :, span] = (passed * upward).astype(jnp.bfloat16)
                silu[at, :, span] = passed
                slope[at, :, span] = upward * sigmoid * (1.0 + gate * (1.0 - sigmoid))

        def when_there(at, there):
            @pl.when(there)
            def _():
                arrived(at)
                forward(at)

        chunk = held // place.dps
        early = chunk % 128 == 0

        def back(owner, part):
            def each(at, _):
                dinner[owner, at] = lax.dot_general(
                    grads[at], part, contract_cols, preferred_element_type=jnp.float32
                )
                return 0

            lax.fori_loop(0, chips, each, 0)

        def back_from(owner):
            back(owner, full[owner].reshape(chunk, width))

        def tick(hop, half):
            step(hop, half)
            if early and hop == 1 and half == 1:
                copies[2].wait()
                back(place.d, shard[...].reshape(chunk, width))
            if hop == 1 and half == 0:
                own.wait()
                copies[0].wait()
                copies[1].wait()
                arrived(chip)
                forward(chip)
            if hop > 1 and half == 0:
                when_there(chip - hop + 1, chip - hop + 1 >= 0)
            if hop > 1 and half == SUB - 1:
                when_there(chip + hop - 1, chip + hop - 1 < chips)

        def finish():
            last = chips - 1
            when_there(chip - last, chip - last >= 0)
            when_there(chip + last, chip + last < chips)
            copies[3].wait()
            if not early:
                copies[2].wait()
                ring[2]()
                last_all()
            else:
                ring[2](True)
                if place.hops > 2:
                    back_between()
                back_from(place.ring(place.hops))

                def each(at, _):
                    for q in range(place.dps):
                        span = slice(q * chunk, (q + 1) * chunk)
                        grad = dinner[q, at]
                        dgate[at, :, span] = (grad * slope[at, :, span]).astype(jnp.bfloat16)
                        dup[at, :, span] = (grad * silu[at, :, span]).astype(jnp.bfloat16)
                    return 0

                lax.fori_loop(0, chips, each, 0)
            sent()

        def back_between():
            for hop in range(1, place.hops):
                back_from(place.ring(hop))
                back_from(place.ring(-hop))

        def last_all():
            def each(at, _):
                rows = grads[at]
                for first in range(0, held, wide):
                    span = slice(first, first + wide)
                    part = full[first // chunk : (first + wide) // chunk].reshape(wide, width)
                    grad = lax.dot_general(
                        rows, part, contract_cols, preferred_element_type=jnp.float32
                    )
                    dgate[at, :, span] = (grad * slope[at, :, span]).astype(jnp.bfloat16)
                    dup[at, :, span] = (grad * silu[at, :, span]).astype(jnp.bfloat16)
                return 0

            lax.fori_loop(0, chips, each, 0)

        ticks = {
            (hop - 1) * SUB + half: functools.partial(tick, hop, half)
            for hop in range(1, chips)
            for half in range(SUB)
        }

        def with_ring(tick, hop):
            ticks[tick]()
            ring[1](hop)

        def with_near(tick):
            ticks[tick]()
            ring[3]()
            if place.hops == 2:
                back_between()

        merged = dict(ticks)
        for hop in range(1, place.hops):
            merged[2 * hop - 1] = functools.partial(with_ring, 2 * hop - 1, hop)
        if early:
            merged[2 * place.hops - 1] = functools.partial(with_near, 2 * place.hops - 1)
        return start, merged, finish


class FeedBack:
    def __init__(self, inner, dgate, dup, gate, up, down, normed, grads, dps, groups):
        length, held = inner.shape
        width, chips = normed.shape[1], groups // 2
        rows = length // groups
        shape = (SUB, rows // SUB, width)
        owned = (2, held // dps // 2, width)
        hops = dps // 2
        tile = (2, SUB, rows // SUB, width)
        self.inputs = [inner, dgate, dup, gate, up, down, normed, grads]
        self.in_specs = [ANY] * 8
        self.outs = [
            jax.ShapeDtypeStruct(shape, jnp.float32),
            jax.ShapeDtypeStruct(owned, jnp.float32),
            jax.ShapeDtypeStruct((held // TILE,) + tile, jnp.bfloat16),
            jax.ShapeDtypeStruct((held // TILE,) + tile, jnp.bfloat16),
            jax.ShapeDtypeStruct((chips,) + tile, jnp.bfloat16),
        ]
        self.out_specs = [VM, VM, ANY, ANY, ANY]
        act = pltpu.VMEM((length, held), jnp.bfloat16)
        weight = pltpu.VMEM((held, width), jnp.bfloat16)
        tokens = pltpu.VMEM((length, width), jnp.bfloat16)
        self.scratch = [act] * 3 + [weight] * 3 + [tokens] * 2
        self.scratch += [
            pltpu.VMEM((groups,) + shape, jnp.bfloat16),
            pltpu.VMEM((dps,) + owned, jnp.bfloat16),
            pltpu.VMEM((2,) + tile, jnp.bfloat16),
            DMA((8,)),
            DMA((2,)),
        ]
        self.scratch += line_scatter_scratch(chips, shape)
        self.scratch += (
            [pltpu.VMEM((hops,) + owned, jnp.bfloat16)] * 2
            + [pltpu.VMEM((hops - 1,) + owned, jnp.bfloat16)] * 2
            + ring_sems(hops)
        )
        self.result = lambda total, mine, gate_term, up_term, out: (
            total.reshape(rows, width),
            mine.reshape(held // dps, width),
            gate_term.reshape(held, width),
            up_term.reshape(held, width),
            out.reshape(length, width),
        )

    def bind(self, place, *refs):
        sources, refs = refs[:8], refs[8:]
        total_ref, own_ref, gate_out, up_out, result_out = refs[:5]
        inner, dgate, dup, gate, up, down, normed, grads = refs[5:13]
        p_ref, term, stage, loads, stage_sem = refs[13:18]
        line_refs, ring_refs = refs[18:27], refs[27:]
        chip, chips, hops = place.chip, place.chips, place.hops
        held, width = gate.shape
        pair = inner.shape[0] // chips
        chunk = held // place.dps
        wide = 1024 if width % 1024 == 0 else width
        send, step, finish_line = line_scatter(place, p_ref, total_ref, *line_refs)

        def put(half, value):
            own_ref[half] = value

        ring = ring_scatter(place, lambda at, half: term.at[at, half], put, *ring_refs)
        targets = [inner, dgate, dup, gate, up, down, normed, grads]
        copies = [
            pltpu.make_async_copy(source, target, loads.at[i])
            for i, (source, target) in enumerate(zip(sources, targets))
        ]

        def start():
            for i in (0, 7, 1, 3, 2, 4, 6, 5):
                copies[i].start()

        def rows_of(ref, at):
            return ref[pl.ds(pl.multiple_of(at * pair, pair), pair), :]

        def partial(at):
            left, right = rows_of(dgate, at), rows_of(dup, at)
            for first in range(0, width, wide):
                span = slice(first, first + wide)
                value = jnp.dot(left, gate[:, span], preferred_element_type=jnp.float32)
                value += jnp.dot(right, up[:, span], preferred_element_type=jnp.float32)
                p_ref[pl.ds(2 * at, 2), :, :, span] = value.astype(jnp.bfloat16).reshape(
                    p_ref[pl.ds(2 * at, 2), :, :, span].shape
                )
            send(at)

        def term_rows(ref, other, start, count, span):
            return lax.dot_general(
                ref[:, pl.ds(start, count)],
                other[:, span],
                contract_rows,
                preferred_element_type=jnp.float32,
            ).astype(jnp.bfloat16)

        def down_tile(at):
            if chunk % 128 == 0:
                for first in range(0, width, wide):
                    span = slice(first, first + wide)
                    value = term_rows(inner, grads, pl.multiple_of(at * chunk, chunk), chunk, span)
                    term[at, :, :, span] = value.reshape(2, chunk // 2, wide)

        def down_all():
            if chunk % 128 != 0:
                for row in range(0, held, TILE):
                    for first in range(0, width, wide):
                        span = slice(first, first + wide)
                        value = term_rows(inner, grads, row, TILE, span)
                        term[row // chunk : (row + TILE) // chunk, :, :, span] = value.reshape(
                            TILE // chunk, 2, chunk // 2, wide
                        )

        jobs = []

        def first_job():
            copies[0].wait()
            copies[7].wait()
            down_all()
            down_tile(place.ring(hops))
            ring[3]()

        def next_job(hop):
            down_tile(place.ring(hop))
            down_tile(place.ring(-hop))
            if hop == hops - 1:
                ring[4]()

        for hop in range(hops - 1, 0, -1):
            jobs.append(functools.partial(next_job, hop))
            jobs.append(functools.partial(ring[1], hop))
        jobs.append(lambda: down_tile(place.d))

        count = [0]
        waits = []

        def staged(value_of, target):
            slot = count[0] % 2
            if count[0] >= 2:
                waits[count[0] - 2].wait()
            value_of(stage.at[slot])
            copy = pltpu.make_async_copy(stage.at[slot], target, stage_sem.at[slot])
            copy.start()
            waits.append(copy)
            count[0] += 1

        def weight_tile(ref, row, out):
            def fill(slot):
                for first in range(0, width, wide):
                    span = slice(first, first + wide)
                    value = term_rows(ref, normed, row, TILE, span)
                    slot[:, :, :, span] = value.reshape(slot.shape[:3] + (wide,))

            staged(fill, out.at[row // TILE])

        def result_tile(at):
            def fill(slot):
                left = rows_of(inner, at)
                for first in range(0, width, wide):
                    span = slice(first, first + wide)
                    value = jnp.dot(left, down[:, span], preferred_element_type=jnp.float32)
                    slot[:, :, :, span] = value.astype(jnp.bfloat16).reshape(
                        slot.shape[:3] + (wide,)
                    )

            staged(fill, result_out.at[at])

        def sequence():
            first_job()
            for i in (1, 3, 2, 4):
                copies[i].wait()
            tiles = [
                functools.partial(weight_tile, ref, row, out)
                for ref, out in ((dgate, gate_out), (dup, up_out))
                for row in range(0, held, TILE)
            ]
            tiles += [functools.partial(result_tile, at) for at in range(chips)]
            done = [0]

            def fill(most):
                for _ in range(most):
                    if tiles:
                        if done[0] == 0:
                            copies[6].wait()
                        if done[0] == 2 * (held // TILE):
                            copies[5].wait()
                        done[0] += 1
                        tiles.pop(0)()

            for wave in range(chips - 1):
                high = chips - 1 - wave
                ups = (high > chip).astype(jnp.int32)
                downs = (wave < chip).astype(jnp.int32)

                def each(i, _, high=high, wave=wave, ups=ups):
                    partial(jnp.where(i < ups, high, wave))
                    return 0

                lax.fori_loop(0, ups + downs, each, 0)
                fill(1)
                step(wave, 0)
                if wave == 0:
                    step(wave, 1)
                    jobs.pop(0)()
                else:
                    fill(1)
                    step(wave, 1)
                    if jobs:
                        jobs.pop(0)()
            partial(chip)
            for job in jobs:
                job()
            fill(len(tiles))

        def finish():
            ring[2]()
            finish_line()
            for copy in waits[-2:]:
                copy.wait()

        return start, {0: sequence}, finish


def move(parts, dps, groups, number, greet=greet_near):
    def kernel(*refs):
        place = Place(dps, groups)
        at = [
            0,
            sum(len(part.inputs) for part in parts),
            sum(len(part.inputs) + len(part.outs) for part in parts),
        ]
        bound = []
        for part in parts:
            mine = []
            for kind, length in enumerate((len(part.inputs), len(part.outs), len(part.scratch))):
                mine += refs[at[kind] : at[kind] + length]
                at[kind] += length
            bound.append(part.bind(place, *mine))
        greet(place)
        for start, _, _ in bound:
            start()
        for tick in range(1 + max([0] + [max(list(ticks) + [0]) for _, ticks, _ in bound])):
            for _, ticks, _ in bound:
                if tick in ticks:
                    ticks[tick]()
        for _, _, finish in bound:
            finish()

    outs = pl.pallas_call(
        kernel,
        out_shape=[out for part in parts for out in part.outs],
        in_specs=[spec for part in parts for spec in part.in_specs],
        out_specs=[spec for part in parts for spec in part.out_specs],
        scratch_shapes=[one for part in parts for one in part.scratch],
        compiler_params=pltpu.CompilerParams(
            collective_id=number, has_side_effects=True, vmem_limit_bytes=63 << 20
        ),
        cost_estimate=pl.CostEstimate(flops=0, bytes_accessed=120_000_000, transcendentals=0),
        name=f"move_{number}",
    )(*[x for part in parts for x in part.inputs])
    results, at = [], 0
    for part in parts:
        results.append(part.result(*outs[at : at + len(part.outs)]))
        at += len(part.outs)
    return results


def norm_factor(values):
    return lax.rsqrt(jnp.mean(values * values, axis=-1, keepdims=True) + epsilon)


def norm_grad(values, factor, gain, gradient):
    weighted = gradient * gain
    inner_mean = jnp.mean(weighted * values, axis=-1, keepdims=True)
    return factor * weighted - values * (factor * factor * factor) * inner_mean


def rope_tables(positions, head_width):
    half_width = head_width // 2
    frequency = rope_base ** (-2.0 * jnp.arange(half_width, dtype=jnp.float32) / head_width)
    angles = positions.astype(jnp.float32)[:, None] * frequency[None, :]
    return (jnp.cos(angles)[:, None, :], jnp.sin(angles)[:, None, :])


def rotate(values, cosine_table, sine_table):
    half_width = values.shape[-1] // 2
    first_half = values[..., :half_width]
    second_half = values[..., half_width:]
    return jnp.concatenate(
        [
            first_half * cosine_table - second_half * sine_table,
            second_half * cosine_table + first_half * sine_table,
        ],
        axis=-1,
    )


def block_scores(query_block, key_heads, lower, upper, score_scale):
    scores = (
        jnp.einsum(
            "qhd,kd->hqk", query_block, key_heads[:upper], preferred_element_type=jnp.float32
        )
        * score_scale
    )
    rows_at = lower + jnp.arange(query_block.shape[0], dtype=jnp.int32)
    cols_at = jnp.arange(upper, dtype=jnp.int32)
    allowed = (cols_at[None, :] <= rows_at[:, None])[None]
    return jnp.where(allowed, scores, masked_value)


def per_device(
    tokens,
    qkv_weight,
    out_weight,
    gate_weight,
    up_weight,
    down_weight,
    attn_gain,
    mlp_gain,
    cotangent,
):
    groups = lax.axis_size("seq")
    dps = lax.axis_size("dp")
    tok_rows = tokens.shape[1]
    model_width = tokens.shape[2]
    weight_rows = qkv_weight.shape[0]
    seq_len = tok_rows * groups
    local_heads = HEADS // groups
    local_width = local_heads * HEAD_DIM
    kv_copies = groups // KV_HEADS
    score_scale = HEAD_DIM ** (-0.5)
    block_rows = min(512, seq_len)
    block_count = seq_len // block_rows
    fold = groups // dps
    order = [(at % dps) * fold + at // dps for at in range(groups)]

    q_part = qkv_weight[:, :model_width].reshape(weight_rows, groups, local_width)
    k_part = qkv_weight[:, model_width : model_width + KV_HEADS * HEAD_DIM]
    v_part = qkv_weight[:, model_width + KV_HEADS * HEAD_DIM :]
    k_part = k_part.reshape(weight_rows, KV_HEADS, HEAD_DIM)
    v_part = v_part.reshape(weight_rows, KV_HEADS, HEAD_DIM)
    columns = jnp.stack(
        [
            jnp.concatenate(
                [q_part[:, g], k_part[:, g // kv_copies], v_part[:, g // kv_copies]], axis=1
            )
            for g in order
        ]
    )
    gain_width = attn_gain.shape[0]
    tile = jnp.zeros((8, 128), jnp.float32)
    tile = tile.at[0, :gain_width].set(attn_gain.astype(jnp.float32))
    tile = tile.at[1, :gain_width].set(mlp_gain.astype(jnp.float32))
    qkv_local, out_rows, normed_all, gate_part, gains = move(
        [
            Columns(columns, dps, groups),
            Rows(out_weight, dps, groups),
            LineGather(tokens[0], dps, groups, normed=True),
            RingGather(gate_weight, dps, groups, late=True),
            Spread(tile, False, dps, groups),
        ],
        dps,
        groups,
        1,
        greet_all,
    )
    gain_one = gains[:, 0, :gain_width].reshape(model_width)
    gain_two = gains[:, 1, :gain_width].reshape(model_width)

    x_rows = tokens[0].astype(jnp.float32)
    factor_one = norm_factor(x_rows)
    qkv_gained = (qkv_local.astype(jnp.float32) * gain_one[:, None]).astype(jnp.bfloat16)
    grad_low = cotangent[0]
    grad_low, _ = lax.optimization_barrier((grad_low, gains))
    grad_all = lax.all_gather(grad_low, "seq", axis=0, tiled=True)

    mixed = jnp.dot(normed_all, qkv_gained, preferred_element_type=jnp.float32)
    cosine_table, sine_table = rope_tables(jnp.arange(seq_len, dtype=jnp.int32), HEAD_DIM)
    query_heads = rotate(
        mixed[:, :local_width].reshape(seq_len, local_heads, HEAD_DIM), cosine_table, sine_table
    ).astype(jnp.bfloat16)
    key_heads = rotate(
        mixed[:, None, local_width : local_width + HEAD_DIM], cosine_table, sine_table
    ).astype(jnp.bfloat16)[:, 0]
    value_heads = mixed[:, local_width + HEAD_DIM :].astype(jnp.bfloat16)
    outputs = []
    log_sums = []
    for block in range(block_count):
        lower = block * block_rows
        upper = lower + block_rows
        scores = block_scores(query_heads[lower:upper], key_heads, lower, upper, score_scale)
        highest = jnp.max(scores, axis=-1, keepdims=True)
        log_sum = highest + jnp.log(jnp.sum(jnp.exp(scores - highest), axis=-1, keepdims=True))
        probs = jnp.exp(scores - log_sum).astype(jnp.bfloat16)
        attended = jnp.einsum(
            "hqk,kd->qhd", probs, value_heads[:upper], preferred_element_type=jnp.float32
        )
        outputs.append(attended.astype(jnp.bfloat16))
        log_sums.append(log_sum)
    attended = jnp.concatenate(outputs, axis=0).reshape(seq_len, local_width)
    partial = jnp.dot(attended, out_rows, preferred_element_type=jnp.float32)
    summed, up_part = move(
        [
            LineScatter(partial.astype(jnp.bfloat16), dps, groups),
            RingGather(up_weight, dps, groups),
        ],
        dps,
        groups,
        2,
    )
    hidden = x_rows + summed
    factor_two = norm_factor(hidden)
    normed_two = (hidden * factor_two * gain_two).astype(jnp.bfloat16)
    ((hn_all, down_part, inner, grad_gate, grad_upward),) = move(
        [FeedForward(normed_two, down_weight, gate_part, up_part, grad_all, dps, groups)],
        dps,
        groups,
        3,
    )
    ((grad_normed, down_owned, gate_term, up_term, result),) = move(
        [
            FeedBack(
                inner,
                grad_gate,
                grad_upward,
                gate_part,
                up_part,
                down_part,
                hn_all,
                grad_all,
                dps,
                groups,
            )
        ],
        dps,
        groups,
        4,
    )
    gain_two_term = jnp.sum(grad_normed * hidden * factor_two, axis=0)
    grad_hidden = grad_low.astype(jnp.float32) + norm_grad(
        hidden, factor_two, gain_two, grad_normed
    )
    grad_branch, gate_owned = move(
        [
            LineGather(grad_hidden.astype(jnp.bfloat16), dps, groups),
            RingScatter(gate_term, dps, groups),
        ],
        dps,
        groups,
        5,
    )
    result, grad_branch = lax.optimization_barrier((result, grad_branch))
    mlp_result = lax.psum_scatter(result, "seq", scatter_dimension=0, tiled=True)
    block_out = (hidden + mlp_result.astype(jnp.float32)).astype(jnp.bfloat16)[None]
    out_term = lax.dot_general(
        attended, grad_branch, contract_rows, preferred_element_type=jnp.float32
    ).astype(jnp.bfloat16)
    grad_heads = (
        lax.dot_general(grad_branch, out_rows, contract_cols, preferred_element_type=jnp.float32)
        .astype(jnp.bfloat16)
        .reshape(seq_len, local_heads, HEAD_DIM)
    )
    grad_keys = jnp.zeros((seq_len, HEAD_DIM), jnp.float32)
    grad_values = jnp.zeros((seq_len, HEAD_DIM), jnp.float32)
    grad_queries = []
    for block in range(block_count):
        lower = block * block_rows
        upper = lower + block_rows
        query_block = query_heads[lower:upper]
        grad_block = grad_heads[lower:upper]
        scores = block_scores(query_block, key_heads, lower, upper, score_scale)
        probs = jnp.exp(scores - log_sums[block])
        probs_low = probs.astype(jnp.bfloat16)
        grad_probs = jnp.einsum(
            "qhd,kd->hqk", grad_block, value_heads[:upper], preferred_element_type=jnp.float32
        )
        row_delta = jnp.sum(probs * grad_probs, axis=-1, keepdims=True)
        grad_scores = (probs * (grad_probs - row_delta)).astype(jnp.bfloat16)
        grad_queries.append(
            jnp.einsum(
                "hqk,kd->qhd", grad_scores, key_heads[:upper], preferred_element_type=jnp.float32
            )
            * score_scale
        )
        grad_keys = grad_keys.at[:upper].add(
            jnp.einsum("hqk,qhd->kd", grad_scores, query_block, preferred_element_type=jnp.float32)
            * score_scale
        )
        grad_values = grad_values.at[:upper].add(
            jnp.einsum("hqk,qhd->kd", probs_low, grad_block, preferred_element_type=jnp.float32)
        )
    grad_q = rotate(jnp.concatenate(grad_queries, axis=0), cosine_table, -sine_table)
    grad_k = rotate(grad_keys[:, None], cosine_table, -sine_table)[:, 0]
    grad_mixed = jnp.concatenate(
        [grad_q.reshape(seq_len, local_width), grad_k, grad_values], axis=1
    ).astype(jnp.bfloat16)
    qkv_term = lax.dot_general(
        normed_all, grad_mixed, contract_rows, preferred_element_type=jnp.float32
    )
    partial = lax.dot_general(
        grad_mixed, qkv_local, contract_cols, preferred_element_type=jnp.float32
    )
    gain_one_term = jnp.sum(qkv_term * qkv_local.astype(jnp.float32), axis=1)
    qkv_term = (qkv_term * gain_one[:, None]).astype(jnp.bfloat16)
    terms = jnp.stack([gain_one_term, gain_two_term]).reshape(2, dps * groups, gain_width)
    terms = jnp.pad(terms.transpose(1, 0, 2), ((0, 0), (0, 6), (0, 128 - gain_width)))
    qkv_owned, grad_normed_one, out_owned, up_owned, gain_grads = move(
        [
            ColumnsBack(qkv_term, order, local_width, kv_copies, weight_rows, dps, groups),
            LineScatter(partial.astype(jnp.bfloat16), dps, groups),
            RowsBack(out_term, weight_rows, dps, groups),
            RingScatter(up_term, dps, groups, late=True),
            Spread(terms, True, dps, groups),
        ],
        dps,
        groups,
        6,
        greet_all,
    )
    grad_input = grad_hidden + norm_grad(x_rows, factor_one, gain_one, grad_normed_one)
    return (
        block_out,
        grad_input[None],
        qkv_owned,
        out_owned,
        gate_owned,
        up_owned,
        down_owned,
        gain_grads[0, :gain_width],
        gain_grads[1, :gain_width],
    )


def solution(mesh):
    rows = P(("dp", "seq"), None)
    tokens = P("dp", "seq", None)
    gains = P(("dp", "seq"))
    return jax.shard_map(
        per_device,
        mesh=mesh,
        in_specs=(tokens, rows, rows, rows, rows, rows, gains, gains, tokens),
        out_specs=(tokens, tokens, rows, rows, rows, rows, rows, gains, gains),
        check_vma=False,
    )
```

```python
import functools

import jax
import jax.numpy as jnp
from jax import lax
from jax.experimental import pallas as pl
from jax.experimental.pallas import tpu as pltpu
from jax.sharding import PartitionSpec as P

HEADS = 32
KV_HEADS = 8
HEAD_DIM = 64

MESH = pl.DeviceIdType.MESH
ANY = pl.BlockSpec(memory_space=pl.ANY)
VM = pl.BlockSpec(memory_space=pltpu.VMEM)
SUB = 2

epsilon = 1e-05
rope_base = 500000.0
masked_value = -1e30
contract_rows = (((0,), (0,)), ((), ()))
contract_cols = (((1,), (1,)), ((), ()))


class Place:
    def __init__(self, dps, groups):
        self.dps, self.groups, self.chips, self.hops = dps, groups, groups // 2, dps // 2
        self.d, self.s = lax.axis_index("dp"), lax.axis_index("seq")
        self.chip, self.core = self.s // 2, self.s % 2
        self.partner = 2 * self.chip + 1 - self.core
        row, side = self.d // 2, self.d % 2
        self.turn = side * (dps - 1 - row) + (1 - side) * row

    def ring(self, distance):
        at = (self.turn + distance + self.dps) % self.dps
        side = at // self.hops
        return (1 - side) * 2 * at + side * (2 * (self.dps - 1 - at) + 1)


def remote(src, dst, send, recv, **target):
    return pltpu.make_async_remote_copy(
        src_ref=src, dst_ref=dst, send_sem=send, recv_sem=recv, device_id=target, device_id_type=MESH
    )


def greet_near(place):
    barrier = pltpu.get_barrier_semaphore()

    def signal(**target):
        pl.semaphore_signal(barrier, inc=1, device_id=target, device_id_type=MESH)

    signal(seq=place.partner)
    signal(dp=place.ring(1))
    signal(dp=place.ring(-1))

    @pl.when(place.chip > 0)
    def _():
        signal(seq=place.s - 2)

    @pl.when(place.chip < place.chips - 1)
    def _():
        signal(seq=place.s + 2)

    ends = (place.chips - place.chip) // place.chips + (place.chip + 1) // place.chips
    pl.semaphore_wait(barrier, 5 - ends)


def greet_all(place):
    barrier = pltpu.get_barrier_semaphore()
    count = place.dps * place.groups
    me = place.d * place.groups + place.s

    def signal(i, _):
        other = (me + i) % count
        pl.semaphore_signal(
            barrier,
            inc=1,
            device_id={"dp": other // place.groups, "seq": other % place.groups},
            device_id_type=MESH,
        )
        return 0

    lax.fori_loop(1, count, signal, 0)
    pl.semaphore_wait(barrier, count - 1)


DMA = pltpu.SemaphoreType.DMA


def line_gather(place, x_ref, out_ref, own_sem, us, ur, ds, dr, ps, pr):
    s, chip, chips = place.s, place.chip, place.chips

    def copy(src, group, half, sends, recvs, at, target):
        return remote(
            src, out_ref.at[group, half], sends.at[at, half], recvs.at[at, half], seq=target
        )

    def up(src, group, hop, half):
        return copy(src, group, half, us, ur, hop, s + 2)

    def down(src, group, hop, half):
        return copy(src, group, half, ds, dr, hop, s - 2)

    def pair(src, group, half):
        return copy(src, group, half, ps, pr, group // 2, place.partner)

    own = pltpu.make_async_copy(x_ref, out_ref.at[s], own_sem)

    def start():
        own.start()
        for half in range(SUB):

            @pl.when(chip < chips - 1)
            def _():
                up(x_ref.at[half], s, 0, half).start()

            @pl.when(chip > 0)
            def _():
                down(x_ref.at[half], s, 0, half).start()

        for half in range(SUB):
            pair(x_ref.at[half], s, half).start()

    def step(hop, half):
        below, above = s - 2 * hop, s + 2 * hop

        @pl.when(chip - hop >= 0)
        def _():
            block = out_ref.at[below, half]
            up(block, below, hop - 1, half).wait_recv()

            @pl.when(chip < chips - 1)
            def _():
                up(block, below, hop, half).start()

            pair(block, below, half).start()

        @pl.when(chip + hop < chips)
        def _():
            block = out_ref.at[above, half]
            down(block, above, hop - 1, half).wait_recv()

            @pl.when(chip > 0)
            def _():
                down(block, above, hop, half).start()

            pair(block, above, half).start()

    def arrived(at):
        for half in range(SUB):
            group = 2 * at + 1 - place.core
            pair(out_ref.at[group, half], group, half).wait_recv()

    def sent():
        def each(i, _):
            k, half = i // SUB, i % SUB
            mine = 2 * k + place.core
            block = out_ref.at[mine, half]
            pair(block, mine, half).wait_send()

            @pl.when(jnp.logical_and(chip - k >= 0, chip < chips - 1))
            def _():
                up(block, mine, k, half).wait_send()

            @pl.when(jnp.logical_and(chip + k < chips, chip > 0))
            def _():
                down(block, mine, k, half).wait_send()

            return 0

        lax.fori_loop(0, chips * SUB, each, 0)

    return own, start, step, arrived, sent


class LineGather:
    def __init__(self, x, dps, groups, normed=False):
        rows, width = x.shape
        shape = (SUB, rows // SUB, width)
        self.normed = normed
        self.inputs, self.in_specs = [x.reshape(shape)], [VM]
        self.outs, self.out_specs = [jax.ShapeDtypeStruct((groups,) + shape, x.dtype)], [ANY]
        self.scratch = [DMA] + [DMA((groups // 2, SUB))] * 6
        if normed:
            self.scratch = [pltpu.VMEM(shape, x.dtype)] + self.scratch
        self.result = lambda out: out.reshape(groups * rows, width)

    def bind(self, place, x_ref, out_ref, *refs):
        if self.normed:
            source, x_ref, refs = x_ref, refs[0], refs[1:]
            many = 16 if x_ref.shape[1] % 16 == 0 else x_ref.shape[1]

            def norm(i, _):
                span = pl.ds(pl.multiple_of(i * many, many), many)
                for half in range(SUB):
                    values = source[half, span, :].astype(jnp.float32)
                    x_ref[half, span, :] = (values * norm_factor(values)).astype(x_ref.dtype)
                return 0

            lax.fori_loop(0, x_ref.shape[1] // many, norm, 0)
        own, start, step, arrived, sent = line_gather(place, x_ref, out_ref, *refs)

        def finish():
            own.wait()

            def each(at, _):
                arrived(at)
                return 0

            lax.fori_loop(0, place.chips, each, 0)
            sent()

        ticks = {
            (hop - 1) * SUB + half: functools.partial(step, hop, half)
            for hop in range(1, place.chips)
            for half in range(SUB)
        }
        return start, ticks, finish


def line_scatter(place, p_ref, out_ref, pairbuf, upbuf, downbuf, us, ur, ds, dr, ps, pr):
    s, chip, chips, core = place.s, place.chip, place.chips, place.core

    def copy(src, buffer, at, half, sends, recvs, target):
        return remote(src, buffer.at[at, half], sends.at[at, half], recvs.at[at, half], seq=target)

    def pair(at, half):
        src = p_ref.at[2 * at + 1 - core, half]
        return copy(src, pairbuf, at, half, ps, pr, place.partner)

    def up(at, half):
        return copy(upbuf.at[at, half], upbuf, at, half, us, ur, s + 2)

    def down(at, half):
        return copy(downbuf.at[at, half], downbuf, at, half, ds, dr, s - 2)

    def wide(ref, *at):
        return ref[at].astype(jnp.float32)

    def local(at, half):
        return wide(p_ref, 2 * at + core, half) + wide(pairbuf, at, half)

    def send(at):
        for half in range(SUB):
            pair(at, half).start()

    def step(wave, half):
        high, low = chips - 1 - wave + chip, wave - (chips - 1 - chip)

        @pl.when(chip <= wave)
        def _():
            pair(high, half).wait_recv()

            @pl.when(chip > 0)
            def _():
                up(high, half).wait_recv()
                total = local(high, half) + wide(upbuf, high, half)
                upbuf[high, half] = total.astype(jnp.bfloat16)

            @pl.when(chip == 0)
            def _():
                upbuf[high, half] = local(high, half).astype(jnp.bfloat16)

            up(high, half).start()

        @pl.when(low >= 0)
        def _():
            pair(low, half).wait_recv()

            @pl.when(chip < chips - 1)
            def _():
                down(low, half).wait_recv()
                total = local(low, half) + wide(downbuf, low, half)
                downbuf[low, half] = total.astype(jnp.bfloat16)

            @pl.when(chip == chips - 1)
            def _():
                downbuf[low, half] = local(low, half).astype(jnp.bfloat16)

            down(low, half).start()

    def finish():
        for half in range(SUB):
            pair(chip, half).wait_recv()
            out_ref[half] = local(chip, half)

            @pl.when(chip > 0)
            def _():
                up(chip, half).wait_recv()
                out_ref[half] += wide(upbuf, chip, half)

            @pl.when(chip < chips - 1)
            def _():
                down(chip, half).wait_recv()
                out_ref[half] += wide(downbuf, chip, half)

        def each(i, _):
            at, half = i // SUB, i % SUB
            pair(at, half).wait_send()

            @pl.when(at > chip)
            def _():
                up(at, half).wait_send()

            @pl.when(at < chip)
            def _():
                down(at, half).wait_send()

            return 0

        lax.fori_loop(0, chips * SUB, each, 0)

    return send, step, finish


def line_scatter_scratch(chips, shape):
    return [pltpu.VMEM((chips,) + shape, jnp.bfloat16)] * 3 + [DMA((chips, SUB))] * 6


class LineProduct:
    def __init__(self, left, right, dims, dps, groups):
        total, inner = left.shape
        width = right.shape[1 - dims[0][1][0]]
        rows, chips = total // groups, groups // 2
        shape = (SUB, rows // SUB, width)
        self.dims = dims
        self.inputs, self.in_specs = [left.reshape(chips, 2 * rows, inner), right], [VM, VM]
        self.outs, self.out_specs = [jax.ShapeDtypeStruct(shape, jnp.float32)], [VM]
        self.scratch = [pltpu.VMEM((groups,) + shape, jnp.bfloat16)]
        self.scratch += line_scatter_scratch(chips, shape)
        self.result = lambda out: out.reshape(rows, width)

    def bind(self, place, left, right, out_ref, p_ref, *refs):
        send, step, finish = line_scatter(place, p_ref, out_ref, *refs)
        chip, chips = place.chip, place.chips
        width = p_ref.shape[3]
        wide = 512 if width % 512 == 0 else width

        def partial(at):
            for first in range(0, width, wide):
                span = slice(first, first + wide)
                part = right[:, span] if self.dims[0][1][0] == 0 else right[span, :]
                value = lax.dot_general(
                    left[at], part, self.dims, preferred_element_type=jnp.float32
                )
                p_ref[pl.ds(2 * at, 2), :, :, span] = value.astype(jnp.bfloat16).reshape(
                    (2,) + p_ref.shape[1:3] + (wide,)
                )
            send(at)

        def partials(wave):
            if wave == chips - 1:
                partial(chip)
                return

            @pl.when(chips - 1 - wave > chip)
            def _():
                partial(chips - 1 - wave)

            @pl.when(wave < chip)
            def _():
                partial(wave)

        def tick(wave, half):
            step(wave, half)
            if half == SUB - 1:
                partials(wave + 1)

        ticks = {
            i: functools.partial(tick, i // SUB, i % SUB) for i in range((chips - 1) * SUB)
        }
        return lambda: partials(0), ticks, finish


def ring_sems(hops):
    return [DMA((hops, 2))] * 4


def ring_gather(place, own, out, rs, rr, ls, lr):
    hops = place.hops

    def right(src, chunk, hop, half):
        return remote(
            src, out(chunk, half), rs.at[hop - 1, half], rr.at[hop - 1, half], dp=place.ring(1)
        )

    def left(src, chunk, hop, half):
        return remote(
            src, out(chunk, half), ls.at[hop - 1, half], lr.at[hop - 1, half], dp=place.ring(-1)
        )

    def begin(half):
        right(own(half), place.d, 1, half).start()
        left(own(1 - half), place.d, 1, 1 - half).start()

    def start():
        begin(0)
        begin(1)

    def forward(hop):
        before, after = place.ring(-hop), place.ring(hop)
        full = hop < hops - 1
        right(out(before, 0), before, hop, 0).wait_recv()
        right(out(before, 0), before, hop + 1, 0).start()
        left(out(after, 1), after, hop, 1).wait_recv()
        left(out(after, 1), after, hop + 1, 1).start()
        if full:
            right(out(before, 1), before, hop, 1).wait_recv()
            left(out(after, 0), after, hop, 0).wait_recv()
            right(out(before, 1), before, hop + 1, 1).start()
            left(out(after, 0), after, hop + 1, 0).start()

    def near():
        before, after = place.ring(1 - hops), place.ring(hops - 1)
        right(out(before, 1), before, hops - 1, 1).wait_recv()
        left(out(after, 0), after, hops - 1, 0).wait_recv()

    def finish(waited=False):
        if not waited:
            near()
        right(out(place.d, 0), place.ring(-hops), hops, 0).wait_recv()
        left(out(place.d, 1), place.ring(hops), hops, 1).wait_recv()
        for hop in range(1, hops + 1):
            for half in range(2):
                if hop < hops or half == 0:
                    right(out(place.d, half), place.d, hop, half).wait_send()
                if hop < hops or half == 1:
                    left(out(place.d, half), place.d, hop, half).wait_send()

    return start, forward, finish, near, begin


def ring_scatter(place, part, put, rbuf, lbuf, rout, lout, rs, rr, ls, lr):
    hops = place.hops

    def wide(ref):
        return ref[...].astype(jnp.float32)

    def right(src, hop, half):
        return remote(
            src,
            rbuf.at[hop - 1, half],
            rs.at[hop - 1, half],
            rr.at[hop - 1, half],
            dp=place.ring(1),
        )

    def left(src, hop, half):
        return remote(
            src,
            lbuf.at[hop - 1, half],
            ls.at[hop - 1, half],
            lr.at[hop - 1, half],
            dp=place.ring(-1),
        )

    def start_far():
        right(part(place.ring(hops), 0), hops, 0).start()
        left(part(place.ring(-hops), 1), hops, 1).start()

    def start_next():
        right(part(place.ring(hops - 1), 1), hops - 1, 1).start()
        left(part(place.ring(1 - hops), 0), hops - 1, 0).start()

    def start():
        start_far()
        start_next()

    def forward(hop):
        for first in range(2 if hop < hops - 1 else 1):
            half = first
            right(rbuf.at[hop, half], hop + 1, half).wait_recv()
            total = wide(part(place.ring(hop), half)) + wide(rbuf.at[hop, half])
            rout[hop - 1, half] = total.astype(jnp.bfloat16)
            right(rout.at[hop - 1, half], hop, half).start()
            half = 1 - first
            left(lbuf.at[hop, half], hop + 1, half).wait_recv()
            total = wide(part(place.ring(-hop), half)) + wide(lbuf.at[hop, half])
            lout[hop - 1, half] = total.astype(jnp.bfloat16)
            left(lout.at[hop - 1, half], hop, half).start()

    def finish():
        for half in range(2):
            right(rbuf.at[0, half], 1, half).wait_recv()
            left(lbuf.at[0, half], 1, half).wait_recv()
            put(
                half,
                wide(part(place.d, half)) + wide(rbuf.at[0, half]) + wide(lbuf.at[0, half]),
            )
        for hop in range(1, hops + 1):
            for half in range(2):
                if hop < hops or half == 0:
                    right(rbuf.at[0, half], hop, half).wait_send()
                if hop < hops or half == 1:
                    left(lbuf.at[0, half], hop, half).wait_send()

    return start, forward, finish, start_far, start_next


class RingGather:
    def __init__(self, x, dps, groups, late=False):
        self.late = late
        rows, width = x.shape
        shape = (2, rows // 2, width)
        self.inputs, self.in_specs = [x.reshape(shape)], [VM]
        self.outs, self.out_specs = [jax.ShapeDtypeStruct((dps,) + shape, x.dtype)], [ANY]
        self.scratch = [DMA] + ring_sems(dps // 2)
        self.result = lambda out: out.reshape(dps * rows, width)

    def bind(self, place, x_ref, out_ref, own_sem, *sems):
        own = pltpu.make_async_copy(x_ref, out_ref.at[place.d], own_sem)
        ring = ring_gather(
            place, lambda half: x_ref.at[half], lambda chunk, half: out_ref.at[chunk, half], *sems
        )

        def start():
            ring[4](0)
            if not self.late:
                ring[4](1)
            own.start()

        def second():
            ring[4](1)
            ring[1](1)

        def finish():
            own.wait()
            ring[2]()

        ticks = {2 * hop - 1: functools.partial(ring[1], hop) for hop in range(1, place.hops)}
        if self.late:
            ticks[1] = second
        return start, ticks, finish


class RingScatter:
    def __init__(self, partial, dps, groups, late=False):
        self.late = late
        total, width = partial.shape
        rows, hops = total // dps, dps // 2
        shape = (2, rows // 2, width)
        self.inputs, self.in_specs = [partial.reshape((dps,) + shape)], [VM]
        self.outs, self.out_specs = [jax.ShapeDtypeStruct(shape, jnp.float32)], [VM]
        self.scratch = (
            [pltpu.VMEM((hops,) + shape, jnp.bfloat16)] * 2
            + [pltpu.VMEM((hops - 1,) + shape, jnp.bfloat16)] * 2
            + ring_sems(hops)
        )
        self.result = lambda out: out.reshape(rows, width)

    def bind(self, place, p_ref, out_ref, *scratch):
        def put(half, value):
            out_ref[half] = value

        ring = ring_scatter(place, lambda chunk, half: p_ref.at[chunk, half], put, *scratch)
        first = 1 if self.late else -1
        ticks = {
            2 * (place.hops - hop) + first: functools.partial(ring[1], hop)
            for hop in range(1, place.hops)
        }
        if self.late:
            ticks[1] = ring[0]
            return lambda: None, ticks, ring[2]
        return ring[0], ticks, ring[2]


class Columns:
    def __init__(self, blocks, dps, groups):
        _, rows, width = blocks.shape
        self.inputs, self.in_specs = [blocks], [VM]
        self.outs = [jax.ShapeDtypeStruct((dps, groups, rows, width), blocks.dtype)]
        self.out_specs = [ANY]
        self.scratch = [
            pltpu.VMEM((groups, rows, width), blocks.dtype),
            DMA((2,)),
            DMA((groups,)),
            DMA((groups,)),
        ] + ring_sems(dps // 2)
        self.result = lambda out: out.reshape(dps * groups * rows, width)

    def bind(self, place, x_ref, out_ref, landing, own_sem, sends, recvs, *sems):
        s, groups = place.s, place.groups
        half_of = groups // 2
        here = pltpu.make_async_copy(x_ref.at[s], landing.at[s], own_sem.at[0])
        own = pltpu.make_async_copy(landing, out_ref.at[place.d], own_sem.at[1])

        def swap(i):
            to = (s + i) % groups
            return remote(x_ref.at[to], landing.at[s], sends.at[i], recvs.at[i], seq=to)

        ring = ring_gather(
            place,
            lambda half: landing.at[pl.ds(half * half_of, half_of)],
            lambda chunk, half: out_ref.at[chunk, pl.ds(half * half_of, half_of)],
            *sems,
        )

        def start():
            here.start()
            for i in range(1, groups):
                swap(i).start()

        def middle():
            here.wait()
            for i in range(1, groups):
                swap(i).wait_recv()
            ring[0]()
            own.start()

        def finish():
            for i in range(1, groups):
                swap(i).wait_send()
            own.wait()
            ring[2]()

        ticks = {1 + 2 * hop: functools.partial(ring[1], hop) for hop in range(1, place.hops)}
        ticks[1] = middle
        return start, ticks, finish


class ColumnsBack:
    def __init__(self, partial, order, heads_width, copies, rows, dps, groups):
        width, hops = partial.shape[1], dps // 2
        shape = (groups, rows, width)
        halves = (2, groups // 2, rows, width)
        self.where = [order.index(g) for g in range(groups)]
        self.heads_width, self.copies = heads_width, copies
        joint = groups * heads_width + 2 * KV_HEADS * HEAD_DIM
        self.inputs, self.in_specs = [partial.reshape((dps,) + halves)], [VM]
        self.outs, self.out_specs = [jax.ShapeDtypeStruct((rows, joint), jnp.float32)], [VM]
        self.scratch = (
            [pltpu.VMEM(shape, jnp.bfloat16), pltpu.VMEM(halves, jnp.bfloat16)]
            + [DMA, DMA((groups,)), DMA((groups,))]
            + [pltpu.VMEM((hops,) + halves, jnp.bfloat16)] * 2
            + [pltpu.VMEM((hops - 1,) + halves, jnp.bfloat16)] * 2
            + ring_sems(hops)
        )
        self.result = lambda out: out

    def bind(self, place, p_ref, joint_ref, out_ref, total, own_sem, sends, recvs, *scratch):
        s, groups = place.s, place.groups
        half_of = groups // 2

        def put(half, value):
            total[half] = value.astype(jnp.bfloat16)

        ring = ring_scatter(place, lambda chunk, half: p_ref.at[chunk, half], put, *scratch)
        here = pltpu.make_async_copy(
            total.at[s // half_of, s % half_of], out_ref.at[s], own_sem
        )

        def swap(i):
            to = (s + i) % groups
            src = total.at[to // half_of, to % half_of]
            return remote(src, out_ref.at[s], sends.at[i], recvs.at[i], seq=to)

        def last():
            ring[2]()
            here.start()
            for i in range(1, groups):
                swap(i).start()

        def keys_values(head):
            first = self.where[head * self.copies]
            span = slice(self.heads_width, self.heads_width + 2 * HEAD_DIM)
            value = out_ref[first, :, span].astype(jnp.float32)
            for i in range(1, self.copies):
                value += out_ref[self.where[head * self.copies + i], :, span].astype(jnp.float32)
            return value

        def finish():
            here.wait()
            for i in range(1, groups):
                swap(i).wait_recv()
                swap(i).wait_send()
            heads = self.heads_width
            for g in range(groups):
                value = out_ref[self.where[g], :, :heads]
                joint_ref[:, g * heads : (g + 1) * heads] = value.astype(jnp.float32)
            for head in range(0, KV_HEADS, 2):
                even, odd = keys_values(head), keys_values(head + 1)
                lanes = lax.broadcasted_iota(jnp.int32, even.shape, 1)
                at = groups * heads + head * HEAD_DIM
                joint_ref[:, at : at + 2 * HEAD_DIM] = jnp.where(
                    lanes < HEAD_DIM, even, pltpu.roll(odd, HEAD_DIM, 1)
                )
                at += KV_HEADS * HEAD_DIM
                joint_ref[:, at : at + 2 * HEAD_DIM] = jnp.where(
                    lanes < HEAD_DIM, pltpu.roll(even, HEAD_DIM, 1), odd
                )

        ticks = {
            2 * (place.hops - hop) - 1: functools.partial(ring[1], hop)
            for hop in range(1, place.hops)
        }
        ticks[2 * place.hops - 1] = last
        return ring[0], ticks, finish


class Rows:
    def __init__(self, x, dps, groups):
        rows, width = x.shape
        shape = (2, rows // 2, width)
        self.inputs, self.in_specs = [x.reshape(shape)], [VM]
        self.outs, self.out_specs = [jax.ShapeDtypeStruct((dps,) + shape, x.dtype)], [ANY]
        self.scratch = [
            pltpu.VMEM((dps,) + shape, x.dtype),
            DMA((2,)),
            DMA((dps,)),
            DMA((dps,)),
        ] + ring_sems(dps // 2)
        self.result = lambda out: out.reshape(dps * rows, width)

    def bind(self, place, x_ref, out_ref, landing, own_sem, sends, recvs, *sems):
        s, dps = place.s, place.dps
        slot, base = s % dps, s // dps * dps
        first = pltpu.make_async_copy(x_ref, landing.at[place.d], own_sem.at[0])
        here = pltpu.make_async_copy(landing.at[slot], out_ref.at[slot], own_sem.at[1])
        ring = ring_gather(
            place, lambda half: x_ref.at[half], lambda chunk, half: landing.at[chunk, half], *sems
        )

        def swap(i):
            to = (slot + i) % dps
            return remote(landing.at[to], out_ref.at[slot], sends.at[i], recvs.at[i], seq=base + to)

        def start():
            ring[0]()
            first.start()

        def last():
            first.wait()
            ring[2]()
            here.start()
            for i in range(1, dps):
                swap(i).start()

        def finish():
            here.wait()
            for i in range(1, dps):
                swap(i).wait_recv()
                swap(i).wait_send()

        ticks = {2 * hop - 2: functools.partial(ring[1], hop) for hop in range(1, place.hops)}
        ticks[2 * place.hops - 2] = last
        return start, ticks, finish


class RowsBack:
    def __init__(self, partial, rows, dps, groups):
        width, hops = partial.shape[1], dps // 2
        shape = (2, rows // 2, width)
        self.inputs, self.in_specs = [partial.reshape((dps,) + shape)], [VM]
        self.outs, self.out_specs = [jax.ShapeDtypeStruct(shape, jnp.float32)], [VM]
        self.scratch = (
            [pltpu.VMEM((dps,) + shape, jnp.bfloat16), DMA, DMA((dps,)), DMA((dps,))]
            + [pltpu.VMEM((hops,) + shape, jnp.bfloat16)] * 2
            + [pltpu.VMEM((hops - 1,) + shape, jnp.bfloat16)] * 2
            + ring_sems(hops)
        )
        self.result = lambda out: out.reshape(rows, width)

    def bind(self, place, p_ref, out_ref, landing, own_sem, sends, recvs, *scratch):
        s, dps = place.s, place.dps
        slot, base = s % dps, s // dps * dps
        here = pltpu.make_async_copy(p_ref.at[slot], landing.at[slot], own_sem)

        def swap(i):
            to = (slot + i) % dps
            return remote(p_ref.at[to], landing.at[slot], sends.at[i], recvs.at[i], seq=base + to)

        def put(half, value):
            out_ref[half] = value

        ring = ring_scatter(place, lambda chunk, half: landing.at[chunk, half], put, *scratch)

        def start():
            here.start()
            for i in range(1, dps):
                swap(i).start()

        def middle():
            here.wait()
            for i in range(1, dps):
                swap(i).wait_recv()
            ring[0]()

        def finish():
            for i in range(1, dps):
                swap(i).wait_send()
            ring[2]()

        ticks = {
            2 * (place.hops - hop) + 2: functools.partial(ring[1], hop)
            for hop in range(1, place.hops)
        }
        ticks[2] = middle
        return start, ticks, finish


class Spread:
    def __init__(self, tiles, total, dps, groups):
        count, shape = dps * groups, tiles.shape[-2:]
        self.total = total
        self.inputs, self.in_specs = [tiles], [VM]
        out = shape if total else (count,) + shape
        self.outs, self.out_specs = [jax.ShapeDtypeStruct(out, jnp.float32)], [VM]
        self.scratch = [pltpu.VMEM((count,) + shape, jnp.float32), DMA((count,)), DMA((count,))]
        self.result = lambda out: out

    def bind(self, place, x_ref, out_ref, landing, sends, recvs):
        count = place.dps * place.groups
        me = place.d * place.groups + place.s

        def copy(i):
            other = (me + i) % count
            return remote(
                x_ref.at[other] if self.total else x_ref,
                landing.at[me],
                sends.at[i],
                recvs.at[i],
                dp=other // place.groups,
                seq=other % place.groups,
            )

        def start():
            def each(i, _):
                copy(i).start()
                return 0

            lax.fori_loop(1, count, each, 0)

        def finish():
            def each(i, _):
                copy(i).wait_recv()
                copy(i).wait_send()
                return 0

            lax.fori_loop(1, count, each, 0)
            landing[me] = x_ref[me] if self.total else x_ref[...]
            out_ref[...] = jnp.sum(landing[...], axis=0) if self.total else landing[...]

        return start, {}, finish


TILE = 256


class FeedForward:
    def __init__(self, normed, down, gate, up, grad_all, dps, groups):
        rows, width = normed.shape
        shape, chips = (SUB, rows // SUB, width), groups // 2
        held = gate.shape[0]
        ring = (2, down.shape[0] // 2, width)
        pair = 2 * rows
        self.inputs = [
            normed.reshape(shape),
            down.reshape(ring),
            gate,
            up,
            grad_all.reshape(chips, pair, width),
        ]
        self.in_specs = [VM, VM, ANY, ANY, ANY]
        act = jax.ShapeDtypeStruct((chips, pair, held), jnp.bfloat16)
        self.outs = [
            jax.ShapeDtypeStruct((groups,) + shape, jnp.bfloat16),
            jax.ShapeDtypeStruct((dps,) + ring, jnp.bfloat16),
            act,
            act,
            act,
        ]
        self.out_specs = [VM] * 5
        self.scratch = [
            pltpu.VMEM((held, width), jnp.bfloat16),
            pltpu.VMEM((held, width), jnp.bfloat16),
            pltpu.VMEM((chips, pair, width), jnp.bfloat16),
            pltpu.VMEM((chips, pair, held), jnp.float32),
            pltpu.VMEM((chips, pair, held), jnp.float32),
            pltpu.VMEM((dps, chips, pair, held // dps), jnp.float32),
            DMA((4,)),
            DMA,
        ]
        self.scratch += [DMA((chips, SUB))] * 6 + ring_sems(dps // 2)
        self.result = lambda hn, full, *acts: (
            hn.reshape(groups * rows, width),
            full.reshape(held, width),
            *[one.reshape(groups * rows, held) for one in acts],
        )

    def bind(self, place, x_ref, shard, gate_at, up_at, grad_at, *refs):
        hn, full, inner, dgate, dup, gate_w, up_w, grads, slope, silu, dinner = refs[:11]
        loads, own_line = refs[11:13]
        line_sems, ring_refs = refs[13:19], refs[19:]
        chip, chips = place.chip, place.chips
        pair, held = inner.shape[1:]
        width = gate_w.shape[1]
        own, start_line, step, arrived, sent = line_gather(place, x_ref, hn, own_line, *line_sems)
        ring = ring_gather(
            place,
            lambda half: shard.at[half],
            lambda chunk, half: full.at[chunk, half],
            *ring_refs,
        )
        copies = [
            pltpu.make_async_copy(gate_at, gate_w, loads.at[0]),
            pltpu.make_async_copy(up_at, up_w, loads.at[1]),
            pltpu.make_async_copy(grad_at, grads, loads.at[2]),
            pltpu.make_async_copy(shard, full.at[place.d], loads.at[3]),
        ]
        wide = 512 if held % 512 == 0 else held

        def start():
            start_line()
            ring[0]()
            for one in copies:
                one.start()

        def forward(at):
            rows = hn[pl.ds(2 * at, 2)].reshape(pair, width)
            for first in range(0, held, wide):
                span = slice(first, first + wide)
                gate = lax.dot_general(
                    rows, gate_w[span, :], contract_cols, preferred_element_type=jnp.float32
                )
                upward = lax.dot_general(
                    rows, up_w[span, :], contract_cols, preferred_element_type=jnp.float32
                )
                sigmoid = jax.nn.sigmoid(gate)
                passed = gate * sigmoid
                inner[at, :, span] = (passed * upward).astype(jnp.bfloat16)
                silu[at, :, span] = passed
                slope[at, :, span] = upward * sigmoid * (1.0 + gate * (1.0 - sigmoid))

        def when_there(at, there):
            @pl.when(there)
            def _():
                arrived(at)
                forward(at)

        chunk = held // place.dps
        early = chunk % 128 == 0

        def back(owner, part):
            def each(at, _):
                dinner[owner, at] = lax.dot_general(
                    grads[at], part, contract_cols, preferred_element_type=jnp.float32
                )
                return 0

            lax.fori_loop(0, chips, each, 0)

        def back_from(owner):
            back(owner, full[owner].reshape(chunk, width))

        def tick(hop, half):
            step(hop, half)
            if early and hop == 1 and half == 1:
                copies[2].wait()
                back(place.d, shard[...].reshape(chunk, width))
            if hop == 1 and half == 0:
                own.wait()
                copies[0].wait()
                copies[1].wait()
                arrived(chip)
                forward(chip)
            if hop > 1 and half == 0:
                when_there(chip - hop + 1, chip - hop + 1 >= 0)
            if hop > 1 and half == SUB - 1:
                when_there(chip + hop - 1, chip + hop - 1 < chips)

        def finish():
            last = chips - 1
            when_there(chip - last, chip - last >= 0)
            when_there(chip + last, chip + last < chips)
            copies[3].wait()
            if not early:
                copies[2].wait()
                ring[2]()
                last_all()
            else:
                ring[2](True)
                if place.hops > 2:
                    back_between()
                back_from(place.ring(place.hops))

                def each(at, _):
                    for q in range(place.dps):
                        span = slice(q * chunk, (q + 1) * chunk)
                        grad = dinner[q, at]
                        dgate[at, :, span] = (grad * slope[at, :, span]).astype(jnp.bfloat16)
                        dup[at, :, span] = (grad * silu[at, :, span]).astype(jnp.bfloat16)
                    return 0

                lax.fori_loop(0, chips, each, 0)
            sent()

        def back_between():
            for hop in range(1, place.hops):
                back_from(place.ring(hop))
                back_from(place.ring(-hop))

        def last_all():
            def each(at, _):
                rows = grads[at]
                for first in range(0, held, wide):
                    span = slice(first, first + wide)
                    part = full[first // chunk : (first + wide) // chunk].reshape(wide, width)
                    grad = lax.dot_general(
                        rows, part, contract_cols, preferred_element_type=jnp.float32
                    )
                    dgate[at, :, span] = (grad * slope[at, :, span]).astype(jnp.bfloat16)
                    dup[at, :, span] = (grad * silu[at, :, span]).astype(jnp.bfloat16)
                return 0

            lax.fori_loop(0, chips, each, 0)

        ticks = {
            (hop - 1) * SUB + half: functools.partial(tick, hop, half)
            for hop in range(1, chips)
            for half in range(SUB)
        }

        def with_ring(tick, hop):
            ticks[tick]()
            ring[1](hop)

        def with_near(tick):
            ticks[tick]()
            ring[3]()
            if place.hops == 2:
                back_between()

        merged = dict(ticks)
        for hop in range(1, place.hops):
            merged[2 * hop - 1] = functools.partial(with_ring, 2 * hop - 1, hop)
        if early:
            merged[2 * place.hops - 1] = functools.partial(with_near, 2 * place.hops - 1)
        return start, merged, finish


class FeedBack:
    def __init__(self, inner, dgate, dup, gate, up, down, normed, grads, dps, groups):
        length, held = inner.shape
        width, chips = normed.shape[1], groups // 2
        rows = length // groups
        shape = (SUB, rows // SUB, width)
        owned = (2, held // dps // 2, width)
        hops = dps // 2
        tile = (2, SUB, rows // SUB, width)
        self.inputs = [inner, dgate, dup, gate, up, down, normed, grads]
        self.in_specs = [ANY] * 8
        self.outs = [
            jax.ShapeDtypeStruct(shape, jnp.float32),
            jax.ShapeDtypeStruct(owned, jnp.float32),
            jax.ShapeDtypeStruct((held // TILE,) + tile, jnp.bfloat16),
            jax.ShapeDtypeStruct((held // TILE,) + tile, jnp.bfloat16),
            jax.ShapeDtypeStruct((chips,) + tile, jnp.bfloat16),
        ]
        self.out_specs = [VM, VM, ANY, ANY, ANY]
        act = pltpu.VMEM((length, held), jnp.bfloat16)
        weight = pltpu.VMEM((held, width), jnp.bfloat16)
        tokens = pltpu.VMEM((length, width), jnp.bfloat16)
        self.scratch = [act] * 3 + [weight] * 3 + [tokens] * 2
        self.scratch += [
            pltpu.VMEM((groups,) + shape, jnp.bfloat16),
            pltpu.VMEM((dps,) + owned, jnp.bfloat16),
            pltpu.VMEM((2,) + tile, jnp.bfloat16),
            DMA((8,)),
            DMA((2,)),
        ]
        self.scratch += line_scatter_scratch(chips, shape)
        self.scratch += (
            [pltpu.VMEM((hops,) + owned, jnp.bfloat16)] * 2
            + [pltpu.VMEM((hops - 1,) + owned, jnp.bfloat16)] * 2
            + ring_sems(hops)
        )
        self.result = lambda total, mine, gate_term, up_term, out: (
            total.reshape(rows, width),
            mine.reshape(held // dps, width),
            gate_term.reshape(held, width),
            up_term.reshape(held, width),
            out.reshape(length, width),
        )

    def bind(self, place, *refs):
        sources, refs = refs[:8], refs[8:]
        total_ref, own_ref, gate_out, up_out, result_out = refs[:5]
        inner, dgate, dup, gate, up, down, normed, grads = refs[5:13]
        p_ref, term, stage, loads, stage_sem = refs[13:18]
        line_refs, ring_refs = refs[18:27], refs[27:]
        chip, chips, hops = place.chip, place.chips, place.hops
        held, width = gate.shape
        pair = inner.shape[0] // chips
        chunk = held // place.dps
        wide = 1024 if width % 1024 == 0 else width
        send, step, finish_line = line_scatter(place, p_ref, total_ref, *line_refs)

        def put(half, value):
            own_ref[half] = value

        ring = ring_scatter(place, lambda at, half: term.at[at, half], put, *ring_refs)
        targets = [inner, dgate, dup, gate, up, down, normed, grads]
        copies = [
            pltpu.make_async_copy(source, target, loads.at[i])
            for i, (source, target) in enumerate(zip(sources, targets))
        ]

        def start():
            for i in (0, 7, 1, 3, 2, 4, 6, 5):
                copies[i].start()

        def rows_of(ref, at):
            return ref[pl.ds(pl.multiple_of(at * pair, pair), pair), :]

        def partial(at):
            left, right = rows_of(dgate, at), rows_of(dup, at)
            for first in range(0, width, wide):
                span = slice(first, first + wide)
                value = jnp.dot(left, gate[:, span], preferred_element_type=jnp.float32)
                value += jnp.dot(right, up[:, span], preferred_element_type=jnp.float32)
                p_ref[pl.ds(2 * at, 2), :, :, span] = value.astype(jnp.bfloat16).reshape(
                    p_ref[pl.ds(2 * at, 2), :, :, span].shape
                )
            send(at)

        def term_rows(ref, other, start, count, span):
            return lax.dot_general(
                ref[:, pl.ds(start, count)],
                other[:, span],
                contract_rows,
                preferred_element_type=jnp.float32,
            ).astype(jnp.bfloat16)

        def down_tile(at):
            if chunk % 128 == 0:
                for first in range(0, width, wide):
                    span = slice(first, first + wide)
                    value = term_rows(inner, grads, pl.multiple_of(at * chunk, chunk), chunk, span)
                    term[at, :, :, span] = value.reshape(2, chunk // 2, wide)

        def down_all():
            if chunk % 128 != 0:
                for row in range(0, held, TILE):
                    for first in range(0, width, wide):
                        span = slice(first, first + wide)
                        value = term_rows(inner, grads, row, TILE, span)
                        term[row // chunk : (row + TILE) // chunk, :, :, span] = value.reshape(
                            TILE // chunk, 2, chunk // 2, wide
                        )

        jobs = []

        def first_job():
            copies[0].wait()
            copies[7].wait()
            down_all()
            down_tile(place.ring(hops))
            ring[3]()

        def next_job(hop):
            down_tile(place.ring(hop))
            down_tile(place.ring(-hop))
            if hop == hops - 1:
                ring[4]()

        for hop in range(hops - 1, 0, -1):
            jobs.append(functools.partial(next_job, hop))
            jobs.append(functools.partial(ring[1], hop))
        jobs.append(lambda: down_tile(place.d))

        count = [0]
        waits = []

        def staged(value_of, target):
            slot = count[0] % 2
            if count[0] >= 2:
                waits[count[0] - 2].wait()
            value_of(stage.at[slot])
            copy = pltpu.make_async_copy(stage.at[slot], target, stage_sem.at[slot])
            copy.start()
            waits.append(copy)
            count[0] += 1

        def weight_tile(ref, row, out):
            def fill(slot):
                for first in range(0, width, wide):
                    span = slice(first, first + wide)
                    value = term_rows(ref, normed, row, TILE, span)
                    slot[:, :, :, span] = value.reshape(slot.shape[:3] + (wide,))

            staged(fill, out.at[row // TILE])

        def result_tile(at):
            def fill(slot):
                left = rows_of(inner, at)
                for first in range(0, width, wide):
                    span = slice(first, first + wide)
                    value = jnp.dot(left, down[:, span], preferred_element_type=jnp.float32)
                    slot[:, :, :, span] = value.astype(jnp.bfloat16).reshape(
                        slot.shape[:3] + (wide,)
                    )

            staged(fill, result_out.at[at])

        def sequence():
            first_job()
            for i in (1, 3, 2, 4):
                copies[i].wait()
            tiles = [
                functools.partial(weight_tile, ref, row, out)
                for ref, out in ((dgate, gate_out), (dup, up_out))
                for row in range(0, held, TILE)
            ]
            tiles += [functools.partial(result_tile, at) for at in range(chips)]
            done = [0]

            def fill(most):
                for _ in range(most):
                    if tiles:
                        if done[0] == 0:
                            copies[6].wait()
                        if done[0] == 2 * (held // TILE):
                            copies[5].wait()
                        done[0] += 1
                        tiles.pop(0)()

            for wave in range(chips - 1):
                high = chips - 1 - wave
                ups = (high > chip).astype(jnp.int32)
                downs = (wave < chip).astype(jnp.int32)

                def each(i, _, high=high, wave=wave, ups=ups):
                    partial(jnp.where(i < ups, high, wave))
                    return 0

                lax.fori_loop(0, ups + downs, each, 0)
                fill(1)
                step(wave, 0)
                if wave == 0:
                    step(wave, 1)
                    jobs.pop(0)()
                else:
                    fill(1)
                    step(wave, 1)
                    if jobs:
                        jobs.pop(0)()
            partial(chip)
            for job in jobs:
                job()
            fill(len(tiles))

        def finish():
            ring[2]()
            finish_line()
            for copy in waits[-2:]:
                copy.wait()

        return start, {0: sequence}, finish


def move(parts, dps, groups, number, greet=greet_near):
    def kernel(*refs):
        place = Place(dps, groups)
        at = [
            0,
            sum(len(part.inputs) for part in parts),
            sum(len(part.inputs) + len(part.outs) for part in parts),
        ]
        bound = []
        for part in parts:
            mine = []
            for kind, length in enumerate((len(part.inputs), len(part.outs), len(part.scratch))):
                mine += refs[at[kind] : at[kind] + length]
                at[kind] += length
            bound.append(part.bind(place, *mine))
        greet(place)
        for start, _, _ in bound:
            start()
        for tick in range(1 + max([0] + [max(list(ticks) + [0]) for _, ticks, _ in bound])):
            for _, ticks, _ in bound:
                if tick in ticks:
                    ticks[tick]()
        for _, _, finish in bound:
            finish()

    outs = pl.pallas_call(
        kernel,
        out_shape=[out for part in parts for out in part.outs],
        in_specs=[spec for part in parts for spec in part.in_specs],
        out_specs=[spec for part in parts for spec in part.out_specs],
        scratch_shapes=[one for part in parts for one in part.scratch],
        compiler_params=pltpu.CompilerParams(
            collective_id=number, has_side_effects=True, vmem_limit_bytes=63 << 20
        ),
        cost_estimate=pl.CostEstimate(flops=0, bytes_accessed=120_000_000, transcendentals=0),
        name=f"move_{number}",
    )(*[x for part in parts for x in part.inputs])
    results, at = [], 0
    for part in parts:
        results.append(part.result(*outs[at : at + len(part.outs)]))
        at += len(part.outs)
    return results


def norm_factor(values):
    return lax.rsqrt(jnp.mean(values * values, axis=-1, keepdims=True) + epsilon)


def norm_grad(values, factor, gain, gradient):
    weighted = gradient * gain
    inner_mean = jnp.mean(weighted * values, axis=-1, keepdims=True)
    return factor * weighted - values * (factor * factor * factor) * inner_mean


def rope_tables(positions, head_width):
    half_width = head_width // 2
    frequency = rope_base ** (-2.0 * jnp.arange(half_width, dtype=jnp.float32) / head_width)
    angles = positions.astype(jnp.float32)[:, None] * frequency[None, :]
    return (jnp.cos(angles)[:, None, :], jnp.sin(angles)[:, None, :])


def rotate(values, cosine_table, sine_table):
    half_width = values.shape[-1] // 2
    first_half = values[..., :half_width]
    second_half = values[..., half_width:]
    return jnp.concatenate(
        [
            first_half * cosine_table - second_half * sine_table,
            second_half * cosine_table + first_half * sine_table,
        ],
        axis=-1,
    )


def block_scores(query_block, key_heads, lower, upper, score_scale):
    scores = (
        jnp.einsum(
            "qhd,kd->hqk", query_block, key_heads[:upper], preferred_element_type=jnp.float32
        )
        * score_scale
    )
    rows_at = lower + jnp.arange(query_block.shape[0], dtype=jnp.int32)
    cols_at = jnp.arange(upper, dtype=jnp.int32)
    allowed = (cols_at[None, :] <= rows_at[:, None])[None]
    return jnp.where(allowed, scores, masked_value)


def per_device(
    tokens,
    qkv_weight,
    out_weight,
    gate_weight,
    up_weight,
    down_weight,
    attn_gain,
    mlp_gain,
    cotangent,
):
    groups = lax.axis_size("seq")
    dps = lax.axis_size("dp")
    tok_rows = tokens.shape[1]
    model_width = tokens.shape[2]
    weight_rows = qkv_weight.shape[0]
    seq_len = tok_rows * groups
    local_heads = HEADS // groups
    local_width = local_heads * HEAD_DIM
    kv_copies = groups // KV_HEADS
    score_scale = HEAD_DIM ** (-0.5)
    block_rows = min(512, seq_len)
    block_count = seq_len // block_rows
    fold = groups // dps
    order = [(at % dps) * fold + at // dps for at in range(groups)]

    q_part = qkv_weight[:, :model_width].reshape(weight_rows, groups, local_width)
    k_part = qkv_weight[:, model_width : model_width + KV_HEADS * HEAD_DIM]
    v_part = qkv_weight[:, model_width + KV_HEADS * HEAD_DIM :]
    k_part = k_part.reshape(weight_rows, KV_HEADS, HEAD_DIM)
    v_part = v_part.reshape(weight_rows, KV_HEADS, HEAD_DIM)
    columns = jnp.stack(
        [
            jnp.concatenate(
                [q_part[:, g], k_part[:, g // kv_copies], v_part[:, g // kv_copies]], axis=1
            )
            for g in order
        ]
    )
    gain_width = attn_gain.shape[0]
    tile = jnp.zeros((8, 128), jnp.float32)
    tile = tile.at[0, :gain_width].set(attn_gain.astype(jnp.float32))
    tile = tile.at[1, :gain_width].set(mlp_gain.astype(jnp.float32))
    qkv_local, out_rows, normed_all, gate_part, gains = move(
        [
            Columns(columns, dps, groups),
            Rows(out_weight, dps, groups),
            LineGather(tokens[0], dps, groups, normed=True),
            RingGather(gate_weight, dps, groups, late=True),
            Spread(tile, False, dps, groups),
        ],
        dps,
        groups,
        1,
        greet_all,
    )
    gain_one = gains[:, 0, :gain_width].reshape(model_width)
    gain_two = gains[:, 1, :gain_width].reshape(model_width)

    x_rows = tokens[0].astype(jnp.float32)
    factor_one = norm_factor(x_rows)
    qkv_gained = (qkv_local.astype(jnp.float32) * gain_one[:, None]).astype(jnp.bfloat16)
    grad_low = cotangent[0]
    grad_low, _ = lax.optimization_barrier((grad_low, gains))
    grad_all = lax.all_gather(grad_low, "seq", axis=0, tiled=True)

    mixed = jnp.dot(normed_all, qkv_gained, preferred_element_type=jnp.float32)
    cosine_table, sine_table = rope_tables(jnp.arange(seq_len, dtype=jnp.int32), HEAD_DIM)
    query_heads = rotate(
        mixed[:, :local_width].reshape(seq_len, local_heads, HEAD_DIM), cosine_table, sine_table
    ).astype(jnp.bfloat16)
    key_heads = rotate(
        mixed[:, None, local_width : local_width + HEAD_DIM], cosine_table, sine_table
    ).astype(jnp.bfloat16)[:, 0]
    value_heads = mixed[:, local_width + HEAD_DIM :].astype(jnp.bfloat16)
    outputs = []
    log_sums = []
    for block in range(block_count):
        lower = block * block_rows
        upper = lower + block_rows
        scores = block_scores(query_heads[lower:upper], key_heads, lower, upper, score_scale)
        highest = jnp.max(scores, axis=-1, keepdims=True)
        log_sum = highest + jnp.log(jnp.sum(jnp.exp(scores - highest), axis=-1, keepdims=True))
        probs = jnp.exp(scores - log_sum).astype(jnp.bfloat16)
        attended = jnp.einsum(
            "hqk,kd->qhd", probs, value_heads[:upper], preferred_element_type=jnp.float32
        )
        outputs.append(attended.astype(jnp.bfloat16))
        log_sums.append(log_sum)
    attended = jnp.concatenate(outputs, axis=0).reshape(seq_len, local_width)
    up_part, summed = move(
        [
            RingGather(up_weight, dps, groups),
            LineProduct(attended, out_rows, (((1,), (0,)), ((), ())), dps, groups),
        ],
        dps,
        groups,
        2,
    )
    hidden = x_rows + summed
    factor_two = norm_factor(hidden)
    normed_two = (hidden * factor_two * gain_two).astype(jnp.bfloat16)
    ((hn_all, down_part, inner, grad_gate, grad_upward),) = move(
        [FeedForward(normed_two, down_weight, gate_part, up_part, grad_all, dps, groups)],
        dps,
        groups,
        3,
    )
    ((grad_normed, down_owned, gate_term, up_term, result),) = move(
        [
            FeedBack(
                inner,
                grad_gate,
                grad_upward,
                gate_part,
                up_part,
                down_part,
                hn_all,
                grad_all,
                dps,
                groups,
            )
        ],
        dps,
        groups,
        4,
    )
    gain_two_term = jnp.sum(grad_normed * hidden * factor_two, axis=0)
    grad_hidden = grad_low.astype(jnp.float32) + norm_grad(
        hidden, factor_two, gain_two, grad_normed
    )
    grad_branch, gate_owned = move(
        [
            LineGather(grad_hidden.astype(jnp.bfloat16), dps, groups),
            RingScatter(gate_term, dps, groups),
        ],
        dps,
        groups,
        5,
    )
    result, grad_branch = lax.optimization_barrier((result, grad_branch))
    mlp_result = lax.psum_scatter(result, "seq", scatter_dimension=0, tiled=True)
    block_out = (hidden + mlp_result.astype(jnp.float32)).astype(jnp.bfloat16)[None]
    out_term = lax.dot_general(
        attended, grad_branch, contract_rows, preferred_element_type=jnp.float32
    ).astype(jnp.bfloat16)
    grad_heads = (
        lax.dot_general(grad_branch, out_rows, contract_cols, preferred_element_type=jnp.float32)
        .astype(jnp.bfloat16)
        .reshape(seq_len, local_heads, HEAD_DIM)
    )
    grad_keys = jnp.zeros((seq_len, HEAD_DIM), jnp.float32)
    grad_values = jnp.zeros((seq_len, HEAD_DIM), jnp.float32)
    grad_queries = []
    for block in range(block_count):
        lower = block * block_rows
        upper = lower + block_rows
        query_block = query_heads[lower:upper]
        grad_block = grad_heads[lower:upper]
        scores = block_scores(query_block, key_heads, lower, upper, score_scale)
        probs = jnp.exp(scores - log_sums[block])
        probs_low = probs.astype(jnp.bfloat16)
        grad_probs = jnp.einsum(
            "qhd,kd->hqk", grad_block, value_heads[:upper], preferred_element_type=jnp.float32
        )
        row_delta = jnp.sum(probs * grad_probs, axis=-1, keepdims=True)
        grad_scores = (probs * (grad_probs - row_delta)).astype(jnp.bfloat16)
        grad_queries.append(
            jnp.einsum(
                "hqk,kd->qhd", grad_scores, key_heads[:upper], preferred_element_type=jnp.float32
            )
            * score_scale
        )
        grad_keys = grad_keys.at[:upper].add(
            jnp.einsum("hqk,qhd->kd", grad_scores, query_block, preferred_element_type=jnp.float32)
            * score_scale
        )
        grad_values = grad_values.at[:upper].add(
            jnp.einsum("hqk,qhd->kd", probs_low, grad_block, preferred_element_type=jnp.float32)
        )
    grad_q = rotate(jnp.concatenate(grad_queries, axis=0), cosine_table, -sine_table)
    grad_k = rotate(grad_keys[:, None], cosine_table, -sine_table)[:, 0]
    grad_mixed = jnp.concatenate(
        [grad_q.reshape(seq_len, local_width), grad_k, grad_values], axis=1
    ).astype(jnp.bfloat16)
    qkv_term = lax.dot_general(
        normed_all, grad_mixed, contract_rows, preferred_element_type=jnp.float32
    )
    gain_one_term = jnp.sum(qkv_term * qkv_local.astype(jnp.float32), axis=1)
    qkv_term = (qkv_term * gain_one[:, None]).astype(jnp.bfloat16)
    terms = jnp.stack([gain_one_term, gain_two_term]).reshape(2, dps * groups, gain_width)
    terms = jnp.pad(terms.transpose(1, 0, 2), ((0, 0), (0, 6), (0, 128 - gain_width)))
    qkv_owned, out_owned, grad_normed_one, up_owned, gain_grads = move(
        [
            ColumnsBack(qkv_term, order, local_width, kv_copies, weight_rows, dps, groups),
            RowsBack(out_term, weight_rows, dps, groups),
            LineProduct(grad_mixed, qkv_local, contract_cols, dps, groups),
            RingScatter(up_term, dps, groups, late=True),
            Spread(terms, True, dps, groups),
        ],
        dps,
        groups,
        6,
        greet_all,
    )
    grad_input = grad_hidden + norm_grad(x_rows, factor_one, gain_one, grad_normed_one)
    return (
        block_out,
        grad_input[None],
        qkv_owned,
        out_owned,
        gate_owned,
        up_owned,
        down_owned,
        gain_grads[0, :gain_width],
        gain_grads[1, :gain_width],
    )


def solution(mesh):
    rows = P(("dp", "seq"), None)
    tokens = P("dp", "seq", None)
    gains = P(("dp", "seq"))
    return jax.shard_map(
        per_device,
        mesh=mesh,
        in_specs=(tokens, rows, rows, rows, rows, rows, gains, gains, tokens),
        out_specs=(tokens, tokens, rows, rows, rows, rows, rows, gains, gains),
        check_vma=False,
    )
```

```python
import functools

import jax
import jax.numpy as jnp
from jax import lax
from jax.experimental import pallas as pl
from jax.experimental.pallas import tpu as pltpu
from jax.sharding import PartitionSpec as P

HEADS = 32
KV_HEADS = 8
HEAD_DIM = 64

MESH = pl.DeviceIdType.MESH
ANY = pl.BlockSpec(memory_space=pl.ANY)
VM = pl.BlockSpec(memory_space=pltpu.VMEM)
SUB = 2

epsilon = 1e-05
rope_base = 500000.0
masked_value = -1e30
contract_rows = (((0,), (0,)), ((), ()))
contract_cols = (((1,), (1,)), ((), ()))


class Place:
    def __init__(self, dps, groups):
        self.dps, self.groups, self.chips, self.hops = dps, groups, groups // 2, dps // 2
        self.d, self.s = lax.axis_index("dp"), lax.axis_index("seq")
        self.chip, self.core = self.s // 2, self.s % 2
        self.partner = 2 * self.chip + 1 - self.core
        row, side = self.d // 2, self.d % 2
        self.turn = side * (dps - 1 - row) + (1 - side) * row

    def ring(self, distance):
        at = (self.turn + distance + self.dps) % self.dps
        side = at // self.hops
        return (1 - side) * 2 * at + side * (2 * (self.dps - 1 - at) + 1)


def remote(src, dst, send, recv, **target):
    return pltpu.make_async_remote_copy(
        src_ref=src, dst_ref=dst, send_sem=send, recv_sem=recv, device_id=target, device_id_type=MESH
    )


def greet_near(place):
    barrier = pltpu.get_barrier_semaphore()

    def signal(**target):
        pl.semaphore_signal(barrier, inc=1, device_id=target, device_id_type=MESH)

    signal(seq=place.partner)
    signal(dp=place.ring(1))
    signal(dp=place.ring(-1))

    @pl.when(place.chip > 0)
    def _():
        signal(seq=place.s - 2)

    @pl.when(place.chip < place.chips - 1)
    def _():
        signal(seq=place.s + 2)

    ends = (place.chips - place.chip) // place.chips + (place.chip + 1) // place.chips
    pl.semaphore_wait(barrier, 5 - ends)


def greet_all(place):
    barrier = pltpu.get_barrier_semaphore()
    count = place.dps * place.groups
    me = place.d * place.groups + place.s

    def signal(i, _):
        other = (me + i) % count
        pl.semaphore_signal(
            barrier,
            inc=1,
            device_id={"dp": other // place.groups, "seq": other % place.groups},
            device_id_type=MESH,
        )
        return 0

    lax.fori_loop(1, count, signal, 0)
    pl.semaphore_wait(barrier, count - 1)


DMA = pltpu.SemaphoreType.DMA


def line_gather(place, x_ref, out_ref, own_sem, us, ur, ds, dr, ps, pr):
    s, chip, chips = place.s, place.chip, place.chips

    def copy(src, group, half, sends, recvs, at, target):
        return remote(
            src, out_ref.at[group, half], sends.at[at, half], recvs.at[at, half], seq=target
        )

    def up(src, group, hop, half):
        return copy(src, group, half, us, ur, hop, s + 2)

    def down(src, group, hop, half):
        return copy(src, group, half, ds, dr, hop, s - 2)

    def pair(src, group, half):
        return copy(src, group, half, ps, pr, group // 2, place.partner)

    own = pltpu.make_async_copy(x_ref, out_ref.at[s], own_sem)

    def start():
        own.start()
        for half in range(SUB):

            @pl.when(chip < chips - 1)
            def _():
                up(x_ref.at[half], s, 0, half).start()

            @pl.when(chip > 0)
            def _():
                down(x_ref.at[half], s, 0, half).start()

        for half in range(SUB):
            pair(x_ref.at[half], s, half).start()

    def step(hop, half):
        below, above = s - 2 * hop, s + 2 * hop

        @pl.when(chip - hop >= 0)
        def _():
            block = out_ref.at[below, half]
            up(block, below, hop - 1, half).wait_recv()

            @pl.when(chip < chips - 1)
            def _():
                up(block, below, hop, half).start()

            pair(block, below, half).start()

        @pl.when(chip + hop < chips)
        def _():
            block = out_ref.at[above, half]
            down(block, above, hop - 1, half).wait_recv()

            @pl.when(chip > 0)
            def _():
                down(block, above, hop, half).start()

            pair(block, above, half).start()

    def arrived(at):
        for half in range(SUB):
            group = 2 * at + 1 - place.core
            pair(out_ref.at[group, half], group, half).wait_recv()

    def sent():
        def each(i, _):
            k, half = i // SUB, i % SUB
            mine = 2 * k + place.core
            block = out_ref.at[mine, half]
            pair(block, mine, half).wait_send()

            @pl.when(jnp.logical_and(chip - k >= 0, chip < chips - 1))
            def _():
                up(block, mine, k, half).wait_send()

            @pl.when(jnp.logical_and(chip + k < chips, chip > 0))
            def _():
                down(block, mine, k, half).wait_send()

            return 0

        lax.fori_loop(0, chips * SUB, each, 0)

    return own, start, step, arrived, sent


class LineGather:
    def __init__(self, x, dps, groups, normed=False):
        rows, width = x.shape
        shape = (SUB, rows // SUB, width)
        self.normed = normed
        self.inputs, self.in_specs = [x.reshape(shape)], [VM]
        self.outs, self.out_specs = [jax.ShapeDtypeStruct((groups,) + shape, x.dtype)], [ANY]
        self.scratch = [DMA] + [DMA((groups // 2, SUB))] * 6
        if normed:
            self.scratch = [pltpu.VMEM(shape, x.dtype)] + self.scratch
        self.result = lambda out: out.reshape(groups * rows, width)

    def bind(self, place, x_ref, out_ref, *refs):
        if self.normed:
            source, x_ref, refs = x_ref, refs[0], refs[1:]
            many = 16 if x_ref.shape[1] % 16 == 0 else x_ref.shape[1]

            def norm(i, _):
                span = pl.ds(pl.multiple_of(i * many, many), many)
                for half in range(SUB):
                    values = source[half, span, :].astype(jnp.float32)
                    x_ref[half, span, :] = (values * norm_factor(values)).astype(x_ref.dtype)
                return 0

            lax.fori_loop(0, x_ref.shape[1] // many, norm, 0)
        own, start, step, arrived, sent = line_gather(place, x_ref, out_ref, *refs)

        def finish():
            own.wait()

            def each(at, _):
                arrived(at)
                return 0

            lax.fori_loop(0, place.chips, each, 0)
            sent()

        ticks = {
            (hop - 1) * SUB + half: functools.partial(step, hop, half)
            for hop in range(1, place.chips)
            for half in range(SUB)
        }
        return start, ticks, finish


def line_scatter(place, p_ref, out_ref, pairbuf, upbuf, downbuf, us, ur, ds, dr, ps, pr):
    s, chip, chips, core = place.s, place.chip, place.chips, place.core

    def copy(src, buffer, at, half, sends, recvs, target):
        return remote(src, buffer.at[at, half], sends.at[at, half], recvs.at[at, half], seq=target)

    def pair(at, half):
        src = p_ref.at[2 * at + 1 - core, half]
        return copy(src, pairbuf, at, half, ps, pr, place.partner)

    def up(at, half):
        return copy(upbuf.at[at, half], upbuf, at, half, us, ur, s + 2)

    def down(at, half):
        return copy(downbuf.at[at, half], downbuf, at, half, ds, dr, s - 2)

    def wide(ref, *at):
        return ref[at].astype(jnp.float32)

    def local(at, half):
        return wide(p_ref, 2 * at + core, half) + wide(pairbuf, at, half)

    def send(at):
        for half in range(SUB):
            pair(at, half).start()

    def step(wave, half):
        high, low = chips - 1 - wave + chip, wave - (chips - 1 - chip)

        @pl.when(chip <= wave)
        def _():
            pair(high, half).wait_recv()

            @pl.when(chip > 0)
            def _():
                up(high, half).wait_recv()
                total = local(high, half) + wide(upbuf, high, half)
                upbuf[high, half] = total.astype(jnp.bfloat16)

            @pl.when(chip == 0)
            def _():
                upbuf[high, half] = local(high, half).astype(jnp.bfloat16)

            up(high, half).start()

        @pl.when(low >= 0)
        def _():
            pair(low, half).wait_recv()

            @pl.when(chip < chips - 1)
            def _():
                down(low, half).wait_recv()
                total = local(low, half) + wide(downbuf, low, half)
                downbuf[low, half] = total.astype(jnp.bfloat16)

            @pl.when(chip == chips - 1)
            def _():
                downbuf[low, half] = local(low, half).astype(jnp.bfloat16)

            down(low, half).start()

    def finish():
        for half in range(SUB):
            pair(chip, half).wait_recv()
            out_ref[half] = local(chip, half)

            @pl.when(chip > 0)
            def _():
                up(chip, half).wait_recv()
                out_ref[half] += wide(upbuf, chip, half)

            @pl.when(chip < chips - 1)
            def _():
                down(chip, half).wait_recv()
                out_ref[half] += wide(downbuf, chip, half)

        def each(i, _):
            at, half = i // SUB, i % SUB
            pair(at, half).wait_send()

            @pl.when(at > chip)
            def _():
                up(at, half).wait_send()

            @pl.when(at < chip)
            def _():
                down(at, half).wait_send()

            return 0

        lax.fori_loop(0, chips * SUB, each, 0)

    return send, step, finish


def line_scatter_scratch(chips, shape):
    return [pltpu.VMEM((chips,) + shape, jnp.bfloat16)] * 3 + [DMA((chips, SUB))] * 6


class LineScatter:
    def __init__(self, partial, dps, groups):
        total, width = partial.shape
        rows = total // groups
        shape = (SUB, rows // SUB, width)
        self.inputs, self.in_specs = [partial.reshape((groups,) + shape)], [VM]
        self.outs, self.out_specs = [jax.ShapeDtypeStruct(shape, jnp.float32)], [VM]
        self.scratch = line_scatter_scratch(groups // 2, shape)
        self.result = lambda out: out.reshape(rows, width)

    def bind(self, place, *refs):
        send, step, finish = line_scatter(place, *refs)
        chip, chips = place.chip, place.chips

        def start():
            def issue(low, _):
                high = chips - 1 - low

                @pl.when(high > chip)
                def _():
                    send(high)

                @pl.when(low < chip)
                def _():
                    send(low)

                return 0

            lax.fori_loop(0, chips - 1, issue, 0)
            send(chip)

        ticks = {
            i: functools.partial(step, i // SUB, i % SUB) for i in range((chips - 1) * SUB)
        }
        return start, ticks, finish


class LineProduct:
    def __init__(self, left, right, dims, dps, groups):
        total, inner = left.shape
        width = right.shape[1 - dims[0][1][0]]
        rows, chips = total // groups, groups // 2
        shape = (SUB, rows // SUB, width)
        self.dims = dims
        self.inputs, self.in_specs = [left.reshape(chips, 2 * rows, inner), right], [VM, VM]
        self.outs, self.out_specs = [jax.ShapeDtypeStruct(shape, jnp.float32)], [VM]
        self.scratch = [pltpu.VMEM((groups,) + shape, jnp.bfloat16)]
        self.scratch += line_scatter_scratch(chips, shape)
        self.result = lambda out: out.reshape(rows, width)

    def bind(self, place, left, right, out_ref, p_ref, *refs):
        send, step, finish = line_scatter(place, p_ref, out_ref, *refs)
        chip, chips = place.chip, place.chips
        width = p_ref.shape[3]
        wide = 512 if width % 512 == 0 else width

        def partial(at):
            for first in range(0, width, wide):
                span = slice(first, first + wide)
                part = right[:, span] if self.dims[0][1][0] == 0 else right[span, :]
                value = lax.dot_general(
                    left[at], part, self.dims, preferred_element_type=jnp.float32
                )
                p_ref[pl.ds(2 * at, 2), :, :, span] = value.astype(jnp.bfloat16).reshape(
                    (2,) + p_ref.shape[1:3] + (wide,)
                )
            send(at)

        def partials(wave):
            if wave == chips - 1:
                partial(chip)
                return

            @pl.when(chips - 1 - wave > chip)
            def _():
                partial(chips - 1 - wave)

            @pl.when(wave < chip)
            def _():
                partial(wave)

        def tick(wave, half):
            step(wave, half)
            if half == SUB - 1:
                partials(wave + 1)

        ticks = {
            i: functools.partial(tick, i // SUB, i % SUB) for i in range((chips - 1) * SUB)
        }
        return lambda: partials(0), ticks, finish


def ring_sems(hops):
    return [DMA((hops, 2))] * 4


def ring_gather(place, own, out, rs, rr, ls, lr):
    hops = place.hops

    def right(src, chunk, hop, half):
        return remote(
            src, out(chunk, half), rs.at[hop - 1, half], rr.at[hop - 1, half], dp=place.ring(1)
        )

    def left(src, chunk, hop, half):
        return remote(
            src, out(chunk, half), ls.at[hop - 1, half], lr.at[hop - 1, half], dp=place.ring(-1)
        )

    def begin(half):
        right(own(half), place.d, 1, half).start()
        left(own(1 - half), place.d, 1, 1 - half).start()

    def start():
        begin(0)
        begin(1)

    def forward(hop):
        before, after = place.ring(-hop), place.ring(hop)
        full = hop < hops - 1
        right(out(before, 0), before, hop, 0).wait_recv()
        right(out(before, 0), before, hop + 1, 0).start()
        left(out(after, 1), after, hop, 1).wait_recv()
        left(out(after, 1), after, hop + 1, 1).start()
        if full:
            right(out(before, 1), before, hop, 1).wait_recv()
            left(out(after, 0), after, hop, 0).wait_recv()
            right(out(before, 1), before, hop + 1, 1).start()
            left(out(after, 0), after, hop + 1, 0).start()

    def near():
        before, after = place.ring(1 - hops), place.ring(hops - 1)
        right(out(before, 1), before, hops - 1, 1).wait_recv()
        left(out(after, 0), after, hops - 1, 0).wait_recv()

    def finish(waited=False):
        if not waited:
            near()
        right(out(place.d, 0), place.ring(-hops), hops, 0).wait_recv()
        left(out(place.d, 1), place.ring(hops), hops, 1).wait_recv()
        for hop in range(1, hops + 1):
            for half in range(2):
                if hop < hops or half == 0:
                    right(out(place.d, half), place.d, hop, half).wait_send()
                if hop < hops or half == 1:
                    left(out(place.d, half), place.d, hop, half).wait_send()

    return start, forward, finish, near, begin


def ring_scatter(place, part, put, rbuf, lbuf, rout, lout, rs, rr, ls, lr):
    hops = place.hops

    def wide(ref):
        return ref[...].astype(jnp.float32)

    def right(src, hop, half):
        return remote(
            src,
            rbuf.at[hop - 1, half],
            rs.at[hop - 1, half],
            rr.at[hop - 1, half],
            dp=place.ring(1),
        )

    def left(src, hop, half):
        return remote(
            src,
            lbuf.at[hop - 1, half],
            ls.at[hop - 1, half],
            lr.at[hop - 1, half],
            dp=place.ring(-1),
        )

    def start_far():
        right(part(place.ring(hops), 0), hops, 0).start()
        left(part(place.ring(-hops), 1), hops, 1).start()

    def start_next():
        right(part(place.ring(hops - 1), 1), hops - 1, 1).start()
        left(part(place.ring(1 - hops), 0), hops - 1, 0).start()

    def start():
        start_far()
        start_next()

    def forward(hop):
        for first in range(2 if hop < hops - 1 else 1):
            half = first
            right(rbuf.at[hop, half], hop + 1, half).wait_recv()
            total = wide(part(place.ring(hop), half)) + wide(rbuf.at[hop, half])
            rout[hop - 1, half] = total.astype(jnp.bfloat16)
            right(rout.at[hop - 1, half], hop, half).start()
            half = 1 - first
            left(lbuf.at[hop, half], hop + 1, half).wait_recv()
            total = wide(part(place.ring(-hop), half)) + wide(lbuf.at[hop, half])
            lout[hop - 1, half] = total.astype(jnp.bfloat16)
            left(lout.at[hop - 1, half], hop, half).start()

    def finish():
        for half in range(2):
            right(rbuf.at[0, half], 1, half).wait_recv()
            left(lbuf.at[0, half], 1, half).wait_recv()
            put(
                half,
                wide(part(place.d, half)) + wide(rbuf.at[0, half]) + wide(lbuf.at[0, half]),
            )
        for hop in range(1, hops + 1):
            for half in range(2):
                if hop < hops or half == 0:
                    right(rbuf.at[0, half], hop, half).wait_send()
                if hop < hops or half == 1:
                    left(lbuf.at[0, half], hop, half).wait_send()

    return start, forward, finish, start_far, start_next


class RingGather:
    def __init__(self, x, dps, groups, late=False):
        self.late = late
        rows, width = x.shape
        shape = (2, rows // 2, width)
        self.inputs, self.in_specs = [x.reshape(shape)], [VM]
        self.outs, self.out_specs = [jax.ShapeDtypeStruct((dps,) + shape, x.dtype)], [ANY]
        self.scratch = [DMA] + ring_sems(dps // 2)
        self.result = lambda out: out.reshape(dps * rows, width)

    def bind(self, place, x_ref, out_ref, own_sem, *sems):
        own = pltpu.make_async_copy(x_ref, out_ref.at[place.d], own_sem)
        ring = ring_gather(
            place, lambda half: x_ref.at[half], lambda chunk, half: out_ref.at[chunk, half], *sems
        )

        def start():
            ring[4](0)
            if not self.late:
                ring[4](1)
            own.start()

        def second():
            ring[4](1)
            ring[1](1)

        def finish():
            own.wait()
            ring[2]()

        ticks = {2 * hop - 1: functools.partial(ring[1], hop) for hop in range(1, place.hops)}
        if self.late:
            ticks[1] = second
        return start, ticks, finish


class RingScatter:
    def __init__(self, partial, dps, groups, late=False):
        self.late = late
        total, width = partial.shape
        rows, hops = total // dps, dps // 2
        shape = (2, rows // 2, width)
        self.inputs, self.in_specs = [partial.reshape((dps,) + shape)], [VM]
        self.outs, self.out_specs = [jax.ShapeDtypeStruct(shape, jnp.float32)], [VM]
        self.scratch = (
            [pltpu.VMEM((hops,) + shape, jnp.bfloat16)] * 2
            + [pltpu.VMEM((hops - 1,) + shape, jnp.bfloat16)] * 2
            + ring_sems(hops)
        )
        self.result = lambda out: out.reshape(rows, width)

    def bind(self, place, p_ref, out_ref, *scratch):
        def put(half, value):
            out_ref[half] = value

        ring = ring_scatter(place, lambda chunk, half: p_ref.at[chunk, half], put, *scratch)
        first = 1 if self.late else -1
        ticks = {
            2 * (place.hops - hop) + first: functools.partial(ring[1], hop)
            for hop in range(1, place.hops)
        }
        if self.late:
            ticks[1] = ring[4]
            return ring[3], ticks, ring[2]
        return ring[0], ticks, ring[2]


class Columns:
    def __init__(self, blocks, dps, groups):
        _, rows, width = blocks.shape
        self.inputs, self.in_specs = [blocks], [VM]
        self.outs = [jax.ShapeDtypeStruct((dps, groups, rows, width), blocks.dtype)]
        self.out_specs = [ANY]
        self.scratch = [
            pltpu.VMEM((groups, rows, width), blocks.dtype),
            DMA((2,)),
            DMA((groups,)),
            DMA((groups,)),
        ] + ring_sems(dps // 2)
        self.result = lambda out: out.reshape(dps * groups * rows, width)

    def bind(self, place, x_ref, out_ref, landing, own_sem, sends, recvs, *sems):
        s, groups = place.s, place.groups
        half_of = groups // 2
        here = pltpu.make_async_copy(x_ref.at[s], landing.at[s], own_sem.at[0])
        own = pltpu.make_async_copy(landing, out_ref.at[place.d], own_sem.at[1])

        def swap(i):
            to = (s + i) % groups
            return remote(x_ref.at[to], landing.at[s], sends.at[i], recvs.at[i], seq=to)

        ring = ring_gather(
            place,
            lambda half: landing.at[pl.ds(half * half_of, half_of)],
            lambda chunk, half: out_ref.at[chunk, pl.ds(half * half_of, half_of)],
            *sems,
        )

        def start():
            here.start()
            for i in range(1, groups):
                swap(i).start()

        def middle():
            here.wait()
            for i in range(1, groups):
                swap(i).wait_recv()
            ring[0]()
            own.start()

        def finish():
            for i in range(1, groups):
                swap(i).wait_send()
            own.wait()
            ring[2]()

        ticks = {1 + 2 * hop: functools.partial(ring[1], hop) for hop in range(1, place.hops)}
        ticks[1] = middle
        return start, ticks, finish


class ColumnsBack:
    def __init__(self, partial, order, heads_width, copies, rows, dps, groups):
        width, hops = partial.shape[1], dps // 2
        shape = (groups, rows, width)
        halves = (2, groups // 2, rows, width)
        self.where = [order.index(g) for g in range(groups)]
        self.heads_width, self.copies = heads_width, copies
        joint = groups * heads_width + 2 * KV_HEADS * HEAD_DIM
        self.inputs, self.in_specs = [partial.reshape((dps,) + halves)], [VM]
        self.outs, self.out_specs = [jax.ShapeDtypeStruct((rows, joint), jnp.float32)], [VM]
        self.scratch = (
            [pltpu.VMEM(shape, jnp.bfloat16), pltpu.VMEM(halves, jnp.bfloat16)]
            + [DMA, DMA((groups,)), DMA((groups,))]
            + [pltpu.VMEM((hops,) + halves, jnp.bfloat16)] * 2
            + [pltpu.VMEM((hops - 1,) + halves, jnp.bfloat16)] * 2
            + ring_sems(hops)
        )
        self.result = lambda out: out

    def bind(self, place, p_ref, joint_ref, out_ref, total, own_sem, sends, recvs, *scratch):
        s, groups = place.s, place.groups
        half_of = groups // 2

        def put(half, value):
            total[half] = value.astype(jnp.bfloat16)

        ring = ring_scatter(place, lambda chunk, half: p_ref.at[chunk, half], put, *scratch)
        here = pltpu.make_async_copy(
            total.at[s // half_of, s % half_of], out_ref.at[s], own_sem
        )

        def swap(i):
            to = (s + i) % groups
            src = total.at[to // half_of, to % half_of]
            return remote(src, out_ref.at[s], sends.at[i], recvs.at[i], seq=to)

        def last():
            ring[2]()
            here.start()
            for i in range(1, groups):
                swap(i).start()

        def keys_values(head):
            first = self.where[head * self.copies]
            span = slice(self.heads_width, self.heads_width + 2 * HEAD_DIM)
            value = out_ref[first, :, span].astype(jnp.float32)
            for i in range(1, self.copies):
                value += out_ref[self.where[head * self.copies + i], :, span].astype(jnp.float32)
            return value

        def finish():
            here.wait()
            for i in range(1, groups):
                swap(i).wait_recv()
                swap(i).wait_send()
            heads = self.heads_width
            for g in range(groups):
                value = out_ref[self.where[g], :, :heads]
                joint_ref[:, g * heads : (g + 1) * heads] = value.astype(jnp.float32)
            for head in range(0, KV_HEADS, 2):
                even, odd = keys_values(head), keys_values(head + 1)
                lanes = lax.broadcasted_iota(jnp.int32, even.shape, 1)
                at = groups * heads + head * HEAD_DIM
                joint_ref[:, at : at + 2 * HEAD_DIM] = jnp.where(
                    lanes < HEAD_DIM, even, pltpu.roll(odd, HEAD_DIM, 1)
                )
                at += KV_HEADS * HEAD_DIM
                joint_ref[:, at : at + 2 * HEAD_DIM] = jnp.where(
                    lanes < HEAD_DIM, pltpu.roll(even, HEAD_DIM, 1), odd
                )

        ticks = {
            2 * (place.hops - hop) - 1: functools.partial(ring[1], hop)
            for hop in range(1, place.hops)
        }
        ticks[2 * place.hops - 1] = last
        return ring[0], ticks, finish


class Rows:
    def __init__(self, x, dps, groups):
        rows, width = x.shape
        shape = (2, rows // 2, width)
        self.inputs, self.in_specs = [x.reshape(shape)], [VM]
        self.outs, self.out_specs = [jax.ShapeDtypeStruct((dps,) + shape, x.dtype)], [ANY]
        self.scratch = [
            pltpu.VMEM((dps,) + shape, x.dtype),
            DMA((2,)),
            DMA((dps,)),
            DMA((dps,)),
        ] + ring_sems(dps // 2)
        self.result = lambda out: out.reshape(dps * rows, width)

    def bind(self, place, x_ref, out_ref, landing, own_sem, sends, recvs, *sems):
        s, dps = place.s, place.dps
        slot, base = s % dps, s // dps * dps
        first = pltpu.make_async_copy(x_ref, landing.at[place.d], own_sem.at[0])
        here = pltpu.make_async_copy(landing.at[slot], out_ref.at[slot], own_sem.at[1])
        ring = ring_gather(
            place, lambda half: x_ref.at[half], lambda chunk, half: landing.at[chunk, half], *sems
        )

        def swap(i):
            to = (slot + i) % dps
            return remote(landing.at[to], out_ref.at[slot], sends.at[i], recvs.at[i], seq=base + to)

        def start():
            ring[0]()
            first.start()

        def last():
            first.wait()
            ring[2]()
            here.start()
            for i in range(1, dps):
                swap(i).start()

        def finish():
            here.wait()
            for i in range(1, dps):
                swap(i).wait_recv()
                swap(i).wait_send()

        ticks = {2 * hop - 2: functools.partial(ring[1], hop) for hop in range(1, place.hops)}
        ticks[2 * place.hops - 2] = last
        return start, ticks, finish


class RowsBack:
    def __init__(self, partial, rows, dps, groups):
        width, hops = partial.shape[1], dps // 2
        shape = (2, rows // 2, width)
        self.inputs, self.in_specs = [partial.reshape((dps,) + shape)], [VM]
        self.outs, self.out_specs = [jax.ShapeDtypeStruct(shape, jnp.float32)], [VM]
        self.scratch = (
            [pltpu.VMEM((dps,) + shape, jnp.bfloat16), DMA, DMA((dps,)), DMA((dps,))]
            + [pltpu.VMEM((hops,) + shape, jnp.bfloat16)] * 2
            + [pltpu.VMEM((hops - 1,) + shape, jnp.bfloat16)] * 2
            + ring_sems(hops)
        )
        self.result = lambda out: out.reshape(rows, width)

    def bind(self, place, p_ref, out_ref, landing, own_sem, sends, recvs, *scratch):
        s, dps = place.s, place.dps
        slot, base = s % dps, s // dps * dps
        here = pltpu.make_async_copy(p_ref.at[slot], landing.at[slot], own_sem)

        def swap(i):
            to = (slot + i) % dps
            return remote(p_ref.at[to], landing.at[slot], sends.at[i], recvs.at[i], seq=base + to)

        def put(half, value):
            out_ref[half] = value

        ring = ring_scatter(place, lambda chunk, half: landing.at[chunk, half], put, *scratch)

        def start():
            here.start()
            for i in range(1, dps):
                swap(i).start()

        def middle():
            here.wait()
            for i in range(1, dps):
                swap(i).wait_recv()
            ring[0]()

        def finish():
            for i in range(1, dps):
                swap(i).wait_send()
            ring[2]()

        ticks = {
            2 * (place.hops - hop) + 2: functools.partial(ring[1], hop)
            for hop in range(1, place.hops)
        }
        ticks[2] = middle
        return start, ticks, finish


class Spread:
    def __init__(self, tiles, total, dps, groups):
        count, shape = dps * groups, tiles.shape[-2:]
        self.total = total
        self.inputs, self.in_specs = [tiles], [VM]
        out = shape if total else (count,) + shape
        self.outs, self.out_specs = [jax.ShapeDtypeStruct(out, jnp.float32)], [VM]
        self.scratch = [pltpu.VMEM((count,) + shape, jnp.float32), DMA((count,)), DMA((count,))]
        self.result = lambda out: out

    def bind(self, place, x_ref, out_ref, landing, sends, recvs):
        count = place.dps * place.groups
        me = place.d * place.groups + place.s

        def copy(i):
            other = (me + i) % count
            return remote(
                x_ref.at[other] if self.total else x_ref,
                landing.at[me],
                sends.at[i],
                recvs.at[i],
                dp=other // place.groups,
                seq=other % place.groups,
            )

        def start():
            def each(i, _):
                copy(i).start()
                return 0

            lax.fori_loop(1, count, each, 0)

        def finish():
            def each(i, _):
                copy(i).wait_recv()
                copy(i).wait_send()
                return 0

            lax.fori_loop(1, count, each, 0)
            landing[me] = x_ref[me] if self.total else x_ref[...]
            out_ref[...] = jnp.sum(landing[...], axis=0) if self.total else landing[...]

        return start, {}, finish


TILE = 256


class FeedForward:
    def __init__(self, normed, down, gate, up, grad_all, dps, groups):
        rows, width = normed.shape
        shape, chips = (SUB, rows // SUB, width), groups // 2
        held = gate.shape[0]
        ring = (2, down.shape[0] // 2, width)
        pair = 2 * rows
        self.inputs = [
            normed.reshape(shape),
            down.reshape(ring),
            gate,
            up,
            grad_all.reshape(chips, pair, width),
        ]
        self.in_specs = [VM, VM, ANY, ANY, ANY]
        act = jax.ShapeDtypeStruct((chips, pair, held), jnp.bfloat16)
        self.outs = [
            jax.ShapeDtypeStruct((groups,) + shape, jnp.bfloat16),
            jax.ShapeDtypeStruct((dps,) + ring, jnp.bfloat16),
            act,
            act,
            act,
        ]
        self.out_specs = [VM] * 5
        self.scratch = [
            pltpu.VMEM((held, width), jnp.bfloat16),
            pltpu.VMEM((held, width), jnp.bfloat16),
            pltpu.VMEM((chips, pair, width), jnp.bfloat16),
            pltpu.VMEM((chips, pair, held), jnp.float32),
            pltpu.VMEM((chips, pair, held), jnp.float32),
            pltpu.VMEM((dps, chips, pair, held // dps), jnp.float32),
            DMA((4,)),
            DMA,
        ]
        self.scratch += [DMA((chips, SUB))] * 6 + ring_sems(dps // 2)
        self.result = lambda hn, full, *acts: (
            hn.reshape(groups * rows, width),
            full.reshape(held, width),
            *[one.reshape(groups * rows, held) for one in acts],
        )

    def bind(self, place, x_ref, shard, gate_at, up_at, grad_at, *refs):
        hn, full, inner, dgate, dup, gate_w, up_w, grads, slope, silu, dinner = refs[:11]
        loads, own_line = refs[11:13]
        line_sems, ring_refs = refs[13:19], refs[19:]
        chip, chips = place.chip, place.chips
        pair, held = inner.shape[1:]
        width = gate_w.shape[1]
        own, start_line, step, arrived, sent = line_gather(place, x_ref, hn, own_line, *line_sems)
        ring = ring_gather(
            place,
            lambda half: shard.at[half],
            lambda chunk, half: full.at[chunk, half],
            *ring_refs,
        )
        copies = [
            pltpu.make_async_copy(gate_at, gate_w, loads.at[0]),
            pltpu.make_async_copy(up_at, up_w, loads.at[1]),
            pltpu.make_async_copy(grad_at, grads, loads.at[2]),
            pltpu.make_async_copy(shard, full.at[place.d], loads.at[3]),
        ]
        wide = 512 if held % 512 == 0 else held

        def start():
            start_line()
            ring[0]()
            for one in copies:
                one.start()

        def forward(at):
            rows = hn[pl.ds(2 * at, 2)].reshape(pair, width)
            for first in range(0, held, wide):
                span = slice(first, first + wide)
                gate = lax.dot_general(
                    rows, gate_w[span, :], contract_cols, preferred_element_type=jnp.float32
                )
                upward = lax.dot_general(
                    rows, up_w[span, :], contract_cols, preferred_element_type=jnp.float32
                )
                sigmoid = jax.nn.sigmoid(gate)
                passed = gate * sigmoid
                inner[at, :, span] = (passed * upward).astype(jnp.bfloat16)
                silu[at, :, span] = passed
                slope[at, :, span] = upward * sigmoid * (1.0 + gate * (1.0 - sigmoid))

        def when_there(at, there):
            @pl.when(there)
            def _():
                arrived(at)
                forward(at)

        chunk = held // place.dps
        early = chunk % 128 == 0

        def back(owner, part):
            def each(at, _):
                dinner[owner, at] = lax.dot_general(
                    grads[at], part, contract_cols, preferred_element_type=jnp.float32
                )
                return 0

            lax.fori_loop(0, chips, each, 0)

        def back_from(owner):
            back(owner, full[owner].reshape(chunk, width))

        def tick(hop, half):
            step(hop, half)
            if early and hop == 1 and half == 1:
                copies[2].wait()
                back(place.d, shard[...].reshape(chunk, width))
            if hop == 1 and half == 0:
                own.wait()
                copies[0].wait()
                copies[1].wait()
                arrived(chip)
                forward(chip)
            if hop > 1 and half == 0:
                when_there(chip - hop + 1, chip - hop + 1 >= 0)
            if hop > 1 and half == SUB - 1:
                when_there(chip + hop - 1, chip + hop - 1 < chips)

        def finish():
            last = chips - 1
            when_there(chip - last, chip - last >= 0)
            when_there(chip + last, chip + last < chips)
            copies[3].wait()
            if not early:
                copies[2].wait()
                ring[2]()
                last_all()
            else:
                ring[2](True)
                if place.hops > 2:
                    back_between()
                back_from(place.ring(place.hops))

                def each(at, _):
                    for q in range(place.dps):
                        span = slice(q * chunk, (q + 1) * chunk)
                        grad = dinner[q, at]
                        dgate[at, :, span] = (grad * slope[at, :, span]).astype(jnp.bfloat16)
                        dup[at, :, span] = (grad * silu[at, :, span]).astype(jnp.bfloat16)
                    return 0

                lax.fori_loop(0, chips, each, 0)
            sent()

        def back_between():
            for hop in range(1, place.hops):
                back_from(place.ring(hop))
                back_from(place.ring(-hop))

        def last_all():
            def each(at, _):
                rows = grads[at]
                for first in range(0, held, wide):
                    span = slice(first, first + wide)
                    part = full[first // chunk : (first + wide) // chunk].reshape(wide, width)
                    grad = lax.dot_general(
                        rows, part, contract_cols, preferred_element_type=jnp.float32
                    )
                    dgate[at, :, span] = (grad * slope[at, :, span]).astype(jnp.bfloat16)
                    dup[at, :, span] = (grad * silu[at, :, span]).astype(jnp.bfloat16)
                return 0

            lax.fori_loop(0, chips, each, 0)

        ticks = {
            (hop - 1) * SUB + half: functools.partial(tick, hop, half)
            for hop in range(1, chips)
            for half in range(SUB)
        }

        def with_ring(tick, hop):
            ticks[tick]()
            ring[1](hop)

        def with_near(tick):
            ticks[tick]()
            ring[3]()
            if place.hops == 2:
                back_between()

        merged = dict(ticks)
        for hop in range(1, place.hops):
            merged[2 * hop - 1] = functools.partial(with_ring, 2 * hop - 1, hop)
        if early:
            merged[2 * place.hops - 1] = functools.partial(with_near, 2 * place.hops - 1)
        return start, merged, finish


class Loaded:
    start = wait = staticmethod(lambda: None)


class FeedBack:
    def __init__(self, inner, dgate, dup, gate, up, down, normed, grads, dps, groups):
        length, held = inner.shape
        width, chips = normed.shape[1], groups // 2
        rows = length // groups
        shape = (SUB, rows // SUB, width)
        owned = (2, held // dps // 2, width)
        hops = dps // 2
        tile = (2, SUB, rows // SUB, width)
        self.inputs = [inner, dgate, dup, gate, up, down, normed, grads]
        self.in_specs = [ANY] * 8
        self.outs = [
            jax.ShapeDtypeStruct(shape, jnp.float32),
            jax.ShapeDtypeStruct(owned, jnp.float32),
            jax.ShapeDtypeStruct((held // TILE,) + tile, jnp.bfloat16),
            jax.ShapeDtypeStruct((held // TILE,) + tile, jnp.bfloat16),
            jax.ShapeDtypeStruct((chips,) + tile, jnp.bfloat16),
        ]
        self.out_specs = [VM, VM, ANY, ANY, ANY]
        act = pltpu.VMEM((length, held), jnp.bfloat16)
        weight = pltpu.VMEM((held, width), jnp.bfloat16)
        tokens = pltpu.VMEM((length, width), jnp.bfloat16)
        self.scratch = [act] * 3 + [weight] * 3 + [tokens] * 2
        self.scratch += [
            pltpu.VMEM((groups,) + shape, jnp.bfloat16),
            pltpu.VMEM((dps,) + owned, jnp.bfloat16),
            pltpu.VMEM((2,) + tile, jnp.bfloat16),
            DMA((8,)),
            DMA((2,)),
        ]
        self.scratch += line_scatter_scratch(chips, shape)
        self.scratch += (
            [pltpu.VMEM((hops,) + owned, jnp.bfloat16)] * 2
            + [pltpu.VMEM((hops - 1,) + owned, jnp.bfloat16)] * 2
            + ring_sems(hops)
        )
        self.result = lambda total, mine, gate_term, up_term, out: (
            total.reshape(rows, width),
            mine.reshape(held // dps, width),
            gate_term.reshape(held, width),
            up_term.reshape(held, width),
            out.reshape(length, width),
        )

    def bind(self, place, *refs):
        sources, refs = refs[:8], refs[8:]
        total_ref, own_ref, gate_out, up_out, result_out = refs[:5]
        inner, dgate, dup, gate, up, down, normed, grads = refs[5:13]
        p_ref, term, stage, loads, stage_sem = refs[13:18]
        line_refs, ring_refs = refs[18:27], refs[27:]
        chip, chips, hops = place.chip, place.chips, place.hops
        held, width = gate.shape
        pair = (inner.shape[0] if len(inner.shape) == 2 else inner.shape[0] * inner.shape[1]) // chips

        def flat(ref, lanes):
            value = ref[(slice(None),) * (len(ref.shape) - 1) + (lanes,)]
            return value.reshape(-1, value.shape[-1])

        chunk = held // place.dps
        wide = 1024 if width % 1024 == 0 else width
        send, step, finish_line = line_scatter(place, p_ref, total_ref, *line_refs)

        def put(half, value):
            own_ref[half] = value

        ring = ring_scatter(place, lambda at, half: term.at[at, half], put, *ring_refs)
        targets = [inner, dgate, dup, gate, up, down, normed, grads]
        copies = [
            pltpu.make_async_copy(source, target, loads.at[i])
            for i, (source, target) in enumerate(zip(sources, targets))
            if source is not None
        ] or [Loaded] * len(targets)

        def start():
            for i in (0, 7, 1, 3, 2, 4, 6, 5):
                copies[i].start()

        def rows_of(ref, at):
            if len(ref.shape) == 3:
                return ref[at]
            return ref[pl.ds(pl.multiple_of(at * pair, pair), pair), :]

        def partial(at):
            left, right = rows_of(dgate, at), rows_of(dup, at)
            for first in range(0, width, wide):
                span = slice(first, first + wide)
                value = jnp.dot(left, gate[:, span], preferred_element_type=jnp.float32)
                value += jnp.dot(right, up[:, span], preferred_element_type=jnp.float32)
                p_ref[pl.ds(2 * at, 2), :, :, span] = value.astype(jnp.bfloat16).reshape(
                    p_ref[pl.ds(2 * at, 2), :, :, span].shape
                )
            send(at)

        def term_rows(ref, other, start, count, span):
            return lax.dot_general(
                flat(ref, pl.ds(start, count)),
                flat(other, span),
                contract_rows,
                preferred_element_type=jnp.float32,
            ).astype(jnp.bfloat16)

        def down_tile(at):
            if chunk % 128 == 0:
                for first in range(0, width, wide):
                    span = slice(first, first + wide)
                    value = term_rows(inner, grads, pl.multiple_of(at * chunk, chunk), chunk, span)
                    term[at, :, :, span] = value.reshape(2, chunk // 2, wide)

        def down_all():
            if chunk % 128 != 0:
                for row in range(0, held, TILE):
                    for first in range(0, width, wide):
                        span = slice(first, first + wide)
                        value = term_rows(inner, grads, row, TILE, span)
                        term[row // chunk : (row + TILE) // chunk, :, :, span] = value.reshape(
                            TILE // chunk, 2, chunk // 2, wide
                        )

        jobs = []

        def first_job():
            copies[0].wait()
            copies[7].wait()
            down_all()
            down_tile(place.ring(hops))
            ring[3]()

        def next_job(hop):
            down_tile(place.ring(hop))
            down_tile(place.ring(-hop))
            if hop == hops - 1:
                ring[4]()

        for hop in range(hops - 1, 0, -1):
            jobs.append(functools.partial(next_job, hop))
            jobs.append(functools.partial(ring[1], hop))
        jobs.append(lambda: down_tile(place.d))

        count = [0]
        waits = []

        def staged(value_of, target):
            slot = count[0] % 2
            if count[0] >= 2:
                waits[count[0] - 2].wait()
            value_of(stage.at[slot])
            copy = pltpu.make_async_copy(stage.at[slot], target, stage_sem.at[slot])
            copy.start()
            waits.append(copy)
            count[0] += 1

        def weight_tile(ref, row, out):
            def fill(slot):
                for first in range(0, width, wide):
                    span = slice(first, first + wide)
                    value = term_rows(ref, normed, row, TILE, span)
                    slot[:, :, :, span] = value.reshape(slot.shape[:3] + (wide,))

            staged(fill, out.at[row // TILE])

        def result_tile(at):
            def fill(slot):
                left = rows_of(inner, at)
                for first in range(0, width, wide):
                    span = slice(first, first + wide)
                    value = jnp.dot(left, flat(down, span), preferred_element_type=jnp.float32)
                    slot[:, :, :, span] = value.astype(jnp.bfloat16).reshape(
                        slot.shape[:3] + (wide,)
                    )

            staged(fill, result_out.at[at])

        def sequence():
            first_job()
            for i in (1, 3, 2, 4):
                copies[i].wait()
            tiles = [
                functools.partial(weight_tile, ref, row, out)
                for ref, out in ((dgate, gate_out), (dup, up_out))
                for row in range(0, held, TILE)
            ]
            tiles += [functools.partial(result_tile, at) for at in range(chips)]
            done = [0]

            def fill(most):
                for _ in range(most):
                    if tiles:
                        if done[0] == 0:
                            copies[6].wait()
                        if done[0] == 2 * (held // TILE):
                            copies[5].wait()
                        done[0] += 1
                        tiles.pop(0)()

            for wave in range(chips - 1):
                high = chips - 1 - wave
                ups = (high > chip).astype(jnp.int32)
                downs = (wave < chip).astype(jnp.int32)

                def each(i, _, high=high, wave=wave, ups=ups):
                    partial(jnp.where(i < ups, high, wave))
                    return 0

                lax.fori_loop(0, ups + downs, each, 0)
                fill(1)
                step(wave, 0)
                if wave == 0:
                    step(wave, 1)
                    jobs.pop(0)()
                else:
                    fill(1)
                    step(wave, 1)
                    if jobs:
                        jobs.pop(0)()
            partial(chip)
            for job in jobs:
                job()
            fill(len(tiles))

        def finish():
            ring[2]()
            finish_line()
            for copy in waits[-2:]:
                copy.wait()

        return start, {0: sequence}, finish


class Feed:
    def __init__(self, normed, down, gate, up, grad_all, dps, groups):
        forth = FeedForward(normed, down, gate, up, grad_all, dps, groups)
        act = jax.ShapeDtypeStruct((grad_all.shape[0], gate.shape[0]), jnp.bfloat16)
        back = FeedBack(act, act, act, gate, up, gate, grad_all, grad_all, dps, groups)
        self.forth, self.back = forth, back
        self.inputs, self.in_specs = forth.inputs, forth.in_specs
        self.outs, self.out_specs, self.result = back.outs, back.out_specs, back.result
        self.scratch = [pltpu.VMEM(out.shape, out.dtype) for out in forth.outs]
        self.scratch += forth.scratch[:3] + forth.scratch[6:] + back.scratch[12:]

    def bind(self, place, *refs):
        inputs, outs, held, refs = refs[:5], refs[5:10], refs[10:18], refs[18:]
        hn, full, inner, dgate, dup, gate, up, grads = held
        split = len(self.forth.scratch) - 6
        forth_sems, back_refs = refs[:split], refs[split:]

        def run_forth(*local):
            start, ticks, finish = self.forth.bind(place, *inputs, *held, *local, *forth_sems)
            start()
            for tick in sorted(ticks):
                ticks[tick]()
            finish()

        def run_back(*local):
            shared = (inner, dgate, dup, gate, up, full, hn, grads)
            _, ticks, finish = self.back.bind(
                place, *[None] * 8, *outs, *shared, *local, None, *back_refs
            )
            ticks[0]()
            finish()

        def run():
            pl.run_scoped(run_forth, *self.forth.scratch[3:6])
            pl.run_scoped(run_back, *self.back.scratch[8:11])

        return lambda: None, {0: run}, lambda: None


def move(parts, dps, groups, number, greet=greet_near):
    def kernel(*refs):
        place = Place(dps, groups)
        at = [
            0,
            sum(len(part.inputs) for part in parts),
            sum(len(part.inputs) + len(part.outs) for part in parts),
        ]
        bound = []
        for part in parts:
            mine = []
            for kind, length in enumerate((len(part.inputs), len(part.outs), len(part.scratch))):
                mine += refs[at[kind] : at[kind] + length]
                at[kind] += length
            bound.append(part.bind(place, *mine))
        greet(place)
        for start, _, _ in bound:
            start()
        for tick in range(1 + max([0] + [max(list(ticks) + [0]) for _, ticks, _ in bound])):
            for _, ticks, _ in bound:
                if tick in ticks:
                    ticks[tick]()
        for _, _, finish in bound:
            finish()

    outs = pl.pallas_call(
        kernel,
        out_shape=[out for part in parts for out in part.outs],
        in_specs=[spec for part in parts for spec in part.in_specs],
        out_specs=[spec for part in parts for spec in part.out_specs],
        scratch_shapes=[one for part in parts for one in part.scratch],
        compiler_params=pltpu.CompilerParams(
            collective_id=number, has_side_effects=True, vmem_limit_bytes=63 << 20
        ),
        cost_estimate=pl.CostEstimate(flops=0, bytes_accessed=120_000_000, transcendentals=0),
        name=f"move_{number}",
    )(*[x for part in parts for x in part.inputs])
    results, at = [], 0
    for part in parts:
        results.append(part.result(*outs[at : at + len(part.outs)]))
        at += len(part.outs)
    return results


def norm_factor(values):
    return lax.rsqrt(jnp.mean(values * values, axis=-1, keepdims=True) + epsilon)


def norm_grad(values, factor, gain, gradient):
    weighted = gradient * gain
    inner_mean = jnp.mean(weighted * values, axis=-1, keepdims=True)
    return factor * weighted - values * (factor * factor * factor) * inner_mean


def rope_tables(positions, head_width):
    half_width = head_width // 2
    frequency = rope_base ** (-2.0 * jnp.arange(half_width, dtype=jnp.float32) / head_width)
    angles = positions.astype(jnp.float32)[:, None] * frequency[None, :]
    return (jnp.cos(angles)[:, None, :], jnp.sin(angles)[:, None, :])


def rotate(values, cosine_table, sine_table):
    half_width = values.shape[-1] // 2
    first_half = values[..., :half_width]
    second_half = values[..., half_width:]
    return jnp.concatenate(
        [
            first_half * cosine_table - second_half * sine_table,
            second_half * cosine_table + first_half * sine_table,
        ],
        axis=-1,
    )


def block_scores(query_block, key_heads, lower, upper, score_scale):
    scores = (
        jnp.einsum(
            "qhd,kd->hqk", query_block, key_heads[:upper], preferred_element_type=jnp.float32
        )
        * score_scale
    )
    rows_at = lower + jnp.arange(query_block.shape[0], dtype=jnp.int32)
    cols_at = jnp.arange(upper, dtype=jnp.int32)
    allowed = (cols_at[None, :] <= rows_at[:, None])[None]
    return jnp.where(allowed, scores, masked_value)


def per_device(
    tokens,
    qkv_weight,
    out_weight,
    gate_weight,
    up_weight,
    down_weight,
    attn_gain,
    mlp_gain,
    cotangent,
):
    groups = lax.axis_size("seq")
    dps = lax.axis_size("dp")
    tok_rows = tokens.shape[1]
    model_width = tokens.shape[2]
    weight_rows = qkv_weight.shape[0]
    seq_len = tok_rows * groups
    local_heads = HEADS // groups
    local_width = local_heads * HEAD_DIM
    kv_copies = groups // KV_HEADS
    score_scale = HEAD_DIM ** (-0.5)
    block_rows = min(512, seq_len)
    block_count = seq_len // block_rows
    fold = groups // dps
    order = [(at % dps) * fold + at // dps for at in range(groups)]

    q_part = qkv_weight[:, :model_width].reshape(weight_rows, groups, local_width)
    k_part = qkv_weight[:, model_width : model_width + KV_HEADS * HEAD_DIM]
    v_part = qkv_weight[:, model_width + KV_HEADS * HEAD_DIM :]
    k_part = k_part.reshape(weight_rows, KV_HEADS, HEAD_DIM)
    v_part = v_part.reshape(weight_rows, KV_HEADS, HEAD_DIM)
    columns = jnp.stack(
        [
            jnp.concatenate(
                [q_part[:, g], k_part[:, g // kv_copies], v_part[:, g // kv_copies]], axis=1
            )
            for g in order
        ]
    )
    gain_width = attn_gain.shape[0]
    tile = jnp.zeros((8, 128), jnp.float32)
    tile = tile.at[0, :gain_width].set(attn_gain.astype(jnp.float32))
    tile = tile.at[1, :gain_width].set(mlp_gain.astype(jnp.float32))
    qkv_local, out_rows, normed_all, gate_part, gains = move(
        [
            Columns(columns, dps, groups),
            Rows(out_weight, dps, groups),
            LineGather(tokens[0], dps, groups, normed=True),
            RingGather(gate_weight, dps, groups, late=True),
            Spread(tile, False, dps, groups),
        ],
        dps,
        groups,
        1,
        greet_all,
    )
    gain_one = gains[:, 0, :gain_width].reshape(model_width)
    gain_two = gains[:, 1, :gain_width].reshape(model_width)

    x_rows = tokens[0].astype(jnp.float32)
    factor_one = norm_factor(x_rows)
    qkv_gained = (qkv_local.astype(jnp.float32) * gain_one[:, None]).astype(jnp.bfloat16)
    grad_low = cotangent[0]
    grad_low, _ = lax.optimization_barrier((grad_low, gains))
    grad_all = lax.all_gather(grad_low, "seq", axis=0, tiled=True)

    mixed = jnp.dot(normed_all, qkv_gained, preferred_element_type=jnp.float32)
    cosine_table, sine_table = rope_tables(jnp.arange(seq_len, dtype=jnp.int32), HEAD_DIM)
    query_heads = rotate(
        mixed[:, :local_width].reshape(seq_len, local_heads, HEAD_DIM), cosine_table, sine_table
    ).astype(jnp.bfloat16)
    key_heads = rotate(
        mixed[:, None, local_width : local_width + HEAD_DIM], cosine_table, sine_table
    ).astype(jnp.bfloat16)[:, 0]
    value_heads = mixed[:, local_width + HEAD_DIM :].astype(jnp.bfloat16)
    outputs = []
    log_sums = []
    for block in range(block_count):
        lower = block * block_rows
        upper = lower + block_rows
        scores = block_scores(query_heads[lower:upper], key_heads, lower, upper, score_scale)
        highest = jnp.max(scores, axis=-1, keepdims=True)
        log_sum = highest + jnp.log(jnp.sum(jnp.exp(scores - highest), axis=-1, keepdims=True))
        probs = jnp.exp(scores - log_sum).astype(jnp.bfloat16)
        attended = jnp.einsum(
            "hqk,kd->qhd", probs, value_heads[:upper], preferred_element_type=jnp.float32
        )
        outputs.append(attended.astype(jnp.bfloat16))
        log_sums.append(log_sum)
    attended = jnp.concatenate(outputs, axis=0).reshape(seq_len, local_width)
    up_part, summed = move(
        [
            RingGather(up_weight, dps, groups),
            LineProduct(attended, out_rows, (((1,), (0,)), ((), ())), dps, groups),
        ],
        dps,
        groups,
        2,
    )
    hidden = x_rows + summed
    factor_two = norm_factor(hidden)
    normed_two = (hidden * factor_two * gain_two).astype(jnp.bfloat16)
    ((grad_normed, down_owned, gate_term, up_term, result),) = move(
        [Feed(normed_two, down_weight, gate_part, up_part, grad_all, dps, groups)],
        dps,
        groups,
        3,
    )
    gain_two_term = jnp.sum(grad_normed * hidden * factor_two, axis=0)
    grad_hidden = grad_low.astype(jnp.float32) + norm_grad(
        hidden, factor_two, gain_two, grad_normed
    )
    grad_branch, gate_owned = move(
        [
            LineGather(grad_hidden.astype(jnp.bfloat16), dps, groups),
            RingScatter(gate_term, dps, groups),
        ],
        dps,
        groups,
        5,
    )
    result, grad_branch = lax.optimization_barrier((result, grad_branch))
    mlp_result = lax.psum_scatter(result, "seq", scatter_dimension=0, tiled=True)
    block_out = (hidden + mlp_result.astype(jnp.float32)).astype(jnp.bfloat16)[None]
    out_term = lax.dot_general(
        attended, grad_branch, contract_rows, preferred_element_type=jnp.float32
    ).astype(jnp.bfloat16)
    grad_heads = (
        lax.dot_general(grad_branch, out_rows, contract_cols, preferred_element_type=jnp.float32)
        .astype(jnp.bfloat16)
        .reshape(seq_len, local_heads, HEAD_DIM)
    )
    grad_keys = jnp.zeros((seq_len, HEAD_DIM), jnp.float32)
    grad_values = jnp.zeros((seq_len, HEAD_DIM), jnp.float32)
    grad_queries = []
    for block in range(block_count):
        lower = block * block_rows
        upper = lower + block_rows
        query_block = query_heads[lower:upper]
        grad_block = grad_heads[lower:upper]
        scores = block_scores(query_block, key_heads, lower, upper, score_scale)
        probs = jnp.exp(scores - log_sums[block])
        probs_low = probs.astype(jnp.bfloat16)
        grad_probs = jnp.einsum(
            "qhd,kd->hqk", grad_block, value_heads[:upper], preferred_element_type=jnp.float32
        )
        row_delta = jnp.sum(probs * grad_probs, axis=-1, keepdims=True)
        grad_scores = (probs * (grad_probs - row_delta)).astype(jnp.bfloat16)
        grad_queries.append(
            jnp.einsum(
                "hqk,kd->qhd", grad_scores, key_heads[:upper], preferred_element_type=jnp.float32
            )
            * score_scale
        )
        grad_keys = grad_keys.at[:upper].add(
            jnp.einsum("hqk,qhd->kd", grad_scores, query_block, preferred_element_type=jnp.float32)
            * score_scale
        )
        grad_values = grad_values.at[:upper].add(
            jnp.einsum("hqk,qhd->kd", probs_low, grad_block, preferred_element_type=jnp.float32)
        )
    grad_q = rotate(jnp.concatenate(grad_queries, axis=0), cosine_table, -sine_table)
    grad_k = rotate(grad_keys[:, None], cosine_table, -sine_table)[:, 0]
    grad_mixed = jnp.concatenate(
        [grad_q.reshape(seq_len, local_width), grad_k, grad_values], axis=1
    ).astype(jnp.bfloat16)
    qkv_term = lax.dot_general(
        normed_all, grad_mixed, contract_rows, preferred_element_type=jnp.float32
    )
    partial = lax.dot_general(
        grad_mixed, qkv_local, contract_cols, preferred_element_type=jnp.float32
    )
    gain_one_term = jnp.sum(qkv_term * qkv_local.astype(jnp.float32), axis=1)
    qkv_term = (qkv_term * gain_one[:, None]).astype(jnp.bfloat16)
    terms = jnp.stack([gain_one_term, gain_two_term]).reshape(2, dps * groups, gain_width)
    terms = jnp.pad(terms.transpose(1, 0, 2), ((0, 0), (0, 6), (0, 128 - gain_width)))
    qkv_owned, out_owned, grad_normed_one, up_owned, gain_grads = move(
        [
            ColumnsBack(qkv_term, order, local_width, kv_copies, weight_rows, dps, groups),
            RowsBack(out_term, weight_rows, dps, groups),
            LineScatter(partial.astype(jnp.bfloat16), dps, groups),
            RingScatter(up_term, dps, groups, late=True),
            Spread(terms, True, dps, groups),
        ],
        dps,
        groups,
        6,
        greet_all,
    )
    grad_input = grad_hidden + norm_grad(x_rows, factor_one, gain_one, grad_normed_one)
    return (
        block_out,
        grad_input[None],
        qkv_owned,
        out_owned,
        gate_owned,
        up_owned,
        down_owned,
        gain_grads[0, :gain_width],
        gain_grads[1, :gain_width],
    )


def solution(mesh):
    rows = P(("dp", "seq"), None)
    tokens = P("dp", "seq", None)
    gains = P(("dp", "seq"))
    return jax.shard_map(
        per_device,
        mesh=mesh,
        in_specs=(tokens, rows, rows, rows, rows, rows, gains, gains, tokens),
        out_specs=(tokens, tokens, rows, rows, rows, rows, rows, gains, gains),
        check_vma=False,
    )
```

```python
import functools

import jax
import jax.numpy as jnp
from jax import lax
from jax.experimental import pallas as pl
from jax.experimental.pallas import tpu as pltpu
from jax.sharding import PartitionSpec as P

HEADS = 32
KV_HEADS = 8
HEAD_DIM = 64

MESH = pl.DeviceIdType.MESH
ANY = pl.BlockSpec(memory_space=pl.ANY)
VM = pl.BlockSpec(memory_space=pltpu.VMEM)
SUB = 2

epsilon = 1e-05
rope_base = 500000.0
masked_value = -1e30
contract_rows = (((0,), (0,)), ((), ()))
contract_cols = (((1,), (1,)), ((), ()))


class Place:
    def __init__(self, dps, groups):
        self.dps, self.groups, self.chips, self.hops = dps, groups, groups // 2, dps // 2
        self.d, self.s = lax.axis_index("dp"), lax.axis_index("seq")
        self.chip, self.core = self.s // 2, self.s % 2
        self.partner = 2 * self.chip + 1 - self.core
        row, side = self.d // 2, self.d % 2
        self.turn = side * (dps - 1 - row) + (1 - side) * row

    def ring(self, distance):
        at = (self.turn + distance + self.dps) % self.dps
        side = at // self.hops
        return (1 - side) * 2 * at + side * (2 * (self.dps - 1 - at) + 1)


def remote(src, dst, send, recv, **target):
    return pltpu.make_async_remote_copy(
        src_ref=src, dst_ref=dst, send_sem=send, recv_sem=recv, device_id=target, device_id_type=MESH
    )


def greet_near(place):
    barrier = pltpu.get_barrier_semaphore()

    def signal(**target):
        pl.semaphore_signal(barrier, inc=1, device_id=target, device_id_type=MESH)

    signal(seq=place.partner)
    signal(dp=place.ring(1))
    signal(dp=place.ring(-1))

    @pl.when(place.chip > 0)
    def _():
        signal(seq=place.s - 2)

    @pl.when(place.chip < place.chips - 1)
    def _():
        signal(seq=place.s + 2)

    ends = (place.chips - place.chip) // place.chips + (place.chip + 1) // place.chips
    pl.semaphore_wait(barrier, 5 - ends)


def greet_all(place):
    barrier = pltpu.get_barrier_semaphore()
    count = place.dps * place.groups
    me = place.d * place.groups + place.s

    def signal(i, _):
        other = (me + i) % count
        pl.semaphore_signal(
            barrier,
            inc=1,
            device_id={"dp": other // place.groups, "seq": other % place.groups},
            device_id_type=MESH,
        )
        return 0

    lax.fori_loop(1, count, signal, 0)
    pl.semaphore_wait(barrier, count - 1)


DMA = pltpu.SemaphoreType.DMA


def line_gather(place, x_ref, out_ref, own_sem, us, ur, ds, dr, ps, pr):
    s, chip, chips = place.s, place.chip, place.chips

    def copy(src, group, half, sends, recvs, at, target):
        return remote(
            src, out_ref.at[group, half], sends.at[at, half], recvs.at[at, half], seq=target
        )

    def up(src, group, hop, half):
        return copy(src, group, half, us, ur, hop, s + 2)

    def down(src, group, hop, half):
        return copy(src, group, half, ds, dr, hop, s - 2)

    def pair(src, group, half):
        return copy(src, group, half, ps, pr, group // 2, place.partner)

    own = pltpu.make_async_copy(x_ref, out_ref.at[s], own_sem)

    def start():
        own.start()
        for half in range(SUB):

            @pl.when(chip < chips - 1)
            def _():
                up(x_ref.at[half], s, 0, half).start()

            @pl.when(chip > 0)
            def _():
                down(x_ref.at[half], s, 0, half).start()

        for half in range(SUB):
            pair(x_ref.at[half], s, half).start()

    def step(hop, half):
        below, above = s - 2 * hop, s + 2 * hop

        @pl.when(chip - hop >= 0)
        def _():
            block = out_ref.at[below, half]
            up(block, below, hop - 1, half).wait_recv()

            @pl.when(chip < chips - 1)
            def _():
                up(block, below, hop, half).start()

            pair(block, below, half).start()

        @pl.when(chip + hop < chips)
        def _():
            block = out_ref.at[above, half]
            down(block, above, hop - 1, half).wait_recv()

            @pl.when(chip > 0)
            def _():
                down(block, above, hop, half).start()

            pair(block, above, half).start()

    def arrived(at):
        for half in range(SUB):
            group = 2 * at + 1 - place.core
            pair(out_ref.at[group, half], group, half).wait_recv()

    def sent():
        def each(i, _):
            k, half = i // SUB, i % SUB
            mine = 2 * k + place.core
            block = out_ref.at[mine, half]
            pair(block, mine, half).wait_send()

            @pl.when(jnp.logical_and(chip - k >= 0, chip < chips - 1))
            def _():
                up(block, mine, k, half).wait_send()

            @pl.when(jnp.logical_and(chip + k < chips, chip > 0))
            def _():
                down(block, mine, k, half).wait_send()

            return 0

        lax.fori_loop(0, chips * SUB, each, 0)

    return own, start, step, arrived, sent


class LineGather:
    def __init__(self, x, dps, groups, normed=False):
        rows, width = x.shape
        shape = (SUB, rows // SUB, width)
        self.normed = normed
        self.inputs, self.in_specs = [x.reshape(shape)], [VM]
        self.outs, self.out_specs = [jax.ShapeDtypeStruct((groups,) + shape, x.dtype)], [ANY]
        self.scratch = [DMA] + [DMA((groups // 2, SUB))] * 6
        if normed:
            self.scratch = [pltpu.VMEM(shape, x.dtype)] + self.scratch
        self.result = lambda out: out.reshape(groups * rows, width)

    def bind(self, place, x_ref, out_ref, *refs):
        if self.normed:
            source, x_ref, refs = x_ref, refs[0], refs[1:]
            many = 16 if x_ref.shape[1] % 16 == 0 else x_ref.shape[1]

            def norm(i, _):
                span = pl.ds(pl.multiple_of(i * many, many), many)
                for half in range(SUB):
                    values = source[half, span, :].astype(jnp.float32)
                    x_ref[half, span, :] = (values * norm_factor(values)).astype(x_ref.dtype)
                return 0

            lax.fori_loop(0, x_ref.shape[1] // many, norm, 0)
        own, start, step, arrived, sent = line_gather(place, x_ref, out_ref, *refs)

        def finish():
            own.wait()

            def each(at, _):
                arrived(at)
                return 0

            lax.fori_loop(0, place.chips, each, 0)
            sent()

        ticks = {
            (hop - 1) * SUB + half: functools.partial(step, hop, half)
            for hop in range(1, place.chips)
            for half in range(SUB)
        }
        return start, ticks, finish


def line_scatter(place, p_ref, out_ref, pairbuf, upbuf, downbuf, us, ur, ds, dr, ps, pr):
    s, chip, chips, core = place.s, place.chip, place.chips, place.core

    def copy(src, buffer, at, half, sends, recvs, target):
        return remote(src, buffer.at[at, half], sends.at[at, half], recvs.at[at, half], seq=target)

    def pair(at, half):
        src = p_ref.at[2 * at + 1 - core, half]
        return copy(src, pairbuf, at, half, ps, pr, place.partner)

    def up(at, half):
        return copy(upbuf.at[at, half], upbuf, at, half, us, ur, s + 2)

    def down(at, half):
        return copy(downbuf.at[at, half], downbuf, at, half, ds, dr, s - 2)

    def wide(ref, *at):
        return ref[at].astype(jnp.float32)

    def local(at, half):
        return wide(p_ref, 2 * at + core, half) + wide(pairbuf, at, half)

    def send(at):
        for half in range(SUB):
            pair(at, half).start()

    def step(wave, half):
        high, low = chips - 1 - wave + chip, wave - (chips - 1 - chip)

        @pl.when(chip <= wave)
        def _():
            pair(high, half).wait_recv()

            @pl.when(chip > 0)
            def _():
                up(high, half).wait_recv()
                total = local(high, half) + wide(upbuf, high, half)
                upbuf[high, half] = total.astype(jnp.bfloat16)

            @pl.when(chip == 0)
            def _():
                upbuf[high, half] = local(high, half).astype(jnp.bfloat16)

            up(high, half).start()

        @pl.when(low >= 0)
        def _():
            pair(low, half).wait_recv()

            @pl.when(chip < chips - 1)
            def _():
                down(low, half).wait_recv()
                total = local(low, half) + wide(downbuf, low, half)
                downbuf[low, half] = total.astype(jnp.bfloat16)

            @pl.when(chip == chips - 1)
            def _():
                downbuf[low, half] = local(low, half).astype(jnp.bfloat16)

            down(low, half).start()

    def finish():
        for half in range(SUB):
            pair(chip, half).wait_recv()
            out_ref[half] = local(chip, half)

            @pl.when(chip > 0)
            def _():
                up(chip, half).wait_recv()
                out_ref[half] += wide(upbuf, chip, half)

            @pl.when(chip < chips - 1)
            def _():
                down(chip, half).wait_recv()
                out_ref[half] += wide(downbuf, chip, half)

        def each(i, _):
            at, half = i // SUB, i % SUB
            pair(at, half).wait_send()

            @pl.when(at > chip)
            def _():
                up(at, half).wait_send()

            @pl.when(at < chip)
            def _():
                down(at, half).wait_send()

            return 0

        lax.fori_loop(0, chips * SUB, each, 0)

    return send, step, finish


def line_scatter_scratch(chips, shape):
    return [pltpu.VMEM((chips,) + shape, jnp.bfloat16)] * 3 + [DMA((chips, SUB))] * 6


class LineScatter:
    def __init__(self, partial, dps, groups):
        total, width = partial.shape
        rows = total // groups
        shape = (SUB, rows // SUB, width)
        self.inputs, self.in_specs = [partial.reshape((groups,) + shape)], [VM]
        self.outs, self.out_specs = [jax.ShapeDtypeStruct(shape, jnp.float32)], [VM]
        self.scratch = line_scatter_scratch(groups // 2, shape)
        self.result = lambda out: out.reshape(rows, width)

    def bind(self, place, *refs):
        send, step, finish = line_scatter(place, *refs)
        chip, chips = place.chip, place.chips

        def start():
            def issue(low, _):
                high = chips - 1 - low

                @pl.when(high > chip)
                def _():
                    send(high)

                @pl.when(low < chip)
                def _():
                    send(low)

                return 0

            lax.fori_loop(0, chips - 1, issue, 0)
            send(chip)

        ticks = {
            i: functools.partial(step, i // SUB, i % SUB) for i in range((chips - 1) * SUB)
        }
        return start, ticks, finish


class LineProduct:
    def __init__(self, left, right, dims, dps, groups):
        total, inner = left.shape
        width = right.shape[1 - dims[0][1][0]]
        rows, chips = total // groups, groups // 2
        shape = (SUB, rows // SUB, width)
        self.dims = dims
        self.inputs, self.in_specs = [left.reshape(chips, 2 * rows, inner), right], [VM, VM]
        self.outs, self.out_specs = [jax.ShapeDtypeStruct(shape, jnp.float32)], [VM]
        self.scratch = [pltpu.VMEM((groups,) + shape, jnp.bfloat16)]
        self.scratch += line_scatter_scratch(chips, shape)
        self.result = lambda out: out.reshape(rows, width)

    def bind(self, place, left, right, out_ref, p_ref, *refs):
        send, step, finish = line_scatter(place, p_ref, out_ref, *refs)
        chip, chips = place.chip, place.chips
        width = p_ref.shape[3]
        wide = 512 if width % 512 == 0 else width

        def partial(at):
            for first in range(0, width, wide):
                span = slice(first, first + wide)
                part = right[:, span] if self.dims[0][1][0] == 0 else right[span, :]
                value = lax.dot_general(
                    left[at], part, self.dims, preferred_element_type=jnp.float32
                )
                p_ref[pl.ds(2 * at, 2), :, :, span] = value.astype(jnp.bfloat16).reshape(
                    (2,) + p_ref.shape[1:3] + (wide,)
                )
            send(at)

        def partials(wave):
            if wave == chips - 1:
                partial(chip)
                return

            @pl.when(chips - 1 - wave > chip)
            def _():
                partial(chips - 1 - wave)

            @pl.when(wave < chip)
            def _():
                partial(wave)

        def tick(wave, half):
            step(wave, half)
            if half == SUB - 1:
                partials(wave + 1)

        ticks = {
            i: functools.partial(tick, i // SUB, i % SUB) for i in range((chips - 1) * SUB)
        }
        return lambda: partials(0), ticks, finish


def ring_sems(hops):
    return [DMA((hops, 2))] * 4


def ring_gather(place, own, out, rs, rr, ls, lr):
    hops = place.hops

    def right(src, chunk, hop, half):
        return remote(
            src, out(chunk, half), rs.at[hop - 1, half], rr.at[hop - 1, half], dp=place.ring(1)
        )

    def left(src, chunk, hop, half):
        return remote(
            src, out(chunk, half), ls.at[hop - 1, half], lr.at[hop - 1, half], dp=place.ring(-1)
        )

    def begin(half):
        right(own(half), place.d, 1, half).start()
        left(own(1 - half), place.d, 1, 1 - half).start()

    def start():
        begin(0)
        begin(1)

    def forward(hop):
        before, after = place.ring(-hop), place.ring(hop)
        full = hop < hops - 1
        right(out(before, 0), before, hop, 0).wait_recv()
        right(out(before, 0), before, hop + 1, 0).start()
        left(out(after, 1), after, hop, 1).wait_recv()
        left(out(after, 1), after, hop + 1, 1).start()
        if full:
            right(out(before, 1), before, hop, 1).wait_recv()
            left(out(after, 0), after, hop, 0).wait_recv()
            right(out(before, 1), before, hop + 1, 1).start()
            left(out(after, 0), after, hop + 1, 0).start()

    def near():
        before, after = place.ring(1 - hops), place.ring(hops - 1)
        right(out(before, 1), before, hops - 1, 1).wait_recv()
        left(out(after, 0), after, hops - 1, 0).wait_recv()

    def finish(waited=False):
        if not waited:
            near()
        right(out(place.d, 0), place.ring(-hops), hops, 0).wait_recv()
        left(out(place.d, 1), place.ring(hops), hops, 1).wait_recv()
        for hop in range(1, hops + 1):
            for half in range(2):
                if hop < hops or half == 0:
                    right(out(place.d, half), place.d, hop, half).wait_send()
                if hop < hops or half == 1:
                    left(out(place.d, half), place.d, hop, half).wait_send()

    return start, forward, finish, near, begin


def ring_scatter(place, part, put, rbuf, lbuf, rout, lout, rs, rr, ls, lr):
    hops = place.hops

    def wide(ref):
        return ref[...].astype(jnp.float32)

    def right(src, hop, half):
        return remote(
            src,
            rbuf.at[hop - 1, half],
            rs.at[hop - 1, half],
            rr.at[hop - 1, half],
            dp=place.ring(1),
        )

    def left(src, hop, half):
        return remote(
            src,
            lbuf.at[hop - 1, half],
            ls.at[hop - 1, half],
            lr.at[hop - 1, half],
            dp=place.ring(-1),
        )

    def start_far():
        right(part(place.ring(hops), 0), hops, 0).start()
        left(part(place.ring(-hops), 1), hops, 1).start()

    def start_next():
        right(part(place.ring(hops - 1), 1), hops - 1, 1).start()
        left(part(place.ring(1 - hops), 0), hops - 1, 0).start()

    def start():
        start_far()
        start_next()

    def forward(hop):
        for first in range(2 if hop < hops - 1 else 1):
            half = first
            right(rbuf.at[hop, half], hop + 1, half).wait_recv()
            total = wide(part(place.ring(hop), half)) + wide(rbuf.at[hop, half])
            rout[hop - 1, half] = total.astype(jnp.bfloat16)
            right(rout.at[hop - 1, half], hop, half).start()
            half = 1 - first
            left(lbuf.at[hop, half], hop + 1, half).wait_recv()
            total = wide(part(place.ring(-hop), half)) + wide(lbuf.at[hop, half])
            lout[hop - 1, half] = total.astype(jnp.bfloat16)
            left(lout.at[hop - 1, half], hop, half).start()

    def finish():
        for half in range(2):
            right(rbuf.at[0, half], 1, half).wait_recv()
            left(lbuf.at[0, half], 1, half).wait_recv()
            put(
                half,
                wide(part(place.d, half)) + wide(rbuf.at[0, half]) + wide(lbuf.at[0, half]),
            )
        for hop in range(1, hops + 1):
            for half in range(2):
                if hop < hops or half == 0:
                    right(rbuf.at[0, half], hop, half).wait_send()
                if hop < hops or half == 1:
                    left(lbuf.at[0, half], hop, half).wait_send()

    return start, forward, finish, start_far, start_next


class RingGather:
    def __init__(self, x, dps, groups, late=False):
        self.late = late
        rows, width = x.shape
        shape = (2, rows // 2, width)
        self.inputs, self.in_specs = [x.reshape(shape)], [VM]
        self.outs, self.out_specs = [jax.ShapeDtypeStruct((dps,) + shape, x.dtype)], [ANY]
        self.scratch = [DMA] + ring_sems(dps // 2)
        self.result = lambda out: out.reshape(dps * rows, width)

    def bind(self, place, x_ref, out_ref, own_sem, *sems):
        own = pltpu.make_async_copy(x_ref, out_ref.at[place.d], own_sem)
        ring = ring_gather(
            place, lambda half: x_ref.at[half], lambda chunk, half: out_ref.at[chunk, half], *sems
        )

        def start():
            ring[4](0)
            if not self.late:
                ring[4](1)
            own.start()

        def second():
            ring[4](1)
            ring[1](1)

        def finish():
            own.wait()
            ring[2]()

        ticks = {2 * hop - 1: functools.partial(ring[1], hop) for hop in range(1, place.hops)}
        if self.late:
            ticks[1] = second
        return start, ticks, finish


class RingScatter:
    def __init__(self, partial, dps, groups, late=False):
        self.late = late
        total, width = partial.shape
        rows, hops = total // dps, dps // 2
        shape = (2, rows // 2, width)
        self.inputs, self.in_specs = [partial.reshape((dps,) + shape)], [VM]
        self.outs, self.out_specs = [jax.ShapeDtypeStruct(shape, jnp.float32)], [VM]
        self.scratch = (
            [pltpu.VMEM((hops,) + shape, jnp.bfloat16)] * 2
            + [pltpu.VMEM((hops - 1,) + shape, jnp.bfloat16)] * 2
            + ring_sems(hops)
        )
        self.result = lambda out: out.reshape(rows, width)

    def bind(self, place, p_ref, out_ref, *scratch):
        def put(half, value):
            out_ref[half] = value

        ring = ring_scatter(place, lambda chunk, half: p_ref.at[chunk, half], put, *scratch)
        first = 1 if self.late else -1
        ticks = {
            2 * (place.hops - hop) + first: functools.partial(ring[1], hop)
            for hop in range(1, place.hops)
        }
        if self.late:
            ticks[1] = ring[4]
            return ring[3], ticks, ring[2]
        return ring[0], ticks, ring[2]


class Columns:
    def __init__(self, joint, order, heads_width, copies, dps, groups):
        rows, width = joint.shape[0], heads_width + 2 * HEAD_DIM
        self.order, self.heads_width, self.copies = order, heads_width, copies
        self.inputs, self.in_specs = [joint], [VM]
        self.outs = [jax.ShapeDtypeStruct((dps, groups, rows, width), joint.dtype)]
        self.out_specs = [ANY]
        self.scratch = [
            pltpu.VMEM((groups, rows, width), joint.dtype),
            pltpu.VMEM((groups, rows, width), joint.dtype),
            DMA((2,)),
            DMA((groups,)),
            DMA((groups,)),
        ] + ring_sems(dps // 2)
        self.result = lambda out: out.reshape(dps * groups * rows, width)

    def bind(self, place, joint_ref, out_ref, x_ref, landing, own_sem, sends, recvs, *sems):
        s, groups = place.s, place.groups
        half_of = groups // 2
        heads, pair = self.heads_width, 2 * HEAD_DIM

        def pair_of(head, first):
            at = groups * heads + first + head // 2 * pair
            value = joint_ref[:, at : at + pair].astype(jnp.float32)
            return value, pltpu.roll(value, HEAD_DIM, 1)

        for at, g in enumerate(self.order):
            x_ref[at, :, :heads] = joint_ref[:, g * heads : (g + 1) * heads]
            head = g // self.copies
            keys, values = pair_of(head, 0), pair_of(head, KV_HEADS * HEAD_DIM)
            lanes = lax.broadcasted_iota(jnp.int32, keys[0].shape, 1)
            both = jnp.where(lanes < HEAD_DIM, keys[head % 2], values[1 - head % 2])
            x_ref[at, :, heads:] = both.astype(x_ref.dtype)

        here = pltpu.make_async_copy(x_ref.at[s], landing.at[s], own_sem.at[0])
        own = pltpu.make_async_copy(landing, out_ref.at[place.d], own_sem.at[1])

        def swap(i):
            to = (s + i) % groups
            return remote(x_ref.at[to], landing.at[s], sends.at[i], recvs.at[i], seq=to)

        ring = ring_gather(
            place,
            lambda half: landing.at[pl.ds(half * half_of, half_of)],
            lambda chunk, half: out_ref.at[chunk, pl.ds(half * half_of, half_of)],
            *sems,
        )

        def start():
            here.start()
            for i in range(1, groups):
                swap(i).start()

        def middle():
            here.wait()
            for i in range(1, groups):
                swap(i).wait_recv()
            ring[0]()
            own.start()

        def finish():
            for i in range(1, groups):
                swap(i).wait_send()
            own.wait()
            ring[2]()

        ticks = {1 + 2 * hop: functools.partial(ring[1], hop) for hop in range(1, place.hops)}
        ticks[1] = middle
        return start, ticks, finish


class ColumnsBack:
    def __init__(self, partial, order, heads_width, copies, rows, dps, groups):
        width, hops = partial.shape[1], dps // 2
        shape = (groups, rows, width)
        halves = (2, groups // 2, rows, width)
        self.where = [order.index(g) for g in range(groups)]
        self.heads_width, self.copies = heads_width, copies
        joint = groups * heads_width + 2 * KV_HEADS * HEAD_DIM
        self.inputs, self.in_specs = [partial.reshape((dps,) + halves)], [VM]
        self.outs, self.out_specs = [jax.ShapeDtypeStruct((rows, joint), jnp.float32)], [VM]
        self.scratch = (
            [pltpu.VMEM(shape, jnp.bfloat16), pltpu.VMEM(halves, jnp.bfloat16)]
            + [DMA, DMA((groups,)), DMA((groups,))]
            + [pltpu.VMEM((hops,) + halves, jnp.bfloat16)] * 2
            + [pltpu.VMEM((hops - 1,) + halves, jnp.bfloat16)] * 2
            + ring_sems(hops)
        )
        self.result = lambda out: out

    def bind(self, place, p_ref, joint_ref, out_ref, total, own_sem, sends, recvs, *scratch):
        s, groups = place.s, place.groups
        half_of = groups // 2

        def put(half, value):
            total[half] = value.astype(jnp.bfloat16)

        ring = ring_scatter(place, lambda chunk, half: p_ref.at[chunk, half], put, *scratch)
        here = pltpu.make_async_copy(
            total.at[s // half_of, s % half_of], out_ref.at[s], own_sem
        )

        def swap(i):
            to = (s + i) % groups
            src = total.at[to // half_of, to % half_of]
            return remote(src, out_ref.at[s], sends.at[i], recvs.at[i], seq=to)

        def last():
            ring[2]()
            here.start()
            for i in range(1, groups):
                swap(i).start()

        def keys_values(head):
            first = self.where[head * self.copies]
            span = slice(self.heads_width, self.heads_width + 2 * HEAD_DIM)
            value = out_ref[first, :, span].astype(jnp.float32)
            for i in range(1, self.copies):
                value += out_ref[self.where[head * self.copies + i], :, span].astype(jnp.float32)
            return value

        def finish():
            here.wait()
            for i in range(1, groups):
                swap(i).wait_recv()
                swap(i).wait_send()
            heads = self.heads_width
            for g in range(groups):
                value = out_ref[self.where[g], :, :heads]
                joint_ref[:, g * heads : (g + 1) * heads] = value.astype(jnp.float32)
            for head in range(0, KV_HEADS, 2):
                even, odd = keys_values(head), keys_values(head + 1)
                lanes = lax.broadcasted_iota(jnp.int32, even.shape, 1)
                at = groups * heads + head * HEAD_DIM
                joint_ref[:, at : at + 2 * HEAD_DIM] = jnp.where(
                    lanes < HEAD_DIM, even, pltpu.roll(odd, HEAD_DIM, 1)
                )
                at += KV_HEADS * HEAD_DIM
                joint_ref[:, at : at + 2 * HEAD_DIM] = jnp.where(
                    lanes < HEAD_DIM, pltpu.roll(even, HEAD_DIM, 1), odd
                )

        ticks = {
            2 * (place.hops - hop) - 1: functools.partial(ring[1], hop)
            for hop in range(1, place.hops)
        }
        ticks[2 * place.hops - 1] = last
        return ring[0], ticks, finish


class Rows:
    def __init__(self, x, dps, groups):
        rows, width = x.shape
        shape = (2, rows // 2, width)
        self.inputs, self.in_specs = [x.reshape(shape)], [VM]
        self.outs, self.out_specs = [jax.ShapeDtypeStruct((dps,) + shape, x.dtype)], [ANY]
        self.scratch = [
            pltpu.VMEM((dps,) + shape, x.dtype),
            DMA((2,)),
            DMA((dps,)),
            DMA((dps,)),
        ] + ring_sems(dps // 2)
        self.result = lambda out: out.reshape(dps * rows, width)

    def bind(self, place, x_ref, out_ref, landing, own_sem, sends, recvs, *sems):
        s, dps = place.s, place.dps
        slot, base = s % dps, s // dps * dps
        first = pltpu.make_async_copy(x_ref, landing.at[place.d], own_sem.at[0])
        here = pltpu.make_async_copy(landing.at[slot], out_ref.at[slot], own_sem.at[1])
        ring = ring_gather(
            place, lambda half: x_ref.at[half], lambda chunk, half: landing.at[chunk, half], *sems
        )

        def swap(i):
            to = (slot + i) % dps
            return remote(landing.at[to], out_ref.at[slot], sends.at[i], recvs.at[i], seq=base + to)

        def start():
            ring[0]()
            first.start()

        def last():
            first.wait()
            ring[2]()
            here.start()
            for i in range(1, dps):
                swap(i).start()

        def finish():
            here.wait()
            for i in range(1, dps):
                swap(i).wait_recv()
                swap(i).wait_send()

        ticks = {2 * hop - 2: functools.partial(ring[1], hop) for hop in range(1, place.hops)}
        ticks[2 * place.hops - 2] = last
        return start, ticks, finish


class RowsBack:
    def __init__(self, partial, rows, dps, groups):
        width, hops = partial.shape[1], dps // 2
        shape = (2, rows // 2, width)
        self.inputs, self.in_specs = [partial.reshape((dps,) + shape)], [VM]
        self.outs, self.out_specs = [jax.ShapeDtypeStruct(shape, jnp.float32)], [VM]
        self.scratch = (
            [pltpu.VMEM((dps,) + shape, jnp.bfloat16), DMA, DMA((dps,)), DMA((dps,))]
            + [pltpu.VMEM((hops,) + shape, jnp.bfloat16)] * 2
            + [pltpu.VMEM((hops - 1,) + shape, jnp.bfloat16)] * 2
            + ring_sems(hops)
        )
        self.result = lambda out: out.reshape(rows, width)

    def bind(self, place, p_ref, out_ref, landing, own_sem, sends, recvs, *scratch):
        s, dps = place.s, place.dps
        slot, base = s % dps, s // dps * dps
        here = pltpu.make_async_copy(p_ref.at[slot], landing.at[slot], own_sem)

        def swap(i):
            to = (slot + i) % dps
            return remote(p_ref.at[to], landing.at[slot], sends.at[i], recvs.at[i], seq=base + to)

        def put(half, value):
            out_ref[half] = value

        ring = ring_scatter(place, lambda chunk, half: landing.at[chunk, half], put, *scratch)

        def start():
            here.start()
            for i in range(1, dps):
                swap(i).start()

        def middle():
            here.wait()
            for i in range(1, dps):
                swap(i).wait_recv()
            ring[0]()

        def finish():
            for i in range(1, dps):
                swap(i).wait_send()
            ring[2]()

        ticks = {
            2 * (place.hops - hop) + 2: functools.partial(ring[1], hop)
            for hop in range(1, place.hops)
        }
        ticks[2] = middle
        return start, ticks, finish


class Spread:
    def __init__(self, tiles, total, dps, groups):
        count, shape = dps * groups, tiles.shape[-2:]
        self.total = total
        self.inputs, self.in_specs = [tiles], [VM]
        out = shape if total else (count,) + shape
        self.outs, self.out_specs = [jax.ShapeDtypeStruct(out, jnp.float32)], [VM]
        self.scratch = [pltpu.VMEM((count,) + shape, jnp.float32), DMA((count,)), DMA((count,))]
        self.result = lambda out: out

    def bind(self, place, x_ref, out_ref, landing, sends, recvs):
        count = place.dps * place.groups
        me = place.d * place.groups + place.s

        def copy(i):
            other = (me + i) % count
            return remote(
                x_ref.at[other] if self.total else x_ref,
                landing.at[me],
                sends.at[i],
                recvs.at[i],
                dp=other // place.groups,
                seq=other % place.groups,
            )

        def start():
            def each(i, _):
                copy(i).start()
                return 0

            lax.fori_loop(1, count, each, 0)

        def finish():
            def each(i, _):
                copy(i).wait_recv()
                copy(i).wait_send()
                return 0

            lax.fori_loop(1, count, each, 0)
            landing[me] = x_ref[me] if self.total else x_ref[...]
            out_ref[...] = jnp.sum(landing[...], axis=0) if self.total else landing[...]

        return start, {}, finish


TILE = 256


class FeedForward:
    def __init__(self, normed, down, gate, up, grad_all, dps, groups):
        rows, width = normed.shape
        shape, chips = (SUB, rows // SUB, width), groups // 2
        held = gate.shape[0]
        ring = (2, down.shape[0] // 2, width)
        pair = 2 * rows
        self.inputs = [
            normed.reshape(shape),
            down.reshape(ring),
            gate,
            up,
            grad_all.reshape(chips, pair, width),
        ]
        self.in_specs = [VM, VM, ANY, ANY, ANY]
        act = jax.ShapeDtypeStruct((chips, pair, held), jnp.bfloat16)
        self.outs = [
            jax.ShapeDtypeStruct((groups,) + shape, jnp.bfloat16),
            jax.ShapeDtypeStruct((dps,) + ring, jnp.bfloat16),
            act,
            act,
            act,
        ]
        self.out_specs = [VM] * 5
        self.scratch = [
            pltpu.VMEM((held, width), jnp.bfloat16),
            pltpu.VMEM((held, width), jnp.bfloat16),
            pltpu.VMEM((chips, pair, width), jnp.bfloat16),
            pltpu.VMEM((chips, pair, held), jnp.float32),
            pltpu.VMEM((chips, pair, held), jnp.float32),
            pltpu.VMEM((dps, chips, pair, held // dps), jnp.float32),
            DMA((4,)),
            DMA,
        ]
        self.scratch += [DMA((chips, SUB))] * 6 + ring_sems(dps // 2)
        self.result = lambda hn, full, *acts: (
            hn.reshape(groups * rows, width),
            full.reshape(held, width),
            *[one.reshape(groups * rows, held) for one in acts],
        )

    def bind(self, place, x_ref, shard, gate_at, up_at, grad_at, *refs):
        hn, full, inner, dgate, dup, gate_w, up_w, grads, slope, silu, dinner = refs[:11]
        loads, own_line = refs[11:13]
        line_sems, ring_refs = refs[13:19], refs[19:]
        chip, chips = place.chip, place.chips
        pair, held = inner.shape[1:]
        width = gate_w.shape[1]
        own, start_line, step, arrived, sent = line_gather(place, x_ref, hn, own_line, *line_sems)
        ring = ring_gather(
            place,
            lambda half: shard.at[half],
            lambda chunk, half: full.at[chunk, half],
            *ring_refs,
        )
        copies = [
            pltpu.make_async_copy(gate_at, gate_w, loads.at[0]),
            pltpu.make_async_copy(up_at, up_w, loads.at[1]),
            pltpu.make_async_copy(grad_at, grads, loads.at[2]),
            pltpu.make_async_copy(shard, full.at[place.d], loads.at[3]),
        ]
        wide = 512 if held % 512 == 0 else held

        def start():
            start_line()
            ring[0]()
            for one in copies:
                one.start()

        def forward(at):
            rows = hn[pl.ds(2 * at, 2)].reshape(pair, width)
            for first in range(0, held, wide):
                span = slice(first, first + wide)
                gate = lax.dot_general(
                    rows, gate_w[span, :], contract_cols, preferred_element_type=jnp.float32
                )
                upward = lax.dot_general(
                    rows, up_w[span, :], contract_cols, preferred_element_type=jnp.float32
                )
                sigmoid = jax.nn.sigmoid(gate)
                passed = gate * sigmoid
                inner[at, :, span] = (passed * upward).astype(jnp.bfloat16)
                silu[at, :, span] = passed
                slope[at, :, span] = upward * sigmoid * (1.0 + gate * (1.0 - sigmoid))

        def when_there(at, there):
            @pl.when(there)
            def _():
                arrived(at)
                forward(at)

        chunk = held // place.dps
        early = chunk % 128 == 0

        def back(owner, part):
            def each(at, _):
                dinner[owner, at] = lax.dot_general(
                    grads[at], part, contract_cols, preferred_element_type=jnp.float32
                )
                return 0

            lax.fori_loop(0, chips, each, 0)

        def back_from(owner):
            back(owner, full[owner].reshape(chunk, width))

        def tick(hop, half):
            step(hop, half)
            if early and hop == 1 and half == 1:
                copies[2].wait()
                back(place.d, shard[...].reshape(chunk, width))
            if hop == 1 and half == 0:
                own.wait()
                copies[0].wait()
                copies[1].wait()
                arrived(chip)
                forward(chip)
            if hop > 1 and half == 0:
                when_there(chip - hop + 1, chip - hop + 1 >= 0)
            if hop > 1 and half == SUB - 1:
                when_there(chip + hop - 1, chip + hop - 1 < chips)

        def finish():
            last = chips - 1
            when_there(chip - last, chip - last >= 0)
            when_there(chip + last, chip + last < chips)
            copies[3].wait()
            if not early:
                copies[2].wait()
                ring[2]()
                last_all()
            else:
                ring[2](True)
                if place.hops > 2:
                    back_between()
                back_from(place.ring(place.hops))

                def each(at, _):
                    for q in range(place.dps):
                        span = slice(q * chunk, (q + 1) * chunk)
                        grad = dinner[q, at]
                        dgate[at, :, span] = (grad * slope[at, :, span]).astype(jnp.bfloat16)
                        dup[at, :, span] = (grad * silu[at, :, span]).astype(jnp.bfloat16)
                    return 0

                lax.fori_loop(0, chips, each, 0)
            sent()

        def back_between():
            for hop in range(1, place.hops):
                back_from(place.ring(hop))
                back_from(place.ring(-hop))

        def last_all():
            def each(at, _):
                rows = grads[at]
                for first in range(0, held, wide):
                    span = slice(first, first + wide)
                    part = full[first // chunk : (first + wide) // chunk].reshape(wide, width)
                    grad = lax.dot_general(
                        rows, part, contract_cols, preferred_element_type=jnp.float32
                    )
                    dgate[at, :, span] = (grad * slope[at, :, span]).astype(jnp.bfloat16)
                    dup[at, :, span] = (grad * silu[at, :, span]).astype(jnp.bfloat16)
                return 0

            lax.fori_loop(0, chips, each, 0)

        ticks = {
            (hop - 1) * SUB + half: functools.partial(tick, hop, half)
            for hop in range(1, chips)
            for half in range(SUB)
        }

        def with_ring(tick, hop):
            ticks[tick]()
            ring[1](hop)

        def with_near(tick):
            ticks[tick]()
            ring[3]()
            if place.hops == 2:
                back_between()

        merged = dict(ticks)
        for hop in range(1, place.hops):
            merged[2 * hop - 1] = functools.partial(with_ring, 2 * hop - 1, hop)
        if early:
            merged[2 * place.hops - 1] = functools.partial(with_near, 2 * place.hops - 1)
        return start, merged, finish


class Loaded:
    start = wait = staticmethod(lambda: None)


class FeedBack:
    def __init__(self, inner, dgate, dup, gate, up, down, normed, grads, dps, groups):
        length, held = inner.shape
        width, chips = normed.shape[1], groups // 2
        rows = length // groups
        shape = (SUB, rows // SUB, width)
        owned = (2, held // dps // 2, width)
        hops = dps // 2
        tile = (2, SUB, rows // SUB, width)
        self.inputs = [inner, dgate, dup, gate, up, down, normed, grads]
        self.in_specs = [ANY] * 8
        self.outs = [
            jax.ShapeDtypeStruct(shape, jnp.float32),
            jax.ShapeDtypeStruct(owned, jnp.float32),
            jax.ShapeDtypeStruct((held // TILE,) + tile, jnp.bfloat16),
            jax.ShapeDtypeStruct((held // TILE,) + tile, jnp.bfloat16),
            jax.ShapeDtypeStruct((chips,) + tile, jnp.bfloat16),
        ]
        self.out_specs = [VM, VM, ANY, ANY, ANY]
        act = pltpu.VMEM((length, held), jnp.bfloat16)
        weight = pltpu.VMEM((held, width), jnp.bfloat16)
        tokens = pltpu.VMEM((length, width), jnp.bfloat16)
        self.scratch = [act] * 3 + [weight] * 3 + [tokens] * 2
        self.scratch += [
            pltpu.VMEM((groups,) + shape, jnp.bfloat16),
            pltpu.VMEM((dps,) + owned, jnp.bfloat16),
            pltpu.VMEM((2,) + tile, jnp.bfloat16),
            DMA((8,)),
            DMA((2,)),
        ]
        self.scratch += line_scatter_scratch(chips, shape)
        self.scratch += (
            [pltpu.VMEM((hops,) + owned, jnp.bfloat16)] * 2
            + [pltpu.VMEM((hops - 1,) + owned, jnp.bfloat16)] * 2
            + ring_sems(hops)
        )
        self.result = lambda total, mine, gate_term, up_term, out: (
            total.reshape(rows, width),
            mine.reshape(held // dps, width),
            gate_term.reshape(held, width),
            up_term.reshape(held, width),
            out.reshape(length, width),
        )

    def bind(self, place, *refs):
        sources, refs = refs[:8], refs[8:]
        total_ref, own_ref, gate_out, up_out, result_out = refs[:5]
        inner, dgate, dup, gate, up, down, normed, grads = refs[5:13]
        p_ref, term, stage, loads, stage_sem = refs[13:18]
        line_refs, ring_refs = refs[18:27], refs[27:]
        chip, chips, hops = place.chip, place.chips, place.hops
        held, width = gate.shape
        pair = (inner.shape[0] if len(inner.shape) == 2 else inner.shape[0] * inner.shape[1]) // chips

        def flat(ref, lanes):
            value = ref[(slice(None),) * (len(ref.shape) - 1) + (lanes,)]
            return value.reshape(-1, value.shape[-1])

        chunk = held // place.dps
        wide = 1024 if width % 1024 == 0 else width
        send, step, finish_line = line_scatter(place, p_ref, total_ref, *line_refs)

        def put(half, value):
            own_ref[half] = value

        ring = ring_scatter(place, lambda at, half: term.at[at, half], put, *ring_refs)
        targets = [inner, dgate, dup, gate, up, down, normed, grads]
        copies = [
            pltpu.make_async_copy(source, target, loads.at[i])
            for i, (source, target) in enumerate(zip(sources, targets))
            if source is not None
        ] or [Loaded] * len(targets)

        def start():
            for i in (0, 7, 1, 3, 2, 4, 6, 5):
                copies[i].start()

        def rows_of(ref, at):
            if len(ref.shape) == 3:
                return ref[at]
            return ref[pl.ds(pl.multiple_of(at * pair, pair), pair), :]

        def partial(at):
            left, right = rows_of(dgate, at), rows_of(dup, at)
            for first in range(0, width, wide):
                span = slice(first, first + wide)
                value = jnp.dot(left, gate[:, span], preferred_element_type=jnp.float32)
                value += jnp.dot(right, up[:, span], preferred_element_type=jnp.float32)
                p_ref[pl.ds(2 * at, 2), :, :, span] = value.astype(jnp.bfloat16).reshape(
                    p_ref[pl.ds(2 * at, 2), :, :, span].shape
                )
            send(at)

        def term_rows(ref, other, start, count, span):
            return lax.dot_general(
                flat(ref, pl.ds(start, count)),
                flat(other, span),
                contract_rows,
                preferred_element_type=jnp.float32,
            ).astype(jnp.bfloat16)

        def down_tile(at):
            if chunk % 128 == 0:
                for first in range(0, width, wide):
                    span = slice(first, first + wide)
                    value = term_rows(inner, grads, pl.multiple_of(at * chunk, chunk), chunk, span)
                    term[at, :, :, span] = value.reshape(2, chunk // 2, wide)

        def down_all():
            if chunk % 128 != 0:
                for row in range(0, held, TILE):
                    for first in range(0, width, wide):
                        span = slice(first, first + wide)
                        value = term_rows(inner, grads, row, TILE, span)
                        term[row // chunk : (row + TILE) // chunk, :, :, span] = value.reshape(
                            TILE // chunk, 2, chunk // 2, wide
                        )

        jobs = []

        def first_job():
            copies[0].wait()
            copies[7].wait()
            down_all()
            down_tile(place.ring(hops))
            ring[3]()

        def next_job(hop):
            down_tile(place.ring(hop))
            down_tile(place.ring(-hop))
            if hop == hops - 1:
                ring[4]()

        for hop in range(hops - 1, 0, -1):
            jobs.append(functools.partial(next_job, hop))
            jobs.append(functools.partial(ring[1], hop))
        jobs.append(lambda: down_tile(place.d))

        count = [0]
        waits = []

        def staged(value_of, target):
            slot = count[0] % 2
            if count[0] >= 2:
                waits[count[0] - 2].wait()
            value_of(stage.at[slot])
            copy = pltpu.make_async_copy(stage.at[slot], target, stage_sem.at[slot])
            copy.start()
            waits.append(copy)
            count[0] += 1

        def weight_tile(ref, row, out):
            def fill(slot):
                for first in range(0, width, wide):
                    span = slice(first, first + wide)
                    value = term_rows(ref, normed, row, TILE, span)
                    slot[:, :, :, span] = value.reshape(slot.shape[:3] + (wide,))

            staged(fill, out.at[row // TILE])

        def result_tile(at):
            def fill(slot):
                left = rows_of(inner, at)
                for first in range(0, width, wide):
                    span = slice(first, first + wide)
                    value = jnp.dot(left, flat(down, span), preferred_element_type=jnp.float32)
                    slot[:, :, :, span] = value.astype(jnp.bfloat16).reshape(
                        slot.shape[:3] + (wide,)
                    )

            staged(fill, result_out.at[at])

        def sequence():
            first_job()
            for i in (1, 3, 2, 4):
                copies[i].wait()
            tiles = [
                functools.partial(weight_tile, ref, row, out)
                for ref, out in ((dgate, gate_out), (dup, up_out))
                for row in range(0, held, TILE)
            ]
            tiles += [functools.partial(result_tile, at) for at in range(chips)]
            done = [0]

            def fill(most):
                for _ in range(most):
                    if tiles:
                        if done[0] == 0:
                            copies[6].wait()
                        if done[0] == 2 * (held // TILE):
                            copies[5].wait()
                        done[0] += 1
                        tiles.pop(0)()

            for wave in range(chips - 1):
                high = chips - 1 - wave
                ups = (high > chip).astype(jnp.int32)
                downs = (wave < chip).astype(jnp.int32)

                def each(i, _, high=high, wave=wave, ups=ups):
                    partial(jnp.where(i < ups, high, wave))
                    return 0

                lax.fori_loop(0, ups + downs, each, 0)
                fill(1)
                step(wave, 0)
                if wave == 0:
                    step(wave, 1)
                    jobs.pop(0)()
                else:
                    fill(1)
                    step(wave, 1)
                    if jobs:
                        jobs.pop(0)()
            partial(chip)
            for job in jobs:
                job()
            fill(len(tiles))

        def finish():
            ring[2]()
            finish_line()
            for copy in waits[-2:]:
                copy.wait()

        return start, {0: sequence}, finish


class Feed:
    def __init__(self, normed, down, gate, up, grad_all, dps, groups):
        forth = FeedForward(normed, down, gate, up, grad_all, dps, groups)
        act = jax.ShapeDtypeStruct((grad_all.shape[0], gate.shape[0]), jnp.bfloat16)
        back = FeedBack(act, act, act, gate, up, gate, grad_all, grad_all, dps, groups)
        self.forth, self.back = forth, back
        self.inputs, self.in_specs = forth.inputs, forth.in_specs
        self.outs, self.out_specs, self.result = back.outs, back.out_specs, back.result
        self.scratch = [pltpu.VMEM(out.shape, out.dtype) for out in forth.outs]
        self.scratch += forth.scratch[:3] + forth.scratch[6:] + back.scratch[12:]

    def bind(self, place, *refs):
        inputs, outs, held, refs = refs[:5], refs[5:10], refs[10:18], refs[18:]
        hn, full, inner, dgate, dup, gate, up, grads = held
        split = len(self.forth.scratch) - 6
        forth_sems, back_refs = refs[:split], refs[split:]

        def run_forth(*local):
            start, ticks, finish = self.forth.bind(place, *inputs, *held, *local, *forth_sems)
            start()
            for tick in sorted(ticks):
                ticks[tick]()
            finish()

        def run_back(*local):
            shared = (inner, dgate, dup, gate, up, full, hn, grads)
            _, ticks, finish = self.back.bind(
                place, *[None] * 8, *outs, *shared, *local, None, *back_refs
            )
            ticks[0]()
            finish()

        def run():
            pl.run_scoped(run_forth, *self.forth.scratch[3:6])
            pl.run_scoped(run_back, *self.back.scratch[8:11])

        return lambda: None, {0: run}, lambda: None


def move(parts, dps, groups, number, greet=greet_near):
    def kernel(*refs):
        place = Place(dps, groups)
        at = [
            0,
            sum(len(part.inputs) for part in parts),
            sum(len(part.inputs) + len(part.outs) for part in parts),
        ]
        bound = []
        for part in parts:
            mine = []
            for kind, length in enumerate((len(part.inputs), len(part.outs), len(part.scratch))):
                mine += refs[at[kind] : at[kind] + length]
                at[kind] += length
            bound.append(part.bind(place, *mine))
        greet(place)
        for start, _, _ in bound:
            start()
        for tick in range(1 + max([0] + [max(list(ticks) + [0]) for _, ticks, _ in bound])):
            for _, ticks, _ in bound:
                if tick in ticks:
                    ticks[tick]()
        for _, _, finish in bound:
            finish()

    outs = pl.pallas_call(
        kernel,
        out_shape=[out for part in parts for out in part.outs],
        in_specs=[spec for part in parts for spec in part.in_specs],
        out_specs=[spec for part in parts for spec in part.out_specs],
        scratch_shapes=[one for part in parts for one in part.scratch],
        compiler_params=pltpu.CompilerParams(
            collective_id=number, has_side_effects=True, vmem_limit_bytes=63 << 20
        ),
        cost_estimate=pl.CostEstimate(flops=0, bytes_accessed=120_000_000, transcendentals=0),
        name=f"move_{number}",
    )(*[x for part in parts for x in part.inputs])
    results, at = [], 0
    for part in parts:
        results.append(part.result(*outs[at : at + len(part.outs)]))
        at += len(part.outs)
    return results


def norm_factor(values):
    return lax.rsqrt(jnp.mean(values * values, axis=-1, keepdims=True) + epsilon)


def norm_grad(values, factor, gain, gradient):
    weighted = gradient * gain
    inner_mean = jnp.mean(weighted * values, axis=-1, keepdims=True)
    return factor * weighted - values * (factor * factor * factor) * inner_mean


def rope_tables(positions, head_width):
    half_width = head_width // 2
    frequency = rope_base ** (-2.0 * jnp.arange(half_width, dtype=jnp.float32) / head_width)
    angles = positions.astype(jnp.float32)[:, None] * frequency[None, :]
    return (jnp.cos(angles)[:, None, :], jnp.sin(angles)[:, None, :])


def rotate(values, cosine_table, sine_table):
    half_width = values.shape[-1] // 2
    first_half = values[..., :half_width]
    second_half = values[..., half_width:]
    return jnp.concatenate(
        [
            first_half * cosine_table - second_half * sine_table,
            second_half * cosine_table + first_half * sine_table,
        ],
        axis=-1,
    )


def block_scores(query_block, key_heads, lower, upper, score_scale):
    scores = (
        jnp.einsum(
            "qhd,kd->hqk", query_block, key_heads[:upper], preferred_element_type=jnp.float32
        )
        * score_scale
    )
    rows_at = lower + jnp.arange(query_block.shape[0], dtype=jnp.int32)
    cols_at = jnp.arange(upper, dtype=jnp.int32)
    allowed = (cols_at[None, :] <= rows_at[:, None])[None]
    return jnp.where(allowed, scores, masked_value)


def per_device(
    tokens,
    qkv_weight,
    out_weight,
    gate_weight,
    up_weight,
    down_weight,
    attn_gain,
    mlp_gain,
    cotangent,
):
    groups = lax.axis_size("seq")
    dps = lax.axis_size("dp")
    tok_rows = tokens.shape[1]
    model_width = tokens.shape[2]
    weight_rows = qkv_weight.shape[0]
    seq_len = tok_rows * groups
    local_heads = HEADS // groups
    local_width = local_heads * HEAD_DIM
    kv_copies = groups // KV_HEADS
    score_scale = HEAD_DIM ** (-0.5)
    block_rows = min(512, seq_len)
    block_count = seq_len // block_rows
    fold = groups // dps
    order = [(at % dps) * fold + at // dps for at in range(groups)]

    gain_width = attn_gain.shape[0]
    tile = jnp.zeros((8, 128), jnp.float32)
    tile = tile.at[0, :gain_width].set(attn_gain.astype(jnp.float32))
    tile = tile.at[1, :gain_width].set(mlp_gain.astype(jnp.float32))
    qkv_local, out_rows, normed_all, gate_part, gains = move(
        [
            Columns(qkv_weight, order, local_width, kv_copies, dps, groups),
            Rows(out_weight, dps, groups),
            LineGather(tokens[0], dps, groups, normed=True),
            RingGather(gate_weight, dps, groups, late=True),
            Spread(tile, False, dps, groups),
        ],
        dps,
        groups,
        1,
        greet_all,
    )
    gain_one = gains[:, 0, :gain_width].reshape(model_width)
    gain_two = gains[:, 1, :gain_width].reshape(model_width)

    x_rows = tokens[0].astype(jnp.float32)
    factor_one = norm_factor(x_rows)
    qkv_gained = (qkv_local.astype(jnp.float32) * gain_one[:, None]).astype(jnp.bfloat16)
    grad_low = cotangent[0]
    grad_low, _ = lax.optimization_barrier((grad_low, gains))
    grad_all = lax.all_gather(grad_low, "seq", axis=0, tiled=True)

    mixed = jnp.dot(normed_all, qkv_gained, preferred_element_type=jnp.float32)
    cosine_table, sine_table = rope_tables(jnp.arange(seq_len, dtype=jnp.int32), HEAD_DIM)
    query_heads = rotate(
        mixed[:, :local_width].reshape(seq_len, local_heads, HEAD_DIM), cosine_table, sine_table
    ).astype(jnp.bfloat16)
    key_heads = rotate(
        mixed[:, None, local_width : local_width + HEAD_DIM], cosine_table, sine_table
    ).astype(jnp.bfloat16)[:, 0]
    value_heads = mixed[:, local_width + HEAD_DIM :].astype(jnp.bfloat16)
    outputs = []
    log_sums = []
    for block in range(block_count):
        lower = block * block_rows
        upper = lower + block_rows
        scores = block_scores(query_heads[lower:upper], key_heads, lower, upper, score_scale)
        highest = jnp.max(scores, axis=-1, keepdims=True)
        log_sum = highest + jnp.log(jnp.sum(jnp.exp(scores - highest), axis=-1, keepdims=True))
        probs = jnp.exp(scores - log_sum).astype(jnp.bfloat16)
        attended = jnp.einsum(
            "hqk,kd->qhd", probs, value_heads[:upper], preferred_element_type=jnp.float32
        )
        outputs.append(attended.astype(jnp.bfloat16))
        log_sums.append(log_sum)
    attended = jnp.concatenate(outputs, axis=0).reshape(seq_len, local_width)
    up_part, summed = move(
        [
            RingGather(up_weight, dps, groups),
            LineProduct(attended, out_rows, (((1,), (0,)), ((), ())), dps, groups),
        ],
        dps,
        groups,
        2,
    )
    hidden = x_rows + summed
    factor_two = norm_factor(hidden)
    normed_two = (hidden * factor_two * gain_two).astype(jnp.bfloat16)
    ((grad_normed, down_owned, gate_term, up_term, result),) = move(
        [Feed(normed_two, down_weight, gate_part, up_part, grad_all, dps, groups)],
        dps,
        groups,
        3,
    )
    gain_two_term = jnp.sum(grad_normed * hidden * factor_two, axis=0)
    grad_hidden = grad_low.astype(jnp.float32) + norm_grad(
        hidden, factor_two, gain_two, grad_normed
    )
    grad_branch, gate_owned = move(
        [
            LineGather(grad_hidden.astype(jnp.bfloat16), dps, groups),
            RingScatter(gate_term, dps, groups),
        ],
        dps,
        groups,
        5,
    )
    result, grad_branch = lax.optimization_barrier((result, grad_branch))
    mlp_result = lax.psum_scatter(result, "seq", scatter_dimension=0, tiled=True)
    block_out = (hidden + mlp_result.astype(jnp.float32)).astype(jnp.bfloat16)[None]
    out_term = lax.dot_general(
        attended, grad_branch, contract_rows, preferred_element_type=jnp.float32
    ).astype(jnp.bfloat16)
    grad_heads = (
        lax.dot_general(grad_branch, out_rows, contract_cols, preferred_element_type=jnp.float32)
        .astype(jnp.bfloat16)
        .reshape(seq_len, local_heads, HEAD_DIM)
    )
    grad_keys = jnp.zeros((seq_len, HEAD_DIM), jnp.float32)
    grad_values = jnp.zeros((seq_len, HEAD_DIM), jnp.float32)
    grad_queries = []
    for block in range(block_count):
        lower = block * block_rows
        upper = lower + block_rows
        query_block = query_heads[lower:upper]
        grad_block = grad_heads[lower:upper]
        scores = block_scores(query_block, key_heads, lower, upper, score_scale)
        probs = jnp.exp(scores - log_sums[block])
        probs_low = probs.astype(jnp.bfloat16)
        grad_probs = jnp.einsum(
            "qhd,kd->hqk", grad_block, value_heads[:upper], preferred_element_type=jnp.float32
        )
        row_delta = jnp.sum(probs * grad_probs, axis=-1, keepdims=True)
        grad_scores = (probs * (grad_probs - row_delta)).astype(jnp.bfloat16)
        grad_queries.append(
            jnp.einsum(
                "hqk,kd->qhd", grad_scores, key_heads[:upper], preferred_element_type=jnp.float32
            )
            * score_scale
        )
        grad_keys = grad_keys.at[:upper].add(
            jnp.einsum("hqk,qhd->kd", grad_scores, query_block, preferred_element_type=jnp.float32)
            * score_scale
        )
        grad_values = grad_values.at[:upper].add(
            jnp.einsum("hqk,qhd->kd", probs_low, grad_block, preferred_element_type=jnp.float32)
        )
    grad_q = rotate(jnp.concatenate(grad_queries, axis=0), cosine_table, -sine_table)
    grad_k = rotate(grad_keys[:, None], cosine_table, -sine_table)[:, 0]
    grad_mixed = jnp.concatenate(
        [grad_q.reshape(seq_len, local_width), grad_k, grad_values], axis=1
    ).astype(jnp.bfloat16)
    qkv_term = lax.dot_general(
        normed_all, grad_mixed, contract_rows, preferred_element_type=jnp.float32
    )
    partial = lax.dot_general(
        grad_mixed, qkv_local, contract_cols, preferred_element_type=jnp.float32
    )
    gain_one_term = jnp.sum(qkv_term * qkv_local.astype(jnp.float32), axis=1)
    qkv_term = (qkv_term * gain_one[:, None]).astype(jnp.bfloat16)
    terms = jnp.stack([gain_one_term, gain_two_term]).reshape(2, dps * groups, gain_width)
    terms = jnp.pad(terms.transpose(1, 0, 2), ((0, 0), (0, 6), (0, 128 - gain_width)))
    qkv_owned, out_owned, grad_normed_one, up_owned, gain_grads = move(
        [
            ColumnsBack(qkv_term, order, local_width, kv_copies, weight_rows, dps, groups),
            RowsBack(out_term, weight_rows, dps, groups),
            LineScatter(partial.astype(jnp.bfloat16), dps, groups),
            RingScatter(up_term, dps, groups, late=True),
            Spread(terms, True, dps, groups),
        ],
        dps,
        groups,
        6,
        greet_all,
    )
    grad_input = grad_hidden + norm_grad(x_rows, factor_one, gain_one, grad_normed_one)
    return (
        block_out,
        grad_input[None],
        qkv_owned,
        out_owned,
        gate_owned,
        up_owned,
        down_owned,
        gain_grads[0, :gain_width],
        gain_grads[1, :gain_width],
    )


def solution(mesh):
    rows = P(("dp", "seq"), None)
    tokens = P("dp", "seq", None)
    gains = P(("dp", "seq"))
    return jax.shard_map(
        per_device,
        mesh=mesh,
        in_specs=(tokens, rows, rows, rows, rows, rows, gains, gains, tokens),
        out_specs=(tokens, tokens, rows, rows, rows, rows, rows, gains, gains),
        check_vma=False,
    )
```
